32 devices in a mesh: dp: 2 (over y), expert: 16 (over z, x, core).
Axes of the slice: x: 2, y: 2, z: 4, core: 2. Of those that a mesh axis runs over, the one named last changes fastest.
Arguments:
- tokens: bfloat16 [4096, 1024], P(('dp', 'expert')), may hold values from -6 to 6
- segments: int32 [4096], P(('dp', 'expert')), may hold values from 0 to 127, never falling along the last dimension, each value on 1 to 128 neighbouring positions
- routes: int32 [4096, 8], P(('dp', 'expert')), may hold values from 0 to 15, all different within a row; in each aligned block of 128 rows (0 to 127, 128 to 255, ...) at most 80 rows name the same one
- first_gain: bfloat16 [1024], P('dp'), may hold values from 0.5 to 1.5
- query_weight: bfloat16 [1024, 1024], P('dp'), may hold values from -0.75 to 0.75
- key_projection_weight: bfloat16 [1024, 512], P('dp'), may hold values from -0.75 to 0.75
- value_projection_weight: bfloat16 [1024, 512], P('dp'), may hold values from -0.1875 to 0.1875
- out_weight: bfloat16 [1024, 1024], P('dp'), may hold values from -0.75 to 0.75
- second_gain: bfloat16 [1024], P('dp'), may hold values from 0.5 to 1.5
- router_weight: bfloat16 [1024, 16], P('dp'), may hold values from -0.375 to 0.375
- gate_weight: bfloat16 [16, 1024, 512], P('expert'), may hold values from -0.1875 to 0.1875
- up_weight: bfloat16 [16, 1024, 512], P('expert'), may hold values from -0.1875 to 0.1875
- down_weight: bfloat16 [16, 512, 1024], P('expert'), may hold values from -0.5 to 0.5
- cotangent: bfloat16 [4096, 1024], P(('dp', 'expert')), may hold values from -6 to 6
Outputs:
- output: bfloat16 [4096, 1024], P(('dp', 'expert'))
- grad_tokens: float32 [4096, 1024], P(('dp', 'expert'))
- first_gain_grad: float32 [1024], P('dp')
- query_weight_grad: float32 [1024, 1024], P('dp')
- key_weight_grad: float32 [1024, 512], P('dp')
- value_weight_grad: float32 [1024, 512], P('dp')
- out_weight_grad: float32 [1024, 1024], P('dp')
- second_gain_grad: float32 [1024], P('dp')
- router_weight_grad: float32 [1024, 16], P('dp')
- gate_weight_grad: float32 [16, 1024, 512], P('expert', 'dp')
- up_weight_grad: float32 [16, 1024, 512], P('expert', 'dp')
- down_weight_grad: float32 [16, 512, 1024], P('expert', None, 'dp')
The draws below stay inside these ranges and needn't reach their ends.
Inputs may be any that keep to these rules, and one draw needn't show every extreme that they name: `routes`: within the rows of one device (aligned blocks of 128 tokens) no expert is named by more than 80 rows; in some block one expert is named by exactly 80. A row names 8 different experts. `segments`: segment numbers never fall along the tokens; a segment holds 1 to 128 tokens and one holds exactly 128.
All inputs are finite; a program needn't handle non-finite values.
Results may differ from the reference program's by a relative error of at most 0.02.
The reference program's roundings to bfloat16 on the way count: a program that leaves them out, or rounds other values in their place, can miss the bound.
Values may be sent and summed in bfloat16 or wider, within the bound.
A program may use at most 128 MiB of HBM per device.

```python
import math
import jax
import jax.numpy as jnp
import numpy as np
from jax import lax

MODEL_DIM = 1024
QUERY_HEADS = 16
KEY_VALUE_HEADS = 8
HEAD_DIM = 64
FF = 512
TOPK = 8
SEQUENCE_LENGTH = 128
TOK_DEV = 128
TOKENS = 4096
EXPERTS = 16
CAP = 80
N_DP = 2
N_EXPERT = 16


def level_of(key, dims, cuts, smallest, largest):
    gain = 1.0
    for axis_at, parts in cuts:
        draws = jax.random.uniform(jax.random.fold_in(jax.random.fold_in(key, 6), axis_at), (parts,), jnp.float32, smallest / len(cuts), largest / len(cuts))
        gain = gain * jnp.repeat(jnp.exp(draws), dims[axis_at] // parts).reshape((-1,) + (1,) * (len(dims) - 1 - axis_at))
    return gain


def split_up(amount, total, reach, skew):
    portions = [(1 << 20) // math.isqrt(grade ** skew) + 1 for grade in range(2, amount + 1)]
    surplus, holding = total - reach - (amount - 1), [1] * (amount - 1)
    while surplus > 0:
        free = [i for i in range(amount - 1) if holding[i] < reach]
        pool, left = sum([portions[i] for i in free]), surplus
        for i in free:
            addition = min(reach - holding[i], max(1, left * portions[i] // pool), surplus)
            holding[i] = holding[i] + addition
            surplus = surplus - addition
    return np.array([reach] + holding)


def uneven(stream_key, count, total, limit, slope):
    if count == 2:
        one = jax.random.randint(stream_key, (), max(1, total - limit), min(limit, total - 1) + 1)
        return jnp.stack([one, total - one])
    sizes = jnp.asarray(split_up(count, total, limit, slope), jnp.int32)
    couples = (count - 1) // 2
    donor, receiver = sizes[1:1 + 2 * couples:2], sizes[2:2 + 2 * couples:2]
    slack = jnp.minimum(donor - 1, limit - receiver)
    moved = jax.random.randint(jax.random.fold_in(stream_key, 1), (couples,), 0, 1 << 20) % (slack + 1)
    sizes = sizes.at[1:1 + 2 * couples:2].set(donor - moved).at[2:2 + 2 * couples:2].set(receiver + moved)
    return sizes[jax.random.permutation(jax.random.fold_in(stream_key, 2), count)]


def assign_block(own_key, own, number, rows, amount, top, bound, skew):
    order = jax.random.permutation(own_key, amount)
    packed, ordinary = load_shares(amount, rows * top, bound, skew, True), load_shares(amount, rows * top, bound, skew, False)
    places = jnp.arange(amount)

    def named(sizes, offset_by):
        used = int((sizes > 0).sum())
        fixed = max(1, used // 4)
        moved = fixed + (places - fixed + offset_by * (used - fixed)) % max(1, amount - fixed)
        return jnp.zeros((amount,), jnp.int32).at[order[jnp.where(places < fixed, places, moved)]].set(jnp.asarray(sizes, jnp.int32))

    sizes = jnp.where(number % 4 == 0, named(packed, number // 4), named(ordinary, number - number // 4 - 1))
    mixed = jax.random.permutation(jax.random.fold_in(own, 3), amount)
    giver, taker = mixed[0:amount // 2 * 2:2], mixed[1:amount // 2 * 2:2]
    slack = jnp.minimum(sizes[giver] - 1, bound - sizes[taker]) // 2
    slack = jnp.where((giver == order[0]) | (taker == order[0]) | (sizes[taker] == 0), 0, jnp.maximum(slack, 0))
    moved = jax.random.randint(jax.random.fold_in(own, 4), (amount // 2,), 0, 1 << 20) % (slack + 1)
    sizes = sizes.at[giver].add(-moved).at[taker].add(moved)
    labels = jnp.searchsorted(jnp.cumsum(sizes), jnp.arange(rows * top), side="right").astype(jnp.int32)
    table = labels.reshape(top, rows).T
    table = table[jax.random.permutation(jax.random.fold_in(own, 1), rows)]
    offset_by = jax.random.randint(jax.random.fold_in(own, 2), (rows, 1), 0, top)
    return jnp.take_along_axis(table, (jnp.arange(top)[None, :] + offset_by) % top, axis=1)


def load_shares(number_of, total, reach, skew, full):
    loads = [(1 << 20) // math.isqrt(rank ** skew) + 1 for rank in range(1, number_of + 1)]
    largest = reach if full else min(reach, max(-(-total // number_of), total * loads[0] // sum(loads)))
    least = 1 if total - largest >= number_of - 1 else 0
    holding, surplus = [largest] + [least] * (number_of - 1), total - largest - least * (number_of - 1)
    while surplus > 0:
        movable = [i for i in range(1, number_of) if holding[i] < largest] or [i for i in range(1, number_of) if holding[i] < reach]
        mass, budget = sum([loads[i] for i in movable]), surplus
        for i in movable:
            addition = min(reach - holding[i], max(1, budget * loads[i] // mass), surplus)
            holding[i] = holding[i] + addition
            surplus = surplus - addition
    return np.array(holding)


def gaussian(own_key, shape, width, most, shards=(), kind=jnp.bfloat16):
    values = jax.random.normal(own_key, shape, jnp.float32) * width
    if len(shards) > 0:
        values = level_of(own_key, shape, shards, -0.22, 0.18) * values
    return jnp.clip(values, min=-most, max=most).astype(kind)


def setup_inputs(seed: int = 0) -> dict:
    seeds = jax.random.split(jax.random.key(seed), 15)
    tokens = gaussian(seeds[0], (TOKENS, MODEL_DIM), 1.0, 6.0, ((0, 32),))
    segments = jnp.searchsorted(jnp.cumsum(uneven(seeds[1], TOKENS // (SEQUENCE_LENGTH // 4), TOKENS, SEQUENCE_LENGTH, 0)), jnp.arange(TOKENS), side="right").astype(jnp.int32)
    routes_keys = jax.random.split(jax.random.fold_in(seeds[2], 1), TOKENS // TOK_DEV)
    routes_turns = jax.random.permutation(jax.random.fold_in(seeds[2], 3), TOKENS // TOK_DEV)
    routes = jax.vmap(lambda own, number: assign_block(jax.random.fold_in(seeds[2], 2), own, number, TOK_DEV, EXPERTS, TOPK, CAP, 1))(routes_keys, routes_turns).reshape((TOKENS, TOPK))
    first_gain = jnp.clip(1.0 + 0.1 * jax.random.normal(seeds[3], (MODEL_DIM,), jnp.float32), 0.5, 1.5).astype(jnp.bfloat16)
    query_weight = gaussian(seeds[4], (MODEL_DIM, QUERY_HEADS * HEAD_DIM), (MODEL_DIM // 16) ** -0.5, 0.75, ((0, 2),))
    key_projection_weight = gaussian(seeds[5], (MODEL_DIM, KEY_VALUE_HEADS * HEAD_DIM), (MODEL_DIM // 16) ** -0.5, 0.75, ((0, 2),))
    value_projection_weight = gaussian(seeds[6], (MODEL_DIM, KEY_VALUE_HEADS * HEAD_DIM), MODEL_DIM ** -0.5, 0.1875, ((0, 2),))
    out_weight = gaussian(seeds[7], (QUERY_HEADS * HEAD_DIM, MODEL_DIM), (QUERY_HEADS * HEAD_DIM // 16) ** -0.5, 0.75, ((0, 2),))
    second_gain = jnp.clip(1.0 + 0.1 * jax.random.normal(seeds[8], (MODEL_DIM,), jnp.float32), 0.5, 1.5).astype(jnp.bfloat16)
    router_weight = gaussian(seeds[9], (MODEL_DIM, EXPERTS), (MODEL_DIM // 4) ** -0.5, 0.375, ((0, 2),))
    gate_weight = gaussian(seeds[10], (EXPERTS, MODEL_DIM, FF), MODEL_DIM ** -0.5, 0.1875, ((0, 16),))
    up_weight = gaussian(seeds[11], (EXPERTS, MODEL_DIM, FF), MODEL_DIM ** -0.5, 0.1875, ((0, 16),))
    down_weight = gaussian(seeds[12], (EXPERTS, FF, MODEL_DIM), (FF // 4) ** -0.5, 0.5, ((0, 16),))
    cotangent = gaussian(seeds[13], (TOKENS, MODEL_DIM), 1.0, 6.0, ((0, 32),))
    return {"tokens": tokens, "segments": segments, "routes": routes, "first_gain": first_gain, "query_weight": query_weight, "key_projection_weight": key_projection_weight, "value_projection_weight": value_projection_weight, "out_weight": out_weight, "second_gain": second_gain, "router_weight": router_weight, "gate_weight": gate_weight, "up_weight": up_weight, "down_weight": down_weight, "cotangent": cotangent}


EPSILON = 1e-06
SCORE_SCALE = 0.015625
ROPE_BASE = 10000.0
MASKED = -1e+30

def product(pattern, left_op, right_op):
    return jnp.einsum(pattern, left_op.astype(jnp.float32), right_op.astype(jnp.float32))

def matrix_multiply(left_op, right_op):
    return jnp.dot(left_op, right_op, preferred_element_type=jnp.float32)

def rope_tables(seq_len, head_size):
    positions = jnp.arange(seq_len, dtype=jnp.float32)
    exponent = jnp.arange(head_size // 2, dtype=jnp.float32) * (2.0 / head_size)
    angles = positions[:, None] * (ROPE_BASE ** (-exponent))[None, :]
    return (jnp.cos(angles)[None, :, None, :], jnp.sin(angles)[None, :, None, :])

def apply_rotary(values, cosine_table, sine_table):
    middle = values.shape[-1] // 2
    first_half = values[..., :middle]
    second_half = values[..., middle:]
    return jnp.concatenate([first_half * cosine_table - second_half * sine_table, second_half * cosine_table + first_half * sine_table], -1)

def inverse_rotary(gradient, cosine_table, sine_table):
    middle = gradient.shape[-1] // 2
    first_half = gradient[..., :middle]
    second_half = gradient[..., middle:]
    return jnp.concatenate([first_half * cosine_table + second_half * sine_table, second_half * cosine_table - first_half * sine_table], -1)

def normalize(values, gain_vec):
    factor = lax.rsqrt(lax.optimization_barrier(jnp.mean(values * values, -1, keepdims=True)) + EPSILON)
    normed = values * factor
    return (normed, factor, (normed * gain_vec).astype(jnp.bfloat16))

def normalize_back(gradient, normed, factor, gain_vec):
    gain_grad = lax.optimization_barrier(jnp.sum(gradient * normed, 0))
    scaled = gradient * gain_vec
    return (factor * (scaled - normed * lax.optimization_barrier(jnp.mean(scaled * normed, -1, keepdims=True))), gain_grad)

def segment_mask(segments):
    seq_len = segments.shape[1]
    causal = jnp.arange(seq_len)[:, None] >= jnp.arange(seq_len)[None, :]
    same_doc = segments[:, :, None] == segments[:, None, :]
    return (same_doc & causal[None])[:, None, None]

def score_table(query_rows, key_row_block, mask_tab):
    raw_scores = product('sqhgw,skhw->shgqk', query_rows, key_row_block) * SCORE_SCALE
    return jnp.where(mask_tab, raw_scores, MASKED)

def mixer_forward(tokens, segments, gain_vec, query_mat, key_matrix, value_matrix, out_mat):
    token_rows = tokens.shape[0]
    local_sequences = token_rows // SEQUENCE_LENGTH
    query_groups = QUERY_HEADS // KEY_VALUE_HEADS
    cosine_table, sine_table = rope_tables(SEQUENCE_LENGTH, HEAD_DIM)
    mask_tab = segment_mask(segments.reshape(local_sequences, SEQUENCE_LENGTH))
    residual = tokens.astype(jnp.float32)
    normed, factor, attention_input = normalize(residual, gain_vec)
    query_rows = apply_rotary(matrix_multiply(attention_input, query_mat).reshape(local_sequences, SEQUENCE_LENGTH, QUERY_HEADS, HEAD_DIM), cosine_table, sine_table)
    query_rows = query_rows.astype(jnp.bfloat16).reshape(local_sequences, SEQUENCE_LENGTH, KEY_VALUE_HEADS, query_groups, HEAD_DIM)
    key_row_block = apply_rotary(matrix_multiply(attention_input, key_matrix).reshape(local_sequences, SEQUENCE_LENGTH, KEY_VALUE_HEADS, HEAD_DIM), cosine_table, sine_table).astype(jnp.bfloat16)
    value_row_block = matrix_multiply(attention_input, value_matrix).astype(jnp.bfloat16).reshape(local_sequences, SEQUENCE_LENGTH, KEY_VALUE_HEADS, HEAD_DIM)
    scores = score_table(query_rows, key_row_block, mask_tab)
    row_peak = lax.optimization_barrier(jnp.max(scores, -1, keepdims=True))
    logsum = row_peak + jnp.log(lax.optimization_barrier(jnp.sum(jnp.exp(scores - row_peak), -1, keepdims=True)))
    weights = jnp.exp(scores - logsum).astype(jnp.bfloat16)
    attended = product('shgqk,skhw->sqhgw', weights, value_row_block).astype(jnp.bfloat16)
    hidden = residual + matrix_multiply(attended.reshape(token_rows, QUERY_HEADS * HEAD_DIM), out_mat)
    saved = (normed, factor, attention_input, query_rows, key_row_block, value_row_block, attended, logsum, mask_tab, cosine_table, sine_table)
    return (hidden, saved)

def mixer_backward(grad_hidden, saved, gain_vec, query_mat, key_matrix, value_matrix, out_mat):
    normed, factor, attention_input, query_rows, key_row_block, value_row_block, attended, logsum, mask_tab, cosine_table, sine_table = saved
    token_rows = grad_hidden.shape[0]
    local_sequences = token_rows // SEQUENCE_LENGTH
    grad_round = grad_hidden.astype(jnp.bfloat16)
    out_grad = matrix_multiply(attended.reshape(token_rows, QUERY_HEADS * HEAD_DIM).T, grad_round)
    grad_attended = matrix_multiply(grad_round, out_mat.T).astype(jnp.bfloat16).reshape(query_rows.shape)
    scores = score_table(query_rows, key_row_block, mask_tab)
    prob_full = jnp.exp(scores - logsum)
    values_gradient = product('shgqk,sqhgw->skhw', prob_full.astype(jnp.bfloat16), grad_attended)
    grad_weights = product('sqhgw,skhw->shgqk', grad_attended, value_row_block)
    row_delta = product('sqhgw,sqhgw->shgq', grad_attended, attended)[..., None]
    grad_scores = (prob_full * (grad_weights - row_delta) * SCORE_SCALE).astype(jnp.bfloat16)
    grad_queries = product('shgqk,skhw->sqhgw', grad_scores, key_row_block)
    keys_gradient = product('shgqk,sqhgw->skhw', grad_scores, query_rows)
    query_grad = inverse_rotary(grad_queries.reshape(local_sequences, SEQUENCE_LENGTH, QUERY_HEADS, HEAD_DIM), cosine_table, sine_table)
    query_grad = query_grad.astype(jnp.bfloat16).reshape(token_rows, QUERY_HEADS * HEAD_DIM)
    key_gradient = inverse_rotary(keys_gradient, cosine_table, sine_table).astype(jnp.bfloat16).reshape(token_rows, KEY_VALUE_HEADS * HEAD_DIM)
    value_gradient = values_gradient.astype(jnp.bfloat16).reshape(token_rows, KEY_VALUE_HEADS * HEAD_DIM)
    query_wgrad = matrix_multiply(attention_input.T, query_grad)
    key_wgrad = matrix_multiply(attention_input.T, key_gradient)
    value_wgrad = matrix_multiply(attention_input.T, value_gradient)
    grad_attn_input = matrix_multiply(query_grad, query_mat.T) + matrix_multiply(key_gradient, key_matrix.T) + matrix_multiply(value_gradient, value_matrix.T)
    grad_normed, gain_grad = normalize_back(grad_attn_input, normed, factor, gain_vec)
    return (grad_hidden + grad_normed, gain_grad, query_wgrad, key_wgrad, value_wgrad, out_grad)

def route_weights(expert_input, router_mat, routes):
    logits = matrix_multiply(expert_input, router_mat)
    chosen_hot = (routes[:, :, None] == jnp.arange(router_mat.shape[1], dtype=jnp.int32)[None, None, :]).astype(jnp.float32)
    chosen = lax.optimization_barrier(jnp.sum(chosen_hot * logits[:, None, :], -1))
    return (jax.nn.softmax(chosen, -1), chosen_hot)

def route_back(route_prob, grad_prob, chosen_hot):
    grad_chosen = route_prob * (grad_prob - lax.optimization_barrier(jnp.sum(route_prob * grad_prob, -1, keepdims=True)))
    return lax.optimization_barrier(jnp.sum(chosen_hot * grad_chosen[:, :, None], 1)).astype(jnp.bfloat16)

def expert_forward(owner_rows, gate_mat, up_mat, down_mat):
    gate_pre = product('erd,edf->erf', owner_rows, gate_mat)
    up_pre = product('erd,edf->erf', owner_rows, up_mat)
    gate_sig = jax.nn.sigmoid(gate_pre)
    gate_act = gate_pre * gate_sig
    inner_acts = (gate_act * up_pre).astype(jnp.bfloat16)
    expert_out = product('erf,efd->erd', inner_acts, down_mat).astype(jnp.bfloat16)
    return (expert_out, (gate_pre, up_pre, gate_sig, gate_act, inner_acts))

def expert_backward(grad_rows, owner_rows, kept_acts, gate_mat, up_mat, down_mat):
    gate_pre, up_pre, gate_sig, gate_act, inner_acts = kept_acts
    grad_inner = product('erd,efd->erf', grad_rows, down_mat)
    down_grad = product('erf,erd->efd', inner_acts, grad_rows)
    silu_slope = gate_sig * (1.0 + gate_pre * (1.0 - gate_sig))
    grad_gate = (grad_inner * up_pre * silu_slope).astype(jnp.bfloat16)
    grad_up = (grad_inner * gate_act).astype(jnp.bfloat16)
    gate_grad = product('erd,erf->edf', owner_rows, grad_gate)
    up_grad = product('erd,erf->edf', owner_rows, grad_up)
    grad_owner_rows = product('erf,edf->erd', grad_gate, gate_mat) + product('erf,edf->erd', grad_up, up_mat)
    return (grad_owner_rows.astype(jnp.bfloat16), gate_grad, up_grad, down_grad)

def reference(tokens, segments, routes, first_gain, query_weight, key_projection_weight, value_projection_weight, out_weight, second_gain, router_weight, gate_weight, up_weight, down_weight, cotangent):
    device_count = N_DP * N_EXPERT
    total_seqs = TOKENS // SEQUENCE_LENGTH
    block_seqs = math.gcd(total_seqs, max(1, 4096 // SEQUENCE_LENGTH))
    block_count = total_seqs // block_seqs
    tok_blocks = tokens.reshape(block_count, block_seqs * SEQUENCE_LENGTH, MODEL_DIM)
    seg_blocks = segments.reshape(block_count, block_seqs * SEQUENCE_LENGTH)

    def forward_block(running, pieces):
        hidden_piece, saved = mixer_forward(pieces[0], pieces[1], first_gain, query_weight, key_projection_weight, value_projection_weight, out_weight)
        return (running, hidden_piece)
    unused, hidden_blocks = lax.scan(forward_block, jnp.zeros((), jnp.float32), (tok_blocks, seg_blocks))
    hidden = hidden_blocks.reshape(TOKENS, MODEL_DIM)
    normed_second, factor_second, expert_input = normalize(hidden, second_gain)
    route_prob, chosen_hot = route_weights(expert_input, router_weight, routes)
    flat_routes = routes.reshape(device_count, TOK_DEV * TOPK)
    route_hot = (flat_routes[..., None] == jnp.arange(EXPERTS, dtype=jnp.int32)[None, None, :]).astype(jnp.int32)
    slot_of = lax.optimization_barrier(jnp.sum(route_hot * jnp.cumsum(route_hot, 1), -1)) - 1
    device_rows = jnp.arange(device_count, dtype=jnp.int32)[:, None]
    target = (flat_routes * (device_count * CAP) + device_rows * CAP + slot_of).reshape(-1).astype(jnp.int32)
    slot_table = jnp.full((EXPERTS * device_count * CAP,), -1, jnp.int32)
    slot_table = slot_table.at[target].set(jnp.arange(TOKENS * TOPK, dtype=jnp.int32))
    slot_table = slot_table.reshape(EXPERTS, device_count * CAP)
    grad_output = cotangent.astype(jnp.float32)
    flat_prob = route_prob.reshape(-1)

    def expert_step(running, pieces):
        mixture, grad_expert_input, grad_prob = running
        gate_slice, up_slice, down_slice, entries = pieces
        live_slot = entries >= 0
        source = jnp.maximum(entries, 0)
        token_of = source // TOPK
        owner_rows = jnp.where(live_slot[:, None], expert_input[token_of], jnp.zeros((), jnp.bfloat16))[None]
        expert_out, kept_acts = expert_forward(owner_rows, gate_slice[None], up_slice[None], down_slice[None])
        out_rows = expert_out[0].astype(jnp.float32)
        weight_rows = jnp.where(live_slot, flat_prob[source], 0.0)
        mixture = mixture.at[token_of].add(weight_rows[:, None] * out_rows)
        grad_prob = grad_prob.at[source].add(jnp.where(live_slot, lax.optimization_barrier(jnp.sum(grad_output[token_of] * out_rows, -1)), 0.0))
        grad_rows = (weight_rows[:, None] * grad_output[token_of]).astype(jnp.bfloat16)[None]
        grad_owner_rows, gate_grad, up_grad, down_grad = expert_backward(grad_rows, owner_rows, kept_acts, gate_slice[None], up_slice[None], down_slice[None])
        grad_expert_input = grad_expert_input.at[token_of].add(jnp.where(live_slot[:, None], grad_owner_rows[0].astype(jnp.float32), 0.0))
        return ((mixture, grad_expert_input, grad_prob), (gate_grad[0], up_grad[0], down_grad[0]))
    start = (jnp.zeros((TOKENS, MODEL_DIM), jnp.float32), jnp.zeros((TOKENS, MODEL_DIM), jnp.float32), jnp.zeros((TOKENS * TOPK,), jnp.float32))
    finals, expert_grads = lax.scan(expert_step, start, (gate_weight, up_weight, down_weight, slot_table))
    mixture, grad_expert_input, grad_prob = finals
    output = (hidden + mixture).astype(jnp.bfloat16)
    router_grad = route_back(route_prob, grad_prob.reshape(TOKENS, TOPK), chosen_hot)
    grad_expert_input = grad_expert_input + matrix_multiply(router_grad, router_weight.T)
    router_wgrad = matrix_multiply(expert_input.T, router_grad)
    grad_normed, second_gain_grad = normalize_back(grad_expert_input, normed_second, factor_second, second_gain)
    grad_hidden = grad_output + grad_normed
    grad_blocks = grad_hidden.reshape(block_count, block_seqs * SEQUENCE_LENGTH, MODEL_DIM)

    def backward_block(running, pieces):
        tok_piece, seg_piece, grad_piece = pieces
        hidden_piece, saved = mixer_forward(tok_piece, seg_piece, first_gain, query_weight, key_projection_weight, value_projection_weight, out_weight)
        results = mixer_backward(grad_piece, saved, first_gain, query_weight, key_projection_weight, value_projection_weight, out_weight)
        totals = tuple((running[index] + results[index + 1] for index in range(5)))
        return (totals, results[0])
    initial_gradients = (jnp.zeros((MODEL_DIM,), jnp.float32), jnp.zeros((MODEL_DIM, QUERY_HEADS * HEAD_DIM), jnp.float32), jnp.zeros((MODEL_DIM, KEY_VALUE_HEADS * HEAD_DIM), jnp.float32), jnp.zeros((MODEL_DIM, KEY_VALUE_HEADS * HEAD_DIM), jnp.float32), jnp.zeros((QUERY_HEADS * HEAD_DIM, MODEL_DIM), jnp.float32))
    totals, grad_token_blocks = lax.scan(backward_block, initial_gradients, (tok_blocks, seg_blocks, grad_blocks))
    grad_tokens = grad_token_blocks.reshape(TOKENS, MODEL_DIM)
    return (output, grad_tokens, totals[0], totals[1], totals[2], totals[3], totals[4], second_gain_grad, router_wgrad, expert_grads[0], expert_grads[1], expert_grads[2])
```

```python
import jax
import jax.numpy as jnp
from jax import lax
from jax.sharding import PartitionSpec as P

QUERY_HEADS = 16
KEY_VALUE_HEADS = 8
HEAD_DIM = 64
SEQUENCE_LENGTH = 128


EPSILON = 1e-06
SCORE_SCALE = 0.015625
ROPE_BASE = 10000.0
MASKED = -1e30


def product(pattern, left_op, right_op):
    return jnp.einsum(pattern, left_op, right_op, preferred_element_type=jnp.float32)


def matrix_multiply(left_op, right_op):
    return jnp.dot(left_op, right_op, preferred_element_type=jnp.float32)


def rope_tables(seq_len, head_size):
    positions = jnp.arange(seq_len, dtype=jnp.float32)
    exponent = jnp.arange(head_size // 2, dtype=jnp.float32) * (2.0 / head_size)
    angles = positions[:, None] * (ROPE_BASE ** (-exponent))[None, :]
    return (jnp.cos(angles)[None, :, None, :], jnp.sin(angles)[None, :, None, :])


def apply_rotary(values, cosine_table, sine_table):
    middle = values.shape[-1] // 2
    first_half = values[..., :middle]
    second_half = values[..., middle:]
    return jnp.concatenate(
        [
            first_half * cosine_table - second_half * sine_table,
            second_half * cosine_table + first_half * sine_table,
        ],
        -1,
    )


def inverse_rotary(gradient, cosine_table, sine_table):
    middle = gradient.shape[-1] // 2
    first_half = gradient[..., :middle]
    second_half = gradient[..., middle:]
    return jnp.concatenate(
        [
            first_half * cosine_table + second_half * sine_table,
            second_half * cosine_table - first_half * sine_table,
        ],
        -1,
    )


def normalize(values, gain_vec):
    factor = lax.rsqrt(jnp.mean(values * values, -1, keepdims=True) + EPSILON)
    normed = values * factor
    return (normed, factor, (normed * gain_vec).astype(jnp.bfloat16))


def normalize_back(gradient, normed, factor, gain_vec):
    gain_grad = jnp.sum(gradient * normed, 0)
    scaled = gradient * gain_vec
    return (factor * (scaled - normed * jnp.mean(scaled * normed, -1, keepdims=True)), gain_grad)


def segment_mask(segments):
    seq_len = segments.shape[1]
    causal = jnp.arange(seq_len)[:, None] >= jnp.arange(seq_len)[None, :]
    same_doc = segments[:, :, None] == segments[:, None, :]
    return (same_doc & causal[None])[:, None, None]


def score_table(query_rows, key_row_block, mask_tab):
    raw_scores = product("sqhgw,skhw->shgqk", query_rows, key_row_block) * SCORE_SCALE
    return jnp.where(mask_tab, raw_scores, MASKED)


def mixer_forward(tokens, segments, gain_vec, query_mat, key_matrix, value_matrix, out_mat):
    token_rows = tokens.shape[0]
    local_sequences = token_rows // SEQUENCE_LENGTH
    query_groups = QUERY_HEADS // KEY_VALUE_HEADS
    cosine_table, sine_table = rope_tables(SEQUENCE_LENGTH, HEAD_DIM)
    mask_tab = segment_mask(segments.reshape(local_sequences, SEQUENCE_LENGTH))
    residual = tokens.astype(jnp.float32)
    normed, factor, attention_input = normalize(turn(residual, 1), gain_vec)
    query_rows = apply_rotary(
        times(attention_input, query_mat).reshape(
            local_sequences, SEQUENCE_LENGTH, QUERY_HEADS, HEAD_DIM
        ),
        cosine_table,
        sine_table,
    )
    query_rows = query_rows.astype(jnp.bfloat16).reshape(
        local_sequences, SEQUENCE_LENGTH, KEY_VALUE_HEADS, query_groups, HEAD_DIM
    )
    key_row_block = apply_rotary(
        times(attention_input, key_matrix).reshape(
            local_sequences, SEQUENCE_LENGTH, KEY_VALUE_HEADS, HEAD_DIM
        ),
        cosine_table,
        sine_table,
    ).astype(jnp.bfloat16)
    value_row_block = (
        times(attention_input, value_matrix)
        .astype(jnp.bfloat16)
        .reshape(local_sequences, SEQUENCE_LENGTH, KEY_VALUE_HEADS, HEAD_DIM)
    )
    scores = score_table(query_rows, key_row_block, mask_tab)
    row_peak = jnp.max(scores, -1, keepdims=True)
    logsum = row_peak + jnp.log(jnp.sum(jnp.exp(scores - row_peak), -1, keepdims=True))
    weights = jnp.exp(scores - logsum).astype(jnp.bfloat16)
    attended = product("shgqk,skhw->sqhgw", weights, value_row_block).astype(jnp.bfloat16)
    turned = turn(attended.reshape(token_rows, QUERY_HEADS * HEAD_DIM), 1)
    hidden = residual + times(turned, out_mat)
    saved = (
        normed,
        factor,
        attention_input,
        query_rows,
        key_row_block,
        value_row_block,
        attended,
        turned,
        logsum,
        mask_tab,
        cosine_table,
        sine_table,
    )
    return (hidden, saved)


def mixer_backward(grad_hidden, saved, gain_vec, query_mat, key_matrix, value_matrix, out_mat):
    (
        normed,
        factor,
        attention_input,
        query_rows,
        key_row_block,
        value_row_block,
        attended,
        _,
        logsum,
        mask_tab,
        cosine_table,
        sine_table,
    ) = saved
    token_rows = grad_hidden.shape[0]
    local_sequences = token_rows // SEQUENCE_LENGTH
    grad_round = grad_hidden.astype(jnp.bfloat16)
    grad_attended = (
        turn(times_back(grad_round, out_mat).astype(jnp.bfloat16), 1).reshape(query_rows.shape)
    )
    scores = score_table(query_rows, key_row_block, mask_tab)
    prob_full = jnp.exp(scores - logsum)
    values_gradient = product("shgqk,sqhgw->skhw", prob_full.astype(jnp.bfloat16), grad_attended)
    grad_weights = product("sqhgw,skhw->shgqk", grad_attended, value_row_block)
    row_delta = product("sqhgw,sqhgw->shgq", grad_attended, attended)[..., None]
    grad_scores = (prob_full * (grad_weights - row_delta) * SCORE_SCALE).astype(jnp.bfloat16)
    grad_queries = product("shgqk,skhw->sqhgw", grad_scores, key_row_block)
    keys_gradient = product("shgqk,sqhgw->skhw", grad_scores, query_rows)
    query_grad = inverse_rotary(
        grad_queries.reshape(local_sequences, SEQUENCE_LENGTH, QUERY_HEADS, HEAD_DIM),
        cosine_table,
        sine_table,
    )
    query_grad = query_grad.astype(jnp.bfloat16).reshape(token_rows, QUERY_HEADS * HEAD_DIM)
    key_gradient = (
        inverse_rotary(keys_gradient, cosine_table, sine_table)
        .astype(jnp.bfloat16)
        .reshape(token_rows, KEY_VALUE_HEADS * HEAD_DIM)
    )
    value_gradient = values_gradient.astype(jnp.bfloat16).reshape(
        token_rows, KEY_VALUE_HEADS * HEAD_DIM
    )
    grad_attn_input = (
        times_back(query_grad, query_mat)
        + times_back(key_gradient, key_matrix)
        + times_back(value_gradient, value_matrix)
    )
    grad_normed, gain_grad = normalize_back(grad_attn_input, normed, factor, gain_vec)
    return (
        grad_hidden + turn(grad_normed, 1),
        turn(gain_grad, 0),
        [query_grad, key_gradient, value_gradient, grad_round],
    )


def route_weights(expert_input, router_mat, routes):
    logits = matrix_multiply(expert_input, router_mat)
    chosen_hot = (
        routes[:, :, None] == jnp.arange(router_mat.shape[1], dtype=jnp.int32)[None, None, :]
    ).astype(jnp.float32)
    chosen = jnp.sum(chosen_hot * logits[:, None, :], -1)
    return (jax.nn.softmax(chosen, -1), chosen_hot)


def route_back(route_prob, grad_prob, chosen_hot):
    grad_chosen = route_prob * (grad_prob - jnp.sum(route_prob * grad_prob, -1, keepdims=True))
    return jnp.sum(chosen_hot * grad_chosen[:, :, None], 1).astype(jnp.bfloat16)


def expert_forward(owner_rows, gate_mat, up_mat, down_mat):
    gate_pre = product("erd,edf->erf", owner_rows, gate_mat)
    up_pre = product("erd,edf->erf", owner_rows, up_mat)
    gate_sig = jax.nn.sigmoid(gate_pre)
    gate_act = gate_pre * gate_sig
    inner_acts = (gate_act * up_pre).astype(jnp.bfloat16)
    expert_out = product("erf,efd->erd", inner_acts, down_mat).astype(jnp.bfloat16)
    return (expert_out, (gate_pre, up_pre, gate_sig, gate_act, inner_acts))


def expert_backward(grad_rows, owner_rows, kept_acts, gate_mat, up_mat, down_mat):
    gate_pre, up_pre, gate_sig, gate_act, inner_acts = kept_acts
    grad_inner = product("erd,efd->erf", grad_rows, down_mat)
    down_grad = product("erf,erd->efd", inner_acts, grad_rows)
    silu_slope = gate_sig * (1.0 + gate_pre * (1.0 - gate_sig))
    grad_gate = (grad_inner * up_pre * silu_slope).astype(jnp.bfloat16)
    grad_up = (grad_inner * gate_act).astype(jnp.bfloat16)
    gate_grad = product("erd,erf->edf", owner_rows, grad_gate)
    up_grad = product("erd,erf->edf", owner_rows, grad_up)
    grad_owner_rows = product("erf,edf->erd", grad_gate, gate_mat) + product(
        "erf,edf->erd", grad_up, up_mat
    )
    return (grad_owner_rows.astype(jnp.bfloat16), gate_grad, up_grad, down_grad)


def gather_dp(local_part):
    dp_count = lax.axis_size("dp")
    owner_count = lax.axis_size("expert")
    if dp_count != 2 or owner_count % 2:
        return lax.all_gather(local_part, "dp", axis=0, tiled=True)
    low, high = jnp.split(local_part, 2, 0)
    even = lax.axis_index("expert") % 2 == 0
    near = lax.ppermute(jnp.where(even, low, high), "dp", [(0, 1), (1, 0)])
    far = lax.ppermute(near, "expert", [(i, i ^ 1) for i in range(owner_count)])
    other = jnp.concatenate([jnp.where(even, near, far), jnp.where(even, far, near)], 0)
    first = lax.axis_index("dp") == 0
    return jnp.concatenate(
        [jnp.where(first, local_part, other), jnp.where(first, other, local_part)], 0
    )


def gather_other(local_part):
    owner_count = lax.axis_size("expert")
    rows = local_part.shape[0] // owner_count
    mine = lax.dynamic_slice_in_dim(local_part, lax.axis_index("expert") * rows, rows, 0)
    arrived = lax.ppermute(mine, "dp", [(0, 1), (1, 0)])
    return lax.all_gather(arrived, "expert", axis=0, tiled=True)


def turn(values, axis):
    if lax.axis_size("dp") != 2:
        return values
    low, high = jnp.split(values, 2, axis)
    first = lax.axis_index("dp") == 0
    return jnp.concatenate([jnp.where(first, low, high), jnp.where(first, high, low)], axis)


def pack_rows(values, width):
    flat = values.reshape(values.shape[0], -1)
    rows = -(-flat.shape[1] // width)
    flat = jnp.pad(flat, ((0, 0), (0, rows * width - flat.shape[1])))
    return flat.reshape(values.shape[0], rows, width)


def times(left_op, pieces):
    total, start = None, 0
    for piece in pieces:
        part = matrix_multiply(left_op[:, start : start + piece.shape[0]], piece)
        total = part if total is None else total + part
        start += piece.shape[0]
    return total


def times_back(left_op, pieces):
    return jnp.concatenate([matrix_multiply(left_op, piece.T) for piece in pieces], 1)


def weight_sums(early, late, extras):
    owner_count = lax.axis_size("expert")
    dp_count = lax.axis_size("dp")
    token_rows = late[0].shape[0]
    slices = [
        grad.T.reshape(owner_count, grad.shape[1] // owner_count, token_rows) for grad in late
    ]
    extra_count, extra_width = extras.shape
    part = extra_width // (owner_count * dp_count)
    spread = (
        extras.reshape(extra_count, dp_count, owner_count, part)
        .transpose(2, 0, 1, 3)
        .astype(jnp.bfloat16)
    )
    payload = jnp.concatenate(slices + [pack_rows(spread, token_rows)], 1)
    arrived = lax.all_to_all(payload, "expert", split_axis=0, concat_axis=0, tiled=True)
    start, tiles = 0, []
    for gathered, piece in zip(early, slices):
        end = start + piece.shape[1]
        tiles.append(product("sct,std->cd", arrived[:, start:end], gathered))
        start = end
    extra_sum = jnp.sum(
        arrived[:, start:]
        .reshape(owner_count, -1)[:, : extra_count * dp_count * part]
        .astype(jnp.float32),
        0,
    ).reshape(extra_count, dp_count, part)
    extra_sum = turn(extra_sum.transpose(1, 0, 2), 0)
    half = tiles[0].shape[1] // dp_count
    packed = pack_rows(extra_sum, half).transpose(1, 0, 2).reshape(-1, dp_count * half)
    tile = jnp.concatenate(tiles + [packed], 0)
    rounded = tile.astype(jnp.bfloat16)
    if dp_count == 2:
        peer = lax.ppermute(rounded[:, half:], "dp", [(0, 1), (1, 0)])
        share = rounded[:, :half].astype(jnp.float32) + peer.astype(jnp.float32)
    else:
        share = lax.psum_scatter(rounded, "dp", scatter_dimension=1, tiled=True)
    everything = lax.all_gather(share.astype(jnp.bfloat16), "expert").astype(jnp.float32)
    start, results = 0, []
    for piece in slices:
        end = start + piece.shape[1]
        results.append(everything[:, start:end].reshape(-1, half).T)
        start = end
    extra_all = everything[:, start:].reshape(owner_count, -1)[:, : extra_count * part]
    extra_all = extra_all.reshape(owner_count, extra_count, part).transpose(1, 0, 2)
    return results, extra_all.reshape(extra_count, -1)


def scatter_dp(partial, axis):
    dp_count = lax.axis_size("dp")
    rounded = partial.astype(jnp.bfloat16)
    if dp_count != 2:
        return lax.psum_scatter(rounded, "dp", scatter_dimension=axis, tiled=True).astype(
            jnp.float32
        )
    low, high = jnp.split(rounded, 2, axis)
    first = lax.axis_index("dp") == 0
    arrived = lax.ppermute(jnp.where(first, high, low), "dp", [(0, 1), (1, 0)])
    return jnp.where(first, low, high).astype(jnp.float32) + arrived.astype(jnp.float32)


def shards(
    tokens,
    segments,
    routes,
    first_gain,
    query_weight,
    key_projection_weight,
    value_projection_weight,
    out_weight,
    second_gain,
    router_weight,
    gate_weight,
    up_weight,
    down_weight,
    cotangent,
):
    token_rows, model_width = tokens.shape
    top_count = routes.shape[1]
    expert_count = router_weight.shape[1]
    owner_count = lax.axis_size("expert")
    local_count = gate_weight.shape[0]
    key_width = key_projection_weight.shape[1]
    query_width = query_weight.shape[1]
    capacity = 5 * token_rows * top_count // (4 * expert_count)
    row_part = router_weight.shape[0]

    own = [
        query_weight,
        key_projection_weight,
        value_projection_weight,
        out_weight,
        router_weight,
        first_gain[:, None],
        second_gain[:, None],
    ]
    joined = jnp.concatenate(own, 1)
    if lax.axis_size("dp") == 2:
        joined = jnp.pad(joined, ((0, 0), (0, -joined.shape[1] % 128)))
        other = gather_other(joined)
        halves = [own, None]
    else:
        other = lax.all_gather(joined, "dp", axis=0, tiled=True)
        halves = [None]
    starts = [0]
    for part in own:
        starts.append(starts[-1] + part.shape[1])
    fetched = [other[:, a:b] for a, b in zip(starts[:-1], starts[1:])]
    halves = [fetched if half is None else half for half in halves]
    query_mat, key_matrix, value_matrix, out_mat = (
        [half[index] for half in halves] for index in range(4)
    )
    router_mat = turn(jnp.concatenate([half[4] for half in halves], 0), 0)
    gain_first = jnp.concatenate([half[5] for half in halves], 0)[:, 0]
    gain_second = turn(jnp.concatenate([half[6] for half in halves], 0)[:, 0], 0)

    routes_all = lax.all_gather(routes, "expert")
    cotangent_all = lax.all_gather(cotangent, "expert")

    mine = lax.axis_index("expert") * local_count + jnp.arange(local_count, dtype=jnp.int32)
    hit = jnp.any(routes_all[None] == mine[:, None, None, None], -1)
    before = (
        jnp.arange(token_rows)[:, None] < jnp.arange(token_rows)[None, :]
    ).astype(jnp.bfloat16)
    rank = product("lst,tu->lsu", hit.astype(jnp.bfloat16), before).astype(jnp.int32)
    slot = jnp.where(hit, rank, -1)
    picked = slot[:, :, None, :] == jnp.arange(capacity, dtype=jnp.int32)[None, None, :, None]
    pick = picked.astype(jnp.bfloat16)

    def rows_of(gathered):
        rows = product("lsct,std->lscd", pick, gathered)
        return rows.reshape(local_count, owner_count * capacity, model_width)

    own_hot = (routes[:, :, None] == jnp.arange(expert_count, dtype=jnp.int32)).any(1)
    own_rank = matrix_multiply(before.T, own_hot.astype(jnp.bfloat16)).astype(jnp.int32)
    own_slot = jnp.where(own_hot, own_rank, -1)
    own_pick = (
        own_slot[:, :, None] == jnp.arange(capacity, dtype=jnp.int32)[None, None, :]
    ).astype(jnp.bfloat16)

    def send_back(rows):
        shaped = rows.reshape(local_count, owner_count, capacity, model_width)
        return lax.all_to_all(
            shaped.transpose(1, 0, 2, 3).reshape(expert_count, capacity, model_width),
            "expert",
            split_axis=0,
            concat_axis=0,
            tiled=True,
        )

    def sum_back(returned):
        flat = returned.reshape(expert_count * capacity, model_width)
        return matrix_multiply(own_pick.reshape(token_rows, expert_count * capacity), flat)

    hidden, saved = mixer_forward(
        tokens, segments, gain_first, query_mat, key_matrix, value_matrix, out_mat
    )
    attention_all = lax.all_gather(saved[2], "expert")
    attended_all = lax.all_gather(saved[7], "expert")
    normed_second, factor_second, expert_input = normalize(hidden, gain_second)
    input_all = lax.all_gather(expert_input, "expert")
    route_prob, chosen_hot = route_weights(expert_input, router_mat, routes)
    dense_prob = jnp.sum(chosen_hot * route_prob[:, :, None], 1)
    prob_all = lax.all_gather(dense_prob, "expert")

    column = jnp.arange(expert_count, dtype=jnp.int32)
    my_column = (mine[:, None] == column[None, :]).astype(jnp.float32)
    my_prob = jnp.sum(prob_all[None] * my_column[:, None, None, :], -1)
    row_prob = jnp.sum(jnp.where(picked, my_prob[:, :, None, :], 0.0), -1).reshape(
        local_count, owner_count * capacity, 1
    )

    owner_rows = rows_of(input_all).astype(jnp.bfloat16)
    cotangent_rows = rows_of(cotangent_all).astype(jnp.bfloat16).astype(jnp.float32)
    expert_out, kept_acts = expert_forward(owner_rows, gate_weight, up_weight, down_weight)
    expert_out = expert_out.astype(jnp.float32)
    weighted = (row_prob * expert_out).astype(jnp.bfloat16)
    row_grad_prob = jnp.sum(expert_out * cotangent_rows, -1).reshape(
        local_count, owner_count, capacity
    )
    token_grad_prob = jnp.sum(jnp.where(picked, row_grad_prob[..., None], 0.0), 2)
    back_prob = lax.all_to_all(
        token_grad_prob.transpose(1, 0, 2).reshape(expert_count, token_rows),
        "expert",
        split_axis=0,
        concat_axis=0,
        tiled=True,
    )
    grad_prob = jnp.sum(chosen_hot * back_prob.T[:, None, :], -1)
    grad_output = cotangent.astype(jnp.float32)

    grad_rows = (row_prob * cotangent_rows).astype(jnp.bfloat16)
    grad_owner_rows, gate_grad, up_grad, down_grad = expert_backward(
        grad_rows, owner_rows, kept_acts, gate_weight, up_weight, down_weight
    )
    grad_back = send_back(grad_owner_rows)
    expert_shares = (
        scatter_dp(gate_grad, 1),
        scatter_dp(up_grad, 1),
        scatter_dp(down_grad, 2),
    )
    grad_back, expert_shares, weighted = lax.optimization_barrier(
        (grad_back, expert_shares, weighted)
    )
    forward_back = send_back(weighted)
    output = (hidden + sum_back(forward_back)).astype(jnp.bfloat16)
    backward_sum = sum_back(grad_back)
    router_grad = route_back(route_prob, grad_prob, chosen_hot)
    grad_expert_input = backward_sum + matrix_multiply(
        router_grad, router_mat.T
    )
    router_wgrad = matrix_multiply(router_grad.T, expert_input)
    grad_normed, second_gain_grad = normalize_back(
        grad_expert_input, normed_second, factor_second, gain_second
    )
    grad_hidden = grad_output + grad_normed
    grad_tokens, first_gain_grad, late = mixer_backward(
        grad_hidden, saved, gain_first, query_mat, key_matrix, value_matrix, out_mat
    )

    extras = jnp.concatenate(
        [router_wgrad, first_gain_grad[None, :], second_gain_grad[None, :]], 0
    )
    (query_share, key_share, value_share, out_share), extras = weight_sums(
        [attention_all] * 3 + [attended_all], late, extras
    )
    router_share = extras[:expert_count].T
    first_share = extras[expert_count]
    second_share = extras[expert_count + 1]
    return (
        output,
        grad_tokens,
        first_share,
        query_share,
        key_share,
        value_share,
        out_share,
        second_share,
        router_share,
        expert_shares[0],
        expert_shares[1],
        expert_shares[2],
    )


def solution(mesh):
    placed = (
        P(("dp", "expert"), None),
        P(("dp", "expert")),
        P(("dp", "expert"), None),
        P("dp"),
        P("dp", None),
        P("dp", None),
        P("dp", None),
        P("dp", None),
        P("dp"),
        P("dp", None),
        P("expert", None, None),
        P("expert", None, None),
        P("expert", None, None),
        P(("dp", "expert"), None),
    )
    return jax.shard_map(
        shards,
        mesh=mesh,
        in_specs=placed,
        out_specs=(
            P(("dp", "expert"), None),
            P(("dp", "expert"), None),
            P("dp"),
            P("dp", None),
            P("dp", None),
            P("dp", None),
            P("dp", None),
            P("dp"),
            P("dp", None),
            P("expert", "dp", None),
            P("expert", "dp", None),
            P("expert", None, "dp"),
        ),
        check_vma=False,
    )
```

```python
import functools

import jax
import jax.numpy as jnp
from jax import lax
from jax.experimental import pallas as pl
from jax.experimental.pallas import tpu as pltpu
from jax.sharding import PartitionSpec as P

QUERY_HEADS = 16
KEY_VALUE_HEADS = 8
HEAD_DIM = 64
SEQUENCE_LENGTH = 128


EPSILON = 1e-06
SCORE_SCALE = 0.015625
ROPE_BASE = 10000.0
MASKED = -1e30


def product(pattern, left_op, right_op):
    return jnp.einsum(pattern, left_op, right_op, preferred_element_type=jnp.float32)


def matrix_multiply(left_op, right_op):
    return jnp.dot(left_op, right_op, preferred_element_type=jnp.float32)


def rope_tables(seq_len, head_size):
    positions = jnp.arange(seq_len, dtype=jnp.float32)
    exponent = jnp.arange(head_size // 2, dtype=jnp.float32) * (2.0 / head_size)
    angles = positions[:, None] * (ROPE_BASE ** (-exponent))[None, :]
    return (jnp.cos(angles)[None, :, None, :], jnp.sin(angles)[None, :, None, :])


def apply_rotary(values, cosine_table, sine_table):
    middle = values.shape[-1] // 2
    first_half = values[..., :middle]
    second_half = values[..., middle:]
    return jnp.concatenate(
        [
            first_half * cosine_table - second_half * sine_table,
            second_half * cosine_table + first_half * sine_table,
        ],
        -1,
    )


def inverse_rotary(gradient, cosine_table, sine_table):
    middle = gradient.shape[-1] // 2
    first_half = gradient[..., :middle]
    second_half = gradient[..., middle:]
    return jnp.concatenate(
        [
            first_half * cosine_table + second_half * sine_table,
            second_half * cosine_table - first_half * sine_table,
        ],
        -1,
    )


def normalize(values, gain_vec):
    factor = lax.rsqrt(jnp.mean(values * values, -1, keepdims=True) + EPSILON)
    normed = values * factor
    return (normed, factor, (normed * gain_vec).astype(jnp.bfloat16))


def normalize_back(gradient, normed, factor, gain_vec):
    gain_grad = jnp.sum(gradient * normed, 0)
    scaled = gradient * gain_vec
    return (factor * (scaled - normed * jnp.mean(scaled * normed, -1, keepdims=True)), gain_grad)


def segment_mask(segments):
    seq_len = segments.shape[1]
    causal = jnp.arange(seq_len)[:, None] >= jnp.arange(seq_len)[None, :]
    same_doc = segments[:, :, None] == segments[:, None, :]
    return (same_doc & causal[None])[:, None, None]


def score_table(query_rows, key_row_block, mask_tab):
    raw_scores = product("sqhgw,skhw->shgqk", query_rows, key_row_block) * SCORE_SCALE
    return jnp.where(mask_tab, raw_scores, MASKED)


def mixer_forward(tokens, segments, gain_vec, query_mat, key_matrix, value_matrix, out_mat):
    token_rows = tokens.shape[0]
    local_sequences = token_rows // SEQUENCE_LENGTH
    query_groups = QUERY_HEADS // KEY_VALUE_HEADS
    cosine_table, sine_table = rope_tables(SEQUENCE_LENGTH, HEAD_DIM)
    mask_tab = segment_mask(segments.reshape(local_sequences, SEQUENCE_LENGTH))
    residual = tokens.astype(jnp.float32)
    normed, factor, attention_input = normalize(residual, gain_vec)
    query_rows = apply_rotary(
        matrix_multiply(attention_input, query_mat).reshape(
            local_sequences, SEQUENCE_LENGTH, QUERY_HEADS, HEAD_DIM
        ),
        cosine_table,
        sine_table,
    )
    query_rows = query_rows.astype(jnp.bfloat16).reshape(
        local_sequences, SEQUENCE_LENGTH, KEY_VALUE_HEADS, query_groups, HEAD_DIM
    )
    key_row_block = apply_rotary(
        matrix_multiply(attention_input, key_matrix).reshape(
            local_sequences, SEQUENCE_LENGTH, KEY_VALUE_HEADS, HEAD_DIM
        ),
        cosine_table,
        sine_table,
    ).astype(jnp.bfloat16)
    value_row_block = (
        matrix_multiply(attention_input, value_matrix)
        .astype(jnp.bfloat16)
        .reshape(local_sequences, SEQUENCE_LENGTH, KEY_VALUE_HEADS, HEAD_DIM)
    )
    scores = score_table(query_rows, key_row_block, mask_tab)
    row_peak = jnp.max(scores, -1, keepdims=True)
    logsum = row_peak + jnp.log(jnp.sum(jnp.exp(scores - row_peak), -1, keepdims=True))
    weights = jnp.exp(scores - logsum).astype(jnp.bfloat16)
    attended = product("shgqk,skhw->sqhgw", weights, value_row_block).astype(jnp.bfloat16)
    hidden = residual + matrix_multiply(
        attended.reshape(token_rows, QUERY_HEADS * HEAD_DIM), out_mat
    )
    saved = (
        normed,
        factor,
        attention_input,
        query_rows,
        key_row_block,
        value_row_block,
        attended,
        logsum,
        mask_tab,
        cosine_table,
        sine_table,
    )
    return (hidden, saved)


def mixer_backward(grad_hidden, saved, gain_vec, query_mat, key_matrix, value_matrix, out_mat):
    (
        normed,
        factor,
        attention_input,
        query_rows,
        key_row_block,
        value_row_block,
        attended,
        logsum,
        mask_tab,
        cosine_table,
        sine_table,
    ) = saved
    token_rows = grad_hidden.shape[0]
    local_sequences = token_rows // SEQUENCE_LENGTH
    grad_round = grad_hidden.astype(jnp.bfloat16)
    out_grad = matrix_multiply(attended.reshape(token_rows, QUERY_HEADS * HEAD_DIM).T, grad_round)
    grad_attended = (
        matrix_multiply(grad_round, out_mat.T).astype(jnp.bfloat16).reshape(query_rows.shape)
    )
    scores = score_table(query_rows, key_row_block, mask_tab)
    prob_full = jnp.exp(scores - logsum)
    values_gradient = product("shgqk,sqhgw->skhw", prob_full.astype(jnp.bfloat16), grad_attended)
    grad_weights = product("sqhgw,skhw->shgqk", grad_attended, value_row_block)
    row_delta = product("sqhgw,sqhgw->shgq", grad_attended, attended)[..., None]
    grad_scores = (prob_full * (grad_weights - row_delta) * SCORE_SCALE).astype(jnp.bfloat16)
    grad_queries = product("shgqk,skhw->sqhgw", grad_scores, key_row_block)
    keys_gradient = product("shgqk,sqhgw->skhw", grad_scores, query_rows)
    query_grad = inverse_rotary(
        grad_queries.reshape(local_sequences, SEQUENCE_LENGTH, QUERY_HEADS, HEAD_DIM),
        cosine_table,
        sine_table,
    )
    query_grad = query_grad.astype(jnp.bfloat16).reshape(token_rows, QUERY_HEADS * HEAD_DIM)
    key_gradient = (
        inverse_rotary(keys_gradient, cosine_table, sine_table)
        .astype(jnp.bfloat16)
        .reshape(token_rows, KEY_VALUE_HEADS * HEAD_DIM)
    )
    value_gradient = values_gradient.astype(jnp.bfloat16).reshape(
        token_rows, KEY_VALUE_HEADS * HEAD_DIM
    )
    query_wgrad = matrix_multiply(attention_input.T, query_grad)
    key_wgrad = matrix_multiply(attention_input.T, key_gradient)
    value_wgrad = matrix_multiply(attention_input.T, value_gradient)
    grad_attn_input = (
        matrix_multiply(query_grad, query_mat.T)
        + matrix_multiply(key_gradient, key_matrix.T)
        + matrix_multiply(value_gradient, value_matrix.T)
    )
    grad_normed, gain_grad = normalize_back(grad_attn_input, normed, factor, gain_vec)
    return (grad_hidden + grad_normed, gain_grad, query_wgrad, key_wgrad, value_wgrad, out_grad)


def route_weights(expert_input, router_mat, routes):
    logits = matrix_multiply(expert_input, router_mat)
    chosen_hot = (
        routes[:, :, None] == jnp.arange(router_mat.shape[1], dtype=jnp.int32)[None, None, :]
    ).astype(jnp.float32)
    chosen = jnp.sum(chosen_hot * logits[:, None, :], -1)
    return (jax.nn.softmax(chosen, -1), chosen_hot)


def route_back(route_prob, grad_prob, chosen_hot):
    grad_chosen = route_prob * (grad_prob - jnp.sum(route_prob * grad_prob, -1, keepdims=True))
    return jnp.sum(chosen_hot * grad_chosen[:, :, None], 1).astype(jnp.bfloat16)


def expert_forward(owner_rows, gate_mat, up_mat, down_mat):
    gate_pre = product("erd,edf->erf", owner_rows, gate_mat)
    up_pre = product("erd,edf->erf", owner_rows, up_mat)
    gate_sig = jax.nn.sigmoid(gate_pre)
    gate_act = gate_pre * gate_sig
    inner_acts = (gate_act * up_pre).astype(jnp.bfloat16)
    expert_out = product("erf,efd->erd", inner_acts, down_mat).astype(jnp.bfloat16)
    return (expert_out, (gate_pre, up_pre, gate_sig, gate_act, inner_acts))


def expert_backward(grad_rows, owner_rows, kept_acts, gate_mat, up_mat, down_mat):
    gate_pre, up_pre, gate_sig, gate_act, inner_acts = kept_acts
    grad_inner = product("erd,efd->erf", grad_rows, down_mat)
    down_grad = product("erf,erd->efd", inner_acts, grad_rows)
    silu_slope = gate_sig * (1.0 + gate_pre * (1.0 - gate_sig))
    grad_gate = (grad_inner * up_pre * silu_slope).astype(jnp.bfloat16)
    grad_up = (grad_inner * gate_act).astype(jnp.bfloat16)
    gate_grad = product("erd,erf->edf", owner_rows, grad_gate)
    up_grad = product("erd,erf->edf", owner_rows, grad_up)
    grad_owner_rows = product("erf,edf->erd", grad_gate, gate_mat) + product(
        "erf,edf->erd", grad_up, up_mat
    )
    return (grad_owner_rows.astype(jnp.bfloat16), gate_grad, up_grad, down_grad)


def gather_dp(local_part):
    dp_count = lax.axis_size("dp")
    owner_count = lax.axis_size("expert")
    if dp_count != 2 or owner_count % 2:
        return lax.all_gather(local_part, "dp", axis=0, tiled=True)
    low, high = jnp.split(local_part, 2, 0)
    even = lax.axis_index("expert") % 2 == 0
    near = lax.ppermute(jnp.where(even, low, high), "dp", [(0, 1), (1, 0)])
    far = lax.ppermute(near, "expert", [(i, i ^ 1) for i in range(owner_count)])
    other = jnp.concatenate([jnp.where(even, near, far), jnp.where(even, far, near)], 0)
    first = lax.axis_index("dp") == 0
    return jnp.concatenate(
        [jnp.where(first, local_part, other), jnp.where(first, other, local_part)], 0
    )


def all_sums(partial):
    owner_count = lax.axis_size("expert")
    dp_count = lax.axis_size("dp")
    width = partial.shape[1]
    pieces = partial.astype(jnp.bfloat16).reshape(dp_count, owner_count, -1, width)
    piece = lax.psum_scatter(
        pieces.transpose(1, 0, 2, 3).reshape(-1, width), "expert", scatter_dimension=0, tiled=True
    )
    piece = scatter_dp(piece, 0).astype(jnp.bfloat16)
    return lax.all_gather(piece, "expert", axis=0, tiled=True).astype(jnp.float32)


def scatter_dp(partial, axis):
    dp_count = lax.axis_size("dp")
    rounded = partial.astype(jnp.bfloat16)
    if dp_count != 2:
        return lax.psum_scatter(rounded, "dp", scatter_dimension=axis, tiled=True).astype(
            jnp.float32
        )
    low, high = jnp.split(rounded, 2, axis)
    first = lax.axis_index("dp") == 0
    arrived = lax.ppermute(jnp.where(first, high, low), "dp", [(0, 1), (1, 0)])
    return jnp.where(first, low, high).astype(jnp.float32) + arrived.astype(jnp.float32)


def shards(
    tokens,
    segments,
    routes,
    first_gain,
    query_weight,
    key_projection_weight,
    value_projection_weight,
    out_weight,
    second_gain,
    router_weight,
    gate_weight,
    up_weight,
    down_weight,
    cotangent,
):
    token_rows, model_width = tokens.shape
    top_count = routes.shape[1]
    expert_count = router_weight.shape[1]
    owner_count = lax.axis_size("expert")
    local_count = gate_weight.shape[0]
    key_width = key_projection_weight.shape[1]
    query_width = query_weight.shape[1]
    capacity = 5 * token_rows * top_count // (4 * expert_count)
    row_part = router_weight.shape[0]

    small = jnp.concatenate(
        [router_weight, first_gain[:, None], second_gain[:, None]], 1
    )
    small_mat = gather_dp(small)
    router_mat = small_mat[:, :expert_count]
    gain_first = small_mat[:, expert_count]
    gain_second = small_mat[:, expert_count + 1]
    joined_mat = gather_dp(
        jnp.concatenate([query_weight, key_projection_weight, value_projection_weight], 1)
    )
    query_mat = joined_mat[:, :query_width]
    key_matrix = joined_mat[:, query_width : query_width + key_width]
    value_matrix = joined_mat[:, query_width + key_width :]
    out_mat = gather_dp(out_weight)

    routes_all = lax.all_gather(routes, "expert")
    cotangent_all = lax.all_gather(cotangent, "expert")

    mine = lax.axis_index("expert") * local_count + jnp.arange(local_count, dtype=jnp.int32)
    hit = jnp.any(routes_all[None] == mine[:, None, None, None], -1)
    before = (
        jnp.arange(token_rows)[:, None] < jnp.arange(token_rows)[None, :]
    ).astype(jnp.bfloat16)
    rank = product("lst,tu->lsu", hit.astype(jnp.bfloat16), before).astype(jnp.int32)
    slot = jnp.where(hit, rank, -1)
    picked = slot[:, :, None, :] == jnp.arange(capacity, dtype=jnp.int32)[None, None, :, None]
    pick = picked.astype(jnp.bfloat16)

    def rows_of(gathered):
        rows = product("lsct,std->lscd", pick, gathered)
        return rows.reshape(local_count, owner_count * capacity, model_width)

    own_hot = (routes[:, :, None] == jnp.arange(expert_count, dtype=jnp.int32)).any(1)
    own_rank = matrix_multiply(before.T, own_hot.astype(jnp.bfloat16)).astype(jnp.int32)
    own_slot = jnp.where(own_hot, own_rank, -1)
    own_pick = (
        own_slot[:, :, None] == jnp.arange(capacity, dtype=jnp.int32)[None, None, :]
    ).astype(jnp.bfloat16)

    def send_back(rows):
        shaped = rows.reshape(local_count, owner_count, capacity, model_width)
        return lax.all_to_all(
            shaped.transpose(1, 0, 2, 3).reshape(expert_count, capacity, model_width),
            "expert",
            split_axis=0,
            concat_axis=0,
            tiled=True,
        )

    def sum_back(returned):
        flat = returned.reshape(expert_count * capacity, model_width)
        return matrix_multiply(own_pick.reshape(token_rows, expert_count * capacity), flat)

    hidden, saved = mixer_forward(
        tokens, segments, gain_first, query_mat, key_matrix, value_matrix, out_mat
    )
    normed_second, factor_second, expert_input = normalize(hidden, gain_second)
    input_all = lax.all_gather(expert_input, "expert")
    route_prob, chosen_hot = route_weights(expert_input, router_mat, routes)
    dense_prob = jnp.sum(chosen_hot * route_prob[:, :, None], 1)
    prob_all = lax.all_gather(dense_prob, "expert")

    column = jnp.arange(expert_count, dtype=jnp.int32)
    my_column = (mine[:, None] == column[None, :]).astype(jnp.float32)
    my_prob = jnp.sum(prob_all[None] * my_column[:, None, None, :], -1)
    row_prob = jnp.sum(jnp.where(picked, my_prob[:, :, None, :], 0.0), -1).reshape(
        local_count, owner_count * capacity, 1
    )

    owner_rows = rows_of(input_all).astype(jnp.bfloat16)
    cotangent_rows = rows_of(cotangent_all).astype(jnp.bfloat16).astype(jnp.float32)
    expert_out, kept_acts = expert_forward(owner_rows, gate_weight, up_weight, down_weight)
    expert_out = expert_out.astype(jnp.float32)
    weighted = (row_prob * expert_out).astype(jnp.bfloat16)
    row_grad_prob = jnp.sum(expert_out * cotangent_rows, -1).reshape(
        local_count, owner_count, capacity
    )
    token_grad_prob = jnp.sum(jnp.where(picked, row_grad_prob[..., None], 0.0), 2)
    back_prob = lax.all_to_all(
        token_grad_prob.transpose(1, 0, 2).reshape(expert_count, token_rows),
        "expert",
        split_axis=0,
        concat_axis=0,
        tiled=True,
    )
    grad_prob = jnp.sum(chosen_hot * back_prob.T[:, None, :], -1)
    grad_output = cotangent.astype(jnp.float32)

    grad_rows = (row_prob * cotangent_rows).astype(jnp.bfloat16)
    grad_owner_rows, gate_grad, up_grad, down_grad = expert_backward(
        grad_rows, owner_rows, kept_acts, gate_weight, up_weight, down_weight
    )
    grad_back = send_back(grad_owner_rows)
    expert_shares = (
        scatter_dp(gate_grad, 1),
        scatter_dp(up_grad, 1),
        scatter_dp(down_grad, 2),
    )
    grad_back, expert_shares, weighted = lax.optimization_barrier(
        (grad_back, expert_shares, weighted)
    )
    forward_back = send_back(weighted)
    output = (hidden + sum_back(forward_back)).astype(jnp.bfloat16)
    backward_sum = sum_back(grad_back)
    router_grad = route_back(route_prob, grad_prob, chosen_hot)
    grad_expert_input = backward_sum + matrix_multiply(
        router_grad, router_mat.T
    )
    router_wgrad = matrix_multiply(router_grad.T, expert_input)
    grad_normed, second_gain_grad = normalize_back(
        grad_expert_input, normed_second, factor_second, gain_second
    )
    grad_hidden = grad_output + grad_normed
    grad_tokens, first_gain_grad, query_wgrad, key_wgrad, value_wgrad, out_wgrad = mixer_backward(
        grad_hidden, saved, gain_first, query_mat, key_matrix, value_matrix, out_mat
    )

    out_share = all_sums(out_wgrad)
    joined = all_sums(jnp.concatenate([query_wgrad, key_wgrad, value_wgrad], 1))
    query_share = joined[:, :query_width]
    key_share = joined[:, query_width : query_width + key_width]
    value_share = joined[:, query_width + key_width :]
    extras = jnp.concatenate(
        [router_wgrad, first_gain_grad[None, :], second_gain_grad[None, :]], 0
    )
    extras = lax.psum(extras.astype(jnp.bfloat16), ("dp", "expert"))
    extras = lax.dynamic_slice_in_dim(
        extras, lax.axis_index("dp") * row_part, row_part, 1
    ).astype(jnp.float32)
    router_share = extras[:expert_count].T
    first_share = extras[expert_count]
    second_share = extras[expert_count + 1]
    return (
        output,
        grad_tokens,
        first_share,
        query_share,
        key_share,
        value_share,
        out_share,
        second_share,
        router_share,
        expert_shares[0],
        expert_shares[1],
        expert_shares[2],
    )


def turn(values, axis):
    if lax.axis_size("dp") != 2:
        return values
    low, high = jnp.split(values, 2, axis)
    first = lax.axis_index("dp") == 0
    return jnp.concatenate([jnp.where(first, low, high), jnp.where(first, high, low)], axis)


def times(left_op, pieces):
    total, start = None, 0
    for piece in pieces:
        part = matrix_multiply(left_op[:, start : start + piece.shape[0]], piece)
        total = part if total is None else total + part
        start += piece.shape[0]
    return total


def times_back(left_op, pieces):
    return jnp.concatenate([matrix_multiply(left_op, piece.T) for piece in pieces], 1)


def halves_forward(tokens, segments, gain_vec, query_mat, key_matrix, value_matrix, out_mat):
    token_rows = tokens.shape[0]
    local_sequences = token_rows // SEQUENCE_LENGTH
    query_groups = QUERY_HEADS // KEY_VALUE_HEADS
    cosine_table, sine_table = rope_tables(SEQUENCE_LENGTH, HEAD_DIM)
    mask_tab = segment_mask(segments.reshape(local_sequences, SEQUENCE_LENGTH))
    residual = tokens.astype(jnp.float32)
    normed, factor, attention_input = normalize(turn(residual, 1), gain_vec)
    query_rows = apply_rotary(
        times(attention_input, query_mat).reshape(
            local_sequences, SEQUENCE_LENGTH, QUERY_HEADS, HEAD_DIM
        ),
        cosine_table,
        sine_table,
    )
    query_rows = query_rows.astype(jnp.bfloat16).reshape(
        local_sequences, SEQUENCE_LENGTH, KEY_VALUE_HEADS, query_groups, HEAD_DIM
    )
    key_row_block = apply_rotary(
        times(attention_input, key_matrix).reshape(
            local_sequences, SEQUENCE_LENGTH, KEY_VALUE_HEADS, HEAD_DIM
        ),
        cosine_table,
        sine_table,
    ).astype(jnp.bfloat16)
    value_row_block = (
        times(attention_input, value_matrix)
        .astype(jnp.bfloat16)
        .reshape(local_sequences, SEQUENCE_LENGTH, KEY_VALUE_HEADS, HEAD_DIM)
    )
    scores = score_table(query_rows, key_row_block, mask_tab)
    row_peak = jnp.max(scores, -1, keepdims=True)
    logsum = row_peak + jnp.log(jnp.sum(jnp.exp(scores - row_peak), -1, keepdims=True))
    weights = jnp.exp(scores - logsum).astype(jnp.bfloat16)
    attended = product("shgqk,skhw->sqhgw", weights, value_row_block).astype(jnp.bfloat16)
    turned = turn(attended.reshape(token_rows, QUERY_HEADS * HEAD_DIM), 1)
    hidden = residual + times(turned, out_mat)
    saved = (
        normed,
        factor,
        attention_input,
        query_rows,
        key_row_block,
        value_row_block,
        attended,
        turned,
        logsum,
        mask_tab,
        cosine_table,
        sine_table,
    )
    return (hidden, saved)


def halves_backward(grad_hidden, saved, gain_vec, query_mat, key_matrix, value_matrix, out_mat):
    (
        normed,
        factor,
        attention_input,
        query_rows,
        key_row_block,
        value_row_block,
        attended,
        _,
        logsum,
        mask_tab,
        cosine_table,
        sine_table,
    ) = saved
    token_rows = grad_hidden.shape[0]
    local_sequences = token_rows // SEQUENCE_LENGTH
    grad_round = grad_hidden.astype(jnp.bfloat16)
    grad_attended = (
        turn(times_back(grad_round, out_mat).astype(jnp.bfloat16), 1).reshape(query_rows.shape)
    )
    scores = score_table(query_rows, key_row_block, mask_tab)
    prob_full = jnp.exp(scores - logsum)
    values_gradient = product("shgqk,sqhgw->skhw", prob_full.astype(jnp.bfloat16), grad_attended)
    grad_weights = product("sqhgw,skhw->shgqk", grad_attended, value_row_block)
    row_delta = product("sqhgw,sqhgw->shgq", grad_attended, attended)[..., None]
    grad_scores = (prob_full * (grad_weights - row_delta) * SCORE_SCALE).astype(jnp.bfloat16)
    grad_queries = product("shgqk,skhw->sqhgw", grad_scores, key_row_block)
    keys_gradient = product("shgqk,sqhgw->skhw", grad_scores, query_rows)
    query_grad = inverse_rotary(
        grad_queries.reshape(local_sequences, SEQUENCE_LENGTH, QUERY_HEADS, HEAD_DIM),
        cosine_table,
        sine_table,
    )
    query_grad = query_grad.astype(jnp.bfloat16).reshape(token_rows, QUERY_HEADS * HEAD_DIM)
    key_gradient = (
        inverse_rotary(keys_gradient, cosine_table, sine_table)
        .astype(jnp.bfloat16)
        .reshape(token_rows, KEY_VALUE_HEADS * HEAD_DIM)
    )
    value_gradient = values_gradient.astype(jnp.bfloat16).reshape(
        token_rows, KEY_VALUE_HEADS * HEAD_DIM
    )
    grad_attn_input = (
        times_back(query_grad, query_mat)
        + times_back(key_gradient, key_matrix)
        + times_back(value_gradient, value_matrix)
    )
    grad_normed, gain_grad = normalize_back(grad_attn_input, normed, factor, gain_vec)
    return (
        grad_hidden + turn(grad_normed, 1),
        turn(gain_grad, 0),
        [query_grad, key_gradient, value_gradient, grad_round],
    )


MESH = pl.DeviceIdType.MESH


def quotient(index, by):
    return index // by if isinstance(index, int) else lax.div(index, jnp.int32(by))


def parity(index):
    return index % 2 if isinstance(index, int) else lax.rem(index, jnp.int32(2))


def flip(index, by):
    total, weight = 0, 1
    for _ in range(6):
        one, two = parity(quotient(index, weight)), parity(quotient(by, weight))
        total = total + weight * (one + two - 2 * one * two)
        weight *= 2
    return total


def expert_at(index):
    return {"expert": index}


def send(src, dst, send_sem, recv_sem, where):
    return pltpu.make_async_remote_copy(
        src_ref=src,
        dst_ref=dst,
        send_sem=send_sem,
        recv_sem=recv_sem,
        device_id=where,
        device_id_type=MESH,
    )


def meet(count, with_dp):
    barrier = pltpu.get_barrier_semaphore()
    me = lax.axis_index("expert")

    def greet(by, carry):
        pl.semaphore_signal(
            barrier, inc=1, device_id=expert_at(flip(me, by)), device_id_type=MESH
        )
        return carry

    lax.fori_loop(1, count, greet, 0)
    if with_dp:
        pl.semaphore_signal(
            barrier, inc=1, device_id={"dp": 1 - lax.axis_index("dp")}, device_id_type=MESH
        )
    pl.semaphore_wait(barrier, count - 1 + (1 if with_dp else 0))


class Gather:
    def __init__(self, own, block_of, count, send_sems, recv_sems):
        self.own, self.block_of, self.count = own, block_of, count
        self.send_sems, self.recv_sems = send_sems, recv_sems
        self.me = lax.axis_index("expert")

    def copy(self, rel, by, src=None):
        block = self.block_of(flip(self.me, rel))
        there = flip(rel, by)
        return send(
            block if src is None else src,
            block,
            self.send_sems.at[there],
            self.recv_sems.at[there],
            expert_at(flip(self.me, by)),
        )

    def wait(self, rel):
        block = self.block_of(flip(self.me, rel))
        send(
            block, block, self.send_sems.at[rel], self.recv_sems.at[rel], expert_at(self.me)
        ).wait_recv()

    def begin(self):
        for by in list(range(4, self.count, 4)) + [2, 1]:
            self.copy(0, by, self.own).start()

    def pass_z(self, rel):
        self.wait(rel)
        self.copy(rel, 2).start()
        self.copy(rel, 1).start()

    def pass_x(self, rel):
        self.wait(rel + 2)
        self.copy(rel + 2, 1).start()

    def wait_sends(self):
        for rel in range(1, self.count):
            block = self.block_of(flip(self.me, rel))
            send(
                block, block, self.send_sems.at[rel], self.recv_sems.at[rel], expert_at(self.me)
            ).wait_send()

    def rest(self):
        self.pass_x(0)
        for rel in range(4, self.count, 4):
            self.pass_z(rel)
        for rel in range(4, self.count, 4):
            self.pass_x(rel)
        for rel in range(1, self.count, 2):
            self.wait(rel)
        self.wait_sends()


def front_kernel(count, pieces, *refs):
    mine, refs = refs[:pieces], refs[pieces:]
    cotangent, refs = refs[0], refs[1:]
    others, refs = refs[:pieces], refs[pieces:]
    gathered, y_send, y_recv, c_send, c_recv, g_send, g_recv, local = refs
    rows = cotangent.shape[0]
    me, dp = lax.axis_index("expert"), lax.axis_index("dp")
    core = parity(me)
    meet(count, True)

    def part(ref, which):
        half = ref.shape[0] // 2
        return ref.at[pl.ds(pl.multiple_of(which * half, half), half)]

    over_y = [
        send(
            part(mine[i], core),
            part(others[i], core),
            y_send.at[i],
            y_recv.at[i],
            {"dp": 1 - dp},
        )
        for i in range(pieces)
    ]
    for copy in over_y:
        copy.start()

    def block_of(index):
        return gathered.at[pl.ds(pl.multiple_of(index * rows, rows), rows)]

    keep = pltpu.make_async_copy(cotangent, block_of(me), local)
    keep.start()
    gather = Gather(cotangent, block_of, count, g_send, g_recv)
    gather.begin()
    over_core = [
        send(
            part(others[i], core),
            part(others[i], core),
            c_send.at[i],
            c_recv.at[i],
            expert_at(flip(me, 1)),
        )
        for i in range(pieces)
    ]
    gather.rest()
    for i in range(pieces):
        over_y[i].wait_recv()
        over_core[i].start()
    for i in range(pieces):
        send(
            part(mine[i], 1 - core),
            part(others[i], 1 - core),
            c_send.at[i],
            c_recv.at[i],
            expert_at(flip(me, 1)),
        ).wait_recv()
        over_core[i].wait_send()
        over_y[i].wait_send()
    keep.wait()


def front(own, cotangent, count):
    pieces = len(own)
    rows, width = cotangent.shape
    anywhere = pl.BlockSpec(memory_space=pl.ANY)
    results = pl.pallas_call(
        functools.partial(front_kernel, count, pieces),
        out_shape=[jax.ShapeDtypeStruct(part.shape, part.dtype) for part in own]
        + [jax.ShapeDtypeStruct((count * rows, width), cotangent.dtype)],
        in_specs=[anywhere] * (pieces + 1),
        out_specs=[anywhere] * (pieces + 1),
        scratch_shapes=[
            pltpu.SemaphoreType.DMA((pieces,)),
            pltpu.SemaphoreType.DMA((pieces,)),
            pltpu.SemaphoreType.DMA((pieces,)),
            pltpu.SemaphoreType.DMA((pieces,)),
            pltpu.SemaphoreType.DMA((count,)),
            pltpu.SemaphoreType.DMA((count,)),
            pltpu.SemaphoreType.DMA,
        ],
        compiler_params=pltpu.CompilerParams(collective_id=0, has_side_effects=True),
        name="front",
    )(*own, cotangent)
    return results[:pieces], results[pieces]


def dot_on(left_op, right_op, left_axis, right_axis):
    return lax.dot_general(
        left_op,
        right_op,
        (((left_axis,), (right_axis,)), ((), ())),
        preferred_element_type=jnp.float32,
    )


def experts_kernel(
    count,
    own_ref,
    cot_ref,
    prob_ref,
    gate_ref,
    up_ref,
    down_ref,
    grad_out,
    mix_out,
    gp_out,
    mine_out,
    mine_down,
    peer_out,
    peer_down,
    x_all,
    prob_all,
    gp_send_buf,
    both_all,
    inner_all,
    ge_all,
    part,
    cbuf,
    xbuf,
    zbuf,
    a_send,
    a_recv,
    p_send,
    p_recv,
    q_send,
    q_recv,
    c_send,
    c_recv,
    x_send,
    x_recv,
    z_send,
    z_recv,
):
    rows, width = own_ref.shape
    hidden = gate_ref.shape[2]
    pair = 2 * rows
    steps = count // 2
    depth = count // 4
    me, dp = lax.axis_index("expert"), lax.axis_index("dp")
    core = parity(me)
    meet(count, False)

    def block_of(index):
        return x_all.at[pl.ds(pl.multiple_of(index * rows, rows), rows)]

    gather = Gather(own_ref, block_of, count, a_send, a_recv)
    gather.begin()

    def prob_copy(by):
        there = flip(me, by)
        return send(
            prob_ref.at[there], prob_all.at[me], p_send.at[by], p_recv.at[by], expert_at(there)
        )

    def prob_start(by, carry):
        prob_copy(by).start()
        return carry

    lax.fori_loop(1, count, prob_start, 0)
    x_all[pl.ds(pl.multiple_of(me * rows, rows), rows)] = own_ref[...]
    prob_all[me] = prob_ref[me]

    def prob_wait(by, carry):
        there = flip(me, by)
        send(
            prob_ref.at[me], prob_all.at[there], p_send.at[by], p_recv.at[by], expert_at(there)
        ).wait_recv()
        return carry

    lax.fori_loop(1, count, prob_wait, 0)

    def rel_of(step):
        z_rel = quotient(step, 2)
        x_rel = jnp.where(step < 2, parity(step), 1 - parity(step))
        return 4 * z_rel + 2 * x_rel, z_rel

    eye = (
        lax.broadcasted_iota(jnp.int32, (pair, pair), 0)
        == lax.broadcasted_iota(jnp.int32, (pair, pair), 1)
    )
    theirs = pl.ds(pl.multiple_of((1 - core) * rows, rows), rows)
    ours = pl.ds(pl.multiple_of(core * rows, rows), rows)

    def core_copy(step):
        return send(
            part.at[step, :, theirs],
            cbuf.at[step],
            c_send.at[step],
            c_recv.at[step],
            expert_at(flip(me, 1)),
        )

    def x_copy(step, z_rel):
        return send(
            part.at[step, :, ours],
            xbuf.at[z_rel],
            x_send.at[z_rel],
            x_recv.at[z_rel],
            expert_at(flip(me, 2)),
        )

    def z_copy(step, z_rel):
        return send(
            part.at[step, :, ours],
            zbuf.at[z_rel],
            z_send.at[z_rel],
            z_recv.at[z_rel],
            expert_at(flip(me, 4 * z_rel)),
        )

    def compute(step):
        rel, _ = rel_of(step)
        chip = quotient(flip(me, rel), 2)
        where = pl.ds(pl.multiple_of(chip * pair, pair), pair)
        x = x_all[where, :]
        gate_pre = dot_on(x, gate_ref[0], 1, 0)
        up_pre = dot_on(x, up_ref[0], 1, 0)
        sig = jax.nn.sigmoid(gate_pre)
        act = gate_pre * sig
        inner = (act * up_pre).astype(jnp.bfloat16)
        inner_all[where, :] = inner
        out = dot_on(inner, down_ref[0], 1, 0).astype(jnp.bfloat16).astype(jnp.float32)
        prob_row = jnp.concatenate(
            [prob_all[2 * chip, 0:1, :], prob_all[2 * chip + 1, 0:1, :]], 1
        )
        prob = jnp.sum(jnp.where(eye, prob_row, 0.0), 1, keepdims=True)
        cot = cot_ref[where, :].astype(jnp.float32)
        part[step, 1] = (prob * out).astype(jnp.bfloat16)
        gp = jnp.sum(out * cot, 1, keepdims=True)
        gp_row = jnp.sum(jnp.where(eye, gp, 0.0), 0, keepdims=True)
        gp_send_buf[2 * chip] = jnp.broadcast_to(gp_row[:, :rows], (8, rows))
        gp_send_buf[2 * chip + 1] = jnp.broadcast_to(gp_row[:, rows:], (8, rows))
        ge = (prob * cot).astype(jnp.bfloat16)
        ge_all[where, :] = ge
        gi = dot_on(ge, down_ref[0], 1, 1)
        slope = sig * (1.0 + gate_pre * (1.0 - sig))
        gg = (gi * up_pre * slope).astype(jnp.bfloat16)
        gu = (gi * act).astype(jnp.bfloat16)
        both_all[where, :hidden] = gg
        both_all[where, hidden:] = gu
        part[step, 0] = (dot_on(gg, gate_ref[0], 1, 1) + dot_on(gu, up_ref[0], 1, 1)).astype(
            jnp.bfloat16
        )

    def finish(step):
        rel, z_rel = rel_of(step)
        core_copy(step).wait_recv()
        total = part[step, :, ours].astype(jnp.float32) + cbuf[step].astype(jnp.float32)

        @pl.when(step == 0)
        def _():
            grad_out[...] = total[0]
            mix_out[...] = total[1]

        @pl.when((step == 1) | ((step > 1) & (parity(step) == 0)))
        def _():
            part[step, :, ours] = total.astype(jnp.bfloat16)
            x_copy(step, z_rel).start()

        @pl.when((step > 1) & (parity(step) == 1))
        def _():
            x_copy(step, z_rel).wait_recv()
            part[step, :, ours] = (total + xbuf[z_rel].astype(jnp.float32)).astype(jnp.bfloat16)
            z_copy(step, z_rel).start()

    def turn_of(step, carry):
        rel, z_rel = rel_of(step)

        gather.wait(rel + 1)
        compute(step)
        core_copy(step).start()

        @pl.when(step > 0)
        def _():
            finish(step - 1)

        @pl.when(step == 0)
        def _():
            gather.pass_x(0)

        @pl.when((parity(step) == 0) & (step < steps - 2))
        def _():
            gather.pass_z(4 * (z_rel + 1))

        @pl.when((parity(step) == 1) & (step < steps - 1))
        def _():
            gather.pass_x(4 * (z_rel + 1))

        return carry

    lax.fori_loop(0, steps, turn_of, 0)
    finish(steps - 1)

    def gp_copy(by):
        there = flip(me, by)
        return send(
            gp_send_buf.at[there], gp_out.at[me], q_send.at[by], q_recv.at[by], expert_at(there)
        )

    def gp_start(by, carry):
        gp_copy(by).start()
        return carry

    lax.fori_loop(1, count, gp_start, 0)
    gp_out[me] = gp_send_buf[me]

    half = width // 2
    for which, target, lower in ((1 - dp, peer_out, peer_down), (dp, mine_out, mine_down)):

        def rows_of(index, carry, which=which, target=target):
            tile = half // 2
            at = pl.multiple_of(which * half + index * tile, tile)
            into = pl.ds(pl.multiple_of(index * tile, tile), tile)
            x = x_all[:, pl.ds(at, tile)]
            both = dot_on(x, both_all[...], 0, 0).astype(target.dtype)
            target[0, into, :] = both[:, :hidden]
            target[1, into, :] = both[:, hidden:]
            return carry

        lax.fori_loop(0, 2, rows_of, 0)

        def down_of(index, carry, which=which, lower=lower):
            tile = hidden // 2
            at = pl.ds(pl.multiple_of(index * tile, tile), tile)
            grads = ge_all[:, pl.ds(pl.multiple_of(which * half, half), half)]
            lower[at, :] = dot_on(inner_all[:, at], grads, 0, 0).astype(lower.dtype)
            return carry

        lax.fori_loop(0, 2, down_of, 0)

    send(
        part.at[0, :, ours], xbuf.at[0], x_send.at[0], x_recv.at[0], expert_at(flip(me, 2))
    ).wait_recv()
    sums = xbuf[0].astype(jnp.float32)
    for z_rel in range(1, depth):
        z_copy(2 * z_rel, z_rel).wait_recv()
        sums = sums + zbuf[z_rel].astype(jnp.float32)
    grad_out[...] += sums[0]
    mix_out[...] += sums[1]

    def settle(by, carry):
        there = flip(me, by)
        send(
            gp_send_buf.at[me], gp_out.at[there], q_send.at[by], q_recv.at[by], expert_at(there)
        ).wait()
        prob_copy(by).wait_send()
        return carry

    lax.fori_loop(1, count, settle, 0)
    gather.wait_sends()
    for step in range(steps):
        core_copy(step).wait_send()
    for z_rel in range(depth):
        x_copy(2 * z_rel, z_rel).wait_send()
    for z_rel in range(1, depth):
        z_copy(2 * z_rel, z_rel).wait_send()


def experts(expert_input, cotangent_all, prob, gate_weight, up_weight, down_weight):
    count = prob.shape[0]
    rows, width = expert_input.shape
    hidden = gate_weight.shape[2]
    total = count * rows
    steps, depth = count // 2, count // 4
    half = width // 2
    local = pl.BlockSpec(memory_space=pltpu.VMEM)
    pairs = [pltpu.SemaphoreType.DMA((n,)) for n in (count, count, count, steps, depth, depth)]
    semaphores = [item for item in pairs for _ in range(2)]
    bf16 = jnp.bfloat16
    return pl.pallas_call(
        functools.partial(experts_kernel, count),
        out_shape=[
            jax.ShapeDtypeStruct((rows, width), jnp.float32),
            jax.ShapeDtypeStruct((rows, width), jnp.float32),
            jax.ShapeDtypeStruct((count, 8, rows), jnp.float32),
            jax.ShapeDtypeStruct((2, half, hidden), jnp.float32),
            jax.ShapeDtypeStruct((hidden, half), jnp.float32),
            jax.ShapeDtypeStruct((2, half, hidden), bf16),
            jax.ShapeDtypeStruct((hidden, half), bf16),
        ],
        in_specs=[local] * 6,
        out_specs=[local] * 7,
        scratch_shapes=[
            pltpu.VMEM((total, width), bf16),
            pltpu.VMEM((count, 8, rows), jnp.float32),
            pltpu.VMEM((count, 8, rows), jnp.float32),
            pltpu.VMEM((total, 2 * hidden), bf16),
            pltpu.VMEM((total, hidden), bf16),
            pltpu.VMEM((total, width), bf16),
            pltpu.VMEM((steps, 2, 2 * rows, width), bf16),
            pltpu.VMEM((steps, 2, rows, width), bf16),
            pltpu.VMEM((depth, 2, rows, width), bf16),
            pltpu.VMEM((depth, 2, rows, width), bf16),
        ]
        + semaphores,
        compiler_params=pltpu.CompilerParams(
            collective_id=1, has_side_effects=True, vmem_limit_bytes=58 * 2**20
        ),
        cost_estimate=pl.CostEstimate(
            flops=18 * total * width * hidden, bytes_accessed=20 * total * width, transcendentals=0
        ),
        name="experts",
    )(expert_input, cotangent_all, prob, gate_weight, up_weight, down_weight)


def late_kernel(
    count,
    cuts,
    pay_ref,
    attention_ref,
    attended_ref,
    all_out,
    arrived,
    peer_buf,
    y_buf,
    mine,
    a_send,
    a_recv,
    g_send,
    g_recv,
    y_send,
    y_recv,
):
    first, last = cuts
    rows = pay_ref.shape[2]
    half = all_out.shape[2]
    me, dp = lax.axis_index("expert"), lax.axis_index("dp")
    meet(count, True)

    def columns(index):
        return pl.ds(pl.multiple_of(index * rows, rows), rows)

    def scatter(by):
        there = flip(me, by)
        return send(
            pay_ref.at[there],
            arrived.at[:, columns(me)],
            a_send.at[by],
            a_recv.at[by],
            expert_at(there),
        )

    def scatter_start(back, carry):
        scatter(count - back).start()
        return carry

    lax.fori_loop(1, count, scatter_start, 0)
    arrived[:, columns(me)] = pay_ref[me]

    def scatter_wait(by, carry):
        there = flip(me, by)
        send(
            pay_ref.at[me],
            arrived.at[:, columns(there)],
            a_send.at[by],
            a_recv.at[by],
            expert_at(there),
        ).wait()
        return carry

    lax.fori_loop(1, count, scatter_wait, 0)

    extra = arrived[last:, :].astype(jnp.float32)
    summed = extra[:, :rows]
    for index in range(1, count):
        summed = summed + extra[:, index * rows : (index + 1) * rows]
    edge = summed.shape[0] // 2
    blank = jnp.zeros((edge, half - rows), jnp.float32)
    own_extra = jnp.concatenate([summed[:edge], blank], 1)
    peer_extra = jnp.concatenate([summed[edge:], blank], 1)
    blank = jnp.zeros((edge, half), jnp.float32)

    def tile_of(at):
        return jnp.concatenate(
            [
                dot_on(arrived[:first, :], attention_ref[:, at], 1, 0),
                dot_on(arrived[first:last, :], attended_ref[:, at], 1, 0),
            ],
            0,
        )

    peer_buf[...] = jnp.concatenate(
        [tile_of(slice(half, 2 * half)), peer_extra, blank], 0
    ).astype(jnp.bfloat16)
    over = send(peer_buf, y_buf, y_send, y_recv, {"dp": 1 - dp})
    over.start()
    own = jnp.concatenate([tile_of(slice(0, half)), own_extra, blank], 0)
    over.wait()
    mine[...] = (
        own + y_buf[...].astype(jnp.float32)
    ).astype(jnp.bfloat16)
    gather = Gather(mine, lambda index: all_out.at[index], count, g_send, g_recv)
    gather.begin()
    all_out[me] = mine[...]
    gather.rest()


def late_sums(payload, attention_all, attended_all, cuts):
    count, lines, rows = payload.shape
    half = attention_all.shape[1] // 2
    local = pl.BlockSpec(memory_space=pltpu.VMEM)
    bf16 = jnp.bfloat16
    return pl.pallas_call(
        functools.partial(late_kernel, count, cuts),
        out_shape=jax.ShapeDtypeStruct((count, lines, half), bf16),
        in_specs=[local] * 3,
        out_specs=local,
        scratch_shapes=[
            pltpu.VMEM((lines, count * rows), bf16),
            pltpu.VMEM((lines, half), bf16),
            pltpu.VMEM((lines, half), bf16),
            pltpu.VMEM((lines, half), bf16),
            pltpu.SemaphoreType.DMA((count,)),
            pltpu.SemaphoreType.DMA((count,)),
            pltpu.SemaphoreType.DMA((count,)),
            pltpu.SemaphoreType.DMA((count,)),
            pltpu.SemaphoreType.DMA,
            pltpu.SemaphoreType.DMA,
        ],
        compiler_params=pltpu.CompilerParams(
            collective_id=2, has_side_effects=True, vmem_limit_bytes=40 * 2**20
        ),
        name="late",
    )(payload, attention_all, attended_all)


def shards_together(
    tokens,
    segments,
    routes,
    first_gain,
    query_weight,
    key_projection_weight,
    value_projection_weight,
    out_weight,
    second_gain,
    router_weight,
    gate_weight,
    up_weight,
    down_weight,
    cotangent,
):
    token_rows = tokens.shape[0]
    expert_count = router_weight.shape[1]
    owner_count = lax.axis_size("expert")
    dp_count = lax.axis_size("dp")

    small = jnp.concatenate([router_weight, first_gain[:, None], second_gain[:, None]], 1)
    small = jnp.pad(small, ((0, 0), (0, -small.shape[1] % 128)))
    own = [query_weight, key_projection_weight, value_projection_weight, out_weight, small]
    other, cotangent_all = front(own, cotangent, owner_count)
    query_mat, key_matrix, value_matrix, out_mat, small = (list(p) for p in zip(own, other))
    small_mat = jnp.concatenate(small, 0)
    router_mat = turn(small_mat[:, :expert_count], 0)
    gain_first = small_mat[:, expert_count]
    gain_second = turn(small_mat[:, expert_count + 1], 0)

    hidden, saved = halves_forward(
        tokens, segments, gain_first, query_mat, key_matrix, value_matrix, out_mat
    )
    attention_all = lax.all_gather(saved[2], "expert", axis=0, tiled=True)
    attended_all = lax.all_gather(saved[7], "expert", axis=0, tiled=True)
    normed_second, factor_second, expert_input = normalize(hidden, gain_second)
    route_prob, chosen_hot = route_weights(expert_input, router_mat, routes)
    dense_prob = jnp.sum(chosen_hot * route_prob[:, :, None], 1)
    prob = jnp.broadcast_to(dense_prob.T[:, None, :], (owner_count, 8, token_rows))
    grad_sum, mixture, back_prob, mine, mine_down, peer, peer_down = experts(
        expert_input, cotangent_all, prob, gate_weight, up_weight, down_weight
    )
    swap = [(0, 1), (1, 0)]
    peer = lax.ppermute(peer, "dp", swap)
    peer_down = lax.ppermute(peer_down, "dp", swap)
    output = (hidden + mixture).astype(jnp.bfloat16)
    grad_prob = jnp.sum(chosen_hot * back_prob[:, 0, :].T[:, None, :], -1)
    router_grad = route_back(route_prob, grad_prob, chosen_hot)
    grad_expert_input = grad_sum + matrix_multiply(router_grad, router_mat.T)
    router_wgrad = matrix_multiply(router_grad.T, expert_input)
    grad_normed, second_gain_grad = normalize_back(
        grad_expert_input, normed_second, factor_second, gain_second
    )
    grad_hidden = cotangent.astype(jnp.float32) + grad_normed
    grad_tokens, first_gain_grad, late = halves_backward(
        grad_hidden, saved, gain_first, query_mat, key_matrix, value_matrix, out_mat
    )

    extras = jnp.concatenate(
        [router_wgrad, first_gain_grad[None, :], second_gain_grad[None, :]], 0
    )
    slices = [
        grad.T.reshape(owner_count, grad.shape[1] // owner_count, token_rows) for grad in late
    ]
    extra_count, extra_width = extras.shape
    part = extra_width // (owner_count * dp_count)
    spread = (
        extras.reshape(extra_count, dp_count, owner_count, part)
        .transpose(2, 1, 0, 3)
        .reshape(owner_count, dp_count, extra_count * part)
        .astype(jnp.bfloat16)
    )
    spread = jnp.pad(spread, ((0, 0), (0, 0), (0, -spread.shape[2] % (8 * token_rows))))
    spread = turn(spread, 1).reshape(owner_count, -1, token_rows)
    payload = jnp.concatenate(slices + [spread], 1)
    last = sum(piece.shape[1] for piece in slices)
    everything = late_sums(
        payload, attention_all, attended_all, (last - slices[3].shape[1], last)
    )
    half = everything.shape[2]
    start, shares = 0, []
    for piece in slices:
        end = start + piece.shape[1]
        shares.append(everything[:, start:end].reshape(-1, half).T.astype(jnp.float32))
        start = end
    edge = spread.shape[1] // 2
    extras = everything[:, last : last + edge, :token_rows].reshape(owner_count, -1)
    extras = extras[:, : extra_count * part].reshape(owner_count, extra_count, part)
    extras = extras.transpose(1, 0, 2).reshape(extra_count, -1).astype(jnp.float32)
    query_share, key_share, value_share, out_share = shares
    return (
        output,
        grad_tokens,
        extras[expert_count],
        query_share,
        key_share,
        value_share,
        out_share,
        extras[expert_count + 1],
        extras[:expert_count].T,
        mine[0:1] + peer[0:1].astype(jnp.float32),
        mine[1:2] + peer[1:2].astype(jnp.float32),
        (mine_down + peer_down.astype(jnp.float32))[None],
    )


def solution(mesh):
    placed = (
        P(("dp", "expert"), None),
        P(("dp", "expert")),
        P(("dp", "expert"), None),
        P("dp"),
        P("dp", None),
        P("dp", None),
        P("dp", None),
        P("dp", None),
        P("dp"),
        P("dp", None),
        P("expert", None, None),
        P("expert", None, None),
        P("expert", None, None),
        P(("dp", "expert"), None),
    )
    owners = mesh.shape["expert"]
    together = mesh.shape["dp"] == 2 and owners >= 8 and owners & (owners - 1) == 0
    return jax.shard_map(
        shards_together if together else shards,
        mesh=mesh,
        in_specs=placed,
        out_specs=(
            P(("dp", "expert"), None),
            P(("dp", "expert"), None),
            P("dp"),
            P("dp", None),
            P("dp", None),
            P("dp", None),
            P("dp", None),
            P("dp"),
            P("dp", None),
            P("expert", "dp", None),
            P("expert", "dp", None),
            P("expert", None, "dp"),
        ),
        check_vma=False,
    )
```

```python
import functools

import jax
import jax.numpy as jnp
from jax import lax
from jax.experimental import pallas as pl
from jax.experimental.pallas import tpu as pltpu
from jax.sharding import PartitionSpec as P

QUERY_HEADS = 16
KEY_VALUE_HEADS = 8
HEAD_DIM = 64
SEQUENCE_LENGTH = 128


EPSILON = 1e-06
SCORE_SCALE = 0.015625
ROPE_BASE = 10000.0
MASKED = -1e30


def product(pattern, left_op, right_op):
    return jnp.einsum(pattern, left_op, right_op, preferred_element_type=jnp.float32)


def matrix_multiply(left_op, right_op):
    return jnp.dot(left_op, right_op, preferred_element_type=jnp.float32)


def rope_tables(seq_len, head_size):
    positions = jnp.arange(seq_len, dtype=jnp.float32)
    exponent = jnp.arange(head_size // 2, dtype=jnp.float32) * (2.0 / head_size)
    angles = positions[:, None] * (ROPE_BASE ** (-exponent))[None, :]
    return (jnp.cos(angles)[None, :, None, :], jnp.sin(angles)[None, :, None, :])


def apply_rotary(values, cosine_table, sine_table):
    middle = values.shape[-1] // 2
    first_half = values[..., :middle]
    second_half = values[..., middle:]
    return jnp.concatenate(
        [
            first_half * cosine_table - second_half * sine_table,
            second_half * cosine_table + first_half * sine_table,
        ],
        -1,
    )


def inverse_rotary(gradient, cosine_table, sine_table):
    middle = gradient.shape[-1] // 2
    first_half = gradient[..., :middle]
    second_half = gradient[..., middle:]
    return jnp.concatenate(
        [
            first_half * cosine_table + second_half * sine_table,
            second_half * cosine_table - first_half * sine_table,
        ],
        -1,
    )


def normalize(values, gain_vec):
    factor = lax.rsqrt(jnp.mean(values * values, -1, keepdims=True) + EPSILON)
    normed = values * factor
    return (normed, factor, (normed * gain_vec).astype(jnp.bfloat16))


def normalize_back(gradient, normed, factor, gain_vec):
    gain_grad = jnp.sum(gradient * normed, 0)
    scaled = gradient * gain_vec
    return (factor * (scaled - normed * jnp.mean(scaled * normed, -1, keepdims=True)), gain_grad)


def segment_mask(segments):
    seq_len = segments.shape[1]
    causal = jnp.arange(seq_len)[:, None] >= jnp.arange(seq_len)[None, :]
    same_doc = segments[:, :, None] == segments[:, None, :]
    return (same_doc & causal[None])[:, None, None]


def score_table(query_rows, key_row_block, mask_tab):
    raw_scores = product("sqhgw,skhw->shgqk", query_rows, key_row_block) * SCORE_SCALE
    return jnp.where(mask_tab, raw_scores, MASKED)


def mixer_forward(tokens, segments, gain_vec, query_mat, key_matrix, value_matrix, out_mat):
    token_rows = tokens.shape[0]
    local_sequences = token_rows // SEQUENCE_LENGTH
    query_groups = QUERY_HEADS // KEY_VALUE_HEADS
    cosine_table, sine_table = rope_tables(SEQUENCE_LENGTH, HEAD_DIM)
    mask_tab = segment_mask(segments.reshape(local_sequences, SEQUENCE_LENGTH))
    residual = tokens.astype(jnp.float32)
    normed, factor, attention_input = normalize(residual, gain_vec)
    query_rows = apply_rotary(
        matrix_multiply(attention_input, query_mat).reshape(
            local_sequences, SEQUENCE_LENGTH, QUERY_HEADS, HEAD_DIM
        ),
        cosine_table,
        sine_table,
    )
    query_rows = query_rows.astype(jnp.bfloat16).reshape(
        local_sequences, SEQUENCE_LENGTH, KEY_VALUE_HEADS, query_groups, HEAD_DIM
    )
    key_row_block = apply_rotary(
        matrix_multiply(attention_input, key_matrix).reshape(
            local_sequences, SEQUENCE_LENGTH, KEY_VALUE_HEADS, HEAD_DIM
        ),
        cosine_table,
        sine_table,
    ).astype(jnp.bfloat16)
    value_row_block = (
        matrix_multiply(attention_input, value_matrix)
        .astype(jnp.bfloat16)
        .reshape(local_sequences, SEQUENCE_LENGTH, KEY_VALUE_HEADS, HEAD_DIM)
    )
    scores = score_table(query_rows, key_row_block, mask_tab)
    row_peak = jnp.max(scores, -1, keepdims=True)
    logsum = row_peak + jnp.log(jnp.sum(jnp.exp(scores - row_peak), -1, keepdims=True))
    weights = jnp.exp(scores - logsum).astype(jnp.bfloat16)
    attended = product("shgqk,skhw->sqhgw", weights, value_row_block).astype(jnp.bfloat16)
    hidden = residual + matrix_multiply(
        attended.reshape(token_rows, QUERY_HEADS * HEAD_DIM), out_mat
    )
    saved = (
        normed,
        factor,
        attention_input,
        query_rows,
        key_row_block,
        value_row_block,
        attended,
        logsum,
        mask_tab,
        cosine_table,
        sine_table,
    )
    return (hidden, saved)


def mixer_backward(grad_hidden, saved, gain_vec, query_mat, key_matrix, value_matrix, out_mat):
    (
        normed,
        factor,
        attention_input,
        query_rows,
        key_row_block,
        value_row_block,
        attended,
        logsum,
        mask_tab,
        cosine_table,
        sine_table,
    ) = saved
    token_rows = grad_hidden.shape[0]
    local_sequences = token_rows // SEQUENCE_LENGTH
    grad_round = grad_hidden.astype(jnp.bfloat16)
    out_grad = matrix_multiply(attended.reshape(token_rows, QUERY_HEADS * HEAD_DIM).T, grad_round)
    grad_attended = (
        matrix_multiply(grad_round, out_mat.T).astype(jnp.bfloat16).reshape(query_rows.shape)
    )
    scores = score_table(query_rows, key_row_block, mask_tab)
    prob_full = jnp.exp(scores - logsum)
    values_gradient = product("shgqk,sqhgw->skhw", prob_full.astype(jnp.bfloat16), grad_attended)
    grad_weights = product("sqhgw,skhw->shgqk", grad_attended, value_row_block)
    row_delta = product("sqhgw,sqhgw->shgq", grad_attended, attended)[..., None]
    grad_scores = (prob_full * (grad_weights - row_delta) * SCORE_SCALE).astype(jnp.bfloat16)
    grad_queries = product("shgqk,skhw->sqhgw", grad_scores, key_row_block)
    keys_gradient = product("shgqk,sqhgw->skhw", grad_scores, query_rows)
    query_grad = inverse_rotary(
        grad_queries.reshape(local_sequences, SEQUENCE_LENGTH, QUERY_HEADS, HEAD_DIM),
        cosine_table,
        sine_table,
    )
    query_grad = query_grad.astype(jnp.bfloat16).reshape(token_rows, QUERY_HEADS * HEAD_DIM)
    key_gradient = (
        inverse_rotary(keys_gradient, cosine_table, sine_table)
        .astype(jnp.bfloat16)
        .reshape(token_rows, KEY_VALUE_HEADS * HEAD_DIM)
    )
    value_gradient = values_gradient.astype(jnp.bfloat16).reshape(
        token_rows, KEY_VALUE_HEADS * HEAD_DIM
    )
    query_wgrad = matrix_multiply(attention_input.T, query_grad)
    key_wgrad = matrix_multiply(attention_input.T, key_gradient)
    value_wgrad = matrix_multiply(attention_input.T, value_gradient)
    grad_attn_input = (
        matrix_multiply(query_grad, query_mat.T)
        + matrix_multiply(key_gradient, key_matrix.T)
        + matrix_multiply(value_gradient, value_matrix.T)
    )
    grad_normed, gain_grad = normalize_back(grad_attn_input, normed, factor, gain_vec)
    return (grad_hidden + grad_normed, gain_grad, query_wgrad, key_wgrad, value_wgrad, out_grad)


def route_weights(expert_input, router_mat, routes):
    logits = matrix_multiply(expert_input, router_mat)
    chosen_hot = (
        routes[:, :, None] == jnp.arange(router_mat.shape[1], dtype=jnp.int32)[None, None, :]
    ).astype(jnp.float32)
    chosen = jnp.sum(chosen_hot * logits[:, None, :], -1)
    return (jax.nn.softmax(chosen, -1), chosen_hot)


def route_back(route_prob, grad_prob, chosen_hot):
    grad_chosen = route_prob * (grad_prob - jnp.sum(route_prob * grad_prob, -1, keepdims=True))
    return jnp.sum(chosen_hot * grad_chosen[:, :, None], 1).astype(jnp.bfloat16)


def expert_forward(owner_rows, gate_mat, up_mat, down_mat):
    gate_pre = product("erd,edf->erf", owner_rows, gate_mat)
    up_pre = product("erd,edf->erf", owner_rows, up_mat)
    gate_sig = jax.nn.sigmoid(gate_pre)
    gate_act = gate_pre * gate_sig
    inner_acts = (gate_act * up_pre).astype(jnp.bfloat16)
    expert_out = product("erf,efd->erd", inner_acts, down_mat).astype(jnp.bfloat16)
    return (expert_out, (gate_pre, up_pre, gate_sig, gate_act, inner_acts))


def expert_backward(grad_rows, owner_rows, kept_acts, gate_mat, up_mat, down_mat):
    gate_pre, up_pre, gate_sig, gate_act, inner_acts = kept_acts
    grad_inner = product("erd,efd->erf", grad_rows, down_mat)
    down_grad = product("erf,erd->efd", inner_acts, grad_rows)
    silu_slope = gate_sig * (1.0 + gate_pre * (1.0 - gate_sig))
    grad_gate = (grad_inner * up_pre * silu_slope).astype(jnp.bfloat16)
    grad_up = (grad_inner * gate_act).astype(jnp.bfloat16)
    gate_grad = product("erd,erf->edf", owner_rows, grad_gate)
    up_grad = product("erd,erf->edf", owner_rows, grad_up)
    grad_owner_rows = product("erf,edf->erd", grad_gate, gate_mat) + product(
        "erf,edf->erd", grad_up, up_mat
    )
    return (grad_owner_rows.astype(jnp.bfloat16), gate_grad, up_grad, down_grad)


def gather_dp(local_part):
    dp_count = lax.axis_size("dp")
    owner_count = lax.axis_size("expert")
    if dp_count != 2 or owner_count % 2:
        return lax.all_gather(local_part, "dp", axis=0, tiled=True)
    low, high = jnp.split(local_part, 2, 0)
    even = lax.axis_index("expert") % 2 == 0
    near = lax.ppermute(jnp.where(even, low, high), "dp", [(0, 1), (1, 0)])
    far = lax.ppermute(near, "expert", [(i, i ^ 1) for i in range(owner_count)])
    other = jnp.concatenate([jnp.where(even, near, far), jnp.where(even, far, near)], 0)
    first = lax.axis_index("dp") == 0
    return jnp.concatenate(
        [jnp.where(first, local_part, other), jnp.where(first, other, local_part)], 0
    )


def all_sums(partial):
    owner_count = lax.axis_size("expert")
    dp_count = lax.axis_size("dp")
    width = partial.shape[1]
    pieces = partial.astype(jnp.bfloat16).reshape(dp_count, owner_count, -1, width)
    piece = lax.psum_scatter(
        pieces.transpose(1, 0, 2, 3).reshape(-1, width), "expert", scatter_dimension=0, tiled=True
    )
    piece = scatter_dp(piece, 0).astype(jnp.bfloat16)
    return lax.all_gather(piece, "expert", axis=0, tiled=True).astype(jnp.float32)


def scatter_dp(partial, axis):
    dp_count = lax.axis_size("dp")
    rounded = partial.astype(jnp.bfloat16)
    if dp_count != 2:
        return lax.psum_scatter(rounded, "dp", scatter_dimension=axis, tiled=True).astype(
            jnp.float32
        )
    low, high = jnp.split(rounded, 2, axis)
    first = lax.axis_index("dp") == 0
    arrived = lax.ppermute(jnp.where(first, high, low), "dp", [(0, 1), (1, 0)])
    return jnp.where(first, low, high).astype(jnp.float32) + arrived.astype(jnp.float32)


def shards(
    tokens,
    segments,
    routes,
    first_gain,
    query_weight,
    key_projection_weight,
    value_projection_weight,
    out_weight,
    second_gain,
    router_weight,
    gate_weight,
    up_weight,
    down_weight,
    cotangent,
):
    token_rows, model_width = tokens.shape
    top_count = routes.shape[1]
    expert_count = router_weight.shape[1]
    owner_count = lax.axis_size("expert")
    local_count = gate_weight.shape[0]
    key_width = key_projection_weight.shape[1]
    query_width = query_weight.shape[1]
    capacity = 5 * token_rows * top_count // (4 * expert_count)
    row_part = router_weight.shape[0]

    small = jnp.concatenate(
        [router_weight, first_gain[:, None], second_gain[:, None]], 1
    )
    small_mat = gather_dp(small)
    router_mat = small_mat[:, :expert_count]
    gain_first = small_mat[:, expert_count]
    gain_second = small_mat[:, expert_count + 1]
    joined_mat = gather_dp(
        jnp.concatenate([query_weight, key_projection_weight, value_projection_weight], 1)
    )
    query_mat = joined_mat[:, :query_width]
    key_matrix = joined_mat[:, query_width : query_width + key_width]
    value_matrix = joined_mat[:, query_width + key_width :]
    out_mat = gather_dp(out_weight)

    routes_all = lax.all_gather(routes, "expert")
    cotangent_all = lax.all_gather(cotangent, "expert")

    mine = lax.axis_index("expert") * local_count + jnp.arange(local_count, dtype=jnp.int32)
    hit = jnp.any(routes_all[None] == mine[:, None, None, None], -1)
    before = (
        jnp.arange(token_rows)[:, None] < jnp.arange(token_rows)[None, :]
    ).astype(jnp.bfloat16)
    rank = product("lst,tu->lsu", hit.astype(jnp.bfloat16), before).astype(jnp.int32)
    slot = jnp.where(hit, rank, -1)
    picked = slot[:, :, None, :] == jnp.arange(capacity, dtype=jnp.int32)[None, None, :, None]
    pick = picked.astype(jnp.bfloat16)

    def rows_of(gathered):
        rows = product("lsct,std->lscd", pick, gathered)
        return rows.reshape(local_count, owner_count * capacity, model_width)

    own_hot = (routes[:, :, None] == jnp.arange(expert_count, dtype=jnp.int32)).any(1)
    own_rank = matrix_multiply(before.T, own_hot.astype(jnp.bfloat16)).astype(jnp.int32)
    own_slot = jnp.where(own_hot, own_rank, -1)
    own_pick = (
        own_slot[:, :, None] == jnp.arange(capacity, dtype=jnp.int32)[None, None, :]
    ).astype(jnp.bfloat16)

    def send_back(rows):
        shaped = rows.reshape(local_count, owner_count, capacity, model_width)
        return lax.all_to_all(
            shaped.transpose(1, 0, 2, 3).reshape(expert_count, capacity, model_width),
            "expert",
            split_axis=0,
            concat_axis=0,
            tiled=True,
        )

    def sum_back(returned):
        flat = returned.reshape(expert_count * capacity, model_width)
        return matrix_multiply(own_pick.reshape(token_rows, expert_count * capacity), flat)

    hidden, saved = mixer_forward(
        tokens, segments, gain_first, query_mat, key_matrix, value_matrix, out_mat
    )
    normed_second, factor_second, expert_input = normalize(hidden, gain_second)
    input_all = lax.all_gather(expert_input, "expert")
    route_prob, chosen_hot = route_weights(expert_input, router_mat, routes)
    dense_prob = jnp.sum(chosen_hot * route_prob[:, :, None], 1)
    prob_all = lax.all_gather(dense_prob, "expert")

    column = jnp.arange(expert_count, dtype=jnp.int32)
    my_column = (mine[:, None] == column[None, :]).astype(jnp.float32)
    my_prob = jnp.sum(prob_all[None] * my_column[:, None, None, :], -1)
    row_prob = jnp.sum(jnp.where(picked, my_prob[:, :, None, :], 0.0), -1).reshape(
        local_count, owner_count * capacity, 1
    )

    owner_rows = rows_of(input_all).astype(jnp.bfloat16)
    cotangent_rows = rows_of(cotangent_all).astype(jnp.bfloat16).astype(jnp.float32)
    expert_out, kept_acts = expert_forward(owner_rows, gate_weight, up_weight, down_weight)
    expert_out = expert_out.astype(jnp.float32)
    weighted = (row_prob * expert_out).astype(jnp.bfloat16)
    row_grad_prob = jnp.sum(expert_out * cotangent_rows, -1).reshape(
        local_count, owner_count, capacity
    )
    token_grad_prob = jnp.sum(jnp.where(picked, row_grad_prob[..., None], 0.0), 2)
    back_prob = lax.all_to_all(
        token_grad_prob.transpose(1, 0, 2).reshape(expert_count, token_rows),
        "expert",
        split_axis=0,
        concat_axis=0,
        tiled=True,
    )
    grad_prob = jnp.sum(chosen_hot * back_prob.T[:, None, :], -1)
    grad_output = cotangent.astype(jnp.float32)

    grad_rows = (row_prob * cotangent_rows).astype(jnp.bfloat16)
    grad_owner_rows, gate_grad, up_grad, down_grad = expert_backward(
        grad_rows, owner_rows, kept_acts, gate_weight, up_weight, down_weight
    )
    grad_back = send_back(grad_owner_rows)
    expert_shares = (
        scatter_dp(gate_grad, 1),
        scatter_dp(up_grad, 1),
        scatter_dp(down_grad, 2),
    )
    grad_back, expert_shares, weighted = lax.optimization_barrier(
        (grad_back, expert_shares, weighted)
    )
    forward_back = send_back(weighted)
    output = (hidden + sum_back(forward_back)).astype(jnp.bfloat16)
    backward_sum = sum_back(grad_back)
    router_grad = route_back(route_prob, grad_prob, chosen_hot)
    grad_expert_input = backward_sum + matrix_multiply(
        router_grad, router_mat.T
    )
    router_wgrad = matrix_multiply(router_grad.T, expert_input)
    grad_normed, second_gain_grad = normalize_back(
        grad_expert_input, normed_second, factor_second, gain_second
    )
    grad_hidden = grad_output + grad_normed
    grad_tokens, first_gain_grad, query_wgrad, key_wgrad, value_wgrad, out_wgrad = mixer_backward(
        grad_hidden, saved, gain_first, query_mat, key_matrix, value_matrix, out_mat
    )

    out_share = all_sums(out_wgrad)
    joined = all_sums(jnp.concatenate([query_wgrad, key_wgrad, value_wgrad], 1))
    query_share = joined[:, :query_width]
    key_share = joined[:, query_width : query_width + key_width]
    value_share = joined[:, query_width + key_width :]
    extras = jnp.concatenate(
        [router_wgrad, first_gain_grad[None, :], second_gain_grad[None, :]], 0
    )
    extras = lax.psum(extras.astype(jnp.bfloat16), ("dp", "expert"))
    extras = lax.dynamic_slice_in_dim(
        extras, lax.axis_index("dp") * row_part, row_part, 1
    ).astype(jnp.float32)
    router_share = extras[:expert_count].T
    first_share = extras[expert_count]
    second_share = extras[expert_count + 1]
    return (
        output,
        grad_tokens,
        first_share,
        query_share,
        key_share,
        value_share,
        out_share,
        second_share,
        router_share,
        expert_shares[0],
        expert_shares[1],
        expert_shares[2],
    )


def turn(values, axis):
    if lax.axis_size("dp") != 2:
        return values
    low, high = jnp.split(values, 2, axis)
    first = lax.axis_index("dp") == 0
    return jnp.concatenate([jnp.where(first, low, high), jnp.where(first, high, low)], axis)


def times(left_op, pieces):
    total, start = None, 0
    for piece in pieces:
        part = matrix_multiply(left_op[:, start : start + piece.shape[0]], piece)
        total = part if total is None else total + part
        start += piece.shape[0]
    return total


def times_back(left_op, pieces):
    return jnp.concatenate([matrix_multiply(left_op, piece.T) for piece in pieces], 1)


def halves_forward(tokens, segments, gain_vec, query_mat, key_matrix, value_matrix, out_mat):
    token_rows = tokens.shape[0]
    local_sequences = token_rows // SEQUENCE_LENGTH
    query_groups = QUERY_HEADS // KEY_VALUE_HEADS
    cosine_table, sine_table = rope_tables(SEQUENCE_LENGTH, HEAD_DIM)
    mask_tab = segment_mask(segments.reshape(local_sequences, SEQUENCE_LENGTH))
    residual = tokens.astype(jnp.float32)
    normed, factor, attention_input = normalize(turn(residual, 1), gain_vec)
    query_rows = apply_rotary(
        times(attention_input, query_mat).reshape(
            local_sequences, SEQUENCE_LENGTH, QUERY_HEADS, HEAD_DIM
        ),
        cosine_table,
        sine_table,
    )
    query_rows = query_rows.astype(jnp.bfloat16).reshape(
        local_sequences, SEQUENCE_LENGTH, KEY_VALUE_HEADS, query_groups, HEAD_DIM
    )
    key_row_block = apply_rotary(
        times(attention_input, key_matrix).reshape(
            local_sequences, SEQUENCE_LENGTH, KEY_VALUE_HEADS, HEAD_DIM
        ),
        cosine_table,
        sine_table,
    ).astype(jnp.bfloat16)
    value_row_block = (
        times(attention_input, value_matrix)
        .astype(jnp.bfloat16)
        .reshape(local_sequences, SEQUENCE_LENGTH, KEY_VALUE_HEADS, HEAD_DIM)
    )
    scores = score_table(query_rows, key_row_block, mask_tab)
    row_peak = jnp.max(scores, -1, keepdims=True)
    logsum = row_peak + jnp.log(jnp.sum(jnp.exp(scores - row_peak), -1, keepdims=True))
    weights = jnp.exp(scores - logsum).astype(jnp.bfloat16)
    attended = product("shgqk,skhw->sqhgw", weights, value_row_block).astype(jnp.bfloat16)
    turned = turn(attended.reshape(token_rows, QUERY_HEADS * HEAD_DIM), 1)
    hidden = residual + times(turned, out_mat)
    saved = (
        normed,
        factor,
        attention_input,
        query_rows,
        key_row_block,
        value_row_block,
        attended,
        turned,
        logsum,
        mask_tab,
        cosine_table,
        sine_table,
    )
    return (hidden, saved)


def halves_backward(grad_hidden, saved, gain_vec, query_mat, key_matrix, value_matrix, out_mat):
    (
        normed,
        factor,
        attention_input,
        query_rows,
        key_row_block,
        value_row_block,
        attended,
        _,
        logsum,
        mask_tab,
        cosine_table,
        sine_table,
    ) = saved
    token_rows = grad_hidden.shape[0]
    local_sequences = token_rows // SEQUENCE_LENGTH
    grad_round = grad_hidden.astype(jnp.bfloat16)
    grad_attended = (
        turn(times_back(grad_round, out_mat).astype(jnp.bfloat16), 1).reshape(query_rows.shape)
    )
    scores = score_table(query_rows, key_row_block, mask_tab)
    prob_full = jnp.exp(scores - logsum)
    values_gradient = product("shgqk,sqhgw->skhw", prob_full.astype(jnp.bfloat16), grad_attended)
    grad_weights = product("sqhgw,skhw->shgqk", grad_attended, value_row_block)
    row_delta = product("sqhgw,sqhgw->shgq", grad_attended, attended)[..., None]
    grad_scores = (prob_full * (grad_weights - row_delta) * SCORE_SCALE).astype(jnp.bfloat16)
    grad_queries = product("shgqk,skhw->sqhgw", grad_scores, key_row_block)
    keys_gradient = product("shgqk,sqhgw->skhw", grad_scores, query_rows)
    query_grad = inverse_rotary(
        grad_queries.reshape(local_sequences, SEQUENCE_LENGTH, QUERY_HEADS, HEAD_DIM),
        cosine_table,
        sine_table,
    )
    query_grad = query_grad.astype(jnp.bfloat16).reshape(token_rows, QUERY_HEADS * HEAD_DIM)
    key_gradient = (
        inverse_rotary(keys_gradient, cosine_table, sine_table)
        .astype(jnp.bfloat16)
        .reshape(token_rows, KEY_VALUE_HEADS * HEAD_DIM)
    )
    value_gradient = values_gradient.astype(jnp.bfloat16).reshape(
        token_rows, KEY_VALUE_HEADS * HEAD_DIM
    )
    grad_attn_input = (
        times_back(query_grad, query_mat)
        + times_back(key_gradient, key_matrix)
        + times_back(value_gradient, value_matrix)
    )
    grad_normed, gain_grad = normalize_back(grad_attn_input, normed, factor, gain_vec)
    return (
        grad_hidden + turn(grad_normed, 1),
        turn(gain_grad, 0),
        [query_grad, key_gradient, value_gradient, grad_round],
    )


MESH = pl.DeviceIdType.MESH


def quotient(index, by):
    return index // by if isinstance(index, int) else lax.div(index, jnp.int32(by))


def parity(index):
    return index % 2 if isinstance(index, int) else lax.rem(index, jnp.int32(2))


def flip(index, by):
    total, weight = 0, 1
    for _ in range(6):
        one, two = parity(quotient(index, weight)), parity(quotient(by, weight))
        total = total + weight * (one + two - 2 * one * two)
        weight *= 2
    return total


def expert_at(index):
    return {"expert": index}


def send(src, dst, send_sem, recv_sem, where):
    return pltpu.make_async_remote_copy(
        src_ref=src,
        dst_ref=dst,
        send_sem=send_sem,
        recv_sem=recv_sem,
        device_id=where,
        device_id_type=MESH,
    )


def meet(count, with_dp):
    barrier = pltpu.get_barrier_semaphore()
    me = lax.axis_index("expert")

    def greet(by, carry):
        pl.semaphore_signal(
            barrier, inc=1, device_id=expert_at(flip(me, by)), device_id_type=MESH
        )
        return carry

    lax.fori_loop(1, count, greet, 0)
    if with_dp:
        pl.semaphore_signal(
            barrier, inc=1, device_id={"dp": 1 - lax.axis_index("dp")}, device_id_type=MESH
        )
    pl.semaphore_wait(barrier, count - 1 + (1 if with_dp else 0))


class Gather:
    def __init__(self, own, block_of, count, send_sems, recv_sems):
        self.own, self.block_of, self.count = own, block_of, count
        self.send_sems, self.recv_sems = send_sems, recv_sems
        self.me = lax.axis_index("expert")

    def copy(self, rel, by, src=None):
        block = self.block_of(flip(self.me, rel))
        there = flip(rel, by)
        return send(
            block if src is None else src,
            block,
            self.send_sems.at[there],
            self.recv_sems.at[there],
            expert_at(flip(self.me, by)),
        )

    def wait(self, rel):
        block = self.block_of(flip(self.me, rel))
        send(
            block, block, self.send_sems.at[rel], self.recv_sems.at[rel], expert_at(self.me)
        ).wait_recv()

    def begin(self, held=()):
        for by in list(range(8, self.count, 4)) + [4, 2, 1]:
            if by not in held:
                self.copy(0, by, self.own).start()

    def release(self, by):
        self.copy(0, by, self.own).start()

    def pass_z(self, rel):
        self.wait(rel)
        self.copy(rel, 2).start()
        self.copy(rel, 1).start()

    def pass_x(self, rel):
        self.wait(rel + 2)
        self.copy(rel + 2, 1).start()

    def wait_sends(self):
        for rel in range(1, self.count):
            block = self.block_of(flip(self.me, rel))
            send(
                block, block, self.send_sems.at[rel], self.recv_sems.at[rel], expert_at(self.me)
            ).wait_send()

    def rest(self):
        self.pass_x(0)
        for rel in range(4, self.count, 4):
            self.pass_z(rel)
        for rel in range(4, self.count, 4):
            self.pass_x(rel)
        for rel in range(1, self.count, 2):
            self.wait(rel)
        self.wait_sends()


def front_kernel(count, pieces, *refs):
    mine, refs = refs[:pieces], refs[pieces:]
    cotangent, refs = refs[0], refs[1:]
    others, refs = refs[:pieces], refs[pieces:]
    gathered, y_send, y_recv, c_send, c_recv, g_send, g_recv, local = refs
    rows = cotangent.shape[0]
    me, dp = lax.axis_index("expert"), lax.axis_index("dp")
    core = parity(me)
    meet(count, True)

    def part(ref, which):
        half = ref.shape[0] // 2
        return ref.at[pl.ds(pl.multiple_of(which * half, half), half)]

    over_y = [
        send(
            part(mine[i], core),
            part(others[i], core),
            y_send.at[i],
            y_recv.at[i],
            {"dp": 1 - dp},
        )
        for i in range(pieces)
    ]
    for copy in over_y:
        copy.start()

    def block_of(index):
        return gathered.at[pl.ds(pl.multiple_of(index * rows, rows), rows)]

    keep = pltpu.make_async_copy(cotangent, block_of(me), local)
    keep.start()
    gather = Gather(cotangent, block_of, count, g_send, g_recv)
    gather.begin()
    over_core = [
        send(
            part(others[i], core),
            part(others[i], core),
            c_send.at[i],
            c_recv.at[i],
            expert_at(flip(me, 1)),
        )
        for i in range(pieces)
    ]
    gather.rest()
    for i in range(pieces):
        over_y[i].wait_recv()
        over_core[i].start()
    for i in range(pieces):
        send(
            part(mine[i], 1 - core),
            part(others[i], 1 - core),
            c_send.at[i],
            c_recv.at[i],
            expert_at(flip(me, 1)),
        ).wait_recv()
        over_core[i].wait_send()
        over_y[i].wait_send()
    keep.wait()


def front(own, cotangent, count):
    pieces = len(own)
    rows, width = cotangent.shape
    anywhere = pl.BlockSpec(memory_space=pl.ANY)
    results = pl.pallas_call(
        functools.partial(front_kernel, count, pieces),
        out_shape=[jax.ShapeDtypeStruct(part.shape, part.dtype) for part in own]
        + [jax.ShapeDtypeStruct((count * rows, width), cotangent.dtype)],
        in_specs=[anywhere] * (pieces + 1),
        out_specs=[anywhere] * (pieces + 1),
        scratch_shapes=[
            pltpu.SemaphoreType.DMA((pieces,)),
            pltpu.SemaphoreType.DMA((pieces,)),
            pltpu.SemaphoreType.DMA((pieces,)),
            pltpu.SemaphoreType.DMA((pieces,)),
            pltpu.SemaphoreType.DMA((count,)),
            pltpu.SemaphoreType.DMA((count,)),
            pltpu.SemaphoreType.DMA,
        ],
        compiler_params=pltpu.CompilerParams(collective_id=0, has_side_effects=True),
        name="front",
    )(*own, cotangent)
    return results[:pieces], results[pieces]


def unfold_kernel(heights, all_ref, *outs):
    start = 0
    for height, out in zip(heights, outs):
        for index in range(0, all_ref.shape[0], 128 // height):
            block = all_ref[index : index + 128 // height, start : start + height, :]
            block = block.astype(jnp.float32).reshape(128, block.shape[2])
            out[:, index * height : index * height + 128] = block.T
        start += height


def unfold(everything, heights):
    count, lines, half = everything.shape
    tile = half // 4
    return pl.pallas_call(
        functools.partial(unfold_kernel, heights),
        grid=(4,),
        out_shape=[
            jax.ShapeDtypeStruct((half, count * height), jnp.float32) for height in heights
        ],
        in_specs=[pl.BlockSpec((count, lines, tile), lambda i: (0, 0, i))],
        out_specs=[pl.BlockSpec((tile, count * height), lambda i: (i, 0)) for height in heights],
        compiler_params=pltpu.CompilerParams(vmem_limit_bytes=40 * 2**20),
        name="unfold",
    )(everything)


def dot_on(left_op, right_op, left_axis, right_axis):
    return lax.dot_general(
        left_op,
        right_op,
        (((left_axis,), (right_axis,)), ((), ())),
        preferred_element_type=jnp.float32,
    )


def experts_kernel(
    count,
    own_ref,
    cot_ref,
    prob_ref,
    gate_ref,
    up_ref,
    down_ref,
    grad_out,
    mix_out,
    mix_away,
    gp_out,
    mine_out,
    mine_down,
    peer_out,
    peer_down,
    x_all,
    prob_all,
    gp_send_buf,
    both_all,
    inner_all,
    ge_all,
    part,
    cbuf,
    xbuf,
    zbuf,
    a_send,
    a_recv,
    p_send,
    p_recv,
    q_send,
    q_recv,
    c_send,
    c_recv,
    x_send,
    x_recv,
    z_send,
    z_recv,
):
    rows, width = own_ref.shape
    hidden = gate_ref.shape[2]
    pair = 2 * rows
    steps = count // 2
    depth = count // 4
    order = [0] + [z for z in (2, 1) if z < depth] + list(range(3, depth))
    me, dp = lax.axis_index("expert"), lax.axis_index("dp")
    core = parity(me)
    meet(count, False)

    def block_of(index):
        return x_all.at[pl.ds(pl.multiple_of(index * rows, rows), rows)]

    gather = Gather(own_ref, block_of, count, a_send, a_recv)
    gather.begin(range(12, count, 4))

    def prob_copy(by):
        there = flip(me, by)
        return send(
            prob_ref.at[there], prob_all.at[me], p_send.at[by], p_recv.at[by], expert_at(there)
        )

    def prob_start(by, carry):
        prob_copy(by).start()
        return carry

    lax.fori_loop(1, count, prob_start, 0)
    x_all[pl.ds(pl.multiple_of(me * rows, rows), rows)] = own_ref[...]
    prob_all[me] = prob_ref[me]

    def prob_wait(by, carry):
        there = flip(me, by)
        send(
            prob_ref.at[me], prob_all.at[there], p_send.at[by], p_recv.at[by], expert_at(there)
        ).wait_recv()
        return carry

    lax.fori_loop(1, count, prob_wait, 0)

    def rel_of(step):
        z_rel = quotient(step, 2)
        x_rel = jnp.where(step < 2, parity(step), 1 - parity(step))
        z_rel = sum(jnp.where(z_rel == at, z, 0) for at, z in enumerate(order))
        return 4 * z_rel + 2 * x_rel, z_rel

    eye = (
        lax.broadcasted_iota(jnp.int32, (pair, pair), 0)
        == lax.broadcasted_iota(jnp.int32, (pair, pair), 1)
    )
    theirs = pl.ds(pl.multiple_of((1 - core) * rows, rows), rows)
    ours = pl.ds(pl.multiple_of(core * rows, rows), rows)

    def core_copy(step):
        return send(
            part.at[step, :, theirs],
            cbuf.at[step],
            c_send.at[step],
            c_recv.at[step],
            expert_at(flip(me, 1)),
        )

    def x_copy(step, z_rel, which):
        return send(
            part.at[step, which, ours],
            xbuf.at[z_rel, which],
            x_send.at[which, z_rel],
            x_recv.at[which, z_rel],
            expert_at(flip(me, 2)),
        )

    def z_copy(step, z_rel):
        return send(
            part.at[step, 0, ours],
            zbuf.at[z_rel],
            z_send.at[z_rel],
            z_recv.at[z_rel],
            expert_at(flip(me, 4 * z_rel)),
        )

    def compute(step):
        rel, _ = rel_of(step)
        chip = quotient(flip(me, rel), 2)
        where = pl.ds(pl.multiple_of(chip * pair, pair), pair)
        x = x_all[where, :]
        gate_pre = dot_on(x, gate_ref[0], 1, 0)
        up_pre = dot_on(x, up_ref[0], 1, 0)
        sig = jax.nn.sigmoid(gate_pre)
        act = gate_pre * sig
        inner = (act * up_pre).astype(jnp.bfloat16)
        inner_all[where, :] = inner
        out = dot_on(inner, down_ref[0], 1, 0).astype(jnp.bfloat16).astype(jnp.float32)
        prob_row = jnp.concatenate(
            [prob_all[2 * chip, 0:1, :], prob_all[2 * chip + 1, 0:1, :]], 1
        )
        prob = jnp.sum(jnp.where(eye, prob_row, 0.0), 1, keepdims=True)
        cot = cot_ref[where, :].astype(jnp.float32)
        part[step, 1] = (prob * out).astype(jnp.bfloat16)
        gp = jnp.sum(out * cot, 1, keepdims=True)
        gp_row = jnp.sum(jnp.where(eye, gp, 0.0), 0, keepdims=True)
        gp_send_buf[2 * chip] = jnp.broadcast_to(gp_row[:, :rows], (8, rows))
        gp_send_buf[2 * chip + 1] = jnp.broadcast_to(gp_row[:, rows:], (8, rows))
        ge = (prob * cot).astype(jnp.bfloat16)
        ge_all[where, :] = ge
        gi = dot_on(ge, down_ref[0], 1, 1)
        slope = sig * (1.0 + gate_pre * (1.0 - sig))
        gg = (gi * up_pre * slope).astype(jnp.bfloat16)
        gu = (gi * act).astype(jnp.bfloat16)
        both_all[where, :hidden] = gg
        both_all[where, hidden:] = gu
        part[step, 0] = (dot_on(gg, gate_ref[0], 1, 1) + dot_on(gu, up_ref[0], 1, 1)).astype(
            jnp.bfloat16
        )

    def add_core(step):
        core_copy(step).wait_recv()
        total = part[step, :, ours].astype(jnp.float32) + cbuf[step].astype(jnp.float32)
        part[step, :, ours] = total.astype(jnp.bfloat16)

    def add_x(at):
        z_rel, step = order[at], 2 * at + 1
        x_copy(step, z_rel, 0).wait_recv()
        total = part[step, 0, ours].astype(jnp.float32) + xbuf[z_rel, 0].astype(jnp.float32)
        part[step, 0, ours] = total.astype(jnp.bfloat16)
        z_copy(step, z_rel).start()

    def on(step, number):
        return pl.when(step == number)

    def turn_of(step, carry):
        rel, _ = rel_of(step)

        for at in range(1, depth):

            @on(step, 2 * at)
            def _(at=at):
                if at == 1:
                    gather.pass_x(4 * order[1])

        gather.wait(rel + 1)
        compute(step)
        core_copy(step).start()

        @on(step, 0)
        def _():
            gather.pass_x(0)

        @on(step, 1)
        def _():
            gather.pass_z(4 * order[1])
            for by in range(12, count, 4):
                gather.release(by)
            if depth > 2:
                gather.pass_z(4 * order[2])
            add_core(0)
            add_core(1)

        for at in range(1, depth):

            @on(step, 2 * at)
            def _(at=at):
                add_core(2 * at - 1) if at > 1 else None
                if at > 1 and at + 1 < depth:
                    gather.pass_z(4 * order[at + 1])

            @on(step, 2 * at + 1)
            def _(at=at):
                add_core(2 * at)
                x_copy(2 * at, order[at], 0).start()
                if at + 1 < depth:
                    gather.pass_x(4 * order[at + 1])

        if depth > 3:

            @on(step, 6)
            def _():
                add_x(1)

        return carry

    lax.fori_loop(0, steps, turn_of, 0)
    add_core(steps - 1)
    x_copy(1, 0, 0).start()
    for at in list(range(1, depth)) + [0]:
        x_copy(2 * at if at else 1, order[at], 1).start()
    for at in range(2 if depth > 3 else 1, depth - 1):
        add_x(at)

    def gp_copy(by):
        there = flip(me, by)
        return send(
            gp_send_buf.at[there], gp_out.at[me], q_send.at[by], q_recv.at[by], expert_at(there)
        )

    def gp_start(by, carry):
        gp_copy(by).start()
        return carry

    lax.fori_loop(1, count, gp_start, 0)
    gp_out[me] = gp_send_buf[me]

    half = width // 2
    for turn_at, (which, target, lower) in enumerate( ((1 - dp, peer_out, peer_down), (dp, mine_out, mine_down))
    ):

        def rows_of(index, carry, which=which, target=target):
            tile = half // 2
            at = pl.multiple_of(which * half + index * tile, tile)
            into = pl.ds(pl.multiple_of(index * tile, tile), tile)
            x = x_all[:, pl.ds(at, tile)]
            both = dot_on(x, both_all[...], 0, 0).astype(target.dtype)
            target[0, into, :] = both[:, :hidden]
            target[1, into, :] = both[:, hidden:]
            return carry

        lax.fori_loop(0, 2, rows_of, 0)

        def down_of(index, carry, which=which, lower=lower):
            tile = hidden // 2
            at = pl.ds(pl.multiple_of(index * tile, tile), tile)
            grads = ge_all[:, pl.ds(pl.multiple_of(which * half, half), half)]
            lower[at, :] = dot_on(inner_all[:, at], grads, 0, 0).astype(lower.dtype)
            return carry

        lax.fori_loop(0, 2, down_of, 0)
        if turn_at == 0:
            add_x(depth - 1)

    def from_x(at, which):
        step = 2 * at + 1 if at else 0
        x_copy(step, order[at], which).wait_recv()
        return part[step, which, ours].astype(jnp.float32) + xbuf[order[at], which].astype(
            jnp.float32
        )

    for at in range(1, depth):
        mix_away[order[at] - 1] = from_x(at, 1).astype(jnp.bfloat16)
    mix_out[...] = from_x(0, 1)
    grads = from_x(0, 0)
    for z_rel in range(1, depth):
        z_copy(0, z_rel).wait_recv()
        grads = grads + zbuf[z_rel].astype(jnp.float32)
    grad_out[...] = grads

    def settle(by, carry):
        there = flip(me, by)
        send(
            gp_send_buf.at[me], gp_out.at[there], q_send.at[by], q_recv.at[by], expert_at(there)
        ).wait()
        prob_copy(by).wait_send()
        return carry

    lax.fori_loop(1, count, settle, 0)
    gather.wait_sends()
    for step in range(steps):
        core_copy(step).wait_send()
    for z_rel in range(depth):
        x_copy(0, z_rel, 0).wait_send()
        x_copy(0, z_rel, 1).wait_send()
    for z_rel in range(1, depth):
        z_copy(0, z_rel).wait_send()


def experts(expert_input, cotangent_all, prob, gate_weight, up_weight, down_weight):
    count = prob.shape[0]
    rows, width = expert_input.shape
    hidden = gate_weight.shape[2]
    total = count * rows
    steps, depth = count // 2, count // 4
    half = width // 2
    local = pl.BlockSpec(memory_space=pltpu.VMEM)
    shapes = ((count,), (count,), (count,), (steps,), (2, depth), (depth,))
    pairs = [pltpu.SemaphoreType.DMA(shape) for shape in shapes]
    semaphores = [item for item in pairs for _ in range(2)]
    bf16 = jnp.bfloat16
    return pl.pallas_call(
        functools.partial(experts_kernel, count),
        out_shape=[
            jax.ShapeDtypeStruct((rows, width), jnp.float32),
            jax.ShapeDtypeStruct((rows, width), jnp.float32),
            jax.ShapeDtypeStruct((depth - 1, rows, width), bf16),
            jax.ShapeDtypeStruct((count, 8, rows), jnp.float32),
            jax.ShapeDtypeStruct((2, half, hidden), jnp.float32),
            jax.ShapeDtypeStruct((hidden, half), jnp.float32),
            jax.ShapeDtypeStruct((2, half, hidden), bf16),
            jax.ShapeDtypeStruct((hidden, half), bf16),
        ],
        in_specs=[local] * 6,
        out_specs=[local] * 8,
        scratch_shapes=[
            pltpu.VMEM((total, width), bf16),
            pltpu.VMEM((count, 8, rows), jnp.float32),
            pltpu.VMEM((count, 8, rows), jnp.float32),
            pltpu.VMEM((total, 2 * hidden), bf16),
            pltpu.VMEM((total, hidden), bf16),
            pltpu.VMEM((total, width), bf16),
            pltpu.VMEM((steps, 2, 2 * rows, width), bf16),
            pltpu.VMEM((steps, 2, rows, width), bf16),
            pltpu.VMEM((depth, 2, rows, width), bf16),
            pltpu.VMEM((depth, rows, width), bf16),
        ]
        + semaphores,
        compiler_params=pltpu.CompilerParams(
            collective_id=1, has_side_effects=True, vmem_limit_bytes=58 * 2**20
        ),
        cost_estimate=pl.CostEstimate(
            flops=18 * total * width * hidden, bytes_accessed=20 * total * width, transcendentals=0
        ),
        name="experts",
    )(expert_input, cotangent_all, prob, gate_weight, up_weight, down_weight)


def late_kernel(
    count,
    cuts,
    pay_ref,
    attention_hbm,
    attended_hbm,
    all_out,
    attention_ref,
    attended_ref,
    fetch_sem,
    arrived,
    peer_buf,
    y_buf,
    mine,
    a_send,
    a_recv,
    g_send,
    g_recv,
    y_send,
    y_recv,
):
    first, last = cuts
    rows = pay_ref.shape[2]
    half = all_out.shape[2]
    me, dp = lax.axis_index("expert"), lax.axis_index("dp")
    meet(count, True)

    def columns(index):
        return pl.ds(pl.multiple_of(index * rows, rows), rows)

    def scatter(by):
        there = flip(me, by)
        return send(
            pay_ref.at[there],
            arrived.at[:, columns(me)],
            a_send.at[by],
            a_recv.at[by],
            expert_at(there),
        )

    def scatter_start(back, carry):
        scatter(count - back).start()
        return carry

    lax.fori_loop(1, count, scatter_start, 0)
    fetches = [
        pltpu.make_async_copy(attention_hbm, attention_ref, fetch_sem.at[0]),
        pltpu.make_async_copy(attended_hbm, attended_ref, fetch_sem.at[1]),
    ]
    for fetch in fetches:
        fetch.start()
    arrived[:, columns(me)] = pay_ref[me]

    def scatter_wait(by, carry):
        there = flip(me, by)
        send(
            pay_ref.at[me],
            arrived.at[:, columns(there)],
            a_send.at[by],
            a_recv.at[by],
            expert_at(there),
        ).wait()
        return carry

    lax.fori_loop(1, count, scatter_wait, 0)

    for fetch in fetches:
        fetch.wait()
    extra = arrived[last:, :].astype(jnp.float32)
    summed = extra[:, :rows]
    for index in range(1, count):
        summed = summed + extra[:, index * rows : (index + 1) * rows]
    edge = summed.shape[0] // 2
    blank = jnp.zeros((edge, half - rows), jnp.float32)
    own_extra = jnp.concatenate([summed[:edge], blank], 1)
    peer_extra = jnp.concatenate([summed[edge:], blank], 1)
    blank = jnp.zeros((edge, half), jnp.float32)

    def tile_of(at):
        return jnp.concatenate(
            [
                dot_on(arrived[:first, :], attention_ref[:, at], 1, 0),
                dot_on(arrived[first:last, :], attended_ref[:, at], 1, 0),
            ],
            0,
        )

    peer_buf[...] = jnp.concatenate(
        [tile_of(slice(half, 2 * half)), peer_extra, blank], 0
    ).astype(jnp.bfloat16)
    over = send(peer_buf, y_buf, y_send, y_recv, {"dp": 1 - dp})
    over.start()
    own = jnp.concatenate([tile_of(slice(0, half)), own_extra, blank], 0)
    over.wait()
    mine[...] = (
        own + y_buf[...].astype(jnp.float32)
    ).astype(jnp.bfloat16)
    gather = Gather(mine, lambda index: all_out.at[index], count, g_send, g_recv)
    gather.begin()
    all_out[me] = mine[...]
    gather.rest()


def late_sums(payload, attention_all, attended_all, cuts):
    count, lines, rows = payload.shape
    half = attention_all.shape[1] // 2
    local = pl.BlockSpec(memory_space=pltpu.VMEM)
    bf16 = jnp.bfloat16
    return pl.pallas_call(
        functools.partial(late_kernel, count, cuts),
        out_shape=jax.ShapeDtypeStruct((count, lines, half), bf16),
        in_specs=[local, pl.BlockSpec(memory_space=pl.ANY), pl.BlockSpec(memory_space=pl.ANY)],
        out_specs=local,
        scratch_shapes=[
            pltpu.VMEM(attention_all.shape, bf16),
            pltpu.VMEM(attended_all.shape, bf16),
            pltpu.SemaphoreType.DMA((2,)),
            pltpu.VMEM((lines, count * rows), bf16),
            pltpu.VMEM((lines, half), bf16),
            pltpu.VMEM((lines, half), bf16),
            pltpu.VMEM((lines, half), bf16),
            pltpu.SemaphoreType.DMA((count,)),
            pltpu.SemaphoreType.DMA((count,)),
            pltpu.SemaphoreType.DMA((count,)),
            pltpu.SemaphoreType.DMA((count,)),
            pltpu.SemaphoreType.DMA,
            pltpu.SemaphoreType.DMA,
        ],
        compiler_params=pltpu.CompilerParams(
            collective_id=2, has_side_effects=True, vmem_limit_bytes=40 * 2**20
        ),
        name="late",
    )(payload, attention_all, attended_all)


def shards_together(
    tokens,
    segments,
    routes,
    first_gain,
    query_weight,
    key_projection_weight,
    value_projection_weight,
    out_weight,
    second_gain,
    router_weight,
    gate_weight,
    up_weight,
    down_weight,
    cotangent,
):
    token_rows = tokens.shape[0]
    expert_count = router_weight.shape[1]
    owner_count = lax.axis_size("expert")
    dp_count = lax.axis_size("dp")

    small = jnp.concatenate([router_weight, first_gain[:, None], second_gain[:, None]], 1)
    small = jnp.pad(small, ((0, 0), (0, -small.shape[1] % 128)))
    own = [query_weight, key_projection_weight, value_projection_weight, out_weight, small]
    other, cotangent_all = front(own, cotangent, owner_count)
    query_mat, key_matrix, value_matrix, out_mat, small = (list(p) for p in zip(own, other))
    small_mat = jnp.concatenate(small, 0)
    router_mat = turn(small_mat[:, :expert_count], 0)
    gain_first = small_mat[:, expert_count]
    gain_second = turn(small_mat[:, expert_count + 1], 0)

    hidden, saved = halves_forward(
        tokens, segments, gain_first, query_mat, key_matrix, value_matrix, out_mat
    )
    attention_all = lax.all_gather(saved[2], "expert", axis=0, tiled=True)
    attended_all = lax.all_gather(saved[7], "expert", axis=0, tiled=True)
    normed_second, factor_second, expert_input = normalize(hidden, gain_second)
    route_prob, chosen_hot = route_weights(expert_input, router_mat, routes)
    dense_prob = jnp.sum(chosen_hot * route_prob[:, :, None], 1)
    prob = jnp.broadcast_to(dense_prob.T[:, None, :], (owner_count, 8, token_rows))
    grad_sum, mixture, mix_away, back_prob, mine, mine_down, peer, peer_down = experts(
        expert_input, cotangent_all, prob, gate_weight, up_weight, down_weight
    )
    swap = [(0, 1), (1, 0)]
    peer = lax.ppermute(peer, "dp", swap)
    peer_down = lax.ppermute(peer_down, "dp", swap)
    mix_here = [
        lax.ppermute(mix_away[z - 1], "expert", [(i, i ^ (4 * z)) for i in range(owner_count)])
        for z in range(1, owner_count // 4)
    ]
    grad_prob = jnp.sum(chosen_hot * back_prob[:, 0, :].T[:, None, :], -1)
    router_grad = route_back(route_prob, grad_prob, chosen_hot)
    grad_expert_input = grad_sum + matrix_multiply(router_grad, router_mat.T)
    router_wgrad = matrix_multiply(router_grad.T, expert_input)
    grad_normed, second_gain_grad = normalize_back(
        grad_expert_input, normed_second, factor_second, gain_second
    )
    grad_hidden = cotangent.astype(jnp.float32) + grad_normed
    grad_tokens, first_gain_grad, late = halves_backward(
        grad_hidden, saved, gain_first, query_mat, key_matrix, value_matrix, out_mat
    )

    extras = jnp.concatenate(
        [router_wgrad, first_gain_grad[None, :], second_gain_grad[None, :]], 0
    )
    slices = [
        grad.T.reshape(owner_count, grad.shape[1] // owner_count, token_rows) for grad in late
    ]
    extra_count, extra_width = extras.shape
    part = extra_width // (owner_count * dp_count)
    spread = (
        extras.reshape(extra_count, dp_count, owner_count, part)
        .transpose(2, 1, 0, 3)
        .reshape(owner_count, dp_count, extra_count * part)
        .astype(jnp.bfloat16)
    )
    spread = jnp.pad(spread, ((0, 0), (0, 0), (0, -spread.shape[2] % (8 * token_rows))))
    spread = turn(spread, 1).reshape(owner_count, -1, token_rows)
    payload = jnp.concatenate(slices + [spread], 1)
    last = sum(piece.shape[1] for piece in slices)
    everything = late_sums(
        payload, attention_all, attended_all, (last - slices[3].shape[1], last)
    )
    everything, peer, peer_down, mix_here = lax.optimization_barrier(
        (everything, peer, peer_down, mix_here)
    )
    output = hidden + mixture
    for piece in mix_here:
        output = output + piece.astype(jnp.float32)
    output = output.astype(jnp.bfloat16)
    shares = unfold(everything, [piece.shape[1] for piece in slices])
    edge = spread.shape[1] // 2
    extras = everything[:, last : last + edge, :token_rows].reshape(owner_count, -1)
    extras = extras[:, : extra_count * part].reshape(owner_count, extra_count, part)
    extras = extras.transpose(1, 0, 2).reshape(extra_count, -1).astype(jnp.float32)
    query_share, key_share, value_share, out_share = shares
    return (
        output,
        grad_tokens,
        extras[expert_count],
        query_share,
        key_share,
        value_share,
        out_share,
        extras[expert_count + 1],
        extras[:expert_count].T,
        mine[0:1] + peer[0:1].astype(jnp.float32),
        mine[1:2] + peer[1:2].astype(jnp.float32),
        (mine_down + peer_down.astype(jnp.float32))[None],
    )


def solution(mesh):
    placed = (
        P(("dp", "expert"), None),
        P(("dp", "expert")),
        P(("dp", "expert"), None),
        P("dp"),
        P("dp", None),
        P("dp", None),
        P("dp", None),
        P("dp", None),
        P("dp"),
        P("dp", None),
        P("expert", None, None),
        P("expert", None, None),
        P("expert", None, None),
        P(("dp", "expert"), None),
    )
    owners = mesh.shape["expert"]
    together = mesh.shape["dp"] == 2 and owners >= 8 and owners & (owners - 1) == 0
    return jax.shard_map(
        shards_together if together else shards,
        mesh=mesh,
        in_specs=placed,
        out_specs=(
            P(("dp", "expert"), None),
            P(("dp", "expert"), None),
            P("dp"),
            P("dp", None),
            P("dp", None),
            P("dp", None),
            P("dp", None),
            P("dp"),
            P("dp", None),
            P("expert", "dp", None),
            P("expert", "dp", None),
            P("expert", None, "dp"),
        ),
        check_vma=False,
    )
```

```python
import functools

import jax
import jax.numpy as jnp
from jax import lax
from jax.experimental import pallas as pl
from jax.experimental.pallas import tpu as pltpu
from jax.sharding import PartitionSpec as P

QUERY_HEADS = 16
KEY_VALUE_HEADS = 8
HEAD_DIM = 64
SEQUENCE_LENGTH = 128


EPSILON = 1e-06
SCORE_SCALE = 0.015625
ROPE_BASE = 10000.0
MASKED = -1e30


def product(pattern, left_op, right_op):
    return jnp.einsum(pattern, left_op, right_op, preferred_element_type=jnp.float32)


def matrix_multiply(left_op, right_op):
    return jnp.dot(left_op, right_op, preferred_element_type=jnp.float32)


def rope_tables(seq_len, head_size):
    positions = jnp.arange(seq_len, dtype=jnp.float32)
    exponent = jnp.arange(head_size // 2, dtype=jnp.float32) * (2.0 / head_size)
    angles = positions[:, None] * (ROPE_BASE ** (-exponent))[None, :]
    return (jnp.cos(angles)[None, :, None, :], jnp.sin(angles)[None, :, None, :])


def apply_rotary(values, cosine_table, sine_table):
    middle = values.shape[-1] // 2
    first_half = values[..., :middle]
    second_half = values[..., middle:]
    return jnp.concatenate(
        [
            first_half * cosine_table - second_half * sine_table,
            second_half * cosine_table + first_half * sine_table,
        ],
        -1,
    )


def inverse_rotary(gradient, cosine_table, sine_table):
    middle = gradient.shape[-1] // 2
    first_half = gradient[..., :middle]
    second_half = gradient[..., middle:]
    return jnp.concatenate(
        [
            first_half * cosine_table + second_half * sine_table,
            second_half * cosine_table - first_half * sine_table,
        ],
        -1,
    )


def normalize(values, gain_vec):
    factor = lax.rsqrt(jnp.mean(values * values, -1, keepdims=True) + EPSILON)
    normed = values * factor
    return (normed, factor, (normed * gain_vec).astype(jnp.bfloat16))


def normalize_back(gradient, normed, factor, gain_vec):
    gain_grad = jnp.sum(gradient * normed, 0)
    scaled = gradient * gain_vec
    return (factor * (scaled - normed * jnp.mean(scaled * normed, -1, keepdims=True)), gain_grad)


def segment_mask(segments):
    seq_len = segments.shape[1]
    causal = jnp.arange(seq_len)[:, None] >= jnp.arange(seq_len)[None, :]
    same_doc = segments[:, :, None] == segments[:, None, :]
    return (same_doc & causal[None])[:, None, None]


def score_table(query_rows, key_row_block, mask_tab):
    raw_scores = product("sqhgw,skhw->shgqk", query_rows, key_row_block) * SCORE_SCALE
    return jnp.where(mask_tab, raw_scores, MASKED)


def mixer_forward(tokens, segments, gain_vec, query_mat, key_matrix, value_matrix, out_mat):
    token_rows = tokens.shape[0]
    local_sequences = token_rows // SEQUENCE_LENGTH
    query_groups = QUERY_HEADS // KEY_VALUE_HEADS
    cosine_table, sine_table = rope_tables(SEQUENCE_LENGTH, HEAD_DIM)
    mask_tab = segment_mask(segments.reshape(local_sequences, SEQUENCE_LENGTH))
    residual = tokens.astype(jnp.float32)
    normed, factor, attention_input = normalize(residual, gain_vec)
    query_rows = apply_rotary(
        matrix_multiply(attention_input, query_mat).reshape(
            local_sequences, SEQUENCE_LENGTH, QUERY_HEADS, HEAD_DIM
        ),
        cosine_table,
        sine_table,
    )
    query_rows = query_rows.astype(jnp.bfloat16).reshape(
        local_sequences, SEQUENCE_LENGTH, KEY_VALUE_HEADS, query_groups, HEAD_DIM
    )
    key_row_block = apply_rotary(
        matrix_multiply(attention_input, key_matrix).reshape(
            local_sequences, SEQUENCE_LENGTH, KEY_VALUE_HEADS, HEAD_DIM
        ),
        cosine_table,
        sine_table,
    ).astype(jnp.bfloat16)
    value_row_block = (
        matrix_multiply(attention_input, value_matrix)
        .astype(jnp.bfloat16)
        .reshape(local_sequences, SEQUENCE_LENGTH, KEY_VALUE_HEADS, HEAD_DIM)
    )
    scores = score_table(query_rows, key_row_block, mask_tab)
    row_peak = jnp.max(scores, -1, keepdims=True)
    logsum = row_peak + jnp.log(jnp.sum(jnp.exp(scores - row_peak), -1, keepdims=True))
    weights = jnp.exp(scores - logsum).astype(jnp.bfloat16)
    attended = product("shgqk,skhw->sqhgw", weights, value_row_block).astype(jnp.bfloat16)
    hidden = residual + matrix_multiply(
        attended.reshape(token_rows, QUERY_HEADS * HEAD_DIM), out_mat
    )
    saved = (
        normed,
        factor,
        attention_input,
        query_rows,
        key_row_block,
        value_row_block,
        attended,
        logsum,
        mask_tab,
        cosine_table,
        sine_table,
    )
    return (hidden, saved)


def mixer_backward(grad_hidden, saved, gain_vec, query_mat, key_matrix, value_matrix, out_mat):
    (
        normed,
        factor,
        attention_input,
        query_rows,
        key_row_block,
        value_row_block,
        attended,
        logsum,
        mask_tab,
        cosine_table,
        sine_table,
    ) = saved
    token_rows = grad_hidden.shape[0]
    local_sequences = token_rows // SEQUENCE_LENGTH
    grad_round = grad_hidden.astype(jnp.bfloat16)
    out_grad = matrix_multiply(attended.reshape(token_rows, QUERY_HEADS * HEAD_DIM).T, grad_round)
    grad_attended = (
        matrix_multiply(grad_round, out_mat.T).astype(jnp.bfloat16).reshape(query_rows.shape)
    )
    scores = score_table(query_rows, key_row_block, mask_tab)
    prob_full = jnp.exp(scores - logsum)
    values_gradient = product("shgqk,sqhgw->skhw", prob_full.astype(jnp.bfloat16), grad_attended)
    grad_weights = product("sqhgw,skhw->shgqk", grad_attended, value_row_block)
    row_delta = product("sqhgw,sqhgw->shgq", grad_attended, attended)[..., None]
    grad_scores = (prob_full * (grad_weights - row_delta) * SCORE_SCALE).astype(jnp.bfloat16)
    grad_queries = product("shgqk,skhw->sqhgw", grad_scores, key_row_block)
    keys_gradient = product("shgqk,sqhgw->skhw", grad_scores, query_rows)
    query_grad = inverse_rotary(
        grad_queries.reshape(local_sequences, SEQUENCE_LENGTH, QUERY_HEADS, HEAD_DIM),
        cosine_table,
        sine_table,
    )
    query_grad = query_grad.astype(jnp.bfloat16).reshape(token_rows, QUERY_HEADS * HEAD_DIM)
    key_gradient = (
        inverse_rotary(keys_gradient, cosine_table, sine_table)
        .astype(jnp.bfloat16)
        .reshape(token_rows, KEY_VALUE_HEADS * HEAD_DIM)
    )
    value_gradient = values_gradient.astype(jnp.bfloat16).reshape(
        token_rows, KEY_VALUE_HEADS * HEAD_DIM
    )
    query_wgrad = matrix_multiply(attention_input.T, query_grad)
    key_wgrad = matrix_multiply(attention_input.T, key_gradient)
    value_wgrad = matrix_multiply(attention_input.T, value_gradient)
    grad_attn_input = (
        matrix_multiply(query_grad, query_mat.T)
        + matrix_multiply(key_gradient, key_matrix.T)
        + matrix_multiply(value_gradient, value_matrix.T)
    )
    grad_normed, gain_grad = normalize_back(grad_attn_input, normed, factor, gain_vec)
    return (grad_hidden + grad_normed, gain_grad, query_wgrad, key_wgrad, value_wgrad, out_grad)


def route_weights(expert_input, router_mat, routes):
    logits = matrix_multiply(expert_input, router_mat)
    chosen_hot = (
        routes[:, :, None] == jnp.arange(router_mat.shape[1], dtype=jnp.int32)[None, None, :]
    ).astype(jnp.float32)
    chosen = jnp.sum(chosen_hot * logits[:, None, :], -1)
    return (jax.nn.softmax(chosen, -1), chosen_hot)


def route_back(route_prob, grad_prob, chosen_hot):
    grad_chosen = route_prob * (grad_prob - jnp.sum(route_prob * grad_prob, -1, keepdims=True))
    return jnp.sum(chosen_hot * grad_chosen[:, :, None], 1).astype(jnp.bfloat16)


def expert_forward(owner_rows, gate_mat, up_mat, down_mat):
    gate_pre = product("erd,edf->erf", owner_rows, gate_mat)
    up_pre = product("erd,edf->erf", owner_rows, up_mat)
    gate_sig = jax.nn.sigmoid(gate_pre)
    gate_act = gate_pre * gate_sig
    inner_acts = (gate_act * up_pre).astype(jnp.bfloat16)
    expert_out = product("erf,efd->erd", inner_acts, down_mat).astype(jnp.bfloat16)
    return (expert_out, (gate_pre, up_pre, gate_sig, gate_act, inner_acts))


def expert_backward(grad_rows, owner_rows, kept_acts, gate_mat, up_mat, down_mat):
    gate_pre, up_pre, gate_sig, gate_act, inner_acts = kept_acts
    grad_inner = product("erd,efd->erf", grad_rows, down_mat)
    down_grad = product("erf,erd->efd", inner_acts, grad_rows)
    silu_slope = gate_sig * (1.0 + gate_pre * (1.0 - gate_sig))
    grad_gate = (grad_inner * up_pre * silu_slope).astype(jnp.bfloat16)
    grad_up = (grad_inner * gate_act).astype(jnp.bfloat16)
    gate_grad = product("erd,erf->edf", owner_rows, grad_gate)
    up_grad = product("erd,erf->edf", owner_rows, grad_up)
    grad_owner_rows = product("erf,edf->erd", grad_gate, gate_mat) + product(
        "erf,edf->erd", grad_up, up_mat
    )
    return (grad_owner_rows.astype(jnp.bfloat16), gate_grad, up_grad, down_grad)


def gather_dp(local_part):
    dp_count = lax.axis_size("dp")
    owner_count = lax.axis_size("expert")
    if dp_count != 2 or owner_count % 2:
        return lax.all_gather(local_part, "dp", axis=0, tiled=True)
    low, high = jnp.split(local_part, 2, 0)
    even = lax.axis_index("expert") % 2 == 0
    near = lax.ppermute(jnp.where(even, low, high), "dp", [(0, 1), (1, 0)])
    far = lax.ppermute(near, "expert", [(i, i ^ 1) for i in range(owner_count)])
    other = jnp.concatenate([jnp.where(even, near, far), jnp.where(even, far, near)], 0)
    first = lax.axis_index("dp") == 0
    return jnp.concatenate(
        [jnp.where(first, local_part, other), jnp.where(first, other, local_part)], 0
    )


def all_sums(partial):
    owner_count = lax.axis_size("expert")
    dp_count = lax.axis_size("dp")
    width = partial.shape[1]
    pieces = partial.astype(jnp.bfloat16).reshape(dp_count, owner_count, -1, width)
    piece = lax.psum_scatter(
        pieces.transpose(1, 0, 2, 3).reshape(-1, width), "expert", scatter_dimension=0, tiled=True
    )
    piece = scatter_dp(piece, 0).astype(jnp.bfloat16)
    return lax.all_gather(piece, "expert", axis=0, tiled=True).astype(jnp.float32)


def scatter_dp(partial, axis):
    dp_count = lax.axis_size("dp")
    rounded = partial.astype(jnp.bfloat16)
    if dp_count != 2:
        return lax.psum_scatter(rounded, "dp", scatter_dimension=axis, tiled=True).astype(
            jnp.float32
        )
    low, high = jnp.split(rounded, 2, axis)
    first = lax.axis_index("dp") == 0
    arrived = lax.ppermute(jnp.where(first, high, low), "dp", [(0, 1), (1, 0)])
    return jnp.where(first, low, high).astype(jnp.float32) + arrived.astype(jnp.float32)


def shards(
    tokens,
    segments,
    routes,
    first_gain,
    query_weight,
    key_projection_weight,
    value_projection_weight,
    out_weight,
    second_gain,
    router_weight,
    gate_weight,
    up_weight,
    down_weight,
    cotangent,
):
    token_rows, model_width = tokens.shape
    top_count = routes.shape[1]
    expert_count = router_weight.shape[1]
    owner_count = lax.axis_size("expert")
    local_count = gate_weight.shape[0]
    key_width = key_projection_weight.shape[1]
    query_width = query_weight.shape[1]
    capacity = 5 * token_rows * top_count // (4 * expert_count)
    row_part = router_weight.shape[0]

    small = jnp.concatenate(
        [router_weight, first_gain[:, None], second_gain[:, None]], 1
    )
    small_mat = gather_dp(small)
    router_mat = small_mat[:, :expert_count]
    gain_first = small_mat[:, expert_count]
    gain_second = small_mat[:, expert_count + 1]
    joined_mat = gather_dp(
        jnp.concatenate([query_weight, key_projection_weight, value_projection_weight], 1)
    )
    query_mat = joined_mat[:, :query_width]
    key_matrix = joined_mat[:, query_width : query_width + key_width]
    value_matrix = joined_mat[:, query_width + key_width :]
    out_mat = gather_dp(out_weight)

    routes_all = lax.all_gather(routes, "expert")
    cotangent_all = lax.all_gather(cotangent, "expert")

    mine = lax.axis_index("expert") * local_count + jnp.arange(local_count, dtype=jnp.int32)
    hit = jnp.any(routes_all[None] == mine[:, None, None, None], -1)
    before = (
        jnp.arange(token_rows)[:, None] < jnp.arange(token_rows)[None, :]
    ).astype(jnp.bfloat16)
    rank = product("lst,tu->lsu", hit.astype(jnp.bfloat16), before).astype(jnp.int32)
    slot = jnp.where(hit, rank, -1)
    picked = slot[:, :, None, :] == jnp.arange(capacity, dtype=jnp.int32)[None, None, :, None]
    pick = picked.astype(jnp.bfloat16)

    def rows_of(gathered):
        rows = product("lsct,std->lscd", pick, gathered)
        return rows.reshape(local_count, owner_count * capacity, model_width)

    own_hot = (routes[:, :, None] == jnp.arange(expert_count, dtype=jnp.int32)).any(1)
    own_rank = matrix_multiply(before.T, own_hot.astype(jnp.bfloat16)).astype(jnp.int32)
    own_slot = jnp.where(own_hot, own_rank, -1)
    own_pick = (
        own_slot[:, :, None] == jnp.arange(capacity, dtype=jnp.int32)[None, None, :]
    ).astype(jnp.bfloat16)

    def send_back(rows):
        shaped = rows.reshape(local_count, owner_count, capacity, model_width)
        return lax.all_to_all(
            shaped.transpose(1, 0, 2, 3).reshape(expert_count, capacity, model_width),
            "expert",
            split_axis=0,
            concat_axis=0,
            tiled=True,
        )

    def sum_back(returned):
        flat = returned.reshape(expert_count * capacity, model_width)
        return matrix_multiply(own_pick.reshape(token_rows, expert_count * capacity), flat)

    hidden, saved = mixer_forward(
        tokens, segments, gain_first, query_mat, key_matrix, value_matrix, out_mat
    )
    normed_second, factor_second, expert_input = normalize(hidden, gain_second)
    input_all = lax.all_gather(expert_input, "expert")
    route_prob, chosen_hot = route_weights(expert_input, router_mat, routes)
    dense_prob = jnp.sum(chosen_hot * route_prob[:, :, None], 1)
    prob_all = lax.all_gather(dense_prob, "expert")

    column = jnp.arange(expert_count, dtype=jnp.int32)
    my_column = (mine[:, None] == column[None, :]).astype(jnp.float32)
    my_prob = jnp.sum(prob_all[None] * my_column[:, None, None, :], -1)
    row_prob = jnp.sum(jnp.where(picked, my_prob[:, :, None, :], 0.0), -1).reshape(
        local_count, owner_count * capacity, 1
    )

    owner_rows = rows_of(input_all).astype(jnp.bfloat16)
    cotangent_rows = rows_of(cotangent_all).astype(jnp.bfloat16).astype(jnp.float32)
    expert_out, kept_acts = expert_forward(owner_rows, gate_weight, up_weight, down_weight)
    expert_out = expert_out.astype(jnp.float32)
    weighted = (row_prob * expert_out).astype(jnp.bfloat16)
    row_grad_prob = jnp.sum(expert_out * cotangent_rows, -1).reshape(
        local_count, owner_count, capacity
    )
    token_grad_prob = jnp.sum(jnp.where(picked, row_grad_prob[..., None], 0.0), 2)
    back_prob = lax.all_to_all(
        token_grad_prob.transpose(1, 0, 2).reshape(expert_count, token_rows),
        "expert",
        split_axis=0,
        concat_axis=0,
        tiled=True,
    )
    grad_prob = jnp.sum(chosen_hot * back_prob.T[:, None, :], -1)
    grad_output = cotangent.astype(jnp.float32)

    grad_rows = (row_prob * cotangent_rows).astype(jnp.bfloat16)
    grad_owner_rows, gate_grad, up_grad, down_grad = expert_backward(
        grad_rows, owner_rows, kept_acts, gate_weight, up_weight, down_weight
    )
    grad_back = send_back(grad_owner_rows)
    expert_shares = (
        scatter_dp(gate_grad, 1),
        scatter_dp(up_grad, 1),
        scatter_dp(down_grad, 2),
    )
    grad_back, expert_shares, weighted = lax.optimization_barrier(
        (grad_back, expert_shares, weighted)
    )
    forward_back = send_back(weighted)
    output = (hidden + sum_back(forward_back)).astype(jnp.bfloat16)
    backward_sum = sum_back(grad_back)
    router_grad = route_back(route_prob, grad_prob, chosen_hot)
    grad_expert_input = backward_sum + matrix_multiply(
        router_grad, router_mat.T
    )
    router_wgrad = matrix_multiply(router_grad.T, expert_input)
    grad_normed, second_gain_grad = normalize_back(
        grad_expert_input, normed_second, factor_second, gain_second
    )
    grad_hidden = grad_output + grad_normed
    grad_tokens, first_gain_grad, query_wgrad, key_wgrad, value_wgrad, out_wgrad = mixer_backward(
        grad_hidden, saved, gain_first, query_mat, key_matrix, value_matrix, out_mat
    )

    out_share = all_sums(out_wgrad)
    joined = all_sums(jnp.concatenate([query_wgrad, key_wgrad, value_wgrad], 1))
    query_share = joined[:, :query_width]
    key_share = joined[:, query_width : query_width + key_width]
    value_share = joined[:, query_width + key_width :]
    extras = jnp.concatenate(
        [router_wgrad, first_gain_grad[None, :], second_gain_grad[None, :]], 0
    )
    extras = lax.psum(extras.astype(jnp.bfloat16), ("dp", "expert"))
    extras = lax.dynamic_slice_in_dim(
        extras, lax.axis_index("dp") * row_part, row_part, 1
    ).astype(jnp.float32)
    router_share = extras[:expert_count].T
    first_share = extras[expert_count]
    second_share = extras[expert_count + 1]
    return (
        output,
        grad_tokens,
        first_share,
        query_share,
        key_share,
        value_share,
        out_share,
        second_share,
        router_share,
        expert_shares[0],
        expert_shares[1],
        expert_shares[2],
    )


def turn(values, axis):
    if lax.axis_size("dp") != 2:
        return values
    low, high = jnp.split(values, 2, axis)
    first = lax.axis_index("dp") == 0
    return jnp.concatenate([jnp.where(first, low, high), jnp.where(first, high, low)], axis)


def times(left_op, pieces):
    total, start = None, 0
    for piece in pieces:
        part = matrix_multiply(left_op[:, start : start + piece.shape[0]], piece)
        total = part if total is None else total + part
        start += piece.shape[0]
    return total


def times_back(left_op, pieces):
    return jnp.concatenate([matrix_multiply(left_op, piece.T) for piece in pieces], 1)


def halves_forward(tokens, segments, gain_vec, query_mat, key_matrix, value_matrix, out_mat):
    token_rows = tokens.shape[0]
    local_sequences = token_rows // SEQUENCE_LENGTH
    query_groups = QUERY_HEADS // KEY_VALUE_HEADS
    cosine_table, sine_table = rope_tables(SEQUENCE_LENGTH, HEAD_DIM)
    mask_tab = segment_mask(segments.reshape(local_sequences, SEQUENCE_LENGTH))
    residual = tokens.astype(jnp.float32)
    normed, factor, attention_input = normalize(turn(residual, 1), gain_vec)
    query_rows = apply_rotary(
        times(attention_input, query_mat).reshape(
            local_sequences, SEQUENCE_LENGTH, QUERY_HEADS, HEAD_DIM
        ),
        cosine_table,
        sine_table,
    )
    query_rows = query_rows.astype(jnp.bfloat16).reshape(
        local_sequences, SEQUENCE_LENGTH, KEY_VALUE_HEADS, query_groups, HEAD_DIM
    )
    key_row_block = apply_rotary(
        times(attention_input, key_matrix).reshape(
            local_sequences, SEQUENCE_LENGTH, KEY_VALUE_HEADS, HEAD_DIM
        ),
        cosine_table,
        sine_table,
    ).astype(jnp.bfloat16)
    value_row_block = (
        times(attention_input, value_matrix)
        .astype(jnp.bfloat16)
        .reshape(local_sequences, SEQUENCE_LENGTH, KEY_VALUE_HEADS, HEAD_DIM)
    )
    scores = score_table(query_rows, key_row_block, mask_tab)
    row_peak = jnp.max(scores, -1, keepdims=True)
    logsum = row_peak + jnp.log(jnp.sum(jnp.exp(scores - row_peak), -1, keepdims=True))
    weights = jnp.exp(scores - logsum).astype(jnp.bfloat16)
    attended = product("shgqk,skhw->sqhgw", weights, value_row_block).astype(jnp.bfloat16)
    turned = turn(attended.reshape(token_rows, QUERY_HEADS * HEAD_DIM), 1)
    hidden = residual + times(turned, out_mat)
    saved = (
        normed,
        factor,
        attention_input,
        query_rows,
        key_row_block,
        value_row_block,
        attended,
        turned,
        logsum,
        mask_tab,
        cosine_table,
        sine_table,
    )
    return (hidden, saved)


def halves_backward(grad_hidden, saved, gain_vec, query_mat, key_matrix, value_matrix, out_mat):
    (
        normed,
        factor,
        attention_input,
        query_rows,
        key_row_block,
        value_row_block,
        attended,
        _,
        logsum,
        mask_tab,
        cosine_table,
        sine_table,
    ) = saved
    token_rows = grad_hidden.shape[0]
    local_sequences = token_rows // SEQUENCE_LENGTH
    grad_round = grad_hidden.astype(jnp.bfloat16)
    grad_attended = (
        turn(times_back(grad_round, out_mat).astype(jnp.bfloat16), 1).reshape(query_rows.shape)
    )
    scores = score_table(query_rows, key_row_block, mask_tab)
    prob_full = jnp.exp(scores - logsum)
    values_gradient = product("shgqk,sqhgw->skhw", prob_full.astype(jnp.bfloat16), grad_attended)
    grad_weights = product("sqhgw,skhw->shgqk", grad_attended, value_row_block)
    row_delta = product("sqhgw,sqhgw->shgq", grad_attended, attended)[..., None]
    grad_scores = (prob_full * (grad_weights - row_delta) * SCORE_SCALE).astype(jnp.bfloat16)
    grad_queries = product("shgqk,skhw->sqhgw", grad_scores, key_row_block)
    keys_gradient = product("shgqk,sqhgw->skhw", grad_scores, query_rows)
    query_grad = inverse_rotary(
        grad_queries.reshape(local_sequences, SEQUENCE_LENGTH, QUERY_HEADS, HEAD_DIM),
        cosine_table,
        sine_table,
    )
    query_grad = query_grad.astype(jnp.bfloat16).reshape(token_rows, QUERY_HEADS * HEAD_DIM)
    key_gradient = (
        inverse_rotary(keys_gradient, cosine_table, sine_table)
        .astype(jnp.bfloat16)
        .reshape(token_rows, KEY_VALUE_HEADS * HEAD_DIM)
    )
    value_gradient = values_gradient.astype(jnp.bfloat16).reshape(
        token_rows, KEY_VALUE_HEADS * HEAD_DIM
    )
    grad_attn_input = (
        times_back(query_grad, query_mat)
        + times_back(key_gradient, key_matrix)
        + times_back(value_gradient, value_matrix)
    )
    grad_normed, gain_grad = normalize_back(grad_attn_input, normed, factor, gain_vec)
    return (
        grad_hidden + turn(grad_normed, 1),
        turn(gain_grad, 0),
        [query_grad, key_gradient, value_gradient, grad_round],
    )


MESH = pl.DeviceIdType.MESH


def quotient(index, by):
    return index // by if isinstance(index, int) else lax.div(index, jnp.int32(by))


def parity(index):
    return index % 2 if isinstance(index, int) else lax.rem(index, jnp.int32(2))


def flip(index, by):
    total, weight = 0, 1
    for _ in range(6):
        one, two = parity(quotient(index, weight)), parity(quotient(by, weight))
        total = total + weight * (one + two - 2 * one * two)
        weight *= 2
    return total


def expert_at(index):
    return {"expert": index}


def send(src, dst, send_sem, recv_sem, where):
    return pltpu.make_async_remote_copy(
        src_ref=src,
        dst_ref=dst,
        send_sem=send_sem,
        recv_sem=recv_sem,
        device_id=where,
        device_id_type=MESH,
    )


def meet(count, with_dp):
    barrier = pltpu.get_barrier_semaphore()
    me = lax.axis_index("expert")

    def greet(by, carry):
        pl.semaphore_signal(
            barrier, inc=1, device_id=expert_at(flip(me, by)), device_id_type=MESH
        )
        return carry

    lax.fori_loop(1, count, greet, 0)
    if with_dp:
        pl.semaphore_signal(
            barrier, inc=1, device_id={"dp": 1 - lax.axis_index("dp")}, device_id_type=MESH
        )
    pl.semaphore_wait(barrier, count - 1 + (1 if with_dp else 0))


class Gather:
    def __init__(self, own, block_of, count, send_sems, recv_sems):
        self.own, self.block_of, self.count = own, block_of, count
        self.send_sems, self.recv_sems = send_sems, recv_sems
        self.me = lax.axis_index("expert")

    def copy(self, rel, by, src=None):
        block = self.block_of(flip(self.me, rel))
        there = flip(rel, by)
        return send(
            block if src is None else src,
            block,
            self.send_sems.at[there],
            self.recv_sems.at[there],
            expert_at(flip(self.me, by)),
        )

    def wait(self, rel):
        block = self.block_of(flip(self.me, rel))
        send(
            block, block, self.send_sems.at[rel], self.recv_sems.at[rel], expert_at(self.me)
        ).wait_recv()

    def begin(self, held=()):
        for by in list(range(8, self.count, 4)) + [4, 2, 1]:
            if by not in held:
                self.copy(0, by, self.own).start()

    def release(self, by):
        self.copy(0, by, self.own).start()

    def pass_z(self, rel):
        self.wait(rel)
        self.copy(rel, 2).start()
        self.copy(rel, 1).start()

    def pass_x(self, rel):
        self.wait(rel + 2)
        self.copy(rel + 2, 1).start()

    def wait_sends(self):
        for rel in range(1, self.count):
            block = self.block_of(flip(self.me, rel))
            send(
                block, block, self.send_sems.at[rel], self.recv_sems.at[rel], expert_at(self.me)
            ).wait_send()

    def rest(self):
        far = list(range(12, self.count, 4))
        near = [rel for rel in (8, 4) if rel < self.count]
        self.pass_x(0)
        self.pass_z(near[0])
        for by in far:
            self.release(by)
        for rel in near[1:]:
            self.pass_z(rel)
        for rel in near:
            self.pass_x(rel)
        for rel in far:
            self.pass_z(rel)
            self.pass_x(rel)
        for rel in range(1, self.count, 2):
            self.wait(rel)
        self.wait_sends()


def front_kernel(count, pieces, *refs):
    mine, refs = refs[:pieces], refs[pieces:]
    cotangent, refs = refs[0], refs[1:]
    others, refs = refs[:pieces], refs[pieces:]
    gathered, y_send, y_recv, c_send, c_recv, g_send, g_recv, local = refs
    rows = cotangent.shape[0]
    me, dp = lax.axis_index("expert"), lax.axis_index("dp")
    core = parity(me)
    meet(count, True)

    def part(ref, which):
        half = ref.shape[0] // 2
        return ref.at[pl.ds(pl.multiple_of(which * half, half), half)]

    over_y = [
        send(
            part(mine[i], core),
            part(others[i], core),
            y_send.at[i],
            y_recv.at[i],
            {"dp": 1 - dp},
        )
        for i in range(pieces)
    ]
    for copy in over_y:
        copy.start()

    def block_of(index):
        return gathered.at[pl.ds(pl.multiple_of(index * rows, rows), rows)]

    keep = pltpu.make_async_copy(cotangent, block_of(me), local)
    keep.start()
    gather = Gather(cotangent, block_of, count, g_send, g_recv)
    gather.begin(range(12, count, 4))
    over_core = [
        send(
            part(others[i], core),
            part(others[i], core),
            c_send.at[i],
            c_recv.at[i],
            expert_at(flip(me, 1)),
        )
        for i in range(pieces)
    ]
    gather.rest()
    for i in range(pieces):
        over_y[i].wait_recv()
        over_core[i].start()
    for i in range(pieces):
        send(
            part(mine[i], 1 - core),
            part(others[i], 1 - core),
            c_send.at[i],
            c_recv.at[i],
            expert_at(flip(me, 1)),
        ).wait_recv()
        over_core[i].wait_send()
        over_y[i].wait_send()
    keep.wait()


def front(own, cotangent, count):
    pieces = len(own)
    rows, width = cotangent.shape
    anywhere = pl.BlockSpec(memory_space=pl.ANY)
    results = pl.pallas_call(
        functools.partial(front_kernel, count, pieces),
        out_shape=[jax.ShapeDtypeStruct(part.shape, part.dtype) for part in own]
        + [jax.ShapeDtypeStruct((count * rows, width), cotangent.dtype)],
        in_specs=[anywhere] * (pieces + 1),
        out_specs=[anywhere] * (pieces + 1),
        scratch_shapes=[
            pltpu.SemaphoreType.DMA((pieces,)),
            pltpu.SemaphoreType.DMA((pieces,)),
            pltpu.SemaphoreType.DMA((pieces,)),
            pltpu.SemaphoreType.DMA((pieces,)),
            pltpu.SemaphoreType.DMA((count,)),
            pltpu.SemaphoreType.DMA((count,)),
            pltpu.SemaphoreType.DMA,
        ],
        compiler_params=pltpu.CompilerParams(collective_id=0, has_side_effects=True),
        name="front",
    )(*own, cotangent)
    return results[:pieces], results[pieces]


def finish_kernel(heights, away, *refs):
    all_ref, mine, mine_down, peer, peer_down, hidden, mixture = refs[:7]
    pieces, refs = refs[7 : 7 + away], refs[7 + away :]
    shares, refs = refs[: len(heights)], refs[len(heights) :]
    gate_out, up_out, down_out, output = refs
    start = 0
    for height, out in zip(heights, shares):
        for index in range(0, all_ref.shape[0], 128 // height):
            block = all_ref[index : index + 128 // height, start : start + height, :]
            block = block.astype(jnp.float32).reshape(128, block.shape[2])
            out[:, index * height : index * height + 128] = block.T
        start += height
    gate_out[0] = mine[0] + peer[0].astype(jnp.float32)
    up_out[0] = mine[1] + peer[1].astype(jnp.float32)
    down_out[0] = mine_down[...] + peer_down[...].astype(jnp.float32)
    total = hidden[...] + mixture[...]
    for piece in pieces:
        total = total + piece[...].astype(jnp.float32)
    output[...] = total.astype(jnp.bfloat16)


def finish(everything, heights, mine, mine_down, peer, peer_down, hidden, mixture, pieces):
    count, lines, half = everything.shape
    parts = 4
    rows, width = hidden.shape
    deep = mine.shape[2]
    tile, low, some = half // parts, deep // parts, rows // parts
    three = pl.BlockSpec((2, tile, deep), lambda i: (0, i, 0))
    down = pl.BlockSpec((low, half), lambda i: (i, 0))
    tokens = pl.BlockSpec((some, width), lambda i: (i, 0))
    f32 = jnp.float32
    results = pl.pallas_call(
        functools.partial(finish_kernel, heights, len(pieces)),
        grid=(parts,),
        out_shape=[jax.ShapeDtypeStruct((half, count * height), f32) for height in heights]
        + [
            jax.ShapeDtypeStruct((1, half, deep), f32),
            jax.ShapeDtypeStruct((1, half, deep), f32),
            jax.ShapeDtypeStruct((1, deep, half), f32),
            jax.ShapeDtypeStruct((rows, width), jnp.bfloat16),
        ],
        in_specs=[pl.BlockSpec((count, lines, tile), lambda i: (0, 0, i))]
        + [three, down, three, down, tokens, tokens]
        + [tokens] * len(pieces),
        out_specs=[pl.BlockSpec((tile, count * height), lambda i: (i, 0)) for height in heights]
        + [
            pl.BlockSpec((1, tile, deep), lambda i: (0, i, 0)),
            pl.BlockSpec((1, tile, deep), lambda i: (0, i, 0)),
            pl.BlockSpec((1, low, half), lambda i: (0, i, 0)),
            tokens,
        ],
        compiler_params=pltpu.CompilerParams(vmem_limit_bytes=58 * 2**20),
        name="finish",
    )(everything, mine, mine_down, peer, peer_down, hidden, mixture, *pieces)
    return results[: len(heights)], results[len(heights) :]


def dot_on(left_op, right_op, left_axis, right_axis):
    return lax.dot_general(
        left_op,
        right_op,
        (((left_axis,), (right_axis,)), ((), ())),
        preferred_element_type=jnp.float32,
    )


def experts_kernel(
    count,
    own_ref,
    cot_ref,
    prob_ref,
    gate_ref,
    up_ref,
    down_ref,
    grad_out,
    mix_out,
    mix_away,
    gp_out,
    mine_out,
    mine_down,
    peer_out,
    peer_down,
    x_all,
    prob_all,
    gp_send_buf,
    both_all,
    inner_all,
    ge_all,
    part,
    cbuf,
    xbuf,
    zbuf,
    a_send,
    a_recv,
    p_send,
    p_recv,
    q_send,
    q_recv,
    c_send,
    c_recv,
    x_send,
    x_recv,
    z_send,
    z_recv,
):
    rows, width = own_ref.shape
    hidden = gate_ref.shape[2]
    pair = 2 * rows
    steps = count // 2
    depth = count // 4
    order = [0] + [z for z in (2, 1) if z < depth] + list(range(3, depth))
    me, dp = lax.axis_index("expert"), lax.axis_index("dp")
    core = parity(me)
    meet(count, False)

    def block_of(index):
        return x_all.at[pl.ds(pl.multiple_of(index * rows, rows), rows)]

    gather = Gather(own_ref, block_of, count, a_send, a_recv)
    gather.begin(range(12, count, 4))

    def prob_copy(by):
        there = flip(me, by)
        return send(
            prob_ref.at[there], prob_all.at[me], p_send.at[by], p_recv.at[by], expert_at(there)
        )

    def prob_start(by, carry):
        prob_copy(by).start()
        return carry

    lax.fori_loop(1, count, prob_start, 0)
    x_all[pl.ds(pl.multiple_of(me * rows, rows), rows)] = own_ref[...]
    prob_all[me] = prob_ref[me]

    def prob_wait(by, carry):
        there = flip(me, by)
        send(
            prob_ref.at[me], prob_all.at[there], p_send.at[by], p_recv.at[by], expert_at(there)
        ).wait_recv()
        return carry

    lax.fori_loop(1, count, prob_wait, 0)

    def rel_of(step):
        z_rel = quotient(step, 2)
        x_rel = jnp.where(step < 2, parity(step), 1 - parity(step))
        z_rel = sum(jnp.where(z_rel == at, z, 0) for at, z in enumerate(order))
        return 4 * z_rel + 2 * x_rel, z_rel

    eye = (
        lax.broadcasted_iota(jnp.int32, (pair, pair), 0)
        == lax.broadcasted_iota(jnp.int32, (pair, pair), 1)
    )
    theirs = pl.ds(pl.multiple_of((1 - core) * rows, rows), rows)
    ours = pl.ds(pl.multiple_of(core * rows, rows), rows)

    def core_copy(step):
        return send(
            part.at[step, :, theirs],
            cbuf.at[step],
            c_send.at[step],
            c_recv.at[step],
            expert_at(flip(me, 1)),
        )

    def x_copy(step, z_rel, which):
        return send(
            part.at[step, which, ours],
            xbuf.at[z_rel, which],
            x_send.at[which, z_rel],
            x_recv.at[which, z_rel],
            expert_at(flip(me, 2)),
        )

    def z_copy(step, z_rel):
        return send(
            part.at[step, 0, ours],
            zbuf.at[z_rel],
            z_send.at[z_rel],
            z_recv.at[z_rel],
            expert_at(flip(me, 4 * z_rel)),
        )

    def compute(step):
        rel, _ = rel_of(step)
        chip = quotient(flip(me, rel), 2)
        where = pl.ds(pl.multiple_of(chip * pair, pair), pair)
        x = x_all[where, :]
        gate_pre = dot_on(x, gate_ref[0], 1, 0)
        up_pre = dot_on(x, up_ref[0], 1, 0)
        sig = jax.nn.sigmoid(gate_pre)
        act = gate_pre * sig
        inner = (act * up_pre).astype(jnp.bfloat16)
        inner_all[where, :] = inner
        out = dot_on(inner, down_ref[0], 1, 0).astype(jnp.bfloat16).astype(jnp.float32)
        prob_row = jnp.concatenate(
            [prob_all[2 * chip, 0:1, :], prob_all[2 * chip + 1, 0:1, :]], 1
        )
        prob = jnp.sum(jnp.where(eye, prob_row, 0.0), 1, keepdims=True)
        cot = cot_ref[where, :].astype(jnp.float32)
        part[step, 1] = (prob * out).astype(jnp.bfloat16)
        gp = jnp.sum(out * cot, 1, keepdims=True)
        gp_row = jnp.sum(jnp.where(eye, gp, 0.0), 0, keepdims=True)
        gp_send_buf[2 * chip] = jnp.broadcast_to(gp_row[:, :rows], (8, rows))
        gp_send_buf[2 * chip + 1] = jnp.broadcast_to(gp_row[:, rows:], (8, rows))
        ge = (prob * cot).astype(jnp.bfloat16)
        ge_all[where, :] = ge
        gi = dot_on(ge, down_ref[0], 1, 1)
        slope = sig * (1.0 + gate_pre * (1.0 - sig))
        gg = (gi * up_pre * slope).astype(jnp.bfloat16)
        gu = (gi * act).astype(jnp.bfloat16)
        both_all[where, :hidden] = gg
        both_all[where, hidden:] = gu
        part[step, 0] = (dot_on(gg, gate_ref[0], 1, 1) + dot_on(gu, up_ref[0], 1, 1)).astype(
            jnp.bfloat16
        )

    def add_core(step):
        core_copy(step).wait_recv()
        total = part[step, :, ours].astype(jnp.float32) + cbuf[step].astype(jnp.float32)
        part[step, :, ours] = total.astype(jnp.bfloat16)

    def add_x(at):
        z_rel, step = order[at], 2 * at + 1
        x_copy(step, z_rel, 0).wait_recv()
        total = part[step, 0, ours].astype(jnp.float32) + xbuf[z_rel, 0].astype(jnp.float32)
        part[step, 0, ours] = total.astype(jnp.bfloat16)
        z_copy(step, z_rel).start()

    def on(step, number):
        return pl.when(step == number)

    def turn_of(step, carry):
        rel, _ = rel_of(step)

        for at in range(1, depth):

            @on(step, 2 * at)
            def _(at=at):
                if at == 1:
                    gather.pass_x(4 * order[1])

        gather.wait(rel + 1)
        compute(step)
        core_copy(step).start()

        @on(step, 0)
        def _():
            gather.pass_x(0)

        @on(step, 1)
        def _():
            gather.pass_z(4 * order[1])
            for by in range(12, count, 4):
                gather.release(by)
            if depth > 2:
                gather.pass_z(4 * order[2])
            add_core(0)
            add_core(1)

        for at in range(1, depth):

            @on(step, 2 * at)
            def _(at=at):
                if at == 1:
                    x_copy(1, 0, 0).start()
                    x_copy(1, 0, 1).start()
                else:
                    add_core(2 * at - 1)
                    x_copy(2 * at - 2, order[at - 1], 1).start()
                if at > 1 and at + 1 < depth:
                    gather.pass_z(4 * order[at + 1])

            @on(step, 2 * at + 1)
            def _(at=at):
                add_core(2 * at)
                x_copy(2 * at, order[at], 0).start()
                if at + 1 < depth:
                    gather.pass_x(4 * order[at + 1])

        if depth > 3:

            @on(step, 6)
            def _():
                add_x(1)

        return carry

    lax.fori_loop(0, steps, turn_of, 0)
    add_core(steps - 1)
    x_copy(steps - 2, order[-1], 1).start()
    for at in range(2 if depth > 3 else 1, depth - 1):
        add_x(at)

    def gp_copy(by):
        there = flip(me, by)
        return send(
            gp_send_buf.at[there], gp_out.at[me], q_send.at[by], q_recv.at[by], expert_at(there)
        )

    def gp_start(by, carry):
        gp_copy(by).start()
        return carry

    lax.fori_loop(1, count, gp_start, 0)
    gp_out[me] = gp_send_buf[me]

    half = width // 2
    for turn_at, (which, target, lower) in enumerate( ((1 - dp, peer_out, peer_down), (dp, mine_out, mine_down))
    ):

        def rows_of(index, carry, which=which, target=target):
            tile = half // 2
            at = pl.multiple_of(which * half + index * tile, tile)
            into = pl.ds(pl.multiple_of(index * tile, tile), tile)
            x = x_all[:, pl.ds(at, tile)]
            both = dot_on(x, both_all[...], 0, 0).astype(target.dtype)
            target[0, into, :] = both[:, :hidden]
            target[1, into, :] = both[:, hidden:]
            return carry

        lax.fori_loop(0, 2, rows_of, 0)

        def down_of(index, carry, which=which, lower=lower):
            tile = hidden // 2
            at = pl.ds(pl.multiple_of(index * tile, tile), tile)
            grads = ge_all[:, pl.ds(pl.multiple_of(which * half, half), half)]
            lower[at, :] = dot_on(inner_all[:, at], grads, 0, 0).astype(lower.dtype)
            return carry

        lax.fori_loop(0, 2, down_of, 0)
        if turn_at == 0:
            add_x(depth - 1)

    def from_x(at, which):
        step = 2 * at + 1 if at else 0
        x_copy(step, order[at], which).wait_recv()
        return part[step, which, ours].astype(jnp.float32) + xbuf[order[at], which].astype(
            jnp.float32
        )

    for at in range(1, depth):
        mix_away[order[at] - 1] = from_x(at, 1).astype(jnp.bfloat16)
    mix_out[...] = from_x(0, 1)
    grads = from_x(0, 0)
    for z_rel in range(1, depth):
        z_copy(0, z_rel).wait_recv()
        grads = grads + zbuf[z_rel].astype(jnp.float32)
    grad_out[...] = grads

    def settle(by, carry):
        there = flip(me, by)
        send(
            gp_send_buf.at[me], gp_out.at[there], q_send.at[by], q_recv.at[by], expert_at(there)
        ).wait()
        prob_copy(by).wait_send()
        return carry

    lax.fori_loop(1, count, settle, 0)
    gather.wait_sends()
    for step in range(steps):
        core_copy(step).wait_send()
    for z_rel in range(depth):
        x_copy(0, z_rel, 0).wait_send()
        x_copy(0, z_rel, 1).wait_send()
    for z_rel in range(1, depth):
        z_copy(0, z_rel).wait_send()


def experts(expert_input, cotangent_all, prob, gate_weight, up_weight, down_weight):
    count = prob.shape[0]
    rows, width = expert_input.shape
    hidden = gate_weight.shape[2]
    total = count * rows
    steps, depth = count // 2, count // 4
    half = width // 2
    local = pl.BlockSpec(memory_space=pltpu.VMEM)
    shapes = ((count,), (count,), (count,), (steps,), (2, depth), (depth,))
    pairs = [pltpu.SemaphoreType.DMA(shape) for shape in shapes]
    semaphores = [item for item in pairs for _ in range(2)]
    bf16 = jnp.bfloat16
    return pl.pallas_call(
        functools.partial(experts_kernel, count),
        out_shape=[
            jax.ShapeDtypeStruct((rows, width), jnp.float32),
            jax.ShapeDtypeStruct((rows, width), jnp.float32),
            jax.ShapeDtypeStruct((depth - 1, rows, width), bf16),
            jax.ShapeDtypeStruct((count, 8, rows), jnp.float32),
            jax.ShapeDtypeStruct((2, half, hidden), jnp.float32),
            jax.ShapeDtypeStruct((hidden, half), jnp.float32),
            jax.ShapeDtypeStruct((2, half, hidden), bf16),
            jax.ShapeDtypeStruct((hidden, half), bf16),
        ],
        in_specs=[local] * 6,
        out_specs=[local] * 8,
        scratch_shapes=[
            pltpu.VMEM((total, width), bf16),
            pltpu.VMEM((count, 8, rows), jnp.float32),
            pltpu.VMEM((count, 8, rows), jnp.float32),
            pltpu.VMEM((total, 2 * hidden), bf16),
            pltpu.VMEM((total, hidden), bf16),
            pltpu.VMEM((total, width), bf16),
            pltpu.VMEM((steps, 2, 2 * rows, width), bf16),
            pltpu.VMEM((steps, 2, rows, width), bf16),
            pltpu.VMEM((depth, 2, rows, width), bf16),
            pltpu.VMEM((depth, rows, width), bf16),
        ]
        + semaphores,
        compiler_params=pltpu.CompilerParams(
            collective_id=1, has_side_effects=True, vmem_limit_bytes=58 * 2**20
        ),
        cost_estimate=pl.CostEstimate(
            flops=18 * total * width * hidden, bytes_accessed=20 * total * width, transcendentals=0
        ),
        name="experts",
    )(expert_input, cotangent_all, prob, gate_weight, up_weight, down_weight)


def late_kernel(
    count,
    cuts,
    pay_ref,
    gain_ref,
    tokens_hbm,
    attended_hbm,
    all_out,
    tokens_ref,
    attention_ref,
    attended_ref,
    fetch_sem,
    arrived,
    peer_buf,
    y_buf,
    mine,
    a_send,
    a_recv,
    g_send,
    g_recv,
    y_send,
    y_recv,
):
    first, last = cuts
    rows = pay_ref.shape[2]
    half = all_out.shape[2]
    me, dp = lax.axis_index("expert"), lax.axis_index("dp")
    meet(count, True)

    def columns(index):
        return pl.ds(pl.multiple_of(index * rows, rows), rows)

    def scatter(by):
        there = flip(me, by)
        return send(
            pay_ref.at[there],
            arrived.at[:, columns(me)],
            a_send.at[by],
            a_recv.at[by],
            expert_at(there),
        )

    def scatter_start(back, carry):
        scatter(count - back).start()
        return carry

    lax.fori_loop(1, count, scatter_start, 0)
    fetches = [
        pltpu.make_async_copy(tokens_hbm, tokens_ref, fetch_sem.at[0]),
        pltpu.make_async_copy(attended_hbm, attended_ref, fetch_sem.at[1]),
    ]
    for fetch in fetches:
        fetch.start()
    arrived[:, columns(me)] = pay_ref[me]
    fetches[0].wait()

    def norm_rows(index, carry):
        at = columns(index)
        values = tokens_ref[at, :].astype(jnp.float32)
        mean = jnp.mean(values * values, -1, keepdims=True)
        factor = lax.rsqrt(mean + EPSILON)
        for place, which in ((0, dp), (1, 1 - dp)):
            side = pl.ds(pl.multiple_of(which * half, half), half)
            here = slice(place * half, (place + 1) * half)
            normed = tokens_ref[at, side].astype(jnp.float32) * factor
            attention_ref[at, here] = (normed * gain_ref[:, here]).astype(jnp.bfloat16)
        return carry

    lax.fori_loop(0, count, norm_rows, 0)

    def scatter_wait(by, carry):
        there = flip(me, by)
        send(
            pay_ref.at[me],
            arrived.at[:, columns(there)],
            a_send.at[by],
            a_recv.at[by],
            expert_at(there),
        ).wait()
        return carry

    lax.fori_loop(1, count, scatter_wait, 0)

    fetches[1].wait()
    extra = arrived[last:, :].astype(jnp.float32)
    summed = extra[:, :rows]
    for index in range(1, count):
        summed = summed + extra[:, index * rows : (index + 1) * rows]
    edge = summed.shape[0] // 2
    blank = jnp.zeros((edge, half - rows), jnp.float32)
    own_extra = jnp.concatenate([summed[:edge], blank], 1)
    peer_extra = jnp.concatenate([summed[edge:], blank], 1)
    blank = jnp.zeros((edge, half), jnp.float32)

    def tile_of(at):
        return jnp.concatenate(
            [
                dot_on(arrived[:first, :], attention_ref[:, at], 1, 0),
                dot_on(arrived[first:last, :], attended_ref[:, at], 1, 0),
            ],
            0,
        )

    peer_buf[...] = jnp.concatenate(
        [tile_of(slice(half, 2 * half)), peer_extra, blank], 0
    ).astype(jnp.bfloat16)
    over = send(peer_buf, y_buf, y_send, y_recv, {"dp": 1 - dp})
    over.start()
    own = jnp.concatenate([tile_of(slice(0, half)), own_extra, blank], 0)
    over.wait()
    mine[...] = (
        own + y_buf[...].astype(jnp.float32)
    ).astype(jnp.bfloat16)
    gather = Gather(mine, lambda index: all_out.at[index], count, g_send, g_recv)
    gather.begin(range(12, count, 4))
    all_out[me] = mine[...]
    gather.rest()


def late_sums(payload, tokens_all, attended_all, gain, cuts):
    count, lines, rows = payload.shape
    half = tokens_all.shape[1] // 2
    local = pl.BlockSpec(memory_space=pltpu.VMEM)
    bf16 = jnp.bfloat16
    return pl.pallas_call(
        functools.partial(late_kernel, count, cuts),
        out_shape=jax.ShapeDtypeStruct((count, lines, half), bf16),
        in_specs=[local, local, pl.BlockSpec(memory_space=pl.ANY), pl.BlockSpec(memory_space=pl.ANY)],
        out_specs=local,
        scratch_shapes=[
            pltpu.VMEM(tokens_all.shape, bf16),
            pltpu.VMEM(tokens_all.shape, bf16),
            pltpu.VMEM(attended_all.shape, bf16),
            pltpu.SemaphoreType.DMA((2,)),
            pltpu.VMEM((lines, count * rows), bf16),
            pltpu.VMEM((lines, half), bf16),
            pltpu.VMEM((lines, half), bf16),
            pltpu.VMEM((lines, half), bf16),
            pltpu.SemaphoreType.DMA((count,)),
            pltpu.SemaphoreType.DMA((count,)),
            pltpu.SemaphoreType.DMA((count,)),
            pltpu.SemaphoreType.DMA((count,)),
            pltpu.SemaphoreType.DMA,
            pltpu.SemaphoreType.DMA,
        ],
        compiler_params=pltpu.CompilerParams(
            collective_id=2, has_side_effects=True, vmem_limit_bytes=56 * 2**20
        ),
        name="late",
    )(payload, gain.astype(jnp.float32)[None, :], tokens_all, attended_all)


def shards_together(
    tokens,
    segments,
    routes,
    first_gain,
    query_weight,
    key_projection_weight,
    value_projection_weight,
    out_weight,
    second_gain,
    router_weight,
    gate_weight,
    up_weight,
    down_weight,
    cotangent,
):
    token_rows = tokens.shape[0]
    expert_count = router_weight.shape[1]
    owner_count = lax.axis_size("expert")
    dp_count = lax.axis_size("dp")

    small = jnp.concatenate([router_weight, first_gain[:, None], second_gain[:, None]], 1)
    small = jnp.pad(small, ((0, 0), (0, -small.shape[1] % 128)))
    own = [query_weight, key_projection_weight, value_projection_weight, out_weight, small]
    tokens_all = lax.all_gather(tokens, "expert", axis=0, tiled=True)
    other, cotangent_all = front(own, cotangent, owner_count)
    query_mat, key_matrix, value_matrix, out_mat, small = (list(p) for p in zip(own, other))
    small_mat = jnp.concatenate(small, 0)
    router_mat = turn(small_mat[:, :expert_count], 0)
    gain_first = small_mat[:, expert_count]
    gain_second = turn(small_mat[:, expert_count + 1], 0)

    hidden, saved = halves_forward(
        tokens, segments, gain_first, query_mat, key_matrix, value_matrix, out_mat
    )
    attended_all = lax.all_gather(saved[7], "expert", axis=0, tiled=True)
    normed_second, factor_second, expert_input = normalize(hidden, gain_second)
    route_prob, chosen_hot = route_weights(expert_input, router_mat, routes)
    dense_prob = jnp.sum(chosen_hot * route_prob[:, :, None], 1)
    expert_input, tokens_all = lax.optimization_barrier((expert_input, tokens_all))
    prob = jnp.broadcast_to(dense_prob.T[:, None, :], (owner_count, 8, token_rows))
    grad_sum, mixture, mix_away, back_prob, mine, mine_down, peer, peer_down = experts(
        expert_input, cotangent_all, prob, gate_weight, up_weight, down_weight
    )
    grad_sum, attended_all = lax.optimization_barrier((grad_sum, attended_all))
    swap = [(0, 1), (1, 0)]
    peer = lax.ppermute(peer, "dp", swap)
    peer_down = lax.ppermute(peer_down, "dp", swap)
    mix_here = [
        lax.ppermute(mix_away[z - 1], "expert", [(i, i ^ (4 * z)) for i in range(owner_count)])
        for z in range(1, owner_count // 4)
    ]
    grad_prob = jnp.sum(chosen_hot * back_prob[:, 0, :].T[:, None, :], -1)
    router_grad = route_back(route_prob, grad_prob, chosen_hot)
    grad_expert_input = grad_sum + matrix_multiply(router_grad, router_mat.T)
    router_wgrad = matrix_multiply(router_grad.T, expert_input)
    grad_normed, second_gain_grad = normalize_back(
        grad_expert_input, normed_second, factor_second, gain_second
    )
    grad_hidden = cotangent.astype(jnp.float32) + grad_normed
    grad_tokens, first_gain_grad, late = halves_backward(
        grad_hidden, saved, gain_first, query_mat, key_matrix, value_matrix, out_mat
    )

    extras = jnp.concatenate(
        [router_wgrad, first_gain_grad[None, :], second_gain_grad[None, :]], 0
    )
    slices = [
        grad.T.reshape(owner_count, grad.shape[1] // owner_count, token_rows) for grad in late
    ]
    extra_count, extra_width = extras.shape
    part = extra_width // (owner_count * dp_count)
    spread = (
        extras.reshape(extra_count, dp_count, owner_count, part)
        .transpose(2, 1, 0, 3)
        .reshape(owner_count, dp_count, extra_count * part)
        .astype(jnp.bfloat16)
    )
    spread = jnp.pad(spread, ((0, 0), (0, 0), (0, -spread.shape[2] % (8 * token_rows))))
    spread = turn(spread, 1).reshape(owner_count, -1, token_rows)
    payload = jnp.concatenate(slices + [spread], 1)
    last = sum(piece.shape[1] for piece in slices)
    everything = late_sums(
        payload, tokens_all, attended_all, gain_first, (last - slices[3].shape[1], last)
    )
    everything, peer, peer_down, mix_here = lax.optimization_barrier(
        (everything, peer, peer_down, mix_here)
    )
    shares, (gate_share, up_share, down_share, output) = finish(
        everything,
        [piece.shape[1] for piece in slices],
        mine,
        mine_down,
        peer,
        peer_down,
        hidden,
        mixture,
        mix_here,
    )
    edge = spread.shape[1] // 2
    extras = everything[:, last : last + edge, :token_rows].reshape(owner_count, -1)
    extras = extras[:, : extra_count * part].reshape(owner_count, extra_count, part)
    extras = extras.transpose(1, 0, 2).reshape(extra_count, -1).astype(jnp.float32)
    query_share, key_share, value_share, out_share = shares
    return (
        output,
        grad_tokens,
        extras[expert_count],
        query_share,
        key_share,
        value_share,
        out_share,
        extras[expert_count + 1],
        extras[:expert_count].T,
        gate_share,
        up_share,
        down_share,
    )


def solution(mesh):
    placed = (
        P(("dp", "expert"), None),
        P(("dp", "expert")),
        P(("dp", "expert"), None),
        P("dp"),
        P("dp", None),
        P("dp", None),
        P("dp", None),
        P("dp", None),
        P("dp"),
        P("dp", None),
        P("expert", None, None),
        P("expert", None, None),
        P("expert", None, None),
        P(("dp", "expert"), None),
    )
    owners = mesh.shape["expert"]
    together = mesh.shape["dp"] == 2 and owners >= 8 and owners & (owners - 1) == 0
    return jax.shard_map(
        shards_together if together else shards,
        mesh=mesh,
        in_specs=placed,
        out_specs=(
            P(("dp", "expert"), None),
            P(("dp", "expert"), None),
            P("dp"),
            P("dp", None),
            P("dp", None),
            P("dp", None),
            P("dp", None),
            P("dp"),
            P("dp", None),
            P("expert", "dp", None),
            P("expert", "dp", None),
            P("expert", None, "dp"),
        ),
        check_vma=False,
    )
```

```python
import functools

import jax
import jax.numpy as jnp
from jax import lax
from jax.experimental import pallas as pl
from jax.experimental.pallas import tpu as pltpu
from jax.sharding import PartitionSpec as P

QUERY_HEADS = 16
KEY_VALUE_HEADS = 8
HEAD_DIM = 64
SEQUENCE_LENGTH = 128


EPSILON = 1e-06
SCORE_SCALE = 0.015625
ROPE_BASE = 10000.0
MASKED = -1e30


def product(pattern, left_op, right_op):
    return jnp.einsum(pattern, left_op, right_op, preferred_element_type=jnp.float32)


def matrix_multiply(left_op, right_op):
    return jnp.dot(left_op, right_op, preferred_element_type=jnp.float32)


def rope_tables(seq_len, head_size):
    positions = jnp.arange(seq_len, dtype=jnp.float32)
    exponent = jnp.arange(head_size // 2, dtype=jnp.float32) * (2.0 / head_size)
    angles = positions[:, None] * (ROPE_BASE ** (-exponent))[None, :]
    return (jnp.cos(angles)[None, :, None, :], jnp.sin(angles)[None, :, None, :])


def apply_rotary(values, cosine_table, sine_table):
    middle = values.shape[-1] // 2
    first_half = values[..., :middle]
    second_half = values[..., middle:]
    return jnp.concatenate(
        [
            first_half * cosine_table - second_half * sine_table,
            second_half * cosine_table + first_half * sine_table,
        ],
        -1,
    )


def inverse_rotary(gradient, cosine_table, sine_table):
    middle = gradient.shape[-1] // 2
    first_half = gradient[..., :middle]
    second_half = gradient[..., middle:]
    return jnp.concatenate(
        [
            first_half * cosine_table + second_half * sine_table,
            second_half * cosine_table - first_half * sine_table,
        ],
        -1,
    )


def normalize(values, gain_vec):
    factor = lax.rsqrt(jnp.mean(values * values, -1, keepdims=True) + EPSILON)
    normed = values * factor
    return (normed, factor, (normed * gain_vec).astype(jnp.bfloat16))


def normalize_back(gradient, normed, factor, gain_vec):
    gain_grad = jnp.sum(gradient * normed, 0)
    scaled = gradient * gain_vec
    return (factor * (scaled - normed * jnp.mean(scaled * normed, -1, keepdims=True)), gain_grad)


def segment_mask(segments):
    seq_len = segments.shape[1]
    causal = jnp.arange(seq_len)[:, None] >= jnp.arange(seq_len)[None, :]
    same_doc = segments[:, :, None] == segments[:, None, :]
    return (same_doc & causal[None])[:, None, None]


def score_table(query_rows, key_row_block, mask_tab):
    raw_scores = product("sqhgw,skhw->shgqk", query_rows, key_row_block) * SCORE_SCALE
    return jnp.where(mask_tab, raw_scores, MASKED)


def mixer_forward(tokens, segments, gain_vec, query_mat, key_matrix, value_matrix, out_mat):
    token_rows = tokens.shape[0]
    local_sequences = token_rows // SEQUENCE_LENGTH
    query_groups = QUERY_HEADS // KEY_VALUE_HEADS
    cosine_table, sine_table = rope_tables(SEQUENCE_LENGTH, HEAD_DIM)
    mask_tab = segment_mask(segments.reshape(local_sequences, SEQUENCE_LENGTH))
    residual = tokens.astype(jnp.float32)
    normed, factor, attention_input = normalize(residual, gain_vec)
    query_rows = apply_rotary(
        matrix_multiply(attention_input, query_mat).reshape(
            local_sequences, SEQUENCE_LENGTH, QUERY_HEADS, HEAD_DIM
        ),
        cosine_table,
        sine_table,
    )
    query_rows = query_rows.astype(jnp.bfloat16).reshape(
        local_sequences, SEQUENCE_LENGTH, KEY_VALUE_HEADS, query_groups, HEAD_DIM
    )
    key_row_block = apply_rotary(
        matrix_multiply(attention_input, key_matrix).reshape(
            local_sequences, SEQUENCE_LENGTH, KEY_VALUE_HEADS, HEAD_DIM
        ),
        cosine_table,
        sine_table,
    ).astype(jnp.bfloat16)
    value_row_block = (
        matrix_multiply(attention_input, value_matrix)
        .astype(jnp.bfloat16)
        .reshape(local_sequences, SEQUENCE_LENGTH, KEY_VALUE_HEADS, HEAD_DIM)
    )
    scores = score_table(query_rows, key_row_block, mask_tab)
    row_peak = jnp.max(scores, -1, keepdims=True)
    logsum = row_peak + jnp.log(jnp.sum(jnp.exp(scores - row_peak), -1, keepdims=True))
    weights = jnp.exp(scores - logsum).astype(jnp.bfloat16)
    attended = product("shgqk,skhw->sqhgw", weights, value_row_block).astype(jnp.bfloat16)
    hidden = residual + matrix_multiply(
        attended.reshape(token_rows, QUERY_HEADS * HEAD_DIM), out_mat
    )
    saved = (
        normed,
        factor,
        attention_input,
        query_rows,
        key_row_block,
        value_row_block,
        attended,
        logsum,
        mask_tab,
        cosine_table,
        sine_table,
    )
    return (hidden, saved)


def mixer_backward(grad_hidden, saved, gain_vec, query_mat, key_matrix, value_matrix, out_mat):
    (
        normed,
        factor,
        attention_input,
        query_rows,
        key_row_block,
        value_row_block,
        attended,
        logsum,
        mask_tab,
        cosine_table,
        sine_table,
    ) = saved
    token_rows = grad_hidden.shape[0]
    local_sequences = token_rows // SEQUENCE_LENGTH
    grad_round = grad_hidden.astype(jnp.bfloat16)
    out_grad = matrix_multiply(attended.reshape(token_rows, QUERY_HEADS * HEAD_DIM).T, grad_round)
    grad_attended = (
        matrix_multiply(grad_round, out_mat.T).astype(jnp.bfloat16).reshape(query_rows.shape)
    )
    scores = score_table(query_rows, key_row_block, mask_tab)
    prob_full = jnp.exp(scores - logsum)
    values_gradient = product("shgqk,sqhgw->skhw", prob_full.astype(jnp.bfloat16), grad_attended)
    grad_weights = product("sqhgw,skhw->shgqk", grad_attended, value_row_block)
    row_delta = product("sqhgw,sqhgw->shgq", grad_attended, attended)[..., None]
    grad_scores = (prob_full * (grad_weights - row_delta) * SCORE_SCALE).astype(jnp.bfloat16)
    grad_queries = product("shgqk,skhw->sqhgw", grad_scores, key_row_block)
    keys_gradient = product("shgqk,sqhgw->skhw", grad_scores, query_rows)
    query_grad = inverse_rotary(
        grad_queries.reshape(local_sequences, SEQUENCE_LENGTH, QUERY_HEADS, HEAD_DIM),
        cosine_table,
        sine_table,
    )
    query_grad = query_grad.astype(jnp.bfloat16).reshape(token_rows, QUERY_HEADS * HEAD_DIM)
    key_gradient = (
        inverse_rotary(keys_gradient, cosine_table, sine_table)
        .astype(jnp.bfloat16)
        .reshape(token_rows, KEY_VALUE_HEADS * HEAD_DIM)
    )
    value_gradient = values_gradient.astype(jnp.bfloat16).reshape(
        token_rows, KEY_VALUE_HEADS * HEAD_DIM
    )
    query_wgrad = matrix_multiply(attention_input.T, query_grad)
    key_wgrad = matrix_multiply(attention_input.T, key_gradient)
    value_wgrad = matrix_multiply(attention_input.T, value_gradient)
    grad_attn_input = (
        matrix_multiply(query_grad, query_mat.T)
        + matrix_multiply(key_gradient, key_matrix.T)
        + matrix_multiply(value_gradient, value_matrix.T)
    )
    grad_normed, gain_grad = normalize_back(grad_attn_input, normed, factor, gain_vec)
    return (grad_hidden + grad_normed, gain_grad, query_wgrad, key_wgrad, value_wgrad, out_grad)


def route_weights(expert_input, router_mat, routes):
    logits = matrix_multiply(expert_input, router_mat)
    chosen_hot = (
        routes[:, :, None] == jnp.arange(router_mat.shape[1], dtype=jnp.int32)[None, None, :]
    ).astype(jnp.float32)
    chosen = jnp.sum(chosen_hot * logits[:, None, :], -1)
    return (jax.nn.softmax(chosen, -1), chosen_hot)


def route_back(route_prob, grad_prob, chosen_hot):
    grad_chosen = route_prob * (grad_prob - jnp.sum(route_prob * grad_prob, -1, keepdims=True))
    return jnp.sum(chosen_hot * grad_chosen[:, :, None], 1).astype(jnp.bfloat16)


def expert_forward(owner_rows, gate_mat, up_mat, down_mat):
    gate_pre = product("erd,edf->erf", owner_rows, gate_mat)
    up_pre = product("erd,edf->erf", owner_rows, up_mat)
    gate_sig = jax.nn.sigmoid(gate_pre)
    gate_act = gate_pre * gate_sig
    inner_acts = (gate_act * up_pre).astype(jnp.bfloat16)
    expert_out = product("erf,efd->erd", inner_acts, down_mat).astype(jnp.bfloat16)
    return (expert_out, (gate_pre, up_pre, gate_sig, gate_act, inner_acts))


def expert_backward(grad_rows, owner_rows, kept_acts, gate_mat, up_mat, down_mat):
    gate_pre, up_pre, gate_sig, gate_act, inner_acts = kept_acts
    grad_inner = product("erd,efd->erf", grad_rows, down_mat)
    down_grad = product("erf,erd->efd", inner_acts, grad_rows)
    silu_slope = gate_sig * (1.0 + gate_pre * (1.0 - gate_sig))
    grad_gate = (grad_inner * up_pre * silu_slope).astype(jnp.bfloat16)
    grad_up = (grad_inner * gate_act).astype(jnp.bfloat16)
    gate_grad = product("erd,erf->edf", owner_rows, grad_gate)
    up_grad = product("erd,erf->edf", owner_rows, grad_up)
    grad_owner_rows = product("erf,edf->erd", grad_gate, gate_mat) + product(
        "erf,edf->erd", grad_up, up_mat
    )
    return (grad_owner_rows.astype(jnp.bfloat16), gate_grad, up_grad, down_grad)


def gather_dp(local_part):
    dp_count = lax.axis_size("dp")
    owner_count = lax.axis_size("expert")
    if dp_count != 2 or owner_count % 2:
        return lax.all_gather(local_part, "dp", axis=0, tiled=True)
    low, high = jnp.split(local_part, 2, 0)
    even = lax.axis_index("expert") % 2 == 0
    near = lax.ppermute(jnp.where(even, low, high), "dp", [(0, 1), (1, 0)])
    far = lax.ppermute(near, "expert", [(i, i ^ 1) for i in range(owner_count)])
    other = jnp.concatenate([jnp.where(even, near, far), jnp.where(even, far, near)], 0)
    first = lax.axis_index("dp") == 0
    return jnp.concatenate(
        [jnp.where(first, local_part, other), jnp.where(first, other, local_part)], 0
    )


def all_sums(partial):
    owner_count = lax.axis_size("expert")
    dp_count = lax.axis_size("dp")
    width = partial.shape[1]
    pieces = partial.astype(jnp.bfloat16).reshape(dp_count, owner_count, -1, width)
    piece = lax.psum_scatter(
        pieces.transpose(1, 0, 2, 3).reshape(-1, width), "expert", scatter_dimension=0, tiled=True
    )
    piece = scatter_dp(piece, 0).astype(jnp.bfloat16)
    return lax.all_gather(piece, "expert", axis=0, tiled=True).astype(jnp.float32)


def scatter_dp(partial, axis):
    dp_count = lax.axis_size("dp")
    rounded = partial.astype(jnp.bfloat16)
    if dp_count != 2:
        return lax.psum_scatter(rounded, "dp", scatter_dimension=axis, tiled=True).astype(
            jnp.float32
        )
    low, high = jnp.split(rounded, 2, axis)
    first = lax.axis_index("dp") == 0
    arrived = lax.ppermute(jnp.where(first, high, low), "dp", [(0, 1), (1, 0)])
    return jnp.where(first, low, high).astype(jnp.float32) + arrived.astype(jnp.float32)


def shards(
    tokens,
    segments,
    routes,
    first_gain,
    query_weight,
    key_projection_weight,
    value_projection_weight,
    out_weight,
    second_gain,
    router_weight,
    gate_weight,
    up_weight,
    down_weight,
    cotangent,
):
    token_rows, model_width = tokens.shape
    top_count = routes.shape[1]
    expert_count = router_weight.shape[1]
    owner_count = lax.axis_size("expert")
    local_count = gate_weight.shape[0]
    key_width = key_projection_weight.shape[1]
    query_width = query_weight.shape[1]
    capacity = 5 * token_rows * top_count // (4 * expert_count)
    row_part = router_weight.shape[0]

    small = jnp.concatenate(
        [router_weight, first_gain[:, None], second_gain[:, None]], 1
    )
    small_mat = gather_dp(small)
    router_mat = small_mat[:, :expert_count]
    gain_first = small_mat[:, expert_count]
    gain_second = small_mat[:, expert_count + 1]
    joined_mat = gather_dp(
        jnp.concatenate([query_weight, key_projection_weight, value_projection_weight], 1)
    )
    query_mat = joined_mat[:, :query_width]
    key_matrix = joined_mat[:, query_width : query_width + key_width]
    value_matrix = joined_mat[:, query_width + key_width :]
    out_mat = gather_dp(out_weight)

    routes_all = lax.all_gather(routes, "expert")
    cotangent_all = lax.all_gather(cotangent, "expert")

    mine = lax.axis_index("expert") * local_count + jnp.arange(local_count, dtype=jnp.int32)
    hit = jnp.any(routes_all[None] == mine[:, None, None, None], -1)
    before = (
        jnp.arange(token_rows)[:, None] < jnp.arange(token_rows)[None, :]
    ).astype(jnp.bfloat16)
    rank = product("lst,tu->lsu", hit.astype(jnp.bfloat16), before).astype(jnp.int32)
    slot = jnp.where(hit, rank, -1)
    picked = slot[:, :, None, :] == jnp.arange(capacity, dtype=jnp.int32)[None, None, :, None]
    pick = picked.astype(jnp.bfloat16)

    def rows_of(gathered):
        rows = product("lsct,std->lscd", pick, gathered)
        return rows.reshape(local_count, owner_count * capacity, model_width)

    own_hot = (routes[:, :, None] == jnp.arange(expert_count, dtype=jnp.int32)).any(1)
    own_rank = matrix_multiply(before.T, own_hot.astype(jnp.bfloat16)).astype(jnp.int32)
    own_slot = jnp.where(own_hot, own_rank, -1)
    own_pick = (
        own_slot[:, :, None] == jnp.arange(capacity, dtype=jnp.int32)[None, None, :]
    ).astype(jnp.bfloat16)

    def send_back(rows):
        shaped = rows.reshape(local_count, owner_count, capacity, model_width)
        return lax.all_to_all(
            shaped.transpose(1, 0, 2, 3).reshape(expert_count, capacity, model_width),
            "expert",
            split_axis=0,
            concat_axis=0,
            tiled=True,
        )

    def sum_back(returned):
        flat = returned.reshape(expert_count * capacity, model_width)
        return matrix_multiply(own_pick.reshape(token_rows, expert_count * capacity), flat)

    hidden, saved = mixer_forward(
        tokens, segments, gain_first, query_mat, key_matrix, value_matrix, out_mat
    )
    normed_second, factor_second, expert_input = normalize(hidden, gain_second)
    input_all = lax.all_gather(expert_input, "expert")
    route_prob, chosen_hot = route_weights(expert_input, router_mat, routes)
    dense_prob = jnp.sum(chosen_hot * route_prob[:, :, None], 1)
    prob_all = lax.all_gather(dense_prob, "expert")

    column = jnp.arange(expert_count, dtype=jnp.int32)
    my_column = (mine[:, None] == column[None, :]).astype(jnp.float32)
    my_prob = jnp.sum(prob_all[None] * my_column[:, None, None, :], -1)
    row_prob = jnp.sum(jnp.where(picked, my_prob[:, :, None, :], 0.0), -1).reshape(
        local_count, owner_count * capacity, 1
    )

    owner_rows = rows_of(input_all).astype(jnp.bfloat16)
    cotangent_rows = rows_of(cotangent_all).astype(jnp.bfloat16).astype(jnp.float32)
    expert_out, kept_acts = expert_forward(owner_rows, gate_weight, up_weight, down_weight)
    expert_out = expert_out.astype(jnp.float32)
    weighted = (row_prob * expert_out).astype(jnp.bfloat16)
    row_grad_prob = jnp.sum(expert_out * cotangent_rows, -1).reshape(
        local_count, owner_count, capacity
    )
    token_grad_prob = jnp.sum(jnp.where(picked, row_grad_prob[..., None], 0.0), 2)
    back_prob = lax.all_to_all(
        token_grad_prob.transpose(1, 0, 2).reshape(expert_count, token_rows),
        "expert",
        split_axis=0,
        concat_axis=0,
        tiled=True,
    )
    grad_prob = jnp.sum(chosen_hot * back_prob.T[:, None, :], -1)
    grad_output = cotangent.astype(jnp.float32)

    grad_rows = (row_prob * cotangent_rows).astype(jnp.bfloat16)
    grad_owner_rows, gate_grad, up_grad, down_grad = expert_backward(
        grad_rows, owner_rows, kept_acts, gate_weight, up_weight, down_weight
    )
    grad_back = send_back(grad_owner_rows)
    expert_shares = (
        scatter_dp(gate_grad, 1),
        scatter_dp(up_grad, 1),
        scatter_dp(down_grad, 2),
    )
    grad_back, expert_shares, weighted = lax.optimization_barrier(
        (grad_back, expert_shares, weighted)
    )
    forward_back = send_back(weighted)
    output = (hidden + sum_back(forward_back)).astype(jnp.bfloat16)
    backward_sum = sum_back(grad_back)
    router_grad = route_back(route_prob, grad_prob, chosen_hot)
    grad_expert_input = backward_sum + matrix_multiply(
        router_grad, router_mat.T
    )
    router_wgrad = matrix_multiply(router_grad.T, expert_input)
    grad_normed, second_gain_grad = normalize_back(
        grad_expert_input, normed_second, factor_second, gain_second
    )
    grad_hidden = grad_output + grad_normed
    grad_tokens, first_gain_grad, query_wgrad, key_wgrad, value_wgrad, out_wgrad = mixer_backward(
        grad_hidden, saved, gain_first, query_mat, key_matrix, value_matrix, out_mat
    )

    out_share = all_sums(out_wgrad)
    joined = all_sums(jnp.concatenate([query_wgrad, key_wgrad, value_wgrad], 1))
    query_share = joined[:, :query_width]
    key_share = joined[:, query_width : query_width + key_width]
    value_share = joined[:, query_width + key_width :]
    extras = jnp.concatenate(
        [router_wgrad, first_gain_grad[None, :], second_gain_grad[None, :]], 0
    )
    extras = lax.psum(extras.astype(jnp.bfloat16), ("dp", "expert"))
    extras = lax.dynamic_slice_in_dim(
        extras, lax.axis_index("dp") * row_part, row_part, 1
    ).astype(jnp.float32)
    router_share = extras[:expert_count].T
    first_share = extras[expert_count]
    second_share = extras[expert_count + 1]
    return (
        output,
        grad_tokens,
        first_share,
        query_share,
        key_share,
        value_share,
        out_share,
        second_share,
        router_share,
        expert_shares[0],
        expert_shares[1],
        expert_shares[2],
    )


def turn(values, axis):
    if lax.axis_size("dp") != 2:
        return values
    low, high = jnp.split(values, 2, axis)
    first = lax.axis_index("dp") == 0
    return jnp.concatenate([jnp.where(first, low, high), jnp.where(first, high, low)], axis)


def times(left_op, pieces):
    total, start = None, 0
    for piece in pieces:
        part = matrix_multiply(left_op[:, start : start + piece.shape[0]], piece)
        total = part if total is None else total + part
        start += piece.shape[0]
    return total


def times_back(left_op, pieces):
    return jnp.concatenate([matrix_multiply(left_op, piece.T) for piece in pieces], 1)


def halves_forward(tokens, segments, gain_vec, query_mat, key_matrix, value_matrix, out_mat):
    token_rows = tokens.shape[0]
    local_sequences = token_rows // SEQUENCE_LENGTH
    query_groups = QUERY_HEADS // KEY_VALUE_HEADS
    cosine_table, sine_table = rope_tables(SEQUENCE_LENGTH, HEAD_DIM)
    mask_tab = segment_mask(segments.reshape(local_sequences, SEQUENCE_LENGTH))
    residual = tokens.astype(jnp.float32)
    normed, factor, attention_input = normalize(turn(residual, 1), gain_vec)
    query_rows = apply_rotary(
        times(attention_input, query_mat).reshape(
            local_sequences, SEQUENCE_LENGTH, QUERY_HEADS, HEAD_DIM
        ),
        cosine_table,
        sine_table,
    )
    query_rows = query_rows.astype(jnp.bfloat16).reshape(
        local_sequences, SEQUENCE_LENGTH, KEY_VALUE_HEADS, query_groups, HEAD_DIM
    )
    key_row_block = apply_rotary(
        times(attention_input, key_matrix).reshape(
            local_sequences, SEQUENCE_LENGTH, KEY_VALUE_HEADS, HEAD_DIM
        ),
        cosine_table,
        sine_table,
    ).astype(jnp.bfloat16)
    value_row_block = (
        times(attention_input, value_matrix)
        .astype(jnp.bfloat16)
        .reshape(local_sequences, SEQUENCE_LENGTH, KEY_VALUE_HEADS, HEAD_DIM)
    )
    scores = score_table(query_rows, key_row_block, mask_tab)
    row_peak = jnp.max(scores, -1, keepdims=True)
    logsum = row_peak + jnp.log(jnp.sum(jnp.exp(scores - row_peak), -1, keepdims=True))
    weights = jnp.exp(scores - logsum).astype(jnp.bfloat16)
    attended = product("shgqk,skhw->sqhgw", weights, value_row_block).astype(jnp.bfloat16)
    turned = turn(attended.reshape(token_rows, QUERY_HEADS * HEAD_DIM), 1)
    hidden = residual + times(turned, out_mat)
    saved = (
        normed,
        factor,
        attention_input,
        query_rows,
        key_row_block,
        value_row_block,
        attended,
        turned,
        logsum,
        mask_tab,
        cosine_table,
        sine_table,
    )
    return (hidden, saved)


def halves_backward(grad_hidden, saved, gain_vec, query_mat, key_matrix, value_matrix, out_mat):
    (
        normed,
        factor,
        attention_input,
        query_rows,
        key_row_block,
        value_row_block,
        attended,
        _,
        logsum,
        mask_tab,
        cosine_table,
        sine_table,
    ) = saved
    token_rows = grad_hidden.shape[0]
    local_sequences = token_rows // SEQUENCE_LENGTH
    grad_round = grad_hidden.astype(jnp.bfloat16)
    grad_attended = (
        turn(times_back(grad_round, out_mat).astype(jnp.bfloat16), 1).reshape(query_rows.shape)
    )
    scores = score_table(query_rows, key_row_block, mask_tab)
    prob_full = jnp.exp(scores - logsum)
    values_gradient = product("shgqk,sqhgw->skhw", prob_full.astype(jnp.bfloat16), grad_attended)
    grad_weights = product("sqhgw,skhw->shgqk", grad_attended, value_row_block)
    row_delta = product("sqhgw,sqhgw->shgq", grad_attended, attended)[..., None]
    grad_scores = (prob_full * (grad_weights - row_delta) * SCORE_SCALE).astype(jnp.bfloat16)
    grad_queries = product("shgqk,skhw->sqhgw", grad_scores, key_row_block)
    keys_gradient = product("shgqk,sqhgw->skhw", grad_scores, query_rows)
    query_grad = inverse_rotary(
        grad_queries.reshape(local_sequences, SEQUENCE_LENGTH, QUERY_HEADS, HEAD_DIM),
        cosine_table,
        sine_table,
    )
    query_grad = query_grad.astype(jnp.bfloat16).reshape(token_rows, QUERY_HEADS * HEAD_DIM)
    key_gradient = (
        inverse_rotary(keys_gradient, cosine_table, sine_table)
        .astype(jnp.bfloat16)
        .reshape(token_rows, KEY_VALUE_HEADS * HEAD_DIM)
    )
    value_gradient = values_gradient.astype(jnp.bfloat16).reshape(
        token_rows, KEY_VALUE_HEADS * HEAD_DIM
    )
    grad_attn_input = (
        times_back(query_grad, query_mat)
        + times_back(key_gradient, key_matrix)
        + times_back(value_gradient, value_matrix)
    )
    grad_normed, gain_grad = normalize_back(grad_attn_input, normed, factor, gain_vec)
    return (
        grad_hidden + turn(grad_normed, 1),
        turn(gain_grad, 0),
        [query_grad, key_gradient, value_gradient, grad_round],
    )


MESH = pl.DeviceIdType.MESH


def quotient(index, by):
    return index // by if isinstance(index, int) else lax.div(index, jnp.int32(by))


def parity(index):
    return index % 2 if isinstance(index, int) else lax.rem(index, jnp.int32(2))


def flip(index, by):
    if isinstance(index, int) and isinstance(by, int):
        return index ^ by
    if isinstance(index, int):
        index, by = by, index
    total, weight = (index, 1) if isinstance(by, int) else (0, 1)
    for _ in range(6):
        if isinstance(by, int):
            if by & weight:
                total = total + weight - 2 * weight * parity(quotient(index, weight))
        else:
            one, two = parity(quotient(index, weight)), parity(quotient(by, weight))
            total = total + weight * (one + two - 2 * one * two)
        weight *= 2
    return total


def others(count, act):
    for by in range(1, count):
        act(by)


def expert_at(index):
    return {"expert": index}


def send(src, dst, send_sem, recv_sem, where):
    return pltpu.make_async_remote_copy(
        src_ref=src,
        dst_ref=dst,
        send_sem=send_sem,
        recv_sem=recv_sem,
        device_id=where,
        device_id_type=MESH,
    )


def meet(count, with_dp):
    barrier = pltpu.get_barrier_semaphore()
    me = lax.axis_index("expert")

    def greet(by):
        pl.semaphore_signal(
            barrier, inc=1, device_id=expert_at(flip(me, by)), device_id_type=MESH
        )

    others(count, greet)
    if with_dp:
        pl.semaphore_signal(
            barrier, inc=1, device_id={"dp": 1 - lax.axis_index("dp")}, device_id_type=MESH
        )
    pl.semaphore_wait(barrier, count - 1 + (1 if with_dp else 0))


class Gather:
    def __init__(self, own, block_of, count, send_sems, recv_sems):
        self.own, self.block_of, self.count = own, block_of, count
        self.send_sems, self.recv_sems = send_sems, recv_sems
        self.me = lax.axis_index("expert")

    def copy(self, rel, by, src=None):
        block = self.block_of(flip(self.me, rel))
        there = flip(rel, by)
        return send(
            block if src is None else src,
            block,
            self.send_sems.at[there],
            self.recv_sems.at[there],
            expert_at(flip(self.me, by)),
        )

    def wait(self, rel):
        block = self.block_of(flip(self.me, rel))
        send(
            block, block, self.send_sems.at[rel], self.recv_sems.at[rel], expert_at(self.me)
        ).wait_recv()

    def begin(self, held=()):
        for by in list(range(8, self.count, 4)) + [4, 2, 1]:
            if by not in held:
                self.copy(0, by, self.own).start()

    def release(self, by):
        self.copy(0, by, self.own).start()

    def pass_z(self, rel):
        self.wait(rel)
        self.copy(rel, 2).start()
        self.copy(rel, 1).start()

    def pass_x(self, rel):
        self.wait(rel + 2)
        self.copy(rel + 2, 1).start()

    def wait_sends(self):
        for rel in range(1, self.count):
            block = self.block_of(flip(self.me, rel))
            send(
                block, block, self.send_sems.at[rel], self.recv_sems.at[rel], expert_at(self.me)
            ).wait_send()

    def rest(self):
        far = list(range(12, self.count, 4))
        near = [rel for rel in (8, 4) if rel < self.count]
        self.pass_x(0)
        self.pass_z(near[0])
        for by in far:
            self.release(by)
        for rel in near[1:]:
            self.pass_z(rel)
        for rel in near:
            self.pass_x(rel)
        for rel in far:
            self.pass_z(rel)
            self.pass_x(rel)
        for rel in range(1, self.count, 2):
            self.wait(rel)
        self.wait_sends()


def front_kernel(pieces, *refs):
    mine, refs = refs[:pieces], refs[pieces:]
    fetched, refs = refs[:pieces], refs[pieces:]
    y_send, y_recv, c_send, c_recv = refs
    me, dp = lax.axis_index("expert"), lax.axis_index("dp")
    core = parity(me)
    meet(2, True)

    def part(ref, which):
        half = ref.shape[0] // 2
        return ref.at[pl.ds(pl.multiple_of(which * half, half), half)]

    over_y = [
        send(
            part(mine[i], core),
            part(fetched[i], core),
            y_send.at[i],
            y_recv.at[i],
            {"dp": 1 - dp},
        )
        for i in range(pieces)
    ]
    for copy in over_y:
        copy.start()
    over_core = [
        send(
            part(fetched[i], core),
            part(fetched[i], core),
            c_send.at[i],
            c_recv.at[i],
            expert_at(flip(me, 1)),
        )
        for i in range(pieces)
    ]
    for i in range(pieces):
        over_y[i].wait_recv()
        over_core[i].start()
    for i in range(pieces):
        send(
            part(mine[i], 1 - core),
            part(fetched[i], 1 - core),
            c_send.at[i],
            c_recv.at[i],
            expert_at(flip(me, 1)),
        ).wait_recv()
        over_core[i].wait_send()
        over_y[i].wait_send()


def front(own):
    pieces = len(own)
    anywhere = pl.BlockSpec(memory_space=pl.ANY)
    return pl.pallas_call(
        functools.partial(front_kernel, pieces),
        out_shape=[jax.ShapeDtypeStruct(part.shape, part.dtype) for part in own],
        in_specs=[anywhere] * pieces,
        out_specs=[anywhere] * pieces,
        scratch_shapes=[pltpu.SemaphoreType.DMA((pieces,)) for _ in range(4)],
        compiler_params=pltpu.CompilerParams(collective_id=0, has_side_effects=True),
        name="front",
    )(*own)


def finish_kernel(heights, away, *refs):
    all_ref, mine, mine_down, peer, peer_down, hidden, mixture = refs[:7]
    pieces, refs = refs[7 : 7 + away], refs[7 + away :]
    shares, refs = refs[: len(heights)], refs[len(heights) :]
    gate_out, up_out, down_out, output = refs
    start = 0
    for height, out in zip(heights, shares):
        for index in range(0, all_ref.shape[0], 128 // height):
            block = all_ref[index : index + 128 // height, start : start + height, :]
            block = block.astype(jnp.float32).reshape(128, block.shape[2])
            out[:, index * height : index * height + 128] = block.T
        start += height
    gate_out[0] = mine[0] + peer[0].astype(jnp.float32)
    up_out[0] = mine[1] + peer[1].astype(jnp.float32)
    down_out[0] = mine_down[...] + peer_down[...].astype(jnp.float32)
    total = hidden[...] + mixture[...]
    for piece in pieces:
        total = total + piece[...].astype(jnp.float32)
    output[...] = total.astype(jnp.bfloat16)


def finish(everything, heights, mine, mine_down, peer, peer_down, hidden, mixture, pieces):
    count, lines, half = everything.shape
    parts = 4
    rows, width = hidden.shape
    deep = mine.shape[2]
    tile, low, some = half // parts, deep // parts, rows // parts
    three = pl.BlockSpec((2, tile, deep), lambda i: (0, i, 0))
    down = pl.BlockSpec((low, half), lambda i: (i, 0))
    tokens = pl.BlockSpec((some, width), lambda i: (i, 0))
    f32 = jnp.float32
    results = pl.pallas_call(
        functools.partial(finish_kernel, heights, len(pieces)),
        grid=(parts,),
        out_shape=[jax.ShapeDtypeStruct((half, count * height), f32) for height in heights]
        + [
            jax.ShapeDtypeStruct((1, half, deep), f32),
            jax.ShapeDtypeStruct((1, half, deep), f32),
            jax.ShapeDtypeStruct((1, deep, half), f32),
            jax.ShapeDtypeStruct((rows, width), jnp.bfloat16),
        ],
        in_specs=[pl.BlockSpec((count, lines, tile), lambda i: (0, 0, i))]
        + [three, down, three, down, tokens, tokens]
        + [tokens] * len(pieces),
        out_specs=[pl.BlockSpec((tile, count * height), lambda i: (i, 0)) for height in heights]
        + [
            pl.BlockSpec((1, tile, deep), lambda i: (0, i, 0)),
            pl.BlockSpec((1, tile, deep), lambda i: (0, i, 0)),
            pl.BlockSpec((1, low, half), lambda i: (0, i, 0)),
            tokens,
        ],
        compiler_params=pltpu.CompilerParams(vmem_limit_bytes=58 * 2**20),
        name="finish",
    )(everything, mine, mine_down, peer, peer_down, hidden, mixture, *pieces)
    return results[: len(heights)], results[len(heights) :]


def dot_on(left_op, right_op, left_axis, right_axis):
    return lax.dot_general(
        left_op,
        right_op,
        (((left_axis,), (right_axis,)), ((), ())),
        preferred_element_type=jnp.float32,
    )


def experts_kernel(
    count,
    own_ref,
    cot_ref,
    prob_ref,
    gate_ref,
    up_ref,
    down_ref,
    grad_out,
    mix_out,
    gp_out,
    mine_out,
    mine_down,
    peer_out,
    peer_down,
    x_all,
    prob_all,
    gp_send_buf,
    both_all,
    inner_all,
    ge_all,
    part,
    cbuf,
    xbuf,
    zbuf,
    fbuf,
    a_send,
    a_recv,
    p_send,
    p_recv,
    q_send,
    q_recv,
    c_send,
    c_recv,
    x_send,
    x_recv,
    z_send,
    z_recv,
    f_send,
    f_recv,
):
    rows, width = own_ref.shape
    hidden = gate_ref.shape[2]
    pair = 2 * rows
    steps = count // 2
    depth = count // 4
    order = [0] + [z for z in (2, 1) if z < depth] + list(range(3, depth))
    me, dp = lax.axis_index("expert"), lax.axis_index("dp")
    core = parity(me)
    meet(count, False)

    def block_of(index):
        return x_all.at[pl.ds(pl.multiple_of(index * rows, rows), rows)]

    gather = Gather(own_ref, block_of, count, a_send, a_recv)
    gather.begin(range(12, count, 4))

    def prob_copy(by):
        there = flip(me, by)
        return send(
            prob_ref.at[there], prob_all.at[me], p_send.at[by], p_recv.at[by], expert_at(there)
        )

    def prob_start(by):
        prob_copy(by).start()

    others(count, prob_start)
    x_all[pl.ds(pl.multiple_of(me * rows, rows), rows)] = own_ref[...]
    prob_all[me] = prob_ref[me]

    def prob_wait(by):
        there = flip(me, by)
        send(
            prob_ref.at[me], prob_all.at[there], p_send.at[by], p_recv.at[by], expert_at(there)
        ).wait_recv()

    others(count, prob_wait)

    def rel_of(step):
        z_rel = quotient(step, 2)
        x_rel = jnp.where(step < 2, parity(step), 1 - parity(step))
        z_rel = sum(jnp.where(z_rel == at, z, 0) for at, z in enumerate(order))
        return 4 * z_rel + 2 * x_rel, z_rel

    eye = (
        lax.broadcasted_iota(jnp.int32, (pair, pair), 0)
        == lax.broadcasted_iota(jnp.int32, (pair, pair), 1)
    )
    theirs = pl.ds(pl.multiple_of((1 - core) * rows, rows), rows)
    ours = pl.ds(pl.multiple_of(core * rows, rows), rows)

    def core_copy(step):
        return send(
            part.at[step, :, theirs],
            cbuf.at[step],
            c_send.at[step],
            c_recv.at[step],
            expert_at(flip(me, 1)),
        )

    def x_copy(step, z_rel, which):
        return send(
            part.at[step, which, ours],
            xbuf.at[z_rel, which],
            x_send.at[which, z_rel],
            x_recv.at[which, z_rel],
            expert_at(flip(me, 2)),
        )

    def z_copy(step, z_rel):
        return send(
            part.at[step, 0, ours],
            zbuf.at[z_rel],
            z_send.at[z_rel],
            z_recv.at[z_rel],
            expert_at(flip(me, 4 * z_rel)),
        )

    def compute(step):
        rel, _ = rel_of(step)
        chip = quotient(flip(me, rel), 2)
        where = pl.ds(pl.multiple_of(chip * pair, pair), pair)
        x = x_all[where, :]
        gate_pre = dot_on(x, gate_ref[0], 1, 0)
        up_pre = dot_on(x, up_ref[0], 1, 0)
        sig = jax.nn.sigmoid(gate_pre)
        act = gate_pre * sig
        inner = (act * up_pre).astype(jnp.bfloat16)
        inner_all[where, :] = inner
        out = dot_on(inner, down_ref[0], 1, 0).astype(jnp.bfloat16).astype(jnp.float32)
        prob_row = jnp.concatenate(
            [prob_all[2 * chip, 0:1, :], prob_all[2 * chip + 1, 0:1, :]], 1
        )
        prob = jnp.sum(jnp.where(eye, prob_row, 0.0), 1, keepdims=True)
        cot = cot_ref[where, :].astype(jnp.float32)
        part[step, 1] = (prob * out).astype(jnp.bfloat16)
        gp = jnp.sum(out * cot, 1, keepdims=True)
        gp_row = jnp.sum(jnp.where(eye, gp, 0.0), 0, keepdims=True)
        gp_send_buf[2 * chip] = jnp.broadcast_to(gp_row[:, :rows], (8, rows))
        gp_send_buf[2 * chip + 1] = jnp.broadcast_to(gp_row[:, rows:], (8, rows))
        ge = (prob * cot).astype(jnp.bfloat16)
        ge_all[where, :] = ge
        gi = dot_on(ge, down_ref[0], 1, 1)
        slope = sig * (1.0 + gate_pre * (1.0 - sig))
        gg = (gi * up_pre * slope).astype(jnp.bfloat16)
        gu = (gi * act).astype(jnp.bfloat16)
        both_all[where, :hidden] = gg
        both_all[where, hidden:] = gu
        part[step, 0] = (dot_on(gg, gate_ref[0], 1, 1) + dot_on(gu, up_ref[0], 1, 1)).astype(
            jnp.bfloat16
        )

    def add_core(step):
        core_copy(step).wait_recv()
        total = part[step, :, ours].astype(jnp.float32) + cbuf[step].astype(jnp.float32)
        part[step, :, ours] = total.astype(jnp.bfloat16)

    def add_x(at):
        z_rel, step = order[at], 2 * at + 1
        x_copy(step, z_rel, 0).wait_recv()
        total = part[step, 0, ours].astype(jnp.float32) + xbuf[z_rel, 0].astype(jnp.float32)
        part[step, 0, ours] = total.astype(jnp.bfloat16)
        z_copy(step, z_rel).start()

    def on(step, number):
        return pl.when(step == number)

    def turn_of(step, carry):
        rel, _ = rel_of(step)

        for at in range(1, depth):

            @on(step, 2 * at)
            def _(at=at):
                if at == 1:
                    gather.pass_x(4 * order[1])

        gather.wait(rel + 1)
        compute(step)
        core_copy(step).start()

        @on(step, 0)
        def _():
            gather.pass_x(0)

        @on(step, 1)
        def _():
            gather.pass_z(4 * order[1])
            for by in range(12, count, 4):
                gather.release(by)
            if depth > 2:
                gather.pass_z(4 * order[2])
            add_core(0)
            add_core(1)

        for at in range(1, depth):

            @on(step, 2 * at)
            def _(at=at):
                if at == 1:
                    x_copy(1, 0, 0).start()
                    x_copy(1, 0, 1).start()
                else:
                    add_core(2 * at - 1)
                    x_copy(2 * at - 2, order[at - 1], 1).start()
                if at > 1 and at + 1 < depth:
                    gather.pass_z(4 * order[at + 1])

            @on(step, 2 * at + 1)
            def _(at=at):
                add_core(2 * at)
                x_copy(2 * at, order[at], 0).start()
                if at + 1 < depth:
                    gather.pass_x(4 * order[at + 1])

        if depth > 3:

            @on(step, 6)
            def _():
                add_x(1)

        return carry

    lax.fori_loop(0, steps, turn_of, 0)
    add_core(steps - 1)
    x_copy(steps - 2, order[-1], 1).start()
    for at in range(2 if depth > 3 else 1, depth - 1):
        add_x(at)

    def gp_copy(by):
        there = flip(me, by)
        return send(
            gp_send_buf.at[there], gp_out.at[me], q_send.at[by], q_recv.at[by], expert_at(there)
        )

    def gp_start(by):
        gp_copy(by).start()

    others(count, gp_start)
    gp_out[me] = gp_send_buf[me]

    half = width // 2
    for turn_at, (which, target, lower) in enumerate( ((1 - dp, peer_out, peer_down), (dp, mine_out, mine_down))
    ):

        def rows_of(index, carry, which=which, target=target):
            tile = half // 2
            at = pl.multiple_of(which * half + index * tile, tile)
            into = pl.ds(pl.multiple_of(index * tile, tile), tile)
            x = x_all[:, pl.ds(at, tile)]
            both = dot_on(x, both_all[...], 0, 0).astype(target.dtype)
            target[0, into, :] = both[:, :hidden]
            target[1, into, :] = both[:, hidden:]
            return carry

        lax.fori_loop(0, 2, rows_of, 0)

        def down_of(index, carry, which=which, lower=lower):
            tile = hidden // 2
            at = pl.ds(pl.multiple_of(index * tile, tile), tile)
            grads = ge_all[:, pl.ds(pl.multiple_of(which * half, half), half)]
            lower[at, :] = dot_on(inner_all[:, at], grads, 0, 0).astype(lower.dtype)
            return carry

        lax.fori_loop(0, 2, down_of, 0)
        if turn_at == 0:
            add_x(depth - 1)

    def from_x(at, which):
        step = 2 * at + 1 if at else 0
        x_copy(step, order[at], which).wait_recv()
        return part[step, which, ours].astype(jnp.float32) + xbuf[order[at], which].astype(
            jnp.float32
        )

    def outputs_z(at):
        step, z_rel = 2 * at + 1, order[at]
        return send(
            part.at[step, 1, ours],
            fbuf.at[z_rel],
            f_send.at[z_rel],
            f_recv.at[z_rel],
            expert_at(flip(me, 4 * z_rel)),
        )

    for at in range(1, depth):
        part[2 * at + 1, 1, ours] = from_x(at, 1).astype(jnp.bfloat16)
        outputs_z(at).start()
    mixed = from_x(0, 1)
    grads = from_x(0, 0)
    for z_rel in range(1, depth):
        z_copy(0, z_rel).wait_recv()
        grads = grads + zbuf[z_rel].astype(jnp.float32)
    grad_out[...] = grads
    for at in range(1, depth):
        outputs_z(at).wait()
        mixed = mixed + fbuf[order[at]].astype(jnp.float32)
    mix_out[...] = mixed

    def settle(by):
        there = flip(me, by)
        send(
            gp_send_buf.at[me], gp_out.at[there], q_send.at[by], q_recv.at[by], expert_at(there)
        ).wait()
        prob_copy(by).wait_send()

    others(count, settle)
    gather.wait_sends()
    for step in range(steps):
        core_copy(step).wait_send()
    for z_rel in range(depth):
        x_copy(0, z_rel, 0).wait_send()
        x_copy(0, z_rel, 1).wait_send()
    for z_rel in range(1, depth):
        z_copy(0, z_rel).wait_send()


def experts(expert_input, cotangent_all, prob, gate_weight, up_weight, down_weight):
    count = prob.shape[0]
    rows, width = expert_input.shape
    hidden = gate_weight.shape[2]
    total = count * rows
    steps, depth = count // 2, count // 4
    half = width // 2
    local = pl.BlockSpec(memory_space=pltpu.VMEM)
    shapes = ((count,), (count,), (count,), (steps,), (2, depth), (depth,), (depth,))
    pairs = [pltpu.SemaphoreType.DMA(shape) for shape in shapes]
    semaphores = [item for item in pairs for _ in range(2)]
    bf16 = jnp.bfloat16
    return pl.pallas_call(
        functools.partial(experts_kernel, count),
        out_shape=[
            jax.ShapeDtypeStruct((rows, width), jnp.float32),
            jax.ShapeDtypeStruct((rows, width), jnp.float32),
            jax.ShapeDtypeStruct((count, 8, rows), jnp.float32),
            jax.ShapeDtypeStruct((2, half, hidden), jnp.float32),
            jax.ShapeDtypeStruct((hidden, half), jnp.float32),
            jax.ShapeDtypeStruct((2, half, hidden), bf16),
            jax.ShapeDtypeStruct((hidden, half), bf16),
        ],
        in_specs=[local] * 6,
        out_specs=[local] * 7,
        scratch_shapes=[
            pltpu.VMEM((total, width), bf16),
            pltpu.VMEM((count, 8, rows), jnp.float32),
            pltpu.VMEM((count, 8, rows), jnp.float32),
            pltpu.VMEM((total, 2 * hidden), bf16),
            pltpu.VMEM((total, hidden), bf16),
            pltpu.VMEM((total, width), bf16),
            pltpu.VMEM((steps, 2, 2 * rows, width), bf16),
            pltpu.VMEM((steps, 2, rows, width), bf16),
            pltpu.VMEM((depth, 2, rows, width), bf16),
            pltpu.VMEM((depth, rows, width), bf16),
            pltpu.VMEM((depth, rows, width), bf16),
        ]
        + semaphores,
        compiler_params=pltpu.CompilerParams(
            collective_id=1, has_side_effects=True, vmem_limit_bytes=58 * 2**20
        ),
        cost_estimate=pl.CostEstimate(
            flops=18 * total * width * hidden, bytes_accessed=20 * total * width, transcendentals=0
        ),
        name="experts",
    )(expert_input, cotangent_all, prob, gate_weight, up_weight, down_weight)


def late_kernel(
    count,
    cuts,
    pay_ref,
    gain_ref,
    tokens_hbm,
    attended_hbm,
    both_away,
    down_away,
    all_out,
    both_here,
    down_here,
    swap_send,
    swap_recv,
    tokens_ref,
    attention_ref,
    attended_ref,
    fetch_sem,
    arrived,
    peer_buf,
    y_buf,
    mine,
    a_send,
    a_recv,
    g_send,
    g_recv,
    y_send,
    y_recv,
):
    first, last = cuts
    rows = pay_ref.shape[2]
    half = all_out.shape[2]
    me, dp = lax.axis_index("expert"), lax.axis_index("dp")
    meet(count, True)

    def columns(index):
        return pl.ds(pl.multiple_of(index * rows, rows), rows)

    def scatter(by):
        there = flip(me, by)
        return send(
            pay_ref.at[there],
            arrived.at[:, columns(me)],
            a_send.at[by],
            a_recv.at[by],
            expert_at(there),
        )

    def scatter_start(back):
        scatter(count - back).start()

    others(count, scatter_start)
    peer = {"dp": 1 - dp}
    swap_down = send(down_away, down_here, swap_send.at[0], swap_recv.at[0], peer)
    swap_both = send(both_away, both_here, swap_send.at[1], swap_recv.at[1], peer)
    swap_down.start()
    fetches = [
        pltpu.make_async_copy(tokens_hbm, tokens_ref, fetch_sem.at[0]),
        pltpu.make_async_copy(attended_hbm, attended_ref, fetch_sem.at[1]),
    ]
    for fetch in fetches:
        fetch.start()
    arrived[:, columns(me)] = pay_ref[me]
    fetches[0].wait()

    def norm_rows(index, carry):
        at = columns(index)
        values = tokens_ref[at, :].astype(jnp.float32)
        mean = jnp.mean(values * values, -1, keepdims=True)
        factor = lax.rsqrt(mean + EPSILON)
        for place, which in ((0, dp), (1, 1 - dp)):
            side = pl.ds(pl.multiple_of(which * half, half), half)
            here = slice(place * half, (place + 1) * half)
            normed = tokens_ref[at, side].astype(jnp.float32) * factor
            attention_ref[at, here] = (normed * gain_ref[:, here]).astype(jnp.bfloat16)
        return carry

    lax.fori_loop(0, count, norm_rows, 0)

    def scatter_wait(by):
        there = flip(me, by)
        send(
            pay_ref.at[me],
            arrived.at[:, columns(there)],
            a_send.at[by],
            a_recv.at[by],
            expert_at(there),
        ).wait()

    others(count, scatter_wait)

    fetches[1].wait()
    extra = arrived[last:, :].astype(jnp.float32)
    summed = extra[:, :rows]
    for index in range(1, count):
        summed = summed + extra[:, index * rows : (index + 1) * rows]
    edge = summed.shape[0] // 2
    blank = jnp.zeros((edge, half - rows), jnp.float32)
    own_extra = jnp.concatenate([summed[:edge], blank], 1)
    peer_extra = jnp.concatenate([summed[edge:], blank], 1)
    blank = jnp.zeros((edge, half), jnp.float32)

    def tile_of(at):
        return jnp.concatenate(
            [
                dot_on(arrived[:first, :], attention_ref[:, at], 1, 0),
                dot_on(arrived[first:last, :], attended_ref[:, at], 1, 0),
            ],
            0,
        )

    peer_buf[...] = jnp.concatenate(
        [tile_of(slice(half, 2 * half)), peer_extra, blank], 0
    ).astype(jnp.bfloat16)
    over = send(peer_buf, y_buf, y_send, y_recv, peer)
    over.start()
    own = jnp.concatenate([tile_of(slice(0, half)), own_extra, blank], 0)
    over.wait()
    swap_both.start()
    mine[...] = (
        own + y_buf[...].astype(jnp.float32)
    ).astype(jnp.bfloat16)
    gather = Gather(mine, lambda index: all_out.at[index], count, g_send, g_recv)
    gather.begin(range(12, count, 4))
    all_out[me] = mine[...]
    gather.rest()
    swap_down.wait()
    swap_both.wait()


def late_sums(payload, tokens_all, attended_all, gain, both, down, cuts):
    count, lines, rows = payload.shape
    half = tokens_all.shape[1] // 2
    local = pl.BlockSpec(memory_space=pltpu.VMEM)
    anywhere = pl.BlockSpec(memory_space=pl.ANY)
    bf16 = jnp.bfloat16
    return pl.pallas_call(
        functools.partial(late_kernel, count, cuts),
        out_shape=[
            jax.ShapeDtypeStruct((count, lines, half), bf16),
            jax.ShapeDtypeStruct(both.shape, bf16),
            jax.ShapeDtypeStruct(down.shape, bf16),
        ],
        in_specs=[local, local] + [anywhere] * 4,
        out_specs=[local, anywhere, anywhere],
        scratch_shapes=[
            pltpu.SemaphoreType.DMA((2,)),
            pltpu.SemaphoreType.DMA((2,)),
            pltpu.VMEM(tokens_all.shape, bf16),
            pltpu.VMEM(tokens_all.shape, bf16),
            pltpu.VMEM(attended_all.shape, bf16),
            pltpu.SemaphoreType.DMA((2,)),
            pltpu.VMEM((lines, count * rows), bf16),
            pltpu.VMEM((lines, half), bf16),
            pltpu.VMEM((lines, half), bf16),
            pltpu.VMEM((lines, half), bf16),
            pltpu.SemaphoreType.DMA((count,)),
            pltpu.SemaphoreType.DMA((count,)),
            pltpu.SemaphoreType.DMA((count,)),
            pltpu.SemaphoreType.DMA((count,)),
            pltpu.SemaphoreType.DMA,
            pltpu.SemaphoreType.DMA,
        ],
        compiler_params=pltpu.CompilerParams(
            collective_id=2, has_side_effects=True, vmem_limit_bytes=56 * 2**20
        ),
        name="late",
    )(payload, gain.astype(jnp.float32)[None, :], tokens_all, attended_all, both, down)


def shards_together(
    tokens,
    segments,
    routes,
    first_gain,
    query_weight,
    key_projection_weight,
    value_projection_weight,
    out_weight,
    second_gain,
    router_weight,
    gate_weight,
    up_weight,
    down_weight,
    cotangent,
):
    token_rows = tokens.shape[0]
    expert_count = router_weight.shape[1]
    owner_count = lax.axis_size("expert")
    dp_count = lax.axis_size("dp")

    small = jnp.concatenate([router_weight, first_gain[:, None], second_gain[:, None]], 1)
    small = jnp.pad(small, ((0, 0), (0, -small.shape[1] % 128)))
    own = [query_weight, key_projection_weight, value_projection_weight, out_weight, small]
    cotangent_all = lax.all_gather(cotangent, "expert", axis=0, tiled=True)
    tokens_all = lax.all_gather(tokens, "expert", axis=0, tiled=True)
    other = front(own)
    query_mat, key_matrix, value_matrix, out_mat, small = (list(p) for p in zip(own, other))
    small_mat = jnp.concatenate(small, 0)
    router_mat = turn(small_mat[:, :expert_count], 0)
    gain_first = small_mat[:, expert_count]
    gain_second = turn(small_mat[:, expert_count + 1], 0)

    hidden, saved = halves_forward(
        tokens, segments, gain_first, query_mat, key_matrix, value_matrix, out_mat
    )
    attended_all = lax.all_gather(saved[7], "expert", axis=0, tiled=True)
    normed_second, factor_second, expert_input = normalize(hidden, gain_second)
    route_prob, chosen_hot = route_weights(expert_input, router_mat, routes)
    dense_prob = jnp.sum(chosen_hot * route_prob[:, :, None], 1)
    prob = jnp.broadcast_to(dense_prob.T[:, None, :], (owner_count, 8, token_rows))
    grad_sum, mixture, back_prob, mine, mine_down, peer, peer_down = experts(
        expert_input, cotangent_all, prob, gate_weight, up_weight, down_weight
    )
    grad_sum, attended_all, tokens_all = lax.optimization_barrier(
        (grad_sum, attended_all, tokens_all)
    )
    grad_prob = jnp.sum(chosen_hot * back_prob[:, 0, :].T[:, None, :], -1)
    router_grad = route_back(route_prob, grad_prob, chosen_hot)
    grad_expert_input = grad_sum + matrix_multiply(router_grad, router_mat.T)
    router_wgrad = matrix_multiply(router_grad.T, expert_input)
    grad_normed, second_gain_grad = normalize_back(
        grad_expert_input, normed_second, factor_second, gain_second
    )
    grad_hidden = cotangent.astype(jnp.float32) + grad_normed
    grad_tokens, first_gain_grad, late = halves_backward(
        grad_hidden, saved, gain_first, query_mat, key_matrix, value_matrix, out_mat
    )

    extras = jnp.concatenate(
        [router_wgrad, first_gain_grad[None, :], second_gain_grad[None, :]], 0
    )
    slices = [
        grad.T.reshape(owner_count, grad.shape[1] // owner_count, token_rows) for grad in late
    ]
    extra_count, extra_width = extras.shape
    part = extra_width // (owner_count * dp_count)
    spread = (
        extras.reshape(extra_count, dp_count, owner_count, part)
        .transpose(2, 1, 0, 3)
        .reshape(owner_count, dp_count, extra_count * part)
        .astype(jnp.bfloat16)
    )
    spread = jnp.pad(spread, ((0, 0), (0, 0), (0, -spread.shape[2] % (8 * token_rows))))
    spread = turn(spread, 1).reshape(owner_count, -1, token_rows)
    payload = jnp.concatenate(slices + [spread], 1)
    last = sum(piece.shape[1] for piece in slices)
    everything, peer, peer_down = late_sums(
        payload, tokens_all, attended_all, gain_first, peer, peer_down,
        (last - slices[3].shape[1], last),
    )
    shares, (gate_share, up_share, down_share, output) = finish(
        everything,
        [piece.shape[1] for piece in slices],
        mine,
        mine_down,
        peer,
        peer_down,
        hidden,
        mixture,
        [],
    )
    edge = spread.shape[1] // 2
    extras = everything[:, last : last + edge, :token_rows].reshape(owner_count, -1)
    extras = extras[:, : extra_count * part].reshape(owner_count, extra_count, part)
    extras = extras.transpose(1, 0, 2).reshape(extra_count, -1).astype(jnp.float32)
    query_share, key_share, value_share, out_share = shares
    return (
        output,
        grad_tokens,
        extras[expert_count],
        query_share,
        key_share,
        value_share,
        out_share,
        extras[expert_count + 1],
        extras[:expert_count].T,
        gate_share,
        up_share,
        down_share,
    )


def solution(mesh):
    placed = (
        P(("dp", "expert"), None),
        P(("dp", "expert")),
        P(("dp", "expert"), None),
        P("dp"),
        P("dp", None),
        P("dp", None),
        P("dp", None),
        P("dp", None),
        P("dp"),
        P("dp", None),
        P("expert", None, None),
        P("expert", None, None),
        P("expert", None, None),
        P(("dp", "expert"), None),
    )
    owners = mesh.shape["expert"]
    together = mesh.shape["dp"] == 2 and owners >= 8 and owners & (owners - 1) == 0
    return jax.shard_map(
        shards_together if together else shards,
        mesh=mesh,
        in_specs=placed,
        out_specs=(
            P(("dp", "expert"), None),
            P(("dp", "expert"), None),
            P("dp"),
            P("dp", None),
            P("dp", None),
            P("dp", None),
            P("dp", None),
            P("dp"),
            P("dp", None),
            P("expert", "dp", None),
            P("expert", "dp", None),
            P("expert", None, "dp"),
        ),
        check_vma=False,
    )
```

```python
import functools

import jax
import jax.numpy as jnp
from jax import lax
from jax.experimental import pallas as pl
from jax.experimental.pallas import tpu as pltpu
from jax.sharding import PartitionSpec as P

QUERY_HEADS = 16
KEY_VALUE_HEADS = 8
HEAD_DIM = 64
SEQUENCE_LENGTH = 128


EPSILON = 1e-06
SCORE_SCALE = 0.015625
ROPE_BASE = 10000.0
MASKED = -1e30


def product(pattern, left_op, right_op):
    return jnp.einsum(pattern, left_op, right_op, preferred_element_type=jnp.float32)


def matrix_multiply(left_op, right_op):
    return jnp.dot(left_op, right_op, preferred_element_type=jnp.float32)


def rope_tables(seq_len, head_size):
    positions = jnp.arange(seq_len, dtype=jnp.float32)
    exponent = jnp.arange(head_size // 2, dtype=jnp.float32) * (2.0 / head_size)
    angles = positions[:, None] * (ROPE_BASE ** (-exponent))[None, :]
    return (jnp.cos(angles)[None, :, None, :], jnp.sin(angles)[None, :, None, :])


def apply_rotary(values, cosine_table, sine_table):
    middle = values.shape[-1] // 2
    first_half = values[..., :middle]
    second_half = values[..., middle:]
    return jnp.concatenate(
        [
            first_half * cosine_table - second_half * sine_table,
            second_half * cosine_table + first_half * sine_table,
        ],
        -1,
    )


def inverse_rotary(gradient, cosine_table, sine_table):
    middle = gradient.shape[-1] // 2
    first_half = gradient[..., :middle]
    second_half = gradient[..., middle:]
    return jnp.concatenate(
        [
            first_half * cosine_table + second_half * sine_table,
            second_half * cosine_table - first_half * sine_table,
        ],
        -1,
    )


def normalize(values, gain_vec):
    factor = lax.rsqrt(jnp.mean(values * values, -1, keepdims=True) + EPSILON)
    normed = values * factor
    return (normed, factor, (normed * gain_vec).astype(jnp.bfloat16))


def normalize_back(gradient, normed, factor, gain_vec):
    gain_grad = jnp.sum(gradient * normed, 0)
    scaled = gradient * gain_vec
    return (factor * (scaled - normed * jnp.mean(scaled * normed, -1, keepdims=True)), gain_grad)


def segment_mask(segments):
    seq_len = segments.shape[1]
    causal = jnp.arange(seq_len)[:, None] >= jnp.arange(seq_len)[None, :]
    same_doc = segments[:, :, None] == segments[:, None, :]
    return (same_doc & causal[None])[:, None, None]


def score_table(query_rows, key_row_block, mask_tab):
    raw_scores = product("sqhgw,skhw->shgqk", query_rows, key_row_block) * SCORE_SCALE
    return jnp.where(mask_tab, raw_scores, MASKED)


def mixer_forward(tokens, segments, gain_vec, query_mat, key_matrix, value_matrix, out_mat):
    token_rows = tokens.shape[0]
    local_sequences = token_rows // SEQUENCE_LENGTH
    query_groups = QUERY_HEADS // KEY_VALUE_HEADS
    cosine_table, sine_table = rope_tables(SEQUENCE_LENGTH, HEAD_DIM)
    mask_tab = segment_mask(segments.reshape(local_sequences, SEQUENCE_LENGTH))
    residual = tokens.astype(jnp.float32)
    normed, factor, attention_input = normalize(residual, gain_vec)
    query_rows = apply_rotary(
        matrix_multiply(attention_input, query_mat).reshape(
            local_sequences, SEQUENCE_LENGTH, QUERY_HEADS, HEAD_DIM
        ),
        cosine_table,
        sine_table,
    )
    query_rows = query_rows.astype(jnp.bfloat16).reshape(
        local_sequences, SEQUENCE_LENGTH, KEY_VALUE_HEADS, query_groups, HEAD_DIM
    )
    key_row_block = apply_rotary(
        matrix_multiply(attention_input, key_matrix).reshape(
            local_sequences, SEQUENCE_LENGTH, KEY_VALUE_HEADS, HEAD_DIM
        ),
        cosine_table,
        sine_table,
    ).astype(jnp.bfloat16)
    value_row_block = (
        matrix_multiply(attention_input, value_matrix)
        .astype(jnp.bfloat16)
        .reshape(local_sequences, SEQUENCE_LENGTH, KEY_VALUE_HEADS, HEAD_DIM)
    )
    scores = score_table(query_rows, key_row_block, mask_tab)
    row_peak = jnp.max(scores, -1, keepdims=True)
    logsum = row_peak + jnp.log(jnp.sum(jnp.exp(scores - row_peak), -1, keepdims=True))
    weights = jnp.exp(scores - logsum).astype(jnp.bfloat16)
    attended = product("shgqk,skhw->sqhgw", weights, value_row_block).astype(jnp.bfloat16)
    hidden = residual + matrix_multiply(
        attended.reshape(token_rows, QUERY_HEADS * HEAD_DIM), out_mat
    )
    saved = (
        normed,
        factor,
        attention_input,
        query_rows,
        key_row_block,
        value_row_block,
        attended,
        logsum,
        mask_tab,
        cosine_table,
        sine_table,
    )
    return (hidden, saved)


def mixer_backward(grad_hidden, saved, gain_vec, query_mat, key_matrix, value_matrix, out_mat):
    (
        normed,
        factor,
        attention_input,
        query_rows,
        key_row_block,
        value_row_block,
        attended,
        logsum,
        mask_tab,
        cosine_table,
        sine_table,
    ) = saved
    token_rows = grad_hidden.shape[0]
    local_sequences = token_rows // SEQUENCE_LENGTH
    grad_round = grad_hidden.astype(jnp.bfloat16)
    out_grad = matrix_multiply(attended.reshape(token_rows, QUERY_HEADS * HEAD_DIM).T, grad_round)
    grad_attended = (
        matrix_multiply(grad_round, out_mat.T).astype(jnp.bfloat16).reshape(query_rows.shape)
    )
    scores = score_table(query_rows, key_row_block, mask_tab)
    prob_full = jnp.exp(scores - logsum)
    values_gradient = product("shgqk,sqhgw->skhw", prob_full.astype(jnp.bfloat16), grad_attended)
    grad_weights = product("sqhgw,skhw->shgqk", grad_attended, value_row_block)
    row_delta = product("sqhgw,sqhgw->shgq", grad_attended, attended)[..., None]
    grad_scores = (prob_full * (grad_weights - row_delta) * SCORE_SCALE).astype(jnp.bfloat16)
    grad_queries = product("shgqk,skhw->sqhgw", grad_scores, key_row_block)
    keys_gradient = product("shgqk,sqhgw->skhw", grad_scores, query_rows)
    query_grad = inverse_rotary(
        grad_queries.reshape(local_sequences, SEQUENCE_LENGTH, QUERY_HEADS, HEAD_DIM),
        cosine_table,
        sine_table,
    )
    query_grad = query_grad.astype(jnp.bfloat16).reshape(token_rows, QUERY_HEADS * HEAD_DIM)
    key_gradient = (
        inverse_rotary(keys_gradient, cosine_table, sine_table)
        .astype(jnp.bfloat16)
        .reshape(token_rows, KEY_VALUE_HEADS * HEAD_DIM)
    )
    value_gradient = values_gradient.astype(jnp.bfloat16).reshape(
        token_rows, KEY_VALUE_HEADS * HEAD_DIM
    )
    query_wgrad = matrix_multiply(attention_input.T, query_grad)
    key_wgrad = matrix_multiply(attention_input.T, key_gradient)
    value_wgrad = matrix_multiply(attention_input.T, value_gradient)
    grad_attn_input = (
        matrix_multiply(query_grad, query_mat.T)
        + matrix_multiply(key_gradient, key_matrix.T)
        + matrix_multiply(value_gradient, value_matrix.T)
    )
    grad_normed, gain_grad = normalize_back(grad_attn_input, normed, factor, gain_vec)
    return (grad_hidden + grad_normed, gain_grad, query_wgrad, key_wgrad, value_wgrad, out_grad)


def route_weights(expert_input, router_mat, routes):
    logits = matrix_multiply(expert_input, router_mat)
    chosen_hot = (
        routes[:, :, None] == jnp.arange(router_mat.shape[1], dtype=jnp.int32)[None, None, :]
    ).astype(jnp.float32)
    chosen = jnp.sum(chosen_hot * logits[:, None, :], -1)
    return (jax.nn.softmax(chosen, -1), chosen_hot)


def route_back(route_prob, grad_prob, chosen_hot):
    grad_chosen = route_prob * (grad_prob - jnp.sum(route_prob * grad_prob, -1, keepdims=True))
    return jnp.sum(chosen_hot * grad_chosen[:, :, None], 1).astype(jnp.bfloat16)


def expert_forward(owner_rows, gate_mat, up_mat, down_mat):
    gate_pre = product("erd,edf->erf", owner_rows, gate_mat)
    up_pre = product("erd,edf->erf", owner_rows, up_mat)
    gate_sig = jax.nn.sigmoid(gate_pre)
    gate_act = gate_pre * gate_sig
    inner_acts = (gate_act * up_pre).astype(jnp.bfloat16)
    expert_out = product("erf,efd->erd", inner_acts, down_mat).astype(jnp.bfloat16)
    return (expert_out, (gate_pre, up_pre, gate_sig, gate_act, inner_acts))


def expert_backward(grad_rows, owner_rows, kept_acts, gate_mat, up_mat, down_mat):
    gate_pre, up_pre, gate_sig, gate_act, inner_acts = kept_acts
    grad_inner = product("erd,efd->erf", grad_rows, down_mat)
    down_grad = product("erf,erd->efd", inner_acts, grad_rows)
    silu_slope = gate_sig * (1.0 + gate_pre * (1.0 - gate_sig))
    grad_gate = (grad_inner * up_pre * silu_slope).astype(jnp.bfloat16)
    grad_up = (grad_inner * gate_act).astype(jnp.bfloat16)
    gate_grad = product("erd,erf->edf", owner_rows, grad_gate)
    up_grad = product("erd,erf->edf", owner_rows, grad_up)
    grad_owner_rows = product("erf,edf->erd", grad_gate, gate_mat) + product(
        "erf,edf->erd", grad_up, up_mat
    )
    return (grad_owner_rows.astype(jnp.bfloat16), gate_grad, up_grad, down_grad)


def gather_dp(local_part):
    dp_count = lax.axis_size("dp")
    owner_count = lax.axis_size("expert")
    if dp_count != 2 or owner_count % 2:
        return lax.all_gather(local_part, "dp", axis=0, tiled=True)
    low, high = jnp.split(local_part, 2, 0)
    even = lax.axis_index("expert") % 2 == 0
    near = lax.ppermute(jnp.where(even, low, high), "dp", [(0, 1), (1, 0)])
    far = lax.ppermute(near, "expert", [(i, i ^ 1) for i in range(owner_count)])
    other = jnp.concatenate([jnp.where(even, near, far), jnp.where(even, far, near)], 0)
    first = lax.axis_index("dp") == 0
    return jnp.concatenate(
        [jnp.where(first, local_part, other), jnp.where(first, other, local_part)], 0
    )


def all_sums(partial):
    owner_count = lax.axis_size("expert")
    dp_count = lax.axis_size("dp")
    width = partial.shape[1]
    pieces = partial.astype(jnp.bfloat16).reshape(dp_count, owner_count, -1, width)
    piece = lax.psum_scatter(
        pieces.transpose(1, 0, 2, 3).reshape(-1, width), "expert", scatter_dimension=0, tiled=True
    )
    piece = scatter_dp(piece, 0).astype(jnp.bfloat16)
    return lax.all_gather(piece, "expert", axis=0, tiled=True).astype(jnp.float32)


def scatter_dp(partial, axis):
    dp_count = lax.axis_size("dp")
    rounded = partial.astype(jnp.bfloat16)
    if dp_count != 2:
        return lax.psum_scatter(rounded, "dp", scatter_dimension=axis, tiled=True).astype(
            jnp.float32
        )
    low, high = jnp.split(rounded, 2, axis)
    first = lax.axis_index("dp") == 0
    arrived = lax.ppermute(jnp.where(first, high, low), "dp", [(0, 1), (1, 0)])
    return jnp.where(first, low, high).astype(jnp.float32) + arrived.astype(jnp.float32)


def shards(
    tokens,
    segments,
    routes,
    first_gain,
    query_weight,
    key_projection_weight,
    value_projection_weight,
    out_weight,
    second_gain,
    router_weight,
    gate_weight,
    up_weight,
    down_weight,
    cotangent,
):
    token_rows, model_width = tokens.shape
    top_count = routes.shape[1]
    expert_count = router_weight.shape[1]
    owner_count = lax.axis_size("expert")
    local_count = gate_weight.shape[0]
    key_width = key_projection_weight.shape[1]
    query_width = query_weight.shape[1]
    capacity = 5 * token_rows * top_count // (4 * expert_count)
    row_part = router_weight.shape[0]

    small = jnp.concatenate(
        [router_weight, first_gain[:, None], second_gain[:, None]], 1
    )
    small_mat = gather_dp(small)
    router_mat = small_mat[:, :expert_count]
    gain_first = small_mat[:, expert_count]
    gain_second = small_mat[:, expert_count + 1]
    joined_mat = gather_dp(
        jnp.concatenate([query_weight, key_projection_weight, value_projection_weight], 1)
    )
    query_mat = joined_mat[:, :query_width]
    key_matrix = joined_mat[:, query_width : query_width + key_width]
    value_matrix = joined_mat[:, query_width + key_width :]
    out_mat = gather_dp(out_weight)

    routes_all = lax.all_gather(routes, "expert")
    cotangent_all = lax.all_gather(cotangent, "expert")

    mine = lax.axis_index("expert") * local_count + jnp.arange(local_count, dtype=jnp.int32)
    hit = jnp.any(routes_all[None] == mine[:, None, None, None], -1)
    before = (
        jnp.arange(token_rows)[:, None] < jnp.arange(token_rows)[None, :]
    ).astype(jnp.bfloat16)
    rank = product("lst,tu->lsu", hit.astype(jnp.bfloat16), before).astype(jnp.int32)
    slot = jnp.where(hit, rank, -1)
    picked = slot[:, :, None, :] == jnp.arange(capacity, dtype=jnp.int32)[None, None, :, None]
    pick = picked.astype(jnp.bfloat16)

    def rows_of(gathered):
        rows = product("lsct,std->lscd", pick, gathered)
        return rows.reshape(local_count, owner_count * capacity, model_width)

    own_hot = (routes[:, :, None] == jnp.arange(expert_count, dtype=jnp.int32)).any(1)
    own_rank = matrix_multiply(before.T, own_hot.astype(jnp.bfloat16)).astype(jnp.int32)
    own_slot = jnp.where(own_hot, own_rank, -1)
    own_pick = (
        own_slot[:, :, None] == jnp.arange(capacity, dtype=jnp.int32)[None, None, :]
    ).astype(jnp.bfloat16)

    def send_back(rows):
        shaped = rows.reshape(local_count, owner_count, capacity, model_width)
        return lax.all_to_all(
            shaped.transpose(1, 0, 2, 3).reshape(expert_count, capacity, model_width),
            "expert",
            split_axis=0,
            concat_axis=0,
            tiled=True,
        )

    def sum_back(returned):
        flat = returned.reshape(expert_count * capacity, model_width)
        return matrix_multiply(own_pick.reshape(token_rows, expert_count * capacity), flat)

    hidden, saved = mixer_forward(
        tokens, segments, gain_first, query_mat, key_matrix, value_matrix, out_mat
    )
    normed_second, factor_second, expert_input = normalize(hidden, gain_second)
    input_all = lax.all_gather(expert_input, "expert")
    route_prob, chosen_hot = route_weights(expert_input, router_mat, routes)
    dense_prob = jnp.sum(chosen_hot * route_prob[:, :, None], 1)
    prob_all = lax.all_gather(dense_prob, "expert")

    column = jnp.arange(expert_count, dtype=jnp.int32)
    my_column = (mine[:, None] == column[None, :]).astype(jnp.float32)
    my_prob = jnp.sum(prob_all[None] * my_column[:, None, None, :], -1)
    row_prob = jnp.sum(jnp.where(picked, my_prob[:, :, None, :], 0.0), -1).reshape(
        local_count, owner_count * capacity, 1
    )

    owner_rows = rows_of(input_all).astype(jnp.bfloat16)
    cotangent_rows = rows_of(cotangent_all).astype(jnp.bfloat16).astype(jnp.float32)
    expert_out, kept_acts = expert_forward(owner_rows, gate_weight, up_weight, down_weight)
    expert_out = expert_out.astype(jnp.float32)
    weighted = (row_prob * expert_out).astype(jnp.bfloat16)
    row_grad_prob = jnp.sum(expert_out * cotangent_rows, -1).reshape(
        local_count, owner_count, capacity
    )
    token_grad_prob = jnp.sum(jnp.where(picked, row_grad_prob[..., None], 0.0), 2)
    back_prob = lax.all_to_all(
        token_grad_prob.transpose(1, 0, 2).reshape(expert_count, token_rows),
        "expert",
        split_axis=0,
        concat_axis=0,
        tiled=True,
    )
    grad_prob = jnp.sum(chosen_hot * back_prob.T[:, None, :], -1)
    grad_output = cotangent.astype(jnp.float32)

    grad_rows = (row_prob * cotangent_rows).astype(jnp.bfloat16)
    grad_owner_rows, gate_grad, up_grad, down_grad = expert_backward(
        grad_rows, owner_rows, kept_acts, gate_weight, up_weight, down_weight
    )
    grad_back = send_back(grad_owner_rows)
    expert_shares = (
        scatter_dp(gate_grad, 1),
        scatter_dp(up_grad, 1),
        scatter_dp(down_grad, 2),
    )
    grad_back, expert_shares, weighted = lax.optimization_barrier(
        (grad_back, expert_shares, weighted)
    )
    forward_back = send_back(weighted)
    output = (hidden + sum_back(forward_back)).astype(jnp.bfloat16)
    backward_sum = sum_back(grad_back)
    router_grad = route_back(route_prob, grad_prob, chosen_hot)
    grad_expert_input = backward_sum + matrix_multiply(
        router_grad, router_mat.T
    )
    router_wgrad = matrix_multiply(router_grad.T, expert_input)
    grad_normed, second_gain_grad = normalize_back(
        grad_expert_input, normed_second, factor_second, gain_second
    )
    grad_hidden = grad_output + grad_normed
    grad_tokens, first_gain_grad, query_wgrad, key_wgrad, value_wgrad, out_wgrad = mixer_backward(
        grad_hidden, saved, gain_first, query_mat, key_matrix, value_matrix, out_mat
    )

    out_share = all_sums(out_wgrad)
    joined = all_sums(jnp.concatenate([query_wgrad, key_wgrad, value_wgrad], 1))
    query_share = joined[:, :query_width]
    key_share = joined[:, query_width : query_width + key_width]
    value_share = joined[:, query_width + key_width :]
    extras = jnp.concatenate(
        [router_wgrad, first_gain_grad[None, :], second_gain_grad[None, :]], 0
    )
    extras = lax.psum(extras.astype(jnp.bfloat16), ("dp", "expert"))
    extras = lax.dynamic_slice_in_dim(
        extras, lax.axis_index("dp") * row_part, row_part, 1
    ).astype(jnp.float32)
    router_share = extras[:expert_count].T
    first_share = extras[expert_count]
    second_share = extras[expert_count + 1]
    return (
        output,
        grad_tokens,
        first_share,
        query_share,
        key_share,
        value_share,
        out_share,
        second_share,
        router_share,
        expert_shares[0],
        expert_shares[1],
        expert_shares[2],
    )


def turn(values, axis):
    if lax.axis_size("dp") != 2:
        return values
    low, high = jnp.split(values, 2, axis)
    first = lax.axis_index("dp") == 0
    return jnp.concatenate([jnp.where(first, low, high), jnp.where(first, high, low)], axis)


def times(left_op, pieces):
    total, start = None, 0
    for piece in pieces:
        part = matrix_multiply(left_op[:, start : start + piece.shape[0]], piece)
        total = part if total is None else total + part
        start += piece.shape[0]
    return total


def times_back(left_op, pieces):
    return jnp.concatenate([matrix_multiply(left_op, piece.T) for piece in pieces], 1)


def halves_forward(tokens, segments, gain_vec, query_mat, key_matrix, value_matrix, out_mat):
    token_rows = tokens.shape[0]
    local_sequences = token_rows // SEQUENCE_LENGTH
    query_groups = QUERY_HEADS // KEY_VALUE_HEADS
    cosine_table, sine_table = rope_tables(SEQUENCE_LENGTH, HEAD_DIM)
    mask_tab = segment_mask(segments.reshape(local_sequences, SEQUENCE_LENGTH))
    residual = tokens.astype(jnp.float32)
    normed, factor, attention_input = normalize(turn(residual, 1), gain_vec)
    query_rows = apply_rotary(
        times(attention_input, query_mat).reshape(
            local_sequences, SEQUENCE_LENGTH, QUERY_HEADS, HEAD_DIM
        ),
        cosine_table,
        sine_table,
    )
    query_rows = query_rows.astype(jnp.bfloat16).reshape(
        local_sequences, SEQUENCE_LENGTH, KEY_VALUE_HEADS, query_groups, HEAD_DIM
    )
    key_row_block = apply_rotary(
        times(attention_input, key_matrix).reshape(
            local_sequences, SEQUENCE_LENGTH, KEY_VALUE_HEADS, HEAD_DIM
        ),
        cosine_table,
        sine_table,
    ).astype(jnp.bfloat16)
    value_row_block = (
        times(attention_input, value_matrix)
        .astype(jnp.bfloat16)
        .reshape(local_sequences, SEQUENCE_LENGTH, KEY_VALUE_HEADS, HEAD_DIM)
    )
    scores = score_table(query_rows, key_row_block, mask_tab)
    row_peak = jnp.max(scores, -1, keepdims=True)
    logsum = row_peak + jnp.log(jnp.sum(jnp.exp(scores - row_peak), -1, keepdims=True))
    weights = jnp.exp(scores - logsum).astype(jnp.bfloat16)
    attended = product("shgqk,skhw->sqhgw", weights, value_row_block).astype(jnp.bfloat16)
    turned = turn(attended.reshape(token_rows, QUERY_HEADS * HEAD_DIM), 1)
    hidden = residual + times(turned, out_mat)
    saved = (
        normed,
        factor,
        attention_input,
        query_rows,
        key_row_block,
        value_row_block,
        attended,
        turned,
        logsum,
        mask_tab,
        cosine_table,
        sine_table,
    )
    return (hidden, saved)


def halves_backward(grad_hidden, saved, gain_vec, query_mat, key_matrix, value_matrix, out_mat):
    (
        normed,
        factor,
        attention_input,
        query_rows,
        key_row_block,
        value_row_block,
        attended,
        _,
        logsum,
        mask_tab,
        cosine_table,
        sine_table,
    ) = saved
    token_rows = grad_hidden.shape[0]
    local_sequences = token_rows // SEQUENCE_LENGTH
    grad_round = grad_hidden.astype(jnp.bfloat16)
    grad_attended = (
        turn(times_back(grad_round, out_mat).astype(jnp.bfloat16), 1).reshape(query_rows.shape)
    )
    scores = score_table(query_rows, key_row_block, mask_tab)
    prob_full = jnp.exp(scores - logsum)
    values_gradient = product("shgqk,sqhgw->skhw", prob_full.astype(jnp.bfloat16), grad_attended)
    grad_weights = product("sqhgw,skhw->shgqk", grad_attended, value_row_block)
    row_delta = product("sqhgw,sqhgw->shgq", grad_attended, attended)[..., None]
    grad_scores = (prob_full * (grad_weights - row_delta) * SCORE_SCALE).astype(jnp.bfloat16)
    grad_queries = product("shgqk,skhw->sqhgw", grad_scores, key_row_block)
    keys_gradient = product("shgqk,sqhgw->skhw", grad_scores, query_rows)
    query_grad = inverse_rotary(
        grad_queries.reshape(local_sequences, SEQUENCE_LENGTH, QUERY_HEADS, HEAD_DIM),
        cosine_table,
        sine_table,
    )
    query_grad = query_grad.astype(jnp.bfloat16).reshape(token_rows, QUERY_HEADS * HEAD_DIM)
    key_gradient = (
        inverse_rotary(keys_gradient, cosine_table, sine_table)
        .astype(jnp.bfloat16)
        .reshape(token_rows, KEY_VALUE_HEADS * HEAD_DIM)
    )
    value_gradient = values_gradient.astype(jnp.bfloat16).reshape(
        token_rows, KEY_VALUE_HEADS * HEAD_DIM
    )
    grad_attn_input = (
        times_back(query_grad, query_mat)
        + times_back(key_gradient, key_matrix)
        + times_back(value_gradient, value_matrix)
    )
    grad_normed, gain_grad = normalize_back(grad_attn_input, normed, factor, gain_vec)
    return (
        grad_hidden + turn(grad_normed, 1),
        turn(gain_grad, 0),
        [query_grad, key_gradient, value_gradient, grad_round],
    )


MESH = pl.DeviceIdType.MESH


def quotient(index, by):
    return index // by if isinstance(index, int) else lax.div(index, jnp.int32(by))


def parity(index):
    return index % 2 if isinstance(index, int) else lax.rem(index, jnp.int32(2))


def flip(index, by):
    if isinstance(index, int) and isinstance(by, int):
        return index ^ by
    if isinstance(index, int):
        index, by = by, index
    total, weight = (index, 1) if isinstance(by, int) else (0, 1)
    for _ in range(6):
        if isinstance(by, int):
            if by & weight:
                total = total + weight - 2 * weight * parity(quotient(index, weight))
        else:
            one, two = parity(quotient(index, weight)), parity(quotient(by, weight))
            total = total + weight * (one + two - 2 * one * two)
        weight *= 2
    return total


def others(count, act):
    for by in range(1, count):
        act(by)


def expert_at(index):
    return {"expert": index}


def send(src, dst, send_sem, recv_sem, where):
    return pltpu.make_async_remote_copy(
        src_ref=src,
        dst_ref=dst,
        send_sem=send_sem,
        recv_sem=recv_sem,
        device_id=where,
        device_id_type=MESH,
    )


def meet(count, with_dp):
    barrier = pltpu.get_barrier_semaphore()
    me = lax.axis_index("expert")

    def greet(by):
        pl.semaphore_signal(
            barrier, inc=1, device_id=expert_at(flip(me, by)), device_id_type=MESH
        )

    others(count, greet)
    if with_dp:
        pl.semaphore_signal(
            barrier, inc=1, device_id={"dp": 1 - lax.axis_index("dp")}, device_id_type=MESH
        )
    pl.semaphore_wait(barrier, count - 1 + (1 if with_dp else 0))


class Gather:
    def __init__(self, own, block_of, count, send_sems, recv_sems):
        self.own, self.block_of, self.count = own, block_of, count
        self.send_sems, self.recv_sems = send_sems, recv_sems
        self.me = lax.axis_index("expert")

    def copy(self, rel, by, src=None):
        block = self.block_of(flip(self.me, rel))
        there = flip(rel, by)
        return send(
            block if src is None else src,
            block,
            self.send_sems.at[there],
            self.recv_sems.at[there],
            expert_at(flip(self.me, by)),
        )

    def wait(self, rel):
        block = self.block_of(flip(self.me, rel))
        send(
            block, block, self.send_sems.at[rel], self.recv_sems.at[rel], expert_at(self.me)
        ).wait_recv()

    def begin(self, held=()):
        for by in list(range(8, self.count, 4)) + [4, 2, 1]:
            if by < self.count and by not in held:
                self.copy(0, by, self.own).start()

    def release(self, by):
        self.copy(0, by, self.own).start()

    def pass_z(self, rel):
        self.wait(rel)
        self.copy(rel, 2).start()
        self.copy(rel, 1).start()

    def pass_x(self, rel):
        self.wait(rel + 2)
        self.copy(rel + 2, 1).start()

    def wait_sends(self):
        for rel in range(1, self.count):
            block = self.block_of(flip(self.me, rel))
            send(
                block, block, self.send_sems.at[rel], self.recv_sems.at[rel], expert_at(self.me)
            ).wait_send()

    def rest(self):
        far = list(range(12, self.count, 4))
        near = [rel for rel in (8, 4) if rel < self.count]
        self.pass_x(0)
        self.pass_z(near[0])
        for by in far:
            self.release(by)
        for rel in near[1:]:
            self.pass_z(rel)
        for rel in near:
            self.pass_x(rel)
        for rel in far:
            self.pass_z(rel)
            self.pass_x(rel)
        for rel in range(1, self.count, 2):
            self.wait(rel)
        self.wait_sends()


def front_kernel(pieces, *refs):
    mine, refs = refs[:pieces], refs[pieces:]
    fetched, refs = refs[:pieces], refs[pieces:]
    y_send, y_recv, c_send, c_recv = refs
    me, dp = lax.axis_index("expert"), lax.axis_index("dp")
    core = parity(me)
    meet(2, True)

    def part(ref, which):
        half = ref.shape[0] // 2
        return ref.at[pl.ds(pl.multiple_of(which * half, half), half)]

    over_y = [
        send(
            part(mine[i], core),
            part(fetched[i], core),
            y_send.at[i],
            y_recv.at[i],
            {"dp": 1 - dp},
        )
        for i in range(pieces)
    ]
    for copy in over_y:
        copy.start()
    over_core = [
        send(
            part(fetched[i], core),
            part(fetched[i], core),
            c_send.at[i],
            c_recv.at[i],
            expert_at(flip(me, 1)),
        )
        for i in range(pieces)
    ]
    for i in range(pieces):
        over_y[i].wait_recv()
        over_core[i].start()
    for i in range(pieces):
        send(
            part(mine[i], 1 - core),
            part(fetched[i], 1 - core),
            c_send.at[i],
            c_recv.at[i],
            expert_at(flip(me, 1)),
        ).wait_recv()
        over_core[i].wait_send()
        over_y[i].wait_send()


def front(own):
    pieces = len(own)
    anywhere = pl.BlockSpec(memory_space=pl.ANY)
    return pl.pallas_call(
        functools.partial(front_kernel, pieces),
        out_shape=[jax.ShapeDtypeStruct(part.shape, part.dtype) for part in own],
        in_specs=[anywhere] * pieces,
        out_specs=[anywhere] * pieces,
        scratch_shapes=[pltpu.SemaphoreType.DMA((pieces,)) for _ in range(4)],
        compiler_params=pltpu.CompilerParams(collective_id=0, has_side_effects=True),
        name="front",
    )(*own)


def finish_kernel(heights, away, *refs):
    all_ref, mine, mine_down, peer, peer_down, hidden, mixture = refs[:7]
    pieces, refs = refs[7], refs[8:]
    shares, refs = refs[: len(heights)], refs[len(heights) :]
    gate_out, up_out, down_out, output = refs
    start = 0
    for height, out in zip(heights, shares):
        for index in range(0, all_ref.shape[0], 128 // height):
            block = all_ref[index : index + 128 // height, start : start + height, :]
            block = block.astype(jnp.float32).reshape(128, block.shape[2])
            out[:, index * height : index * height + 128] = block.T
        start += height
    gate_out[0] = mine[0] + peer[0].astype(jnp.float32)
    up_out[0] = mine[1] + peer[1].astype(jnp.float32)
    down_out[0] = mine_down[...] + peer_down[...].astype(jnp.float32)
    total = hidden[...] + mixture[...]
    for index in range(away):
        total = total + pieces[index].astype(jnp.float32)
    output[...] = total.astype(jnp.bfloat16)


def finish(everything, heights, mine, mine_down, peer, peer_down, hidden, mixture, pieces):
    count, lines, half = everything.shape
    parts = 4
    rows, width = hidden.shape
    deep = mine.shape[2]
    tile, low, some = half // parts, deep // parts, rows // parts
    three = pl.BlockSpec((2, tile, deep), lambda i: (0, i, 0))
    down = pl.BlockSpec((low, half), lambda i: (i, 0))
    tokens = pl.BlockSpec((some, width), lambda i: (i, 0))
    f32 = jnp.float32
    results = pl.pallas_call(
        functools.partial(finish_kernel, heights, pieces.shape[0]),
        grid=(parts,),
        out_shape=[jax.ShapeDtypeStruct((half, count * height), f32) for height in heights]
        + [
            jax.ShapeDtypeStruct((1, half, deep), f32),
            jax.ShapeDtypeStruct((1, half, deep), f32),
            jax.ShapeDtypeStruct((1, deep, half), f32),
            jax.ShapeDtypeStruct((rows, width), jnp.bfloat16),
        ],
        in_specs=[pl.BlockSpec((count, lines, tile), lambda i: (0, 0, i))]
        + [three, down, three, down, tokens, tokens]
        + [pl.BlockSpec((pieces.shape[0], some, width), lambda i: (0, i, 0))],
        out_specs=[pl.BlockSpec((tile, count * height), lambda i: (i, 0)) for height in heights]
        + [
            pl.BlockSpec((1, tile, deep), lambda i: (0, i, 0)),
            pl.BlockSpec((1, tile, deep), lambda i: (0, i, 0)),
            pl.BlockSpec((1, low, half), lambda i: (0, i, 0)),
            tokens,
        ],
        compiler_params=pltpu.CompilerParams(vmem_limit_bytes=58 * 2**20),
        name="finish",
    )(everything, mine, mine_down, peer, peer_down, hidden, mixture, pieces)
    return results[: len(heights)], results[len(heights) :]


def dot_on(left_op, right_op, left_axis, right_axis):
    return lax.dot_general(
        left_op,
        right_op,
        (((left_axis,), (right_axis,)), ((), ())),
        preferred_element_type=jnp.float32,
    )


def experts_kernel(
    count,
    own_ref,
    cot_ref,
    prob_ref,
    gate_ref,
    up_ref,
    down_ref,
    grad_out,
    mix_out,
    mix_away,
    gp_out,
    mine_out,
    mine_down,
    peer_out,
    peer_down,
    x_all,
    prob_all,
    gp_send_buf,
    both_all,
    inner_all,
    ge_all,
    part,
    cbuf,
    xbuf,
    zbuf,
    a_send,
    a_recv,
    p_send,
    p_recv,
    q_send,
    q_recv,
    c_send,
    c_recv,
    x_send,
    x_recv,
    z_send,
    z_recv,
):
    rows, width = own_ref.shape
    hidden = gate_ref.shape[2]
    pair = 2 * rows
    steps = count // 2
    depth = count // 4
    order = [0] + [z for z in (2, 1) if z < depth] + list(range(3, depth))
    me, dp = lax.axis_index("expert"), lax.axis_index("dp")
    core = parity(me)
    meet(count, False)

    def block_of(index):
        return x_all.at[pl.ds(pl.multiple_of(index * rows, rows), rows)]

    gather = Gather(own_ref, block_of, count, a_send, a_recv)
    gather.begin(range(12, count, 4))

    def prob_copy(by):
        there = flip(me, by)
        return send(
            prob_ref.at[there], prob_all.at[me], p_send.at[by], p_recv.at[by], expert_at(there)
        )

    def prob_start(by):
        prob_copy(by).start()

    others(count, prob_start)
    x_all[pl.ds(pl.multiple_of(me * rows, rows), rows)] = own_ref[...]
    prob_all[me] = prob_ref[me]

    def prob_wait(by):
        there = flip(me, by)
        send(
            prob_ref.at[me], prob_all.at[there], p_send.at[by], p_recv.at[by], expert_at(there)
        ).wait_recv()

    others(count, prob_wait)

    def rel_of(step):
        z_rel = quotient(step, 2)
        x_rel = jnp.where(step < 2, parity(step), 1 - parity(step))
        z_rel = sum(jnp.where(z_rel == at, z, 0) for at, z in enumerate(order))
        return 4 * z_rel + 2 * x_rel, z_rel

    eye = (
        lax.broadcasted_iota(jnp.int32, (pair, pair), 0)
        == lax.broadcasted_iota(jnp.int32, (pair, pair), 1)
    )
    theirs = pl.ds(pl.multiple_of((1 - core) * rows, rows), rows)
    ours = pl.ds(pl.multiple_of(core * rows, rows), rows)

    def core_copy(step):
        return send(
            part.at[step, :, theirs],
            cbuf.at[step],
            c_send.at[step],
            c_recv.at[step],
            expert_at(flip(me, 1)),
        )

    def x_copy(step, z_rel, which):
        return send(
            part.at[step, which, ours],
            xbuf.at[z_rel, which],
            x_send.at[which, z_rel],
            x_recv.at[which, z_rel],
            expert_at(flip(me, 2)),
        )

    def z_copy(step, z_rel):
        return send(
            part.at[step, 0, ours],
            zbuf.at[z_rel],
            z_send.at[z_rel],
            z_recv.at[z_rel],
            expert_at(flip(me, 4 * z_rel)),
        )

    def compute(step):
        rel, _ = rel_of(step)
        chip = quotient(flip(me, rel), 2)
        where = pl.ds(pl.multiple_of(chip * pair, pair), pair)
        x = x_all[where, :]
        gate_pre = dot_on(x, gate_ref[0], 1, 0)
        up_pre = dot_on(x, up_ref[0], 1, 0)
        sig = jax.nn.sigmoid(gate_pre)
        act = gate_pre * sig
        inner = (act * up_pre).astype(jnp.bfloat16)
        inner_all[where, :] = inner
        out = dot_on(inner, down_ref[0], 1, 0).astype(jnp.bfloat16).astype(jnp.float32)
        prob_row = jnp.concatenate(
            [prob_all[2 * chip, 0:1, :], prob_all[2 * chip + 1, 0:1, :]], 1
        )
        prob = jnp.sum(jnp.where(eye, prob_row, 0.0), 1, keepdims=True)
        cot = cot_ref[where, :].astype(jnp.float32)
        part[step, 1] = (prob * out).astype(jnp.bfloat16)
        gp = jnp.sum(out * cot, 1, keepdims=True)
        gp_row = jnp.sum(jnp.where(eye, gp, 0.0), 0, keepdims=True)
        gp_send_buf[2 * chip] = jnp.broadcast_to(gp_row[:, :rows], (8, rows))
        gp_send_buf[2 * chip + 1] = jnp.broadcast_to(gp_row[:, rows:], (8, rows))
        ge = (prob * cot).astype(jnp.bfloat16)
        ge_all[where, :] = ge
        gi = dot_on(ge, down_ref[0], 1, 1)
        slope = sig * (1.0 + gate_pre * (1.0 - sig))
        gg = (gi * up_pre * slope).astype(jnp.bfloat16)
        gu = (gi * act).astype(jnp.bfloat16)
        both_all[where, :hidden] = gg
        both_all[where, hidden:] = gu
        part[step, 0] = (dot_on(gg, gate_ref[0], 1, 1) + dot_on(gu, up_ref[0], 1, 1)).astype(
            jnp.bfloat16
        )

    def add_core(step):
        core_copy(step).wait_recv()
        total = part[step, :, ours].astype(jnp.float32) + cbuf[step].astype(jnp.float32)
        part[step, :, ours] = total.astype(jnp.bfloat16)

    def add_x(at):
        z_rel, step = order[at], 2 * at + 1
        x_copy(step, z_rel, 0).wait_recv()
        total = part[step, 0, ours].astype(jnp.float32) + xbuf[z_rel, 0].astype(jnp.float32)
        part[step, 0, ours] = total.astype(jnp.bfloat16)
        z_copy(step, z_rel).start()

    def on(step, number):
        return pl.when(step == number)

    def turn_of(step, carry):
        rel, _ = rel_of(step)

        for at in range(1, depth):

            @on(step, 2 * at)
            def _(at=at):
                if at == 1:
                    gather.pass_x(4 * order[1])

        gather.wait(rel + 1)
        compute(step)
        core_copy(step).start()

        @on(step, 0)
        def _():
            gather.pass_x(0)

        @on(step, 1)
        def _():
            gather.pass_z(4 * order[1])
            for by in range(12, count, 4):
                gather.release(by)
            if depth > 2:
                gather.pass_z(4 * order[2])
            add_core(0)
            add_core(1)

        for at in range(1, depth):

            @on(step, 2 * at)
            def _(at=at):
                if at == 1:
                    x_copy(1, 0, 0).start()
                    x_copy(1, 0, 1).start()
                else:
                    add_core(2 * at - 1)
                    x_copy(2 * at - 2, order[at - 1], 1).start()
                if at > 1 and at + 1 < depth:
                    gather.pass_z(4 * order[at + 1])

            @on(step, 2 * at + 1)
            def _(at=at):
                add_core(2 * at)
                x_copy(2 * at, order[at], 0).start()
                if at + 1 < depth:
                    gather.pass_x(4 * order[at + 1])

        if depth > 3:

            @on(step, 6)
            def _():
                add_x(1)

        return carry

    lax.fori_loop(0, steps, turn_of, 0)
    add_core(steps - 1)
    x_copy(steps - 2, order[-1], 1).start()
    for at in range(2 if depth > 3 else 1, depth - 1):
        add_x(at)

    def gp_copy(by):
        there = flip(me, by)
        return send(
            gp_send_buf.at[there], gp_out.at[me], q_send.at[by], q_recv.at[by], expert_at(there)
        )

    def gp_start(by):
        gp_copy(by).start()

    others(count, gp_start)
    gp_out[me] = gp_send_buf[me]

    half = width // 2
    for turn_at, (which, target, lower) in enumerate( ((1 - dp, peer_out, peer_down), (dp, mine_out, mine_down))
    ):

        def rows_of(index, carry, which=which, target=target):
            tile = half // 2
            at = pl.multiple_of(which * half + index * tile, tile)
            into = pl.ds(pl.multiple_of(index * tile, tile), tile)
            x = x_all[:, pl.ds(at, tile)]
            both = dot_on(x, both_all[...], 0, 0).astype(target.dtype)
            target[0, into, :] = both[:, :hidden]
            target[1, into, :] = both[:, hidden:]
            return carry

        lax.fori_loop(0, 2, rows_of, 0)

        def down_of(index, carry, which=which, lower=lower):
            tile = hidden // 2
            at = pl.ds(pl.multiple_of(index * tile, tile), tile)
            grads = ge_all[:, pl.ds(pl.multiple_of(which * half, half), half)]
            lower[at, :] = dot_on(inner_all[:, at], grads, 0, 0).astype(lower.dtype)
            return carry

        lax.fori_loop(0, 2, down_of, 0)
        if turn_at == 0:
            add_x(depth - 1)

    def from_x(at, which):
        step = 2 * at + 1 if at else 0
        x_copy(step, order[at], which).wait_recv()
        return part[step, which, ours].astype(jnp.float32) + xbuf[order[at], which].astype(
            jnp.float32
        )

    for at in range(1, depth):
        mix_away[order[at] - 1] = from_x(at, 1).astype(jnp.bfloat16)
    mix_out[...] = from_x(0, 1)
    grads = from_x(0, 0)
    for z_rel in range(1, depth):
        z_copy(0, z_rel).wait_recv()
        grads = grads + zbuf[z_rel].astype(jnp.float32)
    grad_out[...] = grads

    def settle(by):
        there = flip(me, by)
        send(
            gp_send_buf.at[me], gp_out.at[there], q_send.at[by], q_recv.at[by], expert_at(there)
        ).wait()
        prob_copy(by).wait_send()

    others(count, settle)
    gather.wait_sends()
    for step in range(steps):
        core_copy(step).wait_send()
    for z_rel in range(depth):
        x_copy(0, z_rel, 0).wait_send()
        x_copy(0, z_rel, 1).wait_send()
    for z_rel in range(1, depth):
        z_copy(0, z_rel).wait_send()


def experts(expert_input, cotangent_all, prob, gate_weight, up_weight, down_weight):
    count = prob.shape[0]
    rows, width = expert_input.shape
    hidden = gate_weight.shape[2]
    total = count * rows
    steps, depth = count // 2, count // 4
    half = width // 2
    local = pl.BlockSpec(memory_space=pltpu.VMEM)
    shapes = ((count,), (count,), (count,), (steps,), (2, depth), (depth,))
    pairs = [pltpu.SemaphoreType.DMA(shape) for shape in shapes]
    semaphores = [item for item in pairs for _ in range(2)]
    bf16 = jnp.bfloat16
    return pl.pallas_call(
        functools.partial(experts_kernel, count),
        out_shape=[
            jax.ShapeDtypeStruct((rows, width), jnp.float32),
            jax.ShapeDtypeStruct((rows, width), jnp.float32),
            jax.ShapeDtypeStruct((depth - 1, rows, width), bf16),
            jax.ShapeDtypeStruct((count, 8, rows), jnp.float32),
            jax.ShapeDtypeStruct((2, half, hidden), jnp.float32),
            jax.ShapeDtypeStruct((hidden, half), jnp.float32),
            jax.ShapeDtypeStruct((2, half, hidden), bf16),
            jax.ShapeDtypeStruct((hidden, half), bf16),
        ],
        in_specs=[local] * 6,
        out_specs=[local] * 8,
        scratch_shapes=[
            pltpu.VMEM((total, width), bf16),
            pltpu.VMEM((count, 8, rows), jnp.float32),
            pltpu.VMEM((count, 8, rows), jnp.float32),
            pltpu.VMEM((total, 2 * hidden), bf16),
            pltpu.VMEM((total, hidden), bf16),
            pltpu.VMEM((total, width), bf16),
            pltpu.VMEM((steps, 2, 2 * rows, width), bf16),
            pltpu.VMEM((steps, 2, rows, width), bf16),
            pltpu.VMEM((depth, 2, rows, width), bf16),
            pltpu.VMEM((depth, rows, width), bf16),
        ]
        + semaphores,
        compiler_params=pltpu.CompilerParams(
            collective_id=1, has_side_effects=True, vmem_limit_bytes=58 * 2**20
        ),
        cost_estimate=pl.CostEstimate(
            flops=18 * total * width * hidden, bytes_accessed=20 * total * width, transcendentals=0
        ),
        name="experts",
    )(expert_input, cotangent_all, prob, gate_weight, up_weight, down_weight)


def late_kernel(
    count,
    cuts,
    pay_ref,
    attention_ref,
    attended_ref,
    away_hbm,
    both_away,
    down_away,
    all_out,
    here_hbm,
    both_here,
    down_here,
    attention_all,
    attended_all,
    arrived,
    y_out,
    y_in,
    kept,
    z_in,
    mine,
    swap_send,
    swap_recv,
    m_send,
    m_recv,
    t_send,
    t_recv,
    d_send,
    d_recv,
    a_send,
    a_recv,
    y_send,
    y_recv,
    z_send,
    z_recv,
    g_send,
    g_recv,
):
    first, last = cuts
    depth, _, lines, rows = pay_ref.shape
    half = all_out.shape[2]
    me, dp = lax.axis_index("expert"), lax.axis_index("dp")
    place = me - 4 * quotient(me, 4)
    level = quotient(me, 4)
    peer = {"dp": 1 - dp}
    order = [z for z in (2, 3) if z < depth] + list(range(4, depth)) + [1, 0]
    meet(count, True)

    def at_place(ref):
        return lambda index: ref.at[
            pl.ds(pl.multiple_of((index - 4 * quotient(index, 4)) * rows, rows), rows)
        ]

    gathers = [
        Gather(attention_ref, at_place(attention_all), 4, t_send, t_recv),
        Gather(attended_ref, at_place(attended_all), 4, d_send, d_recv),
    ]
    columns = pl.ds(pl.multiple_of(place * rows, rows), rows)

    def share(by):
        there = flip(place, by)
        return send(
            pay_ref.at[:, there],
            arrived.at[:, :, columns],
            a_send.at[by],
            a_recv.at[by],
            expert_at(flip(me, by)),
        )

    swap_down = send(down_away, down_here, swap_send.at[0], swap_recv.at[0], peer)
    swap_both = send(both_away, both_here, swap_send.at[1], swap_recv.at[1], peer)

    def outputs_z(z_rel):
        return send(
            away_hbm.at[z_rel - 1],
            here_hbm.at[z_rel - 1],
            m_send.at[z_rel],
            m_recv.at[z_rel],
            expert_at(flip(me, 4 * z_rel)),
        )

    for gather in gathers:
        gather.begin()
    for by in (2, 3, 1):
        share(by).start()
    swap_down.start()
    for z_rel in range(1, depth):
        outputs_z(z_rel).start()
    attention_all[columns, :] = attention_ref[...]
    attended_all[columns, :] = attended_ref[...]
    arrived[:, :, columns] = pay_ref[:, place]
    for gather in gathers:
        gather.pass_x(0)
    for by in (2, 3, 1):
        there = flip(place, by)
        send(
            pay_ref.at[:, there],
            arrived.at[:, :, pl.ds(pl.multiple_of(there * rows, rows), rows)],
            a_send.at[by],
            a_recv.at[by],
            expert_at(flip(me, by)),
        ).wait()
    for gather in gathers:
        gather.wait(1)
        gather.wait(3)
        gather.wait_sends()

    blank = jnp.zeros((lines - last - (lines - last) // 2, half), jnp.float32)

    def tile_of(z_rel, side):
        at = flip(level, z_rel)
        where = slice(side * half, (side + 1) * half)
        extra = arrived[at, last:, :].astype(jnp.float32)
        summed = extra[:, :rows]
        for index in range(1, 4):
            summed = summed + extra[:, index * rows : (index + 1) * rows]
        edge = summed.shape[0] // 2
        summed = summed[side * edge : (side + 1) * edge]
        return jnp.concatenate(
            [
                dot_on(arrived[at, :first, :], attention_all[:, where], 1, 0),
                dot_on(arrived[at, first:last, :], attended_all[:, where], 1, 0),
                jnp.concatenate([summed, jnp.zeros((edge, half - rows), jnp.float32)], 1),
                blank,
            ],
            0,
        )

    def over_y(z_rel):
        return send(
            y_out.at[z_rel], y_in.at[z_rel], y_send.at[z_rel], y_recv.at[z_rel], peer
        )

    def over_z(z_rel):
        return send(
            y_out.at[z_rel],
            z_in.at[z_rel],
            z_send.at[z_rel],
            z_recv.at[z_rel],
            expert_at(flip(me, 4 * z_rel)),
        )

    for z_rel in order:
        y_out[z_rel] = tile_of(z_rel, 1).astype(jnp.bfloat16)
        over_y(z_rel).start()
    for z_rel in order:
        kept[z_rel] = tile_of(z_rel, 0)
    total = None
    for z_rel in order:
        over_y(z_rel).wait()
        total = kept[z_rel] + y_in[z_rel].astype(jnp.float32)
        if z_rel:
            y_out[z_rel] = total.astype(jnp.bfloat16)
            over_z(z_rel).start()
    swap_both.start()
    for z_rel in order[:-1]:
        over_z(z_rel).wait()
        total = total + z_in[z_rel].astype(jnp.float32)
    mine[...] = total.astype(jnp.bfloat16)
    gather = Gather(mine, lambda index: all_out.at[index], count, g_send, g_recv)
    gather.begin(range(12, count, 4))
    all_out[me] = mine[...]
    gather.rest()
    swap_down.wait()
    for z_rel in range(1, depth):
        outputs_z(z_rel).wait()
    swap_both.wait()


def late_sums(payload, attention, attended, away, both, down, cuts):
    count, lines, rows = payload.shape
    width = attention.shape[1]
    half, depth = width // 2, count // 4
    local = pl.BlockSpec(memory_space=pltpu.VMEM)
    anywhere = pl.BlockSpec(memory_space=pl.ANY)
    bf16 = jnp.bfloat16
    sizes = (2, depth, 4, 4, 4, depth, depth, count)
    return pl.pallas_call(
        functools.partial(late_kernel, count, cuts),
        out_shape=[
            jax.ShapeDtypeStruct((count, lines, half), bf16),
            jax.ShapeDtypeStruct(away.shape, bf16),
            jax.ShapeDtypeStruct(both.shape, bf16),
            jax.ShapeDtypeStruct(down.shape, bf16),
        ],
        in_specs=[local] * 3 + [anywhere] * 3,
        out_specs=[local] + [anywhere] * 3,
        scratch_shapes=[
            pltpu.VMEM((4 * rows, width), bf16),
            pltpu.VMEM((4 * rows, width), bf16),
            pltpu.VMEM((depth, lines, 4 * rows), bf16),
            pltpu.VMEM((depth, lines, half), bf16),
            pltpu.VMEM((depth, lines, half), bf16),
            pltpu.VMEM((depth, lines, half), jnp.float32),
            pltpu.VMEM((depth, lines, half), bf16),
            pltpu.VMEM((lines, half), bf16),
        ]
        + [pltpu.SemaphoreType.DMA((size,)) for size in sizes for _ in range(2)],
        compiler_params=pltpu.CompilerParams(
            collective_id=2, has_side_effects=True, vmem_limit_bytes=56 * 2**20
        ),
        name="late",
    )(payload.reshape(depth, 4, lines, rows), attention, attended, away, both, down)


def shards_together(
    tokens,
    segments,
    routes,
    first_gain,
    query_weight,
    key_projection_weight,
    value_projection_weight,
    out_weight,
    second_gain,
    router_weight,
    gate_weight,
    up_weight,
    down_weight,
    cotangent,
):
    token_rows = tokens.shape[0]
    expert_count = router_weight.shape[1]
    owner_count = lax.axis_size("expert")
    dp_count = lax.axis_size("dp")

    small = jnp.concatenate([router_weight, first_gain[:, None], second_gain[:, None]], 1)
    small = jnp.pad(small, ((0, 0), (0, -small.shape[1] % 128)))
    own = [query_weight, key_projection_weight, value_projection_weight, out_weight, small]
    cotangent_all = lax.all_gather(cotangent, "expert", axis=0, tiled=True)
    other = front(own)
    query_mat, key_matrix, value_matrix, out_mat, small = (list(p) for p in zip(own, other))
    small_mat = jnp.concatenate(small, 0)
    router_mat = turn(small_mat[:, :expert_count], 0)
    gain_first = small_mat[:, expert_count]
    gain_second = turn(small_mat[:, expert_count + 1], 0)

    hidden, saved = halves_forward(
        tokens, segments, gain_first, query_mat, key_matrix, value_matrix, out_mat
    )
    normed_second, factor_second, expert_input = normalize(hidden, gain_second)
    route_prob, chosen_hot = route_weights(expert_input, router_mat, routes)
    dense_prob = jnp.sum(chosen_hot * route_prob[:, :, None], 1)
    prob = jnp.broadcast_to(dense_prob.T[:, None, :], (owner_count, 8, token_rows))
    grad_sum, mixture, mix_away, back_prob, mine, mine_down, peer, peer_down = experts(
        expert_input, cotangent_all, prob, gate_weight, up_weight, down_weight
    )
    grad_prob = jnp.sum(chosen_hot * back_prob[:, 0, :].T[:, None, :], -1)
    router_grad = route_back(route_prob, grad_prob, chosen_hot)
    grad_expert_input = grad_sum + matrix_multiply(router_grad, router_mat.T)
    router_wgrad = matrix_multiply(router_grad.T, expert_input)
    grad_normed, second_gain_grad = normalize_back(
        grad_expert_input, normed_second, factor_second, gain_second
    )
    grad_hidden = cotangent.astype(jnp.float32) + grad_normed
    grad_tokens, first_gain_grad, late = halves_backward(
        grad_hidden, saved, gain_first, query_mat, key_matrix, value_matrix, out_mat
    )

    extras = jnp.concatenate(
        [router_wgrad, first_gain_grad[None, :], second_gain_grad[None, :]], 0
    )
    slices = [
        grad.T.reshape(owner_count, grad.shape[1] // owner_count, token_rows) for grad in late
    ]
    extra_count, extra_width = extras.shape
    part = extra_width // (owner_count * dp_count)
    spread = (
        extras.reshape(extra_count, dp_count, owner_count, part)
        .transpose(2, 1, 0, 3)
        .reshape(owner_count, dp_count, extra_count * part)
        .astype(jnp.bfloat16)
    )
    spread = jnp.pad(spread, ((0, 0), (0, 0), (0, -spread.shape[2] % (8 * token_rows))))
    spread = turn(spread, 1).reshape(owner_count, -1, token_rows)
    payload = jnp.concatenate(slices + [spread], 1)
    last = sum(piece.shape[1] for piece in slices)
    cuts = (last - slices[3].shape[1], last)
    everything, mix_here, peer, peer_down = late_sums(
        payload, saved[2], saved[7], mix_away, peer, peer_down, cuts
    )
    shares, (gate_share, up_share, down_share, output) = finish(
        everything,
        [piece.shape[1] for piece in slices],
        mine,
        mine_down,
        peer,
        peer_down,
        hidden,
        mixture,
        mix_here,
    )
    edge = spread.shape[1] // 2
    extras = everything[:, last : last + edge, :token_rows].reshape(owner_count, -1)
    extras = extras[:, : extra_count * part].reshape(owner_count, extra_count, part)
    extras = extras.transpose(1, 0, 2).reshape(extra_count, -1).astype(jnp.float32)
    query_share, key_share, value_share, out_share = shares
    return (
        output,
        grad_tokens,
        extras[expert_count],
        query_share,
        key_share,
        value_share,
        out_share,
        extras[expert_count + 1],
        extras[:expert_count].T,
        gate_share,
        up_share,
        down_share,
    )


def solution(mesh):
    placed = (
        P(("dp", "expert"), None),
        P(("dp", "expert")),
        P(("dp", "expert"), None),
        P("dp"),
        P("dp", None),
        P("dp", None),
        P("dp", None),
        P("dp", None),
        P("dp"),
        P("dp", None),
        P("expert", None, None),
        P("expert", None, None),
        P("expert", None, None),
        P(("dp", "expert"), None),
    )
    owners = mesh.shape["expert"]
    together = mesh.shape["dp"] == 2 and owners >= 8 and owners & (owners - 1) == 0
    return jax.shard_map(
        shards_together if together else shards,
        mesh=mesh,
        in_specs=placed,
        out_specs=(
            P(("dp", "expert"), None),
            P(("dp", "expert"), None),
            P("dp"),
            P("dp", None),
            P("dp", None),
            P("dp", None),
            P("dp", None),
            P("dp"),
            P("dp", None),
            P("expert", "dp", None),
            P("expert", "dp", None),
            P("expert", None, "dp"),
        ),
        check_vma=False,
    )
```

```python
import functools

import jax
import jax.numpy as jnp
from jax import lax
from jax.experimental import pallas as pl
from jax.experimental.pallas import tpu as pltpu
from jax.sharding import PartitionSpec as P

QUERY_HEADS = 16
KEY_VALUE_HEADS = 8
HEAD_DIM = 64
SEQUENCE_LENGTH = 128


EPSILON = 1e-06
SCORE_SCALE = 0.015625
ROPE_BASE = 10000.0
MASKED = -1e30


def product(pattern, left_op, right_op):
    return jnp.einsum(pattern, left_op, right_op, preferred_element_type=jnp.float32)


def matrix_multiply(left_op, right_op):
    return jnp.dot(left_op, right_op, preferred_element_type=jnp.float32)


def rope_tables(seq_len, head_size):
    positions = jnp.arange(seq_len, dtype=jnp.float32)
    exponent = jnp.arange(head_size // 2, dtype=jnp.float32) * (2.0 / head_size)
    angles = positions[:, None] * (ROPE_BASE ** (-exponent))[None, :]
    return (jnp.cos(angles)[None, :, None, :], jnp.sin(angles)[None, :, None, :])


def apply_rotary(values, cosine_table, sine_table):
    middle = values.shape[-1] // 2
    first_half = values[..., :middle]
    second_half = values[..., middle:]
    return jnp.concatenate(
        [
            first_half * cosine_table - second_half * sine_table,
            second_half * cosine_table + first_half * sine_table,
        ],
        -1,
    )


def inverse_rotary(gradient, cosine_table, sine_table):
    middle = gradient.shape[-1] // 2
    first_half = gradient[..., :middle]
    second_half = gradient[..., middle:]
    return jnp.concatenate(
        [
            first_half * cosine_table + second_half * sine_table,
            second_half * cosine_table - first_half * sine_table,
        ],
        -1,
    )


def normalize(values, gain_vec):
    factor = lax.rsqrt(jnp.mean(values * values, -1, keepdims=True) + EPSILON)
    normed = values * factor
    return (normed, factor, (normed * gain_vec).astype(jnp.bfloat16))


def normalize_back(gradient, normed, factor, gain_vec):
    gain_grad = jnp.sum(gradient * normed, 0)
    scaled = gradient * gain_vec
    return (factor * (scaled - normed * jnp.mean(scaled * normed, -1, keepdims=True)), gain_grad)


def segment_mask(segments):
    seq_len = segments.shape[1]
    causal = jnp.arange(seq_len)[:, None] >= jnp.arange(seq_len)[None, :]
    same_doc = segments[:, :, None] == segments[:, None, :]
    return (same_doc & causal[None])[:, None, None]


def score_table(query_rows, key_row_block, mask_tab):
    raw_scores = product("sqhgw,skhw->shgqk", query_rows, key_row_block) * SCORE_SCALE
    return jnp.where(mask_tab, raw_scores, MASKED)


def mixer_forward(tokens, segments, gain_vec, query_mat, key_matrix, value_matrix, out_mat):
    token_rows = tokens.shape[0]
    local_sequences = token_rows // SEQUENCE_LENGTH
    query_groups = QUERY_HEADS // KEY_VALUE_HEADS
    cosine_table, sine_table = rope_tables(SEQUENCE_LENGTH, HEAD_DIM)
    mask_tab = segment_mask(segments.reshape(local_sequences, SEQUENCE_LENGTH))
    residual = tokens.astype(jnp.float32)
    normed, factor, attention_input = normalize(residual, gain_vec)
    query_rows = apply_rotary(
        matrix_multiply(attention_input, query_mat).reshape(
            local_sequences, SEQUENCE_LENGTH, QUERY_HEADS, HEAD_DIM
        ),
        cosine_table,
        sine_table,
    )
    query_rows = query_rows.astype(jnp.bfloat16).reshape(
        local_sequences, SEQUENCE_LENGTH, KEY_VALUE_HEADS, query_groups, HEAD_DIM
    )
    key_row_block = apply_rotary(
        matrix_multiply(attention_input, key_matrix).reshape(
            local_sequences, SEQUENCE_LENGTH, KEY_VALUE_HEADS, HEAD_DIM
        ),
        cosine_table,
        sine_table,
    ).astype(jnp.bfloat16)
    value_row_block = (
        matrix_multiply(attention_input, value_matrix)
        .astype(jnp.bfloat16)
        .reshape(local_sequences, SEQUENCE_LENGTH, KEY_VALUE_HEADS, HEAD_DIM)
    )
    scores = score_table(query_rows, key_row_block, mask_tab)
    row_peak = jnp.max(scores, -1, keepdims=True)
    logsum = row_peak + jnp.log(jnp.sum(jnp.exp(scores - row_peak), -1, keepdims=True))
    weights = jnp.exp(scores - logsum).astype(jnp.bfloat16)
    attended = product("shgqk,skhw->sqhgw", weights, value_row_block).astype(jnp.bfloat16)
    hidden = residual + matrix_multiply(
        attended.reshape(token_rows, QUERY_HEADS * HEAD_DIM), out_mat
    )
    saved = (
        normed,
        factor,
        attention_input,
        query_rows,
        key_row_block,
        value_row_block,
        attended,
        logsum,
        mask_tab,
        cosine_table,
        sine_table,
    )
    return (hidden, saved)


def mixer_backward(grad_hidden, saved, gain_vec, query_mat, key_matrix, value_matrix, out_mat):
    (
        normed,
        factor,
        attention_input,
        query_rows,
        key_row_block,
        value_row_block,
        attended,
        logsum,
        mask_tab,
        cosine_table,
        sine_table,
    ) = saved
    token_rows = grad_hidden.shape[0]
    local_sequences = token_rows // SEQUENCE_LENGTH
    grad_round = grad_hidden.astype(jnp.bfloat16)
    out_grad = matrix_multiply(attended.reshape(token_rows, QUERY_HEADS * HEAD_DIM).T, grad_round)
    grad_attended = (
        matrix_multiply(grad_round, out_mat.T).astype(jnp.bfloat16).reshape(query_rows.shape)
    )
    scores = score_table(query_rows, key_row_block, mask_tab)
    prob_full = jnp.exp(scores - logsum)
    values_gradient = product("shgqk,sqhgw->skhw", prob_full.astype(jnp.bfloat16), grad_attended)
    grad_weights = product("sqhgw,skhw->shgqk", grad_attended, value_row_block)
    row_delta = product("sqhgw,sqhgw->shgq", grad_attended, attended)[..., None]
    grad_scores = (prob_full * (grad_weights - row_delta) * SCORE_SCALE).astype(jnp.bfloat16)
    grad_queries = product("shgqk,skhw->sqhgw", grad_scores, key_row_block)
    keys_gradient = product("shgqk,sqhgw->skhw", grad_scores, query_rows)
    query_grad = inverse_rotary(
        grad_queries.reshape(local_sequences, SEQUENCE_LENGTH, QUERY_HEADS, HEAD_DIM),
        cosine_table,
        sine_table,
    )
    query_grad = query_grad.astype(jnp.bfloat16).reshape(token_rows, QUERY_HEADS * HEAD_DIM)
    key_gradient = (
        inverse_rotary(keys_gradient, cosine_table, sine_table)
        .astype(jnp.bfloat16)
        .reshape(token_rows, KEY_VALUE_HEADS * HEAD_DIM)
    )
    value_gradient = values_gradient.astype(jnp.bfloat16).reshape(
        token_rows, KEY_VALUE_HEADS * HEAD_DIM
    )
    query_wgrad = matrix_multiply(attention_input.T, query_grad)
    key_wgrad = matrix_multiply(attention_input.T, key_gradient)
    value_wgrad = matrix_multiply(attention_input.T, value_gradient)
    grad_attn_input = (
        matrix_multiply(query_grad, query_mat.T)
        + matrix_multiply(key_gradient, key_matrix.T)
        + matrix_multiply(value_gradient, value_matrix.T)
    )
    grad_normed, gain_grad = normalize_back(grad_attn_input, normed, factor, gain_vec)
    return (grad_hidden + grad_normed, gain_grad, query_wgrad, key_wgrad, value_wgrad, out_grad)


def route_weights(expert_input, router_mat, routes):
    logits = matrix_multiply(expert_input, router_mat)
    chosen_hot = (
        routes[:, :, None] == jnp.arange(router_mat.shape[1], dtype=jnp.int32)[None, None, :]
    ).astype(jnp.float32)
    chosen = jnp.sum(chosen_hot * logits[:, None, :], -1)
    return (jax.nn.softmax(chosen, -1), chosen_hot)


def route_back(route_prob, grad_prob, chosen_hot):
    grad_chosen = route_prob * (grad_prob - jnp.sum(route_prob * grad_prob, -1, keepdims=True))
    return jnp.sum(chosen_hot * grad_chosen[:, :, None], 1).astype(jnp.bfloat16)


def expert_forward(owner_rows, gate_mat, up_mat, down_mat):
    gate_pre = product("erd,edf->erf", owner_rows, gate_mat)
    up_pre = product("erd,edf->erf", owner_rows, up_mat)
    gate_sig = jax.nn.sigmoid(gate_pre)
    gate_act = gate_pre * gate_sig
    inner_acts = (gate_act * up_pre).astype(jnp.bfloat16)
    expert_out = product("erf,efd->erd", inner_acts, down_mat).astype(jnp.bfloat16)
    return (expert_out, (gate_pre, up_pre, gate_sig, gate_act, inner_acts))


def expert_backward(grad_rows, owner_rows, kept_acts, gate_mat, up_mat, down_mat):
    gate_pre, up_pre, gate_sig, gate_act, inner_acts = kept_acts
    grad_inner = product("erd,efd->erf", grad_rows, down_mat)
    down_grad = product("erf,erd->efd", inner_acts, grad_rows)
    silu_slope = gate_sig * (1.0 + gate_pre * (1.0 - gate_sig))
    grad_gate = (grad_inner * up_pre * silu_slope).astype(jnp.bfloat16)
    grad_up = (grad_inner * gate_act).astype(jnp.bfloat16)
    gate_grad = product("erd,erf->edf", owner_rows, grad_gate)
    up_grad = product("erd,erf->edf", owner_rows, grad_up)
    grad_owner_rows = product("erf,edf->erd", grad_gate, gate_mat) + product(
        "erf,edf->erd", grad_up, up_mat
    )
    return (grad_owner_rows.astype(jnp.bfloat16), gate_grad, up_grad, down_grad)


def gather_dp(local_part):
    dp_count = lax.axis_size("dp")
    owner_count = lax.axis_size("expert")
    if dp_count != 2 or owner_count % 2:
        return lax.all_gather(local_part, "dp", axis=0, tiled=True)
    low, high = jnp.split(local_part, 2, 0)
    even = lax.axis_index("expert") % 2 == 0
    near = lax.ppermute(jnp.where(even, low, high), "dp", [(0, 1), (1, 0)])
    far = lax.ppermute(near, "expert", [(i, i ^ 1) for i in range(owner_count)])
    other = jnp.concatenate([jnp.where(even, near, far), jnp.where(even, far, near)], 0)
    first = lax.axis_index("dp") == 0
    return jnp.concatenate(
        [jnp.where(first, local_part, other), jnp.where(first, other, local_part)], 0
    )


def all_sums(partial):
    owner_count = lax.axis_size("expert")
    dp_count = lax.axis_size("dp")
    width = partial.shape[1]
    pieces = partial.astype(jnp.bfloat16).reshape(dp_count, owner_count, -1, width)
    piece = lax.psum_scatter(
        pieces.transpose(1, 0, 2, 3).reshape(-1, width), "expert", scatter_dimension=0, tiled=True
    )
    piece = scatter_dp(piece, 0).astype(jnp.bfloat16)
    return lax.all_gather(piece, "expert", axis=0, tiled=True).astype(jnp.float32)


def scatter_dp(partial, axis):
    dp_count = lax.axis_size("dp")
    rounded = partial.astype(jnp.bfloat16)
    if dp_count != 2:
        return lax.psum_scatter(rounded, "dp", scatter_dimension=axis, tiled=True).astype(
            jnp.float32
        )
    low, high = jnp.split(rounded, 2, axis)
    first = lax.axis_index("dp") == 0
    arrived = lax.ppermute(jnp.where(first, high, low), "dp", [(0, 1), (1, 0)])
    return jnp.where(first, low, high).astype(jnp.float32) + arrived.astype(jnp.float32)


def shards(
    tokens,
    segments,
    routes,
    first_gain,
    query_weight,
    key_projection_weight,
    value_projection_weight,
    out_weight,
    second_gain,
    router_weight,
    gate_weight,
    up_weight,
    down_weight,
    cotangent,
):
    token_rows, model_width = tokens.shape
    top_count = routes.shape[1]
    expert_count = router_weight.shape[1]
    owner_count = lax.axis_size("expert")
    local_count = gate_weight.shape[0]
    key_width = key_projection_weight.shape[1]
    query_width = query_weight.shape[1]
    capacity = 5 * token_rows * top_count // (4 * expert_count)
    row_part = router_weight.shape[0]

    small = jnp.concatenate(
        [router_weight, first_gain[:, None], second_gain[:, None]], 1
    )
    small_mat = gather_dp(small)
    router_mat = small_mat[:, :expert_count]
    gain_first = small_mat[:, expert_count]
    gain_second = small_mat[:, expert_count + 1]
    joined_mat = gather_dp(
        jnp.concatenate([query_weight, key_projection_weight, value_projection_weight], 1)
    )
    query_mat = joined_mat[:, :query_width]
    key_matrix = joined_mat[:, query_width : query_width + key_width]
    value_matrix = joined_mat[:, query_width + key_width :]
    out_mat = gather_dp(out_weight)

    routes_all = lax.all_gather(routes, "expert")
    cotangent_all = lax.all_gather(cotangent, "expert")

    mine = lax.axis_index("expert") * local_count + jnp.arange(local_count, dtype=jnp.int32)
    hit = jnp.any(routes_all[None] == mine[:, None, None, None], -1)
    before = (
        jnp.arange(token_rows)[:, None] < jnp.arange(token_rows)[None, :]
    ).astype(jnp.bfloat16)
    rank = product("lst,tu->lsu", hit.astype(jnp.bfloat16), before).astype(jnp.int32)
    slot = jnp.where(hit, rank, -1)
    picked = slot[:, :, None, :] == jnp.arange(capacity, dtype=jnp.int32)[None, None, :, None]
    pick = picked.astype(jnp.bfloat16)

    def rows_of(gathered):
        rows = product("lsct,std->lscd", pick, gathered)
        return rows.reshape(local_count, owner_count * capacity, model_width)

    own_hot = (routes[:, :, None] == jnp.arange(expert_count, dtype=jnp.int32)).any(1)
    own_rank = matrix_multiply(before.T, own_hot.astype(jnp.bfloat16)).astype(jnp.int32)
    own_slot = jnp.where(own_hot, own_rank, -1)
    own_pick = (
        own_slot[:, :, None] == jnp.arange(capacity, dtype=jnp.int32)[None, None, :]
    ).astype(jnp.bfloat16)

    def send_back(rows):
        shaped = rows.reshape(local_count, owner_count, capacity, model_width)
        return lax.all_to_all(
            shaped.transpose(1, 0, 2, 3).reshape(expert_count, capacity, model_width),
            "expert",
            split_axis=0,
            concat_axis=0,
            tiled=True,
        )

    def sum_back(returned):
        flat = returned.reshape(expert_count * capacity, model_width)
        return matrix_multiply(own_pick.reshape(token_rows, expert_count * capacity), flat)

    hidden, saved = mixer_forward(
        tokens, segments, gain_first, query_mat, key_matrix, value_matrix, out_mat
    )
    normed_second, factor_second, expert_input = normalize(hidden, gain_second)
    input_all = lax.all_gather(expert_input, "expert")
    route_prob, chosen_hot = route_weights(expert_input, router_mat, routes)
    dense_prob = jnp.sum(chosen_hot * route_prob[:, :, None], 1)
    prob_all = lax.all_gather(dense_prob, "expert")

    column = jnp.arange(expert_count, dtype=jnp.int32)
    my_column = (mine[:, None] == column[None, :]).astype(jnp.float32)
    my_prob = jnp.sum(prob_all[None] * my_column[:, None, None, :], -1)
    row_prob = jnp.sum(jnp.where(picked, my_prob[:, :, None, :], 0.0), -1).reshape(
        local_count, owner_count * capacity, 1
    )

    owner_rows = rows_of(input_all).astype(jnp.bfloat16)
    cotangent_rows = rows_of(cotangent_all).astype(jnp.bfloat16).astype(jnp.float32)
    expert_out, kept_acts = expert_forward(owner_rows, gate_weight, up_weight, down_weight)
    expert_out = expert_out.astype(jnp.float32)
    weighted = (row_prob * expert_out).astype(jnp.bfloat16)
    row_grad_prob = jnp.sum(expert_out * cotangent_rows, -1).reshape(
        local_count, owner_count, capacity
    )
    token_grad_prob = jnp.sum(jnp.where(picked, row_grad_prob[..., None], 0.0), 2)
    back_prob = lax.all_to_all(
        token_grad_prob.transpose(1, 0, 2).reshape(expert_count, token_rows),
        "expert",
        split_axis=0,
        concat_axis=0,
        tiled=True,
    )
    grad_prob = jnp.sum(chosen_hot * back_prob.T[:, None, :], -1)
    grad_output = cotangent.astype(jnp.float32)

    grad_rows = (row_prob * cotangent_rows).astype(jnp.bfloat16)
    grad_owner_rows, gate_grad, up_grad, down_grad = expert_backward(
        grad_rows, owner_rows, kept_acts, gate_weight, up_weight, down_weight
    )
    grad_back = send_back(grad_owner_rows)
    expert_shares = (
        scatter_dp(gate_grad, 1),
        scatter_dp(up_grad, 1),
        scatter_dp(down_grad, 2),
    )
    grad_back, expert_shares, weighted = lax.optimization_barrier(
        (grad_back, expert_shares, weighted)
    )
    forward_back = send_back(weighted)
    output = (hidden + sum_back(forward_back)).astype(jnp.bfloat16)
    backward_sum = sum_back(grad_back)
    router_grad = route_back(route_prob, grad_prob, chosen_hot)
    grad_expert_input = backward_sum + matrix_multiply(
        router_grad, router_mat.T
    )
    router_wgrad = matrix_multiply(router_grad.T, expert_input)
    grad_normed, second_gain_grad = normalize_back(
        grad_expert_input, normed_second, factor_second, gain_second
    )
    grad_hidden = grad_output + grad_normed
    grad_tokens, first_gain_grad, query_wgrad, key_wgrad, value_wgrad, out_wgrad = mixer_backward(
        grad_hidden, saved, gain_first, query_mat, key_matrix, value_matrix, out_mat
    )

    out_share = all_sums(out_wgrad)
    joined = all_sums(jnp.concatenate([query_wgrad, key_wgrad, value_wgrad], 1))
    query_share = joined[:, :query_width]
    key_share = joined[:, query_width : query_width + key_width]
    value_share = joined[:, query_width + key_width :]
    extras = jnp.concatenate(
        [router_wgrad, first_gain_grad[None, :], second_gain_grad[None, :]], 0
    )
    extras = lax.psum(extras.astype(jnp.bfloat16), ("dp", "expert"))
    extras = lax.dynamic_slice_in_dim(
        extras, lax.axis_index("dp") * row_part, row_part, 1
    ).astype(jnp.float32)
    router_share = extras[:expert_count].T
    first_share = extras[expert_count]
    second_share = extras[expert_count + 1]
    return (
        output,
        grad_tokens,
        first_share,
        query_share,
        key_share,
        value_share,
        out_share,
        second_share,
        router_share,
        expert_shares[0],
        expert_shares[1],
        expert_shares[2],
    )


def turn(values, axis):
    if lax.axis_size("dp") != 2:
        return values
    low, high = jnp.split(values, 2, axis)
    first = lax.axis_index("dp") == 0
    return jnp.concatenate([jnp.where(first, low, high), jnp.where(first, high, low)], axis)


def times(left_op, pieces):
    total, start = None, 0
    for piece in pieces:
        part = matrix_multiply(left_op[:, start : start + piece.shape[0]], piece)
        total = part if total is None else total + part
        start += piece.shape[0]
    return total


def times_back(left_op, pieces):
    return jnp.concatenate([matrix_multiply(left_op, piece.T) for piece in pieces], 1)


def halves_forward(tokens, segments, gain_vec, query_mat, key_matrix, value_matrix, out_mat):
    token_rows = tokens.shape[0]
    local_sequences = token_rows // SEQUENCE_LENGTH
    query_groups = QUERY_HEADS // KEY_VALUE_HEADS
    cosine_table, sine_table = rope_tables(SEQUENCE_LENGTH, HEAD_DIM)
    mask_tab = segment_mask(segments.reshape(local_sequences, SEQUENCE_LENGTH))
    residual = tokens.astype(jnp.float32)
    normed, factor, attention_input = normalize(turn(residual, 1), gain_vec)
    query_rows = apply_rotary(
        times(attention_input, query_mat).reshape(
            local_sequences, SEQUENCE_LENGTH, QUERY_HEADS, HEAD_DIM
        ),
        cosine_table,
        sine_table,
    )
    query_rows = query_rows.astype(jnp.bfloat16).reshape(
        local_sequences, SEQUENCE_LENGTH, KEY_VALUE_HEADS, query_groups, HEAD_DIM
    )
    key_row_block = apply_rotary(
        times(attention_input, key_matrix).reshape(
            local_sequences, SEQUENCE_LENGTH, KEY_VALUE_HEADS, HEAD_DIM
        ),
        cosine_table,
        sine_table,
    ).astype(jnp.bfloat16)
    value_row_block = (
        times(attention_input, value_matrix)
        .astype(jnp.bfloat16)
        .reshape(local_sequences, SEQUENCE_LENGTH, KEY_VALUE_HEADS, HEAD_DIM)
    )
    scores = score_table(query_rows, key_row_block, mask_tab)
    row_peak = jnp.max(scores, -1, keepdims=True)
    logsum = row_peak + jnp.log(jnp.sum(jnp.exp(scores - row_peak), -1, keepdims=True))
    weights = jnp.exp(scores - logsum).astype(jnp.bfloat16)
    attended = product("shgqk,skhw->sqhgw", weights, value_row_block).astype(jnp.bfloat16)
    turned = turn(attended.reshape(token_rows, QUERY_HEADS * HEAD_DIM), 1)
    hidden = residual + times(turned, out_mat)
    saved = (
        normed,
        factor,
        attention_input,
        query_rows,
        key_row_block,
        value_row_block,
        attended,
        turned,
        logsum,
        mask_tab,
        cosine_table,
        sine_table,
    )
    return (hidden, saved)


def halves_backward(grad_hidden, saved, gain_vec, query_mat, key_matrix, value_matrix, out_mat):
    (
        normed,
        factor,
        attention_input,
        query_rows,
        key_row_block,
        value_row_block,
        attended,
        _,
        logsum,
        mask_tab,
        cosine_table,
        sine_table,
    ) = saved
    token_rows = grad_hidden.shape[0]
    local_sequences = token_rows // SEQUENCE_LENGTH
    grad_round = grad_hidden.astype(jnp.bfloat16)
    grad_attended = (
        turn(times_back(grad_round, out_mat).astype(jnp.bfloat16), 1).reshape(query_rows.shape)
    )
    scores = score_table(query_rows, key_row_block, mask_tab)
    prob_full = jnp.exp(scores - logsum)
    values_gradient = product("shgqk,sqhgw->skhw", prob_full.astype(jnp.bfloat16), grad_attended)
    grad_weights = product("sqhgw,skhw->shgqk", grad_attended, value_row_block)
    row_delta = product("sqhgw,sqhgw->shgq", grad_attended, attended)[..., None]
    grad_scores = (prob_full * (grad_weights - row_delta) * SCORE_SCALE).astype(jnp.bfloat16)
    grad_queries = product("shgqk,skhw->sqhgw", grad_scores, key_row_block)
    keys_gradient = product("shgqk,sqhgw->skhw", grad_scores, query_rows)
    query_grad = inverse_rotary(
        grad_queries.reshape(local_sequences, SEQUENCE_LENGTH, QUERY_HEADS, HEAD_DIM),
        cosine_table,
        sine_table,
    )
    query_grad = query_grad.astype(jnp.bfloat16).reshape(token_rows, QUERY_HEADS * HEAD_DIM)
    key_gradient = (
        inverse_rotary(keys_gradient, cosine_table, sine_table)
        .astype(jnp.bfloat16)
        .reshape(token_rows, KEY_VALUE_HEADS * HEAD_DIM)
    )
    value_gradient = values_gradient.astype(jnp.bfloat16).reshape(
        token_rows, KEY_VALUE_HEADS * HEAD_DIM
    )
    grad_attn_input = (
        times_back(query_grad, query_mat)
        + times_back(key_gradient, key_matrix)
        + times_back(value_gradient, value_matrix)
    )
    grad_normed, gain_grad = normalize_back(grad_attn_input, normed, factor, gain_vec)
    return (
        grad_hidden + turn(grad_normed, 1),
        turn(gain_grad, 0),
        [query_grad, key_gradient, value_gradient, grad_round],
    )


MESH = pl.DeviceIdType.MESH


def quotient(index, by):
    return index // by if isinstance(index, int) else lax.div(index, jnp.int32(by))


def parity(index):
    return index % 2 if isinstance(index, int) else lax.rem(index, jnp.int32(2))


def flip(index, by):
    if isinstance(index, int) and isinstance(by, int):
        return index ^ by
    if isinstance(index, int):
        index, by = by, index
    total, weight = (index, 1) if isinstance(by, int) else (0, 1)
    for _ in range(6):
        if isinstance(by, int):
            if by & weight:
                total = total + weight - 2 * weight * parity(quotient(index, weight))
        else:
            one, two = parity(quotient(index, weight)), parity(quotient(by, weight))
            total = total + weight * (one + two - 2 * one * two)
        weight *= 2
    return total


def others(count, act):
    for by in range(1, count):
        act(by)


def expert_at(index):
    return {"expert": index}


def send(src, dst, send_sem, recv_sem, where):
    return pltpu.make_async_remote_copy(
        src_ref=src,
        dst_ref=dst,
        send_sem=send_sem,
        recv_sem=recv_sem,
        device_id=where,
        device_id_type=MESH,
    )


def meet(count, with_dp):
    barrier = pltpu.get_barrier_semaphore()
    me = lax.axis_index("expert")

    def greet(by):
        pl.semaphore_signal(
            barrier, inc=1, device_id=expert_at(flip(me, by)), device_id_type=MESH
        )

    others(count, greet)
    if with_dp:
        pl.semaphore_signal(
            barrier, inc=1, device_id={"dp": 1 - lax.axis_index("dp")}, device_id_type=MESH
        )
    pl.semaphore_wait(barrier, count - 1 + (1 if with_dp else 0))


class Gather:
    def __init__(self, own, block_of, count, send_sems, recv_sems):
        self.own, self.block_of, self.count = own, block_of, count
        self.send_sems, self.recv_sems = send_sems, recv_sems
        self.me = lax.axis_index("expert")

    def copy(self, rel, by, src=None):
        block = self.block_of(flip(self.me, rel))
        there = flip(rel, by)
        return send(
            block if src is None else src,
            block,
            self.send_sems.at[there],
            self.recv_sems.at[there],
            expert_at(flip(self.me, by)),
        )

    def wait(self, rel):
        block = self.block_of(flip(self.me, rel))
        send(
            block, block, self.send_sems.at[rel], self.recv_sems.at[rel], expert_at(self.me)
        ).wait_recv()

    def begin(self, held=()):
        for by in list(range(8, self.count, 4)) + [4, 2, 1]:
            if by < self.count and by not in held:
                self.copy(0, by, self.own).start()

    def release(self, by):
        self.copy(0, by, self.own).start()

    def pass_z(self, rel):
        self.wait(rel)
        self.copy(rel, 2).start()
        self.copy(rel, 1).start()

    def pass_x(self, rel):
        self.wait(rel + 2)
        self.copy(rel + 2, 1).start()

    def wait_sends(self):
        for rel in range(1, self.count):
            block = self.block_of(flip(self.me, rel))
            send(
                block, block, self.send_sems.at[rel], self.recv_sems.at[rel], expert_at(self.me)
            ).wait_send()

    def rest(self):
        far = list(range(12, self.count, 4))
        near = [rel for rel in (8, 4) if rel < self.count]
        self.pass_x(0)
        self.pass_z(near[0])
        for by in far:
            self.release(by)
        for rel in near[1:]:
            self.pass_z(rel)
        for rel in near:
            self.pass_x(rel)
        for rel in far:
            self.pass_z(rel)
            self.pass_x(rel)
        for rel in range(1, self.count, 2):
            self.wait(rel)
        self.wait_sends()


def front_kernel(pieces, *refs):
    mine, refs = refs[:pieces], refs[pieces:]
    tokens, refs = refs[0], refs[1:]
    fetched, refs = refs[:pieces], refs[pieces:]
    tokens_all, y_send, y_recv, c_send, c_recv, t_send, t_recv, local = refs
    rows = tokens.shape[0]
    me, dp = lax.axis_index("expert"), lax.axis_index("dp")
    core = parity(me)
    meet(4, True)

    def part(ref, which):
        half = ref.shape[0] // 2
        return ref.at[pl.ds(pl.multiple_of(which * half, half), half)]

    over_y = [
        send(
            part(mine[i], core),
            part(fetched[i], core),
            y_send.at[i],
            y_recv.at[i],
            {"dp": 1 - dp},
        )
        for i in range(pieces)
    ]
    for copy in over_y:
        copy.start()

    def at_place(index):
        place = index - 4 * quotient(index, 4)
        return tokens_all.at[pl.ds(pl.multiple_of(place * rows, rows), rows)]

    keep = pltpu.make_async_copy(tokens, at_place(me), local)
    keep.start()
    gather = Gather(tokens, at_place, 4, t_send, t_recv)
    gather.begin()
    over_core = [
        send(
            part(fetched[i], core),
            part(fetched[i], core),
            c_send.at[i],
            c_recv.at[i],
            expert_at(flip(me, 1)),
        )
        for i in range(pieces)
    ]
    gather.pass_x(0)
    for i in range(pieces):
        over_y[i].wait_recv()
        over_core[i].start()
    gather.wait(1)
    gather.wait(3)
    gather.wait_sends()
    keep.wait()
    for i in range(pieces):
        send(
            part(mine[i], 1 - core),
            part(fetched[i], 1 - core),
            c_send.at[i],
            c_recv.at[i],
            expert_at(flip(me, 1)),
        ).wait_recv()
        over_core[i].wait_send()
        over_y[i].wait_send()


def front(own, tokens):
    pieces = len(own)
    rows, width = tokens.shape
    anywhere = pl.BlockSpec(memory_space=pl.ANY)
    results = pl.pallas_call(
        functools.partial(front_kernel, pieces),
        out_shape=[jax.ShapeDtypeStruct(part.shape, part.dtype) for part in own]
        + [jax.ShapeDtypeStruct((4 * rows, width), tokens.dtype)],
        in_specs=[anywhere] * (pieces + 1),
        out_specs=[anywhere] * (pieces + 1),
        scratch_shapes=[pltpu.SemaphoreType.DMA((pieces,)) for _ in range(4)]
        + [pltpu.SemaphoreType.DMA((4,)), pltpu.SemaphoreType.DMA((4,))]
        + [pltpu.SemaphoreType.DMA],
        compiler_params=pltpu.CompilerParams(collective_id=0, has_side_effects=True),
        name="front",
    )(*own, tokens)
    return results[:pieces], results[pieces]


def finish_kernel(heights, away, *refs):
    all_ref, mine, mine_down, peer, peer_down, hidden, mixture = refs[:7]
    pieces, refs = refs[7], refs[8:]
    shares, refs = refs[: len(heights)], refs[len(heights) :]
    gate_out, up_out, down_out, output = refs
    start = 0
    for height, out in zip(heights, shares):
        for index in range(0, all_ref.shape[0], 128 // height):
            block = all_ref[index : index + 128 // height, start : start + height, :]
            block = block.astype(jnp.float32).reshape(128, block.shape[2])
            out[:, index * height : index * height + 128] = block.T
        start += height
    gate_out[0] = mine[0] + peer[0].astype(jnp.float32)
    up_out[0] = mine[1] + peer[1].astype(jnp.float32)
    down_out[0] = mine_down[...] + peer_down[...].astype(jnp.float32)
    total = hidden[...] + mixture[...]
    for index in range(away):
        total = total + pieces[index].astype(jnp.float32)
    output[...] = total.astype(jnp.bfloat16)


def finish(everything, heights, mine, mine_down, peer, peer_down, hidden, mixture, pieces):
    count, lines, half = everything.shape
    parts = 4
    rows, width = hidden.shape
    deep = mine.shape[2]
    tile, low, some = half // parts, deep // parts, rows // parts
    three = pl.BlockSpec((2, tile, deep), lambda i: (0, i, 0))
    down = pl.BlockSpec((low, half), lambda i: (i, 0))
    tokens = pl.BlockSpec((some, width), lambda i: (i, 0))
    f32 = jnp.float32
    results = pl.pallas_call(
        functools.partial(finish_kernel, heights, pieces.shape[0]),
        grid=(parts,),
        out_shape=[jax.ShapeDtypeStruct((half, count * height), f32) for height in heights]
        + [
            jax.ShapeDtypeStruct((1, half, deep), f32),
            jax.ShapeDtypeStruct((1, half, deep), f32),
            jax.ShapeDtypeStruct((1, deep, half), f32),
            jax.ShapeDtypeStruct((rows, width), jnp.bfloat16),
        ],
        in_specs=[pl.BlockSpec((count, lines, tile), lambda i: (0, 0, i))]
        + [three, down, three, down, tokens, tokens]
        + [pl.BlockSpec((pieces.shape[0], some, width), lambda i: (0, i, 0))],
        out_specs=[pl.BlockSpec((tile, count * height), lambda i: (i, 0)) for height in heights]
        + [
            pl.BlockSpec((1, tile, deep), lambda i: (0, i, 0)),
            pl.BlockSpec((1, tile, deep), lambda i: (0, i, 0)),
            pl.BlockSpec((1, low, half), lambda i: (0, i, 0)),
            tokens,
        ],
        compiler_params=pltpu.CompilerParams(vmem_limit_bytes=58 * 2**20),
        name="finish",
    )(everything, mine, mine_down, peer, peer_down, hidden, mixture, pieces)
    return results[: len(heights)], results[len(heights) :]


def dot_on(left_op, right_op, left_axis, right_axis):
    return lax.dot_general(
        left_op,
        right_op,
        (((left_axis,), (right_axis,)), ((), ())),
        preferred_element_type=jnp.float32,
    )


def experts_kernel(
    count,
    own_ref,
    cot_ref,
    prob_ref,
    gate_ref,
    up_ref,
    down_ref,
    grad_out,
    mix_out,
    mix_away,
    gp_out,
    mine_out,
    mine_down,
    peer_out,
    peer_down,
    x_all,
    prob_all,
    gp_send_buf,
    both_all,
    inner_all,
    ge_all,
    part,
    cbuf,
    xbuf,
    zbuf,
    a_send,
    a_recv,
    p_send,
    p_recv,
    q_send,
    q_recv,
    c_send,
    c_recv,
    x_send,
    x_recv,
    z_send,
    z_recv,
):
    rows, width = own_ref.shape
    hidden = gate_ref.shape[2]
    pair = 2 * rows
    steps = count // 2
    depth = count // 4
    order = [0] + [z for z in (2, 1) if z < depth] + list(range(3, depth))
    me, dp = lax.axis_index("expert"), lax.axis_index("dp")
    core = parity(me)
    meet(count, False)

    def block_of(index):
        return x_all.at[pl.ds(pl.multiple_of(index * rows, rows), rows)]

    gather = Gather(own_ref, block_of, count, a_send, a_recv)
    gather.begin(range(12, count, 4))

    def prob_copy(by):
        there = flip(me, by)
        return send(
            prob_ref.at[there], prob_all.at[me], p_send.at[by], p_recv.at[by], expert_at(there)
        )

    def prob_start(by):
        prob_copy(by).start()

    others(count, prob_start)
    x_all[pl.ds(pl.multiple_of(me * rows, rows), rows)] = own_ref[...]
    prob_all[me] = prob_ref[me]

    def prob_wait(by):
        there = flip(me, by)
        send(
            prob_ref.at[me], prob_all.at[there], p_send.at[by], p_recv.at[by], expert_at(there)
        ).wait_recv()

    others(count, prob_wait)

    def rel_of(step):
        z_rel = quotient(step, 2)
        x_rel = jnp.where(step < 2, parity(step), 1 - parity(step))
        z_rel = sum(jnp.where(z_rel == at, z, 0) for at, z in enumerate(order))
        return 4 * z_rel + 2 * x_rel, z_rel

    eye = (
        lax.broadcasted_iota(jnp.int32, (pair, pair), 0)
        == lax.broadcasted_iota(jnp.int32, (pair, pair), 1)
    )
    theirs = pl.ds(pl.multiple_of((1 - core) * rows, rows), rows)
    ours = pl.ds(pl.multiple_of(core * rows, rows), rows)

    def core_copy(step):
        return send(
            part.at[step, :, theirs],
            cbuf.at[step],
            c_send.at[step],
            c_recv.at[step],
            expert_at(flip(me, 1)),
        )

    def x_copy(step, z_rel, which):
        return send(
            part.at[step, which, ours],
            xbuf.at[z_rel, which],
            x_send.at[which, z_rel],
            x_recv.at[which, z_rel],
            expert_at(flip(me, 2)),
        )

    def z_copy(step, z_rel):
        return send(
            part.at[step, 0, ours],
            zbuf.at[z_rel],
            z_send.at[z_rel],
            z_recv.at[z_rel],
            expert_at(flip(me, 4 * z_rel)),
        )

    def compute(step):
        rel, _ = rel_of(step)
        chip = quotient(flip(me, rel), 2)
        where = pl.ds(pl.multiple_of(chip * pair, pair), pair)
        x = x_all[where, :]
        gate_pre = dot_on(x, gate_ref[0], 1, 0)
        up_pre = dot_on(x, up_ref[0], 1, 0)
        sig = jax.nn.sigmoid(gate_pre)
        act = gate_pre * sig
        inner = (act * up_pre).astype(jnp.bfloat16)
        inner_all[where, :] = inner
        out = dot_on(inner, down_ref[0], 1, 0).astype(jnp.bfloat16).astype(jnp.float32)
        prob_row = jnp.concatenate(
            [prob_all[2 * chip, 0:1, :], prob_all[2 * chip + 1, 0:1, :]], 1
        )
        prob = jnp.sum(jnp.where(eye, prob_row, 0.0), 1, keepdims=True)
        cot = cot_ref[where, :].astype(jnp.float32)
        part[step, 1] = (prob * out).astype(jnp.bfloat16)
        gp = jnp.sum(out * cot, 1, keepdims=True)
        gp_row = jnp.sum(jnp.where(eye, gp, 0.0), 0, keepdims=True)
        gp_send_buf[2 * chip] = jnp.broadcast_to(gp_row[:, :rows], (8, rows))
        gp_send_buf[2 * chip + 1] = jnp.broadcast_to(gp_row[:, rows:], (8, rows))
        ge = (prob * cot).astype(jnp.bfloat16)
        ge_all[where, :] = ge
        gi = dot_on(ge, down_ref[0], 1, 1)
        slope = sig * (1.0 + gate_pre * (1.0 - sig))
        gg = (gi * up_pre * slope).astype(jnp.bfloat16)
        gu = (gi * act).astype(jnp.bfloat16)
        both_all[where, :hidden] = gg
        both_all[where, hidden:] = gu
        part[step, 0] = (dot_on(gg, gate_ref[0], 1, 1) + dot_on(gu, up_ref[0], 1, 1)).astype(
            jnp.bfloat16
        )

    def add_core(step):
        core_copy(step).wait_recv()
        total = part[step, :, ours].astype(jnp.float32) + cbuf[step].astype(jnp.float32)
        part[step, :, ours] = total.astype(jnp.bfloat16)

    def add_x(at):
        z_rel, step = order[at], 2 * at + 1
        x_copy(step, z_rel, 0).wait_recv()
        total = part[step, 0, ours].astype(jnp.float32) + xbuf[z_rel, 0].astype(jnp.float32)
        part[step, 0, ours] = total.astype(jnp.bfloat16)
        z_copy(step, z_rel).start()

    def on(step, number):
        return pl.when(step == number)

    def turn_of(step, carry):
        rel, _ = rel_of(step)

        for at in range(1, depth):

            @on(step, 2 * at)
            def _(at=at):
                if at == 1:
                    gather.pass_x(4 * order[1])

        gather.wait(rel + 1)
        compute(step)
        core_copy(step).start()

        @on(step, 0)
        def _():
            gather.pass_x(0)

        @on(step, 1)
        def _():
            gather.pass_z(4 * order[1])
            for by in range(12, count, 4):
                gather.release(by)
            if depth > 2:
                gather.pass_z(4 * order[2])
            add_core(0)
            add_core(1)

        for at in range(1, depth):

            @on(step, 2 * at)
            def _(at=at):
                if at > 1:
                    add_core(2 * at - 1)
                    x_copy(2 * at - 2, order[at - 1], 1).start()
                if at > 1 and at + 1 < depth:
                    gather.pass_z(4 * order[at + 1])

            @on(step, 2 * at + 1)
            def _(at=at):
                add_core(2 * at)
                x_copy(2 * at, order[at], 0).start()
                if at + 1 < depth:
                    gather.pass_x(4 * order[at + 1])

        if depth > 3:

            @on(step, 6)
            def _():
                add_x(1)

        return carry

    lax.fori_loop(0, steps, turn_of, 0)
    add_core(steps - 1)
    x_copy(1, 0, 0).start()
    x_copy(steps - 2, order[-1], 1).start()
    x_copy(1, 0, 1).start()
    for at in range(2 if depth > 3 else 1, depth - 1):
        add_x(at)

    def gp_copy(by):
        there = flip(me, by)
        return send(
            gp_send_buf.at[there], gp_out.at[me], q_send.at[by], q_recv.at[by], expert_at(there)
        )

    def gp_start(by):
        gp_copy(by).start()

    others(count, gp_start)
    gp_out[me] = gp_send_buf[me]

    half = width // 2
    for turn_at, (which, target, lower) in enumerate( ((1 - dp, peer_out, peer_down), (dp, mine_out, mine_down))
    ):

        def rows_of(index, carry, which=which, target=target):
            tile = half // 2
            at = pl.multiple_of(which * half + index * tile, tile)
            into = pl.ds(pl.multiple_of(index * tile, tile), tile)
            x = x_all[:, pl.ds(at, tile)]
            both = dot_on(x, both_all[...], 0, 0).astype(target.dtype)
            target[0, into, :] = both[:, :hidden]
            target[1, into, :] = both[:, hidden:]
            return carry

        lax.fori_loop(0, 2, rows_of, 0)

        def down_of(index, carry, which=which, lower=lower):
            tile = hidden // 2
            at = pl.ds(pl.multiple_of(index * tile, tile), tile)
            grads = ge_all[:, pl.ds(pl.multiple_of(which * half, half), half)]
            lower[at, :] = dot_on(inner_all[:, at], grads, 0, 0).astype(lower.dtype)
            return carry

        lax.fori_loop(0, 2, down_of, 0)
        if turn_at == 0:
            add_x(depth - 1)

    def from_x(at, which):
        step = 2 * at + 1 if at else 0
        x_copy(step, order[at], which).wait_recv()
        return part[step, which, ours].astype(jnp.float32) + xbuf[order[at], which].astype(
            jnp.float32
        )

    for at in range(1, depth):
        mix_away[order[at] - 1] = from_x(at, 1).astype(jnp.bfloat16)
    mix_out[...] = from_x(0, 1)
    grads = from_x(0, 0)
    for z_rel in range(1, depth):
        z_copy(0, z_rel).wait_recv()
        grads = grads + zbuf[z_rel].astype(jnp.float32)
    grad_out[...] = grads

    def settle(by):
        there = flip(me, by)
        send(
            gp_send_buf.at[me], gp_out.at[there], q_send.at[by], q_recv.at[by], expert_at(there)
        ).wait()
        prob_copy(by).wait_send()

    others(count, settle)
    gather.wait_sends()
    for step in range(steps):
        core_copy(step).wait_send()
    for z_rel in range(depth):
        x_copy(0, z_rel, 0).wait_send()
        x_copy(0, z_rel, 1).wait_send()
    for z_rel in range(1, depth):
        z_copy(0, z_rel).wait_send()


def experts(expert_input, cotangent_all, prob, gate_weight, up_weight, down_weight):
    count = prob.shape[0]
    rows, width = expert_input.shape
    hidden = gate_weight.shape[2]
    total = count * rows
    steps, depth = count // 2, count // 4
    half = width // 2
    local = pl.BlockSpec(memory_space=pltpu.VMEM)
    shapes = ((count,), (count,), (count,), (steps,), (2, depth), (depth,))
    pairs = [pltpu.SemaphoreType.DMA(shape) for shape in shapes]
    semaphores = [item for item in pairs for _ in range(2)]
    bf16 = jnp.bfloat16
    return pl.pallas_call(
        functools.partial(experts_kernel, count),
        out_shape=[
            jax.ShapeDtypeStruct((rows, width), jnp.float32),
            jax.ShapeDtypeStruct((rows, width), jnp.float32),
            jax.ShapeDtypeStruct((depth - 1, rows, width), bf16),
            jax.ShapeDtypeStruct((count, 8, rows), jnp.float32),
            jax.ShapeDtypeStruct((2, half, hidden), jnp.float32),
            jax.ShapeDtypeStruct((hidden, half), jnp.float32),
            jax.ShapeDtypeStruct((2, half, hidden), bf16),
            jax.ShapeDtypeStruct((hidden, half), bf16),
        ],
        in_specs=[local] * 6,
        out_specs=[local] * 8,
        scratch_shapes=[
            pltpu.VMEM((total, width), bf16),
            pltpu.VMEM((count, 8, rows), jnp.float32),
            pltpu.VMEM((count, 8, rows), jnp.float32),
            pltpu.VMEM((total, 2 * hidden), bf16),
            pltpu.VMEM((total, hidden), bf16),
            pltpu.VMEM((total, width), bf16),
            pltpu.VMEM((steps, 2, 2 * rows, width), bf16),
            pltpu.VMEM((steps, 2, rows, width), bf16),
            pltpu.VMEM((depth, 2, rows, width), bf16),
            pltpu.VMEM((depth, rows, width), bf16),
        ]
        + semaphores,
        compiler_params=pltpu.CompilerParams(
            collective_id=1, has_side_effects=True, vmem_limit_bytes=58 * 2**20
        ),
        cost_estimate=pl.CostEstimate(
            flops=18 * total * width * hidden, bytes_accessed=20 * total * width, transcendentals=0
        ),
        name="experts",
    )(expert_input, cotangent_all, prob, gate_weight, up_weight, down_weight)


def late_kernel(
    count,
    cuts,
    pay_ref,
    attention_all,
    attended_ref,
    away_hbm,
    both_away,
    down_away,
    all_out,
    here_hbm,
    both_here,
    down_here,
    attended_all,
    arrived,
    y_out,
    y_in,
    kept,
    z_in,
    mine,
    swap_send,
    swap_recv,
    m_send,
    m_recv,
    d_send,
    d_recv,
    a_send,
    a_recv,
    y_send,
    y_recv,
    z_send,
    z_recv,
    g_send,
    g_recv,
):
    first, last = cuts
    depth, _, lines, rows = pay_ref.shape
    half = all_out.shape[2]
    me, dp = lax.axis_index("expert"), lax.axis_index("dp")
    place = me - 4 * quotient(me, 4)
    level = quotient(me, 4)
    peer = {"dp": 1 - dp}
    order = [z for z in (2, 3) if z < depth] + list(range(4, depth)) + [1, 0]
    meet(count, True)

    def at_place(ref):
        return lambda index: ref.at[
            pl.ds(pl.multiple_of((index - 4 * quotient(index, 4)) * rows, rows), rows)
        ]

    gathers = [
        Gather(attended_ref, at_place(attended_all), 4, d_send, d_recv),
    ]
    columns = pl.ds(pl.multiple_of(place * rows, rows), rows)

    def share(by):
        there = flip(place, by)
        return send(
            pay_ref.at[:, there],
            arrived.at[:, :, columns],
            a_send.at[by],
            a_recv.at[by],
            expert_at(flip(me, by)),
        )

    swap_down = send(down_away, down_here, swap_send.at[0], swap_recv.at[0], peer)
    swap_both = send(both_away, both_here, swap_send.at[1], swap_recv.at[1], peer)

    def outputs_z(z_rel):
        return send(
            away_hbm.at[z_rel - 1],
            here_hbm.at[z_rel - 1],
            m_send.at[z_rel],
            m_recv.at[z_rel],
            expert_at(flip(me, 4 * z_rel)),
        )

    for gather in gathers:
        gather.begin()
    for by in (2, 3, 1):
        share(by).start()
    swap_down.start()
    for z_rel in range(1, depth):
        outputs_z(z_rel).start()
    attended_all[columns, :] = attended_ref[...]
    arrived[:, :, columns] = pay_ref[:, place]
    for gather in gathers:
        gather.pass_x(0)
    for by in (2, 3, 1):
        there = flip(place, by)
        send(
            pay_ref.at[:, there],
            arrived.at[:, :, pl.ds(pl.multiple_of(there * rows, rows), rows)],
            a_send.at[by],
            a_recv.at[by],
            expert_at(flip(me, by)),
        ).wait()
    for gather in gathers:
        gather.wait(1)
        gather.wait(3)
        gather.wait_sends()

    blank = jnp.zeros((lines - last - (lines - last) // 2, half), jnp.float32)

    def tile_of(z_rel, side):
        at = flip(level, z_rel)
        where = slice(side * half, (side + 1) * half)
        extra = arrived[at, last:, :].astype(jnp.float32)
        summed = extra[:, :rows]
        for index in range(1, 4):
            summed = summed + extra[:, index * rows : (index + 1) * rows]
        edge = summed.shape[0] // 2
        summed = summed[side * edge : (side + 1) * edge]
        return jnp.concatenate(
            [
                dot_on(arrived[at, :first, :], attention_all[:, where], 1, 0),
                dot_on(arrived[at, first:last, :], attended_all[:, where], 1, 0),
                jnp.concatenate([summed, jnp.zeros((edge, half - rows), jnp.float32)], 1),
                blank,
            ],
            0,
        )

    def over_y(z_rel):
        return send(
            y_out.at[z_rel], y_in.at[z_rel], y_send.at[z_rel], y_recv.at[z_rel], peer
        )

    def over_z(z_rel):
        return send(
            y_out.at[z_rel],
            z_in.at[z_rel],
            z_send.at[z_rel],
            z_recv.at[z_rel],
            expert_at(flip(me, 4 * z_rel)),
        )

    for z_rel in order:
        y_out[z_rel] = tile_of(z_rel, 1).astype(jnp.bfloat16)
        over_y(z_rel).start()
    for z_rel in order:
        kept[z_rel] = tile_of(z_rel, 0)
    total = None
    for z_rel in order:
        over_y(z_rel).wait()
        total = kept[z_rel] + y_in[z_rel].astype(jnp.float32)
        if z_rel:
            y_out[z_rel] = total.astype(jnp.bfloat16)
            over_z(z_rel).start()
    swap_both.start()
    for z_rel in order[:-1]:
        over_z(z_rel).wait()
        total = total + z_in[z_rel].astype(jnp.float32)
    mine[...] = total.astype(jnp.bfloat16)
    gather = Gather(mine, lambda index: all_out.at[index], count, g_send, g_recv)
    gather.begin(range(12, count, 4))
    all_out[me] = mine[...]
    gather.rest()
    swap_down.wait()
    for z_rel in range(1, depth):
        outputs_z(z_rel).wait()
    swap_both.wait()


def late_sums(payload, attention, attended, away, both, down, cuts):
    count, lines, rows = payload.shape
    width = attention.shape[1]
    half, depth = width // 2, count // 4
    local = pl.BlockSpec(memory_space=pltpu.VMEM)
    anywhere = pl.BlockSpec(memory_space=pl.ANY)
    bf16 = jnp.bfloat16
    sizes = (2, depth, 4, 4, depth, depth, count)
    return pl.pallas_call(
        functools.partial(late_kernel, count, cuts),
        out_shape=[
            jax.ShapeDtypeStruct((count, lines, half), bf16),
            jax.ShapeDtypeStruct(away.shape, bf16),
            jax.ShapeDtypeStruct(both.shape, bf16),
            jax.ShapeDtypeStruct(down.shape, bf16),
        ],
        in_specs=[local] * 3 + [anywhere] * 3,
        out_specs=[local] + [anywhere] * 3,
        scratch_shapes=[
            pltpu.VMEM((4 * rows, width), bf16),
            pltpu.VMEM((depth, lines, 4 * rows), bf16),
            pltpu.VMEM((depth, lines, half), bf16),
            pltpu.VMEM((depth, lines, half), bf16),
            pltpu.VMEM((depth, lines, half), jnp.float32),
            pltpu.VMEM((depth, lines, half), bf16),
            pltpu.VMEM((lines, half), bf16),
        ]
        + [pltpu.SemaphoreType.DMA((size,)) for size in sizes for _ in range(2)],
        compiler_params=pltpu.CompilerParams(
            collective_id=2, has_side_effects=True, vmem_limit_bytes=56 * 2**20
        ),
        name="late",
    )(payload.reshape(depth, 4, lines, rows), attention, attended, away, both, down)


def shards_together(
    tokens,
    segments,
    routes,
    first_gain,
    query_weight,
    key_projection_weight,
    value_projection_weight,
    out_weight,
    second_gain,
    router_weight,
    gate_weight,
    up_weight,
    down_weight,
    cotangent,
):
    token_rows = tokens.shape[0]
    expert_count = router_weight.shape[1]
    owner_count = lax.axis_size("expert")
    dp_count = lax.axis_size("dp")

    small = jnp.concatenate([router_weight, first_gain[:, None], second_gain[:, None]], 1)
    small = jnp.pad(small, ((0, 0), (0, -small.shape[1] % 128)))
    own = [query_weight, key_projection_weight, value_projection_weight, out_weight, small]
    cotangent_all = lax.all_gather(cotangent, "expert", axis=0, tiled=True)
    other, tokens_near = front(own, tokens)
    query_mat, key_matrix, value_matrix, out_mat, small = (list(p) for p in zip(own, other))
    small_mat = jnp.concatenate(small, 0)
    router_mat = turn(small_mat[:, :expert_count], 0)
    gain_first = small_mat[:, expert_count]
    gain_second = turn(small_mat[:, expert_count + 1], 0)

    near = turn(tokens_near.astype(jnp.float32), 1)
    _, _, attention_near = normalize(near, gain_first)
    hidden, saved = halves_forward(
        tokens, segments, gain_first, query_mat, key_matrix, value_matrix, out_mat
    )
    normed_second, factor_second, expert_input = normalize(hidden, gain_second)
    route_prob, chosen_hot = route_weights(expert_input, router_mat, routes)
    dense_prob = jnp.sum(chosen_hot * route_prob[:, :, None], 1)
    prob = jnp.broadcast_to(dense_prob.T[:, None, :], (owner_count, 8, token_rows))
    grad_sum, mixture, mix_away, back_prob, mine, mine_down, peer, peer_down = experts(
        expert_input, cotangent_all, prob, gate_weight, up_weight, down_weight
    )
    grad_prob = jnp.sum(chosen_hot * back_prob[:, 0, :].T[:, None, :], -1)
    router_grad = route_back(route_prob, grad_prob, chosen_hot)
    grad_expert_input = grad_sum + matrix_multiply(router_grad, router_mat.T)
    router_wgrad = matrix_multiply(router_grad.T, expert_input)
    grad_normed, second_gain_grad = normalize_back(
        grad_expert_input, normed_second, factor_second, gain_second
    )
    grad_hidden = cotangent.astype(jnp.float32) + grad_normed
    grad_tokens, first_gain_grad, late = halves_backward(
        grad_hidden, saved, gain_first, query_mat, key_matrix, value_matrix, out_mat
    )

    extras = jnp.concatenate(
        [router_wgrad, first_gain_grad[None, :], second_gain_grad[None, :]], 0
    )
    slices = [
        grad.T.reshape(owner_count, grad.shape[1] // owner_count, token_rows) for grad in late
    ]
    extra_count, extra_width = extras.shape
    part = extra_width // (owner_count * dp_count)
    spread = (
        extras.reshape(extra_count, dp_count, owner_count, part)
        .transpose(2, 1, 0, 3)
        .reshape(owner_count, dp_count, extra_count * part)
        .astype(jnp.bfloat16)
    )
    spread = jnp.pad(spread, ((0, 0), (0, 0), (0, -spread.shape[2] % (8 * token_rows))))
    spread = turn(spread, 1).reshape(owner_count, -1, token_rows)
    payload = jnp.concatenate(slices + [spread], 1)
    last = sum(piece.shape[1] for piece in slices)
    cuts = (last - slices[3].shape[1], last)
    everything, mix_here, peer, peer_down = late_sums(
        payload, attention_near, saved[7], mix_away, peer, peer_down, cuts
    )
    shares, (gate_share, up_share, down_share, output) = finish(
        everything,
        [piece.shape[1] for piece in slices],
        mine,
        mine_down,
        peer,
        peer_down,
        hidden,
        mixture,
        mix_here,
    )
    edge = spread.shape[1] // 2
    extras = everything[:, last : last + edge, :token_rows].reshape(owner_count, -1)
    extras = extras[:, : extra_count * part].reshape(owner_count, extra_count, part)
    extras = extras.transpose(1, 0, 2).reshape(extra_count, -1).astype(jnp.float32)
    query_share, key_share, value_share, out_share = shares
    return (
        output,
        grad_tokens,
        extras[expert_count],
        query_share,
        key_share,
        value_share,
        out_share,
        extras[expert_count + 1],
        extras[:expert_count].T,
        gate_share,
        up_share,
        down_share,
    )


def solution(mesh):
    placed = (
        P(("dp", "expert"), None),
        P(("dp", "expert")),
        P(("dp", "expert"), None),
        P("dp"),
        P("dp", None),
        P("dp", None),
        P("dp", None),
        P("dp", None),
        P("dp"),
        P("dp", None),
        P("expert", None, None),
        P("expert", None, None),
        P("expert", None, None),
        P(("dp", "expert"), None),
    )
    owners = mesh.shape["expert"]
    together = mesh.shape["dp"] == 2 and owners >= 8 and owners & (owners - 1) == 0
    return jax.shard_map(
        shards_together if together else shards,
        mesh=mesh,
        in_specs=placed,
        out_specs=(
            P(("dp", "expert"), None),
            P(("dp", "expert"), None),
            P("dp"),
            P("dp", None),
            P("dp", None),
            P("dp", None),
            P("dp", None),
            P("dp"),
            P("dp", None),
            P("expert", "dp", None),
            P("expert", "dp", None),
            P("expert", None, "dp"),
        ),
        check_vma=False,
    )
```

```python
import functools

import jax
import jax.numpy as jnp
from jax import lax
from jax.experimental import pallas as pl
from jax.experimental.pallas import tpu as pltpu
from jax.sharding import PartitionSpec as P

QUERY_HEADS = 16
KEY_VALUE_HEADS = 8
HEAD_DIM = 64
SEQUENCE_LENGTH = 128


EPSILON = 1e-06
SCORE_SCALE = 0.015625
ROPE_BASE = 10000.0
MASKED = -1e30


def product(pattern, left_op, right_op):
    return jnp.einsum(pattern, left_op, right_op, preferred_element_type=jnp.float32)


def matrix_multiply(left_op, right_op):
    return jnp.dot(left_op, right_op, preferred_element_type=jnp.float32)


def rope_tables(seq_len, head_size):
    positions = jnp.arange(seq_len, dtype=jnp.float32)
    exponent = jnp.arange(head_size // 2, dtype=jnp.float32) * (2.0 / head_size)
    angles = positions[:, None] * (ROPE_BASE ** (-exponent))[None, :]
    return (jnp.cos(angles)[None, :, None, :], jnp.sin(angles)[None, :, None, :])


def apply_rotary(values, cosine_table, sine_table):
    middle = values.shape[-1] // 2
    first_half = values[..., :middle]
    second_half = values[..., middle:]
    return jnp.concatenate(
        [
            first_half * cosine_table - second_half * sine_table,
            second_half * cosine_table + first_half * sine_table,
        ],
        -1,
    )


def inverse_rotary(gradient, cosine_table, sine_table):
    middle = gradient.shape[-1] // 2
    first_half = gradient[..., :middle]
    second_half = gradient[..., middle:]
    return jnp.concatenate(
        [
            first_half * cosine_table + second_half * sine_table,
            second_half * cosine_table - first_half * sine_table,
        ],
        -1,
    )


def normalize(values, gain_vec):
    factor = lax.rsqrt(jnp.mean(values * values, -1, keepdims=True) + EPSILON)
    normed = values * factor
    return (normed, factor, (normed * gain_vec).astype(jnp.bfloat16))


def normalize_back(gradient, normed, factor, gain_vec):
    gain_grad = jnp.sum(gradient * normed, 0)
    scaled = gradient * gain_vec
    return (factor * (scaled - normed * jnp.mean(scaled * normed, -1, keepdims=True)), gain_grad)


def segment_mask(segments):
    seq_len = segments.shape[1]
    causal = jnp.arange(seq_len)[:, None] >= jnp.arange(seq_len)[None, :]
    same_doc = segments[:, :, None] == segments[:, None, :]
    return (same_doc & causal[None])[:, None, None]


def score_table(query_rows, key_row_block, mask_tab):
    raw_scores = product("sqhgw,skhw->shgqk", query_rows, key_row_block) * SCORE_SCALE
    return jnp.where(mask_tab, raw_scores, MASKED)


def mixer_forward(tokens, segments, gain_vec, query_mat, key_matrix, value_matrix, out_mat):
    token_rows = tokens.shape[0]
    local_sequences = token_rows // SEQUENCE_LENGTH
    query_groups = QUERY_HEADS // KEY_VALUE_HEADS
    cosine_table, sine_table = rope_tables(SEQUENCE_LENGTH, HEAD_DIM)
    mask_tab = segment_mask(segments.reshape(local_sequences, SEQUENCE_LENGTH))
    residual = tokens.astype(jnp.float32)
    normed, factor, attention_input = normalize(residual, gain_vec)
    query_rows = apply_rotary(
        matrix_multiply(attention_input, query_mat).reshape(
            local_sequences, SEQUENCE_LENGTH, QUERY_HEADS, HEAD_DIM
        ),
        cosine_table,
        sine_table,
    )
    query_rows = query_rows.astype(jnp.bfloat16).reshape(
        local_sequences, SEQUENCE_LENGTH, KEY_VALUE_HEADS, query_groups, HEAD_DIM
    )
    key_row_block = apply_rotary(
        matrix_multiply(attention_input, key_matrix).reshape(
            local_sequences, SEQUENCE_LENGTH, KEY_VALUE_HEADS, HEAD_DIM
        ),
        cosine_table,
        sine_table,
    ).astype(jnp.bfloat16)
    value_row_block = (
        matrix_multiply(attention_input, value_matrix)
        .astype(jnp.bfloat16)
        .reshape(local_sequences, SEQUENCE_LENGTH, KEY_VALUE_HEADS, HEAD_DIM)
    )
    scores = score_table(query_rows, key_row_block, mask_tab)
    row_peak = jnp.max(scores, -1, keepdims=True)
    logsum = row_peak + jnp.log(jnp.sum(jnp.exp(scores - row_peak), -1, keepdims=True))
    weights = jnp.exp(scores - logsum).astype(jnp.bfloat16)
    attended = product("shgqk,skhw->sqhgw", weights, value_row_block).astype(jnp.bfloat16)
    hidden = residual + matrix_multiply(
        attended.reshape(token_rows, QUERY_HEADS * HEAD_DIM), out_mat
    )
    saved = (
        normed,
        factor,
        attention_input,
        query_rows,
        key_row_block,
        value_row_block,
        attended,
        logsum,
        mask_tab,
        cosine_table,
        sine_table,
    )
    return (hidden, saved)


def mixer_backward(grad_hidden, saved, gain_vec, query_mat, key_matrix, value_matrix, out_mat):
    (
        normed,
        factor,
        attention_input,
        query_rows,
        key_row_block,
        value_row_block,
        attended,
        logsum,
        mask_tab,
        cosine_table,
        sine_table,
    ) = saved
    token_rows = grad_hidden.shape[0]
    local_sequences = token_rows // SEQUENCE_LENGTH
    grad_round = grad_hidden.astype(jnp.bfloat16)
    out_grad = matrix_multiply(attended.reshape(token_rows, QUERY_HEADS * HEAD_DIM).T, grad_round)
    grad_attended = (
        matrix_multiply(grad_round, out_mat.T).astype(jnp.bfloat16).reshape(query_rows.shape)
    )
    scores = score_table(query_rows, key_row_block, mask_tab)
    prob_full = jnp.exp(scores - logsum)
    values_gradient = product("shgqk,sqhgw->skhw", prob_full.astype(jnp.bfloat16), grad_attended)
    grad_weights = product("sqhgw,skhw->shgqk", grad_attended, value_row_block)
    row_delta = product("sqhgw,sqhgw->shgq", grad_attended, attended)[..., None]
    grad_scores = (prob_full * (grad_weights - row_delta) * SCORE_SCALE).astype(jnp.bfloat16)
    grad_queries = product("shgqk,skhw->sqhgw", grad_scores, key_row_block)
    keys_gradient = product("shgqk,sqhgw->skhw", grad_scores, query_rows)
    query_grad = inverse_rotary(
        grad_queries.reshape(local_sequences, SEQUENCE_LENGTH, QUERY_HEADS, HEAD_DIM),
        cosine_table,
        sine_table,
    )
    query_grad = query_grad.astype(jnp.bfloat16).reshape(token_rows, QUERY_HEADS * HEAD_DIM)
    key_gradient = (
        inverse_rotary(keys_gradient, cosine_table, sine_table)
        .astype(jnp.bfloat16)
        .reshape(token_rows, KEY_VALUE_HEADS * HEAD_DIM)
    )
    value_gradient = values_gradient.astype(jnp.bfloat16).reshape(
        token_rows, KEY_VALUE_HEADS * HEAD_DIM
    )
    query_wgrad = matrix_multiply(attention_input.T, query_grad)
    key_wgrad = matrix_multiply(attention_input.T, key_gradient)
    value_wgrad = matrix_multiply(attention_input.T, value_gradient)
    grad_attn_input = (
        matrix_multiply(query_grad, query_mat.T)
        + matrix_multiply(key_gradient, key_matrix.T)
        + matrix_multiply(value_gradient, value_matrix.T)
    )
    grad_normed, gain_grad = normalize_back(grad_attn_input, normed, factor, gain_vec)
    return (grad_hidden + grad_normed, gain_grad, query_wgrad, key_wgrad, value_wgrad, out_grad)


def route_weights(expert_input, router_mat, routes):
    logits = matrix_multiply(expert_input, router_mat)
    chosen_hot = (
        routes[:, :, None] == jnp.arange(router_mat.shape[1], dtype=jnp.int32)[None, None, :]
    ).astype(jnp.float32)
    chosen = jnp.sum(chosen_hot * logits[:, None, :], -1)
    return (jax.nn.softmax(chosen, -1), chosen_hot)


def route_back(route_prob, grad_prob, chosen_hot):
    grad_chosen = route_prob * (grad_prob - jnp.sum(route_prob * grad_prob, -1, keepdims=True))
    return jnp.sum(chosen_hot * grad_chosen[:, :, None], 1).astype(jnp.bfloat16)


def expert_forward(owner_rows, gate_mat, up_mat, down_mat):
    gate_pre = product("erd,edf->erf", owner_rows, gate_mat)
    up_pre = product("erd,edf->erf", owner_rows, up_mat)
    gate_sig = jax.nn.sigmoid(gate_pre)
    gate_act = gate_pre * gate_sig
    inner_acts = (gate_act * up_pre).astype(jnp.bfloat16)
    expert_out = product("erf,efd->erd", inner_acts, down_mat).astype(jnp.bfloat16)
    return (expert_out, (gate_pre, up_pre, gate_sig, gate_act, inner_acts))


def expert_backward(grad_rows, owner_rows, kept_acts, gate_mat, up_mat, down_mat):
    gate_pre, up_pre, gate_sig, gate_act, inner_acts = kept_acts
    grad_inner = product("erd,efd->erf", grad_rows, down_mat)
    down_grad = product("erf,erd->efd", inner_acts, grad_rows)
    silu_slope = gate_sig * (1.0 + gate_pre * (1.0 - gate_sig))
    grad_gate = (grad_inner * up_pre * silu_slope).astype(jnp.bfloat16)
    grad_up = (grad_inner * gate_act).astype(jnp.bfloat16)
    gate_grad = product("erd,erf->edf", owner_rows, grad_gate)
    up_grad = product("erd,erf->edf", owner_rows, grad_up)
    grad_owner_rows = product("erf,edf->erd", grad_gate, gate_mat) + product(
        "erf,edf->erd", grad_up, up_mat
    )
    return (grad_owner_rows.astype(jnp.bfloat16), gate_grad, up_grad, down_grad)


def gather_dp(local_part):
    dp_count = lax.axis_size("dp")
    owner_count = lax.axis_size("expert")
    if dp_count != 2 or owner_count % 2:
        return lax.all_gather(local_part, "dp", axis=0, tiled=True)
    low, high = jnp.split(local_part, 2, 0)
    even = lax.axis_index("expert") % 2 == 0
    near = lax.ppermute(jnp.where(even, low, high), "dp", [(0, 1), (1, 0)])
    far = lax.ppermute(near, "expert", [(i, i ^ 1) for i in range(owner_count)])
    other = jnp.concatenate([jnp.where(even, near, far), jnp.where(even, far, near)], 0)
    first = lax.axis_index("dp") == 0
    return jnp.concatenate(
        [jnp.where(first, local_part, other), jnp.where(first, other, local_part)], 0
    )


def all_sums(partial):
    owner_count = lax.axis_size("expert")
    dp_count = lax.axis_size("dp")
    width = partial.shape[1]
    pieces = partial.astype(jnp.bfloat16).reshape(dp_count, owner_count, -1, width)
    piece = lax.psum_scatter(
        pieces.transpose(1, 0, 2, 3).reshape(-1, width), "expert", scatter_dimension=0, tiled=True
    )
    piece = scatter_dp(piece, 0).astype(jnp.bfloat16)
    return lax.all_gather(piece, "expert", axis=0, tiled=True).astype(jnp.float32)


def scatter_dp(partial, axis):
    dp_count = lax.axis_size("dp")
    rounded = partial.astype(jnp.bfloat16)
    if dp_count != 2:
        return lax.psum_scatter(rounded, "dp", scatter_dimension=axis, tiled=True).astype(
            jnp.float32
        )
    low, high = jnp.split(rounded, 2, axis)
    first = lax.axis_index("dp") == 0
    arrived = lax.ppermute(jnp.where(first, high, low), "dp", [(0, 1), (1, 0)])
    return jnp.where(first, low, high).astype(jnp.float32) + arrived.astype(jnp.float32)


def shards(
    tokens,
    segments,
    routes,
    first_gain,
    query_weight,
    key_projection_weight,
    value_projection_weight,
    out_weight,
    second_gain,
    router_weight,
    gate_weight,
    up_weight,
    down_weight,
    cotangent,
):
    token_rows, model_width = tokens.shape
    top_count = routes.shape[1]
    expert_count = router_weight.shape[1]
    owner_count = lax.axis_size("expert")
    local_count = gate_weight.shape[0]
    key_width = key_projection_weight.shape[1]
    query_width = query_weight.shape[1]
    capacity = 5 * token_rows * top_count // (4 * expert_count)
    row_part = router_weight.shape[0]

    small = jnp.concatenate(
        [router_weight, first_gain[:, None], second_gain[:, None]], 1
    )
    small_mat = gather_dp(small)
    router_mat = small_mat[:, :expert_count]
    gain_first = small_mat[:, expert_count]
    gain_second = small_mat[:, expert_count + 1]
    joined_mat = gather_dp(
        jnp.concatenate([query_weight, key_projection_weight, value_projection_weight], 1)
    )
    query_mat = joined_mat[:, :query_width]
    key_matrix = joined_mat[:, query_width : query_width + key_width]
    value_matrix = joined_mat[:, query_width + key_width :]
    out_mat = gather_dp(out_weight)

    routes_all = lax.all_gather(routes, "expert")
    cotangent_all = lax.all_gather(cotangent, "expert")

    mine = lax.axis_index("expert") * local_count + jnp.arange(local_count, dtype=jnp.int32)
    hit = jnp.any(routes_all[None] == mine[:, None, None, None], -1)
    before = (
        jnp.arange(token_rows)[:, None] < jnp.arange(token_rows)[None, :]
    ).astype(jnp.bfloat16)
    rank = product("lst,tu->lsu", hit.astype(jnp.bfloat16), before).astype(jnp.int32)
    slot = jnp.where(hit, rank, -1)
    picked = slot[:, :, None, :] == jnp.arange(capacity, dtype=jnp.int32)[None, None, :, None]
    pick = picked.astype(jnp.bfloat16)

    def rows_of(gathered):
        rows = product("lsct,std->lscd", pick, gathered)
        return rows.reshape(local_count, owner_count * capacity, model_width)

    own_hot = (routes[:, :, None] == jnp.arange(expert_count, dtype=jnp.int32)).any(1)
    own_rank = matrix_multiply(before.T, own_hot.astype(jnp.bfloat16)).astype(jnp.int32)
    own_slot = jnp.where(own_hot, own_rank, -1)
    own_pick = (
        own_slot[:, :, None] == jnp.arange(capacity, dtype=jnp.int32)[None, None, :]
    ).astype(jnp.bfloat16)

    def send_back(rows):
        shaped = rows.reshape(local_count, owner_count, capacity, model_width)
        return lax.all_to_all(
            shaped.transpose(1, 0, 2, 3).reshape(expert_count, capacity, model_width),
            "expert",
            split_axis=0,
            concat_axis=0,
            tiled=True,
        )

    def sum_back(returned):
        flat = returned.reshape(expert_count * capacity, model_width)
        return matrix_multiply(own_pick.reshape(token_rows, expert_count * capacity), flat)

    hidden, saved = mixer_forward(
        tokens, segments, gain_first, query_mat, key_matrix, value_matrix, out_mat
    )
    normed_second, factor_second, expert_input = normalize(hidden, gain_second)
    input_all = lax.all_gather(expert_input, "expert")
    route_prob, chosen_hot = route_weights(expert_input, router_mat, routes)
    dense_prob = jnp.sum(chosen_hot * route_prob[:, :, None], 1)
    prob_all = lax.all_gather(dense_prob, "expert")

    column = jnp.arange(expert_count, dtype=jnp.int32)
    my_column = (mine[:, None] == column[None, :]).astype(jnp.float32)
    my_prob = jnp.sum(prob_all[None] * my_column[:, None, None, :], -1)
    row_prob = jnp.sum(jnp.where(picked, my_prob[:, :, None, :], 0.0), -1).reshape(
        local_count, owner_count * capacity, 1
    )

    owner_rows = rows_of(input_all).astype(jnp.bfloat16)
    cotangent_rows = rows_of(cotangent_all).astype(jnp.bfloat16).astype(jnp.float32)
    expert_out, kept_acts = expert_forward(owner_rows, gate_weight, up_weight, down_weight)
    expert_out = expert_out.astype(jnp.float32)
    weighted = (row_prob * expert_out).astype(jnp.bfloat16)
    row_grad_prob = jnp.sum(expert_out * cotangent_rows, -1).reshape(
        local_count, owner_count, capacity
    )
    token_grad_prob = jnp.sum(jnp.where(picked, row_grad_prob[..., None], 0.0), 2)
    back_prob = lax.all_to_all(
        token_grad_prob.transpose(1, 0, 2).reshape(expert_count, token_rows),
        "expert",
        split_axis=0,
        concat_axis=0,
        tiled=True,
    )
    grad_prob = jnp.sum(chosen_hot * back_prob.T[:, None, :], -1)
    grad_output = cotangent.astype(jnp.float32)

    grad_rows = (row_prob * cotangent_rows).astype(jnp.bfloat16)
    grad_owner_rows, gate_grad, up_grad, down_grad = expert_backward(
        grad_rows, owner_rows, kept_acts, gate_weight, up_weight, down_weight
    )
    grad_back = send_back(grad_owner_rows)
    expert_shares = (
        scatter_dp(gate_grad, 1),
        scatter_dp(up_grad, 1),
        scatter_dp(down_grad, 2),
    )
    grad_back, expert_shares, weighted = lax.optimization_barrier(
        (grad_back, expert_shares, weighted)
    )
    forward_back = send_back(weighted)
    output = (hidden + sum_back(forward_back)).astype(jnp.bfloat16)
    backward_sum = sum_back(grad_back)
    router_grad = route_back(route_prob, grad_prob, chosen_hot)
    grad_expert_input = backward_sum + matrix_multiply(
        router_grad, router_mat.T
    )
    router_wgrad = matrix_multiply(router_grad.T, expert_input)
    grad_normed, second_gain_grad = normalize_back(
        grad_expert_input, normed_second, factor_second, gain_second
    )
    grad_hidden = grad_output + grad_normed
    grad_tokens, first_gain_grad, query_wgrad, key_wgrad, value_wgrad, out_wgrad = mixer_backward(
        grad_hidden, saved, gain_first, query_mat, key_matrix, value_matrix, out_mat
    )

    out_share = all_sums(out_wgrad)
    joined = all_sums(jnp.concatenate([query_wgrad, key_wgrad, value_wgrad], 1))
    query_share = joined[:, :query_width]
    key_share = joined[:, query_width : query_width + key_width]
    value_share = joined[:, query_width + key_width :]
    extras = jnp.concatenate(
        [router_wgrad, first_gain_grad[None, :], second_gain_grad[None, :]], 0
    )
    extras = lax.psum(extras.astype(jnp.bfloat16), ("dp", "expert"))
    extras = lax.dynamic_slice_in_dim(
        extras, lax.axis_index("dp") * row_part, row_part, 1
    ).astype(jnp.float32)
    router_share = extras[:expert_count].T
    first_share = extras[expert_count]
    second_share = extras[expert_count + 1]
    return (
        output,
        grad_tokens,
        first_share,
        query_share,
        key_share,
        value_share,
        out_share,
        second_share,
        router_share,
        expert_shares[0],
        expert_shares[1],
        expert_shares[2],
    )


def turn(values, axis):
    if lax.axis_size("dp") != 2:
        return values
    low, high = jnp.split(values, 2, axis)
    first = lax.axis_index("dp") == 0
    return jnp.concatenate([jnp.where(first, low, high), jnp.where(first, high, low)], axis)


def times(left_op, pieces):
    total, start = None, 0
    for piece in pieces:
        part = matrix_multiply(left_op[:, start : start + piece.shape[0]], piece)
        total = part if total is None else total + part
        start += piece.shape[0]
    return total


def times_back(left_op, pieces):
    return jnp.concatenate([matrix_multiply(left_op, piece.T) for piece in pieces], 1)


def halves_forward(tokens, segments, gain_vec, query_mat, key_matrix, value_matrix, out_mat):
    token_rows = tokens.shape[0]
    local_sequences = token_rows // SEQUENCE_LENGTH
    query_groups = QUERY_HEADS // KEY_VALUE_HEADS
    cosine_table, sine_table = rope_tables(SEQUENCE_LENGTH, HEAD_DIM)
    mask_tab = segment_mask(segments.reshape(local_sequences, SEQUENCE_LENGTH))
    residual = tokens.astype(jnp.float32)
    normed, factor, attention_input = normalize(turn(residual, 1), gain_vec)
    query_rows = apply_rotary(
        times(attention_input, query_mat).reshape(
            local_sequences, SEQUENCE_LENGTH, QUERY_HEADS, HEAD_DIM
        ),
        cosine_table,
        sine_table,
    )
    query_rows = query_rows.astype(jnp.bfloat16).reshape(
        local_sequences, SEQUENCE_LENGTH, KEY_VALUE_HEADS, query_groups, HEAD_DIM
    )
    key_row_block = apply_rotary(
        times(attention_input, key_matrix).reshape(
            local_sequences, SEQUENCE_LENGTH, KEY_VALUE_HEADS, HEAD_DIM
        ),
        cosine_table,
        sine_table,
    ).astype(jnp.bfloat16)
    value_row_block = (
        times(attention_input, value_matrix)
        .astype(jnp.bfloat16)
        .reshape(local_sequences, SEQUENCE_LENGTH, KEY_VALUE_HEADS, HEAD_DIM)
    )
    scores = score_table(query_rows, key_row_block, mask_tab)
    row_peak = jnp.max(scores, -1, keepdims=True)
    logsum = row_peak + jnp.log(jnp.sum(jnp.exp(scores - row_peak), -1, keepdims=True))
    weights = jnp.exp(scores - logsum).astype(jnp.bfloat16)
    attended = product("shgqk,skhw->sqhgw", weights, value_row_block).astype(jnp.bfloat16)
    turned = turn(attended.reshape(token_rows, QUERY_HEADS * HEAD_DIM), 1)
    hidden = residual + times(turned, out_mat)
    saved = (
        normed,
        factor,
        attention_input,
        query_rows,
        key_row_block,
        value_row_block,
        attended,
        turned,
        logsum,
        mask_tab,
        cosine_table,
        sine_table,
    )
    return (hidden, saved)


def halves_backward(grad_hidden, saved, gain_vec, query_mat, key_matrix, value_matrix, out_mat):
    (
        normed,
        factor,
        attention_input,
        query_rows,
        key_row_block,
        value_row_block,
        attended,
        _,
        logsum,
        mask_tab,
        cosine_table,
        sine_table,
    ) = saved
    token_rows = grad_hidden.shape[0]
    local_sequences = token_rows // SEQUENCE_LENGTH
    grad_round = grad_hidden.astype(jnp.bfloat16)
    grad_attended = (
        turn(times_back(grad_round, out_mat).astype(jnp.bfloat16), 1).reshape(query_rows.shape)
    )
    scores = score_table(query_rows, key_row_block, mask_tab)
    prob_full = jnp.exp(scores - logsum)
    values_gradient = product("shgqk,sqhgw->skhw", prob_full.astype(jnp.bfloat16), grad_attended)
    grad_weights = product("sqhgw,skhw->shgqk", grad_attended, value_row_block)
    row_delta = product("sqhgw,sqhgw->shgq", grad_attended, attended)[..., None]
    grad_scores = (prob_full * (grad_weights - row_delta) * SCORE_SCALE).astype(jnp.bfloat16)
    grad_queries = product("shgqk,skhw->sqhgw", grad_scores, key_row_block)
    keys_gradient = product("shgqk,sqhgw->skhw", grad_scores, query_rows)
    query_grad = inverse_rotary(
        grad_queries.reshape(local_sequences, SEQUENCE_LENGTH, QUERY_HEADS, HEAD_DIM),
        cosine_table,
        sine_table,
    )
    query_grad = query_grad.astype(jnp.bfloat16).reshape(token_rows, QUERY_HEADS * HEAD_DIM)
    key_gradient = (
        inverse_rotary(keys_gradient, cosine_table, sine_table)
        .astype(jnp.bfloat16)
        .reshape(token_rows, KEY_VALUE_HEADS * HEAD_DIM)
    )
    value_gradient = values_gradient.astype(jnp.bfloat16).reshape(
        token_rows, KEY_VALUE_HEADS * HEAD_DIM
    )
    grad_attn_input = (
        times_back(query_grad, query_mat)
        + times_back(key_gradient, key_matrix)
        + times_back(value_gradient, value_matrix)
    )
    grad_normed, gain_grad = normalize_back(grad_attn_input, normed, factor, gain_vec)
    return (
        grad_hidden + turn(grad_normed, 1),
        turn(gain_grad, 0),
        [query_grad, key_gradient, value_gradient, grad_round],
    )


MESH = pl.DeviceIdType.MESH


def quotient(index, by):
    return index // by if isinstance(index, int) else lax.div(index, jnp.int32(by))


def parity(index):
    return index % 2 if isinstance(index, int) else lax.rem(index, jnp.int32(2))


def flip(index, by):
    if isinstance(index, int) and isinstance(by, int):
        return index ^ by
    if isinstance(index, int):
        index, by = by, index
    total, weight = (index, 1) if isinstance(by, int) else (0, 1)
    for _ in range(6):
        if isinstance(by, int):
            if by & weight:
                total = total + weight - 2 * weight * parity(quotient(index, weight))
        else:
            one, two = parity(quotient(index, weight)), parity(quotient(by, weight))
            total = total + weight * (one + two - 2 * one * two)
        weight *= 2
    return total


def others(count, act):
    for by in range(1, count):
        act(by)


def expert_at(index):
    return {"expert": index}


def send(src, dst, send_sem, recv_sem, where):
    return pltpu.make_async_remote_copy(
        src_ref=src,
        dst_ref=dst,
        send_sem=send_sem,
        recv_sem=recv_sem,
        device_id=where,
        device_id_type=MESH,
    )


def meet(count, with_dp):
    barrier = pltpu.get_barrier_semaphore()
    me = lax.axis_index("expert")

    def greet(by):
        pl.semaphore_signal(
            barrier, inc=1, device_id=expert_at(flip(me, by)), device_id_type=MESH
        )

    others(count, greet)
    if with_dp:
        pl.semaphore_signal(
            barrier, inc=1, device_id={"dp": 1 - lax.axis_index("dp")}, device_id_type=MESH
        )
    pl.semaphore_wait(barrier, count - 1 + (1 if with_dp else 0))


class Gather:
    def __init__(self, own, block_of, count, send_sems, recv_sems):
        self.own, self.block_of, self.count = own, block_of, count
        self.send_sems, self.recv_sems = send_sems, recv_sems
        self.me = lax.axis_index("expert")

    def copy(self, rel, by, src=None):
        block = self.block_of(flip(self.me, rel))
        there = flip(rel, by)
        return send(
            block if src is None else src,
            block,
            self.send_sems.at[there],
            self.recv_sems.at[there],
            expert_at(flip(self.me, by)),
        )

    def wait(self, rel):
        block = self.block_of(flip(self.me, rel))
        send(
            block, block, self.send_sems.at[rel], self.recv_sems.at[rel], expert_at(self.me)
        ).wait_recv()

    def begin(self, held=()):
        for by in list(range(8, self.count, 4)) + [4, 2, 1]:
            if by < self.count and by not in held:
                self.copy(0, by, self.own).start()

    def release(self, by):
        self.copy(0, by, self.own).start()

    def pass_z(self, rel):
        self.wait(rel)
        self.copy(rel, 2).start()
        self.copy(rel, 1).start()

    def pass_x(self, rel):
        self.wait(rel + 2)
        self.copy(rel + 2, 1).start()

    def wait_sends(self):
        for rel in range(1, self.count):
            block = self.block_of(flip(self.me, rel))
            send(
                block, block, self.send_sems.at[rel], self.recv_sems.at[rel], expert_at(self.me)
            ).wait_send()

    def rest(self):
        far = list(range(12, self.count, 4))
        near = [rel for rel in (8, 4) if rel < self.count]
        self.pass_x(0)
        self.pass_z(near[0])
        for by in far:
            self.release(by)
        for rel in near[1:]:
            self.pass_z(rel)
        for rel in near:
            self.pass_x(rel)
        for rel in far:
            self.pass_z(rel)
            self.pass_x(rel)
        for rel in range(1, self.count, 2):
            self.wait(rel)
        self.wait_sends()


def front_kernel(pieces, *refs):
    mine, refs = refs[:pieces], refs[pieces:]
    tokens, refs = refs[0], refs[1:]
    fetched, refs = refs[:pieces], refs[pieces:]
    tokens_all, y_send, y_recv, c_send, c_recv, t_send, t_recv, local = refs
    rows = tokens.shape[0]
    me, dp = lax.axis_index("expert"), lax.axis_index("dp")
    core = parity(me)
    meet(4, True)

    def part(ref, which):
        half = ref.shape[0] // 2
        return ref.at[pl.ds(pl.multiple_of(which * half, half), half)]

    over_y = [
        send(
            part(mine[i], core),
            part(fetched[i], core),
            y_send.at[i],
            y_recv.at[i],
            {"dp": 1 - dp},
        )
        for i in range(pieces)
    ]
    for copy in over_y:
        copy.start()

    def at_place(index):
        place = index - 4 * quotient(index, 4)
        return tokens_all.at[pl.ds(pl.multiple_of(place * rows, rows), rows)]

    keep = pltpu.make_async_copy(tokens, at_place(me), local)
    keep.start()
    gather = Gather(tokens, at_place, 4, t_send, t_recv)
    gather.begin()
    over_core = [
        send(
            part(fetched[i], core),
            part(fetched[i], core),
            c_send.at[i],
            c_recv.at[i],
            expert_at(flip(me, 1)),
        )
        for i in range(pieces)
    ]
    gather.pass_x(0)
    for i in range(pieces):
        over_y[i].wait_recv()
        over_core[i].start()
    gather.wait(1)
    gather.wait(3)
    gather.wait_sends()
    keep.wait()
    for i in range(pieces):
        send(
            part(mine[i], 1 - core),
            part(fetched[i], 1 - core),
            c_send.at[i],
            c_recv.at[i],
            expert_at(flip(me, 1)),
        ).wait_recv()
        over_core[i].wait_send()
        over_y[i].wait_send()


def front(own, tokens):
    pieces = len(own)
    rows, width = tokens.shape
    anywhere = pl.BlockSpec(memory_space=pl.ANY)
    results = pl.pallas_call(
        functools.partial(front_kernel, pieces),
        out_shape=[jax.ShapeDtypeStruct(part.shape, part.dtype) for part in own]
        + [jax.ShapeDtypeStruct((4 * rows, width), tokens.dtype)],
        in_specs=[anywhere] * (pieces + 1),
        out_specs=[anywhere] * (pieces + 1),
        scratch_shapes=[pltpu.SemaphoreType.DMA((pieces,)) for _ in range(4)]
        + [pltpu.SemaphoreType.DMA((4,)), pltpu.SemaphoreType.DMA((4,))]
        + [pltpu.SemaphoreType.DMA],
        compiler_params=pltpu.CompilerParams(collective_id=0, has_side_effects=True),
        name="front",
    )(*own, tokens)
    return results[:pieces], results[pieces]


def finish_kernel(heights, away, *refs):
    all_ref, mine, mine_down, peer, peer_down, hidden, mixture = refs[:7]
    pieces, refs = refs[7], refs[8:]
    shares, refs = refs[: len(heights)], refs[len(heights) :]
    gate_out, up_out, down_out, output = refs
    start = 0
    for height, out in zip(heights, shares):
        for index in range(0, all_ref.shape[0], 128 // height):
            block = all_ref[index : index + 128 // height, start : start + height, :]
            block = block.astype(jnp.float32).reshape(128, block.shape[2])
            out[:, index * height : index * height + 128] = block.T
        start += height
    gate_out[0] = mine[0] + peer[0].astype(jnp.float32)
    up_out[0] = mine[1] + peer[1].astype(jnp.float32)
    down_out[0] = mine_down[...] + peer_down[...].astype(jnp.float32)
    total = hidden[...] + mixture[...]
    for index in range(away):
        total = total + pieces[index].astype(jnp.float32)
    output[...] = total.astype(jnp.bfloat16)


def finish(everything, heights, mine, mine_down, peer, peer_down, hidden, mixture, pieces):
    count, lines, half = everything.shape
    parts = 4
    rows, width = hidden.shape
    deep = mine.shape[2]
    tile, low, some = half // parts, deep // parts, rows // parts
    three = pl.BlockSpec((2, tile, deep), lambda i: (0, i, 0))
    down = pl.BlockSpec((low, half), lambda i: (i, 0))
    tokens = pl.BlockSpec((some, width), lambda i: (i, 0))
    f32 = jnp.float32
    results = pl.pallas_call(
        functools.partial(finish_kernel, heights, pieces.shape[0]),
        grid=(parts,),
        out_shape=[jax.ShapeDtypeStruct((half, count * height), f32) for height in heights]
        + [
            jax.ShapeDtypeStruct((1, half, deep), f32),
            jax.ShapeDtypeStruct((1, half, deep), f32),
            jax.ShapeDtypeStruct((1, deep, half), f32),
            jax.ShapeDtypeStruct((rows, width), jnp.bfloat16),
        ],
        in_specs=[pl.BlockSpec((count, lines, tile), lambda i: (0, 0, i))]
        + [three, down, three, down, tokens, tokens]
        + [pl.BlockSpec((pieces.shape[0], some, width), lambda i: (0, i, 0))],
        out_specs=[pl.BlockSpec((tile, count * height), lambda i: (i, 0)) for height in heights]
        + [
            pl.BlockSpec((1, tile, deep), lambda i: (0, i, 0)),
            pl.BlockSpec((1, tile, deep), lambda i: (0, i, 0)),
            pl.BlockSpec((1, low, half), lambda i: (0, i, 0)),
            tokens,
        ],
        compiler_params=pltpu.CompilerParams(vmem_limit_bytes=58 * 2**20),
        name="finish",
    )(everything, mine, mine_down, peer, peer_down, hidden, mixture, pieces)
    return results[: len(heights)], results[len(heights) :]


def dot_on(left_op, right_op, left_axis, right_axis):
    return lax.dot_general(
        left_op,
        right_op,
        (((left_axis,), (right_axis,)), ((), ())),
        preferred_element_type=jnp.float32,
    )


def experts_kernel(
    count,
    own_ref,
    cot_ref,
    prob_ref,
    gate_ref,
    up_ref,
    down_ref,
    grad_out,
    mix_out,
    mix_away,
    gp_out,
    mine_out,
    mine_down,
    peer_out,
    peer_down,
    x_all,
    prob_all,
    gp_send_buf,
    both_all,
    inner_all,
    ge_all,
    part,
    cbuf,
    xbuf,
    zbuf,
    a_send,
    a_recv,
    p_send,
    p_recv,
    q_send,
    q_recv,
    c_send,
    c_recv,
    x_send,
    x_recv,
    z_send,
    z_recv,
):
    rows, width = own_ref.shape
    hidden = gate_ref.shape[2]
    pair = 2 * rows
    steps = count // 2
    depth = count // 4
    order = [0] + [z for z in (2, 1) if z < depth] + list(range(3, depth))
    me, dp = lax.axis_index("expert"), lax.axis_index("dp")
    core = parity(me)
    meet(count, False)

    def block_of(index):
        return x_all.at[pl.ds(pl.multiple_of(index * rows, rows), rows)]

    gather = Gather(own_ref, block_of, count, a_send, a_recv)
    gather.begin(range(12, count, 4))

    def prob_copy(by):
        there = flip(me, by)
        return send(
            prob_ref.at[there], prob_all.at[me], p_send.at[by], p_recv.at[by], expert_at(there)
        )

    def prob_start(by):
        prob_copy(by).start()

    others(count, prob_start)
    x_all[pl.ds(pl.multiple_of(me * rows, rows), rows)] = own_ref[...]
    prob_all[me] = prob_ref[me]

    def prob_wait(by):
        there = flip(me, by)
        send(
            prob_ref.at[me], prob_all.at[there], p_send.at[by], p_recv.at[by], expert_at(there)
        ).wait_recv()

    others(count, prob_wait)

    def rel_of(step):
        z_rel = quotient(step, 2)
        x_rel = jnp.where(step < 2, parity(step), 1 - parity(step))
        z_rel = sum(jnp.where(z_rel == at, z, 0) for at, z in enumerate(order))
        return 4 * z_rel + 2 * x_rel, z_rel

    eye = (
        lax.broadcasted_iota(jnp.int32, (pair, pair), 0)
        == lax.broadcasted_iota(jnp.int32, (pair, pair), 1)
    )
    theirs = pl.ds(pl.multiple_of((1 - core) * rows, rows), rows)
    ours = pl.ds(pl.multiple_of(core * rows, rows), rows)

    def core_copy(step):
        return send(
            part.at[step, :, theirs],
            cbuf.at[step],
            c_send.at[step],
            c_recv.at[step],
            expert_at(flip(me, 1)),
        )

    def x_copy(step, z_rel, which):
        return send(
            part.at[step, which, ours],
            xbuf.at[z_rel, which],
            x_send.at[which, z_rel],
            x_recv.at[which, z_rel],
            expert_at(flip(me, 2)),
        )

    def z_copy(step, z_rel):
        return send(
            part.at[step, 0, ours],
            zbuf.at[z_rel],
            z_send.at[z_rel],
            z_recv.at[z_rel],
            expert_at(flip(me, 4 * z_rel)),
        )

    def compute(step):
        rel, _ = rel_of(step)
        chip = quotient(flip(me, rel), 2)
        where = pl.ds(pl.multiple_of(chip * pair, pair), pair)
        x = x_all[where, :]
        gate_pre = dot_on(x, gate_ref[0], 1, 0)
        up_pre = dot_on(x, up_ref[0], 1, 0)
        sig = jax.nn.sigmoid(gate_pre)
        act = gate_pre * sig
        inner = (act * up_pre).astype(jnp.bfloat16)
        inner_all[where, :] = inner
        out = dot_on(inner, down_ref[0], 1, 0).astype(jnp.bfloat16).astype(jnp.float32)
        prob_row = jnp.concatenate(
            [prob_all[2 * chip, 0:1, :], prob_all[2 * chip + 1, 0:1, :]], 1
        )
        prob = jnp.sum(jnp.where(eye, prob_row, 0.0), 1, keepdims=True)
        cot = cot_ref[where, :].astype(jnp.float32)
        part[step, 1] = (prob * out).astype(jnp.bfloat16)
        gp = jnp.sum(out * cot, 1, keepdims=True)
        gp_row = jnp.sum(jnp.where(eye, gp, 0.0), 0, keepdims=True)
        gp_send_buf[2 * chip] = jnp.broadcast_to(gp_row[:, :rows], (8, rows))
        gp_send_buf[2 * chip + 1] = jnp.broadcast_to(gp_row[:, rows:], (8, rows))
        ge = (prob * cot).astype(jnp.bfloat16)
        ge_all[where, :] = ge
        gi = dot_on(ge, down_ref[0], 1, 1)
        slope = sig * (1.0 + gate_pre * (1.0 - sig))
        gg = (gi * up_pre * slope).astype(jnp.bfloat16)
        gu = (gi * act).astype(jnp.bfloat16)
        both_all[where, :hidden] = gg
        both_all[where, hidden:] = gu
        part[step, 0] = (dot_on(gg, gate_ref[0], 1, 1) + dot_on(gu, up_ref[0], 1, 1)).astype(
            jnp.bfloat16
        )

    def add_core(step):
        core_copy(step).wait_recv()
        total = part[step, :, ours].astype(jnp.float32) + cbuf[step].astype(jnp.float32)
        part[step, :, ours] = total.astype(jnp.bfloat16)

    def add_x(at):
        z_rel, step = order[at], 2 * at + 1
        x_copy(step, z_rel, 0).wait_recv()
        total = part[step, 0, ours].astype(jnp.float32) + xbuf[z_rel, 0].astype(jnp.float32)
        part[step, 0, ours] = total.astype(jnp.bfloat16)
        z_copy(step, z_rel).start()

    def on(step, number):
        return pl.when(step == number)

    def turn_of(step, carry):
        rel, _ = rel_of(step)

        for at in range(1, depth):

            @on(step, 2 * at)
            def _(at=at):
                if at == 1:
                    gather.pass_x(4 * order[1])

        gather.wait(rel + 1)
        compute(step)
        core_copy(step).start()

        @on(step, 0)
        def _():
            gather.pass_x(0)

        @on(step, 1)
        def _():
            gather.pass_z(4 * order[1])
            for by in range(12, count, 4):
                gather.release(by)
            if depth > 2:
                gather.pass_z(4 * order[2])
            add_core(0)
            add_core(1)

        for at in range(1, depth):

            @on(step, 2 * at)
            def _(at=at):
                if at > 1:
                    add_core(2 * at - 1)
                    x_copy(2 * at - 2, order[at - 1], 1).start()
                if at > 1 and at + 1 < depth:
                    gather.pass_z(4 * order[at + 1])

            @on(step, 2 * at + 1)
            def _(at=at):
                add_core(2 * at)
                x_copy(2 * at, order[at], 0).start()
                if at + 1 < depth:
                    gather.pass_x(4 * order[at + 1])

        if depth > 3:

            @on(step, 6)
            def _():
                add_x(1)

        return carry

    lax.fori_loop(0, steps, turn_of, 0)
    add_core(steps - 1)
    x_copy(1, 0, 0).start()
    x_copy(steps - 2, order[-1], 1).start()
    x_copy(1, 0, 1).start()
    for at in range(2 if depth > 3 else 1, depth - 1):
        add_x(at)

    def gp_copy(by):
        there = flip(me, by)
        return send(
            gp_send_buf.at[there], gp_out.at[me], q_send.at[by], q_recv.at[by], expert_at(there)
        )

    def gp_start(by):
        gp_copy(by).start()

    others(count, gp_start)
    gp_out[me] = gp_send_buf[me]

    half = width // 2
    for turn_at, (which, target, lower) in enumerate( ((1 - dp, peer_out, peer_down), (dp, mine_out, mine_down))
    ):

        def rows_of(index, carry, which=which, target=target):
            tile = half // 2
            at = pl.multiple_of(which * half + index * tile, tile)
            into = pl.ds(pl.multiple_of(index * tile, tile), tile)
            x = x_all[:, pl.ds(at, tile)]
            both = dot_on(x, both_all[...], 0, 0).astype(target.dtype)
            target[0, into, :] = both[:, :hidden]
            target[1, into, :] = both[:, hidden:]
            return carry

        lax.fori_loop(0, 2, rows_of, 0)

        def down_of(index, carry, which=which, lower=lower):
            tile = hidden // 2
            at = pl.ds(pl.multiple_of(index * tile, tile), tile)
            grads = ge_all[:, pl.ds(pl.multiple_of(which * half, half), half)]
            lower[at, :] = dot_on(inner_all[:, at], grads, 0, 0).astype(lower.dtype)
            return carry

        lax.fori_loop(0, 2, down_of, 0)
        if turn_at == 0:
            add_x(depth - 1)

    def from_x(at, which):
        step = 2 * at + 1 if at else 0
        x_copy(step, order[at], which).wait_recv()
        return part[step, which, ours].astype(jnp.float32) + xbuf[order[at], which].astype(
            jnp.float32
        )

    for at in range(1, depth):
        mix_away[order[at] - 1] = from_x(at, 1).astype(jnp.bfloat16)
    mix_out[...] = from_x(0, 1)
    grads = from_x(0, 0)
    for z_rel in range(1, depth):
        z_copy(0, z_rel).wait_recv()
        grads = grads + zbuf[z_rel].astype(jnp.float32)
    grad_out[...] = grads

    def settle(by):
        there = flip(me, by)
        send(
            gp_send_buf.at[me], gp_out.at[there], q_send.at[by], q_recv.at[by], expert_at(there)
        ).wait()
        prob_copy(by).wait_send()

    others(count, settle)
    gather.wait_sends()
    for step in range(steps):
        core_copy(step).wait_send()
    for z_rel in range(depth):
        x_copy(0, z_rel, 0).wait_send()
        x_copy(0, z_rel, 1).wait_send()
    for z_rel in range(1, depth):
        z_copy(0, z_rel).wait_send()


def experts(expert_input, cotangent_all, prob, gate_weight, up_weight, down_weight):
    count = prob.shape[0]
    rows, width = expert_input.shape
    hidden = gate_weight.shape[2]
    total = count * rows
    steps, depth = count // 2, count // 4
    half = width // 2
    local = pl.BlockSpec(memory_space=pltpu.VMEM)
    shapes = ((count,), (count,), (count,), (steps,), (2, depth), (depth,))
    pairs = [pltpu.SemaphoreType.DMA(shape) for shape in shapes]
    semaphores = [item for item in pairs for _ in range(2)]
    bf16 = jnp.bfloat16
    return pl.pallas_call(
        functools.partial(experts_kernel, count),
        out_shape=[
            jax.ShapeDtypeStruct((rows, width), jnp.float32),
            jax.ShapeDtypeStruct((rows, width), jnp.float32),
            jax.ShapeDtypeStruct((depth - 1, rows, width), bf16),
            jax.ShapeDtypeStruct((count, 8, rows), jnp.float32),
            jax.ShapeDtypeStruct((2, half, hidden), jnp.float32),
            jax.ShapeDtypeStruct((hidden, half), jnp.float32),
            jax.ShapeDtypeStruct((2, half, hidden), bf16),
            jax.ShapeDtypeStruct((hidden, half), bf16),
        ],
        in_specs=[local] * 6,
        out_specs=[local] * 8,
        scratch_shapes=[
            pltpu.VMEM((total, width), bf16),
            pltpu.VMEM((count, 8, rows), jnp.float32),
            pltpu.VMEM((count, 8, rows), jnp.float32),
            pltpu.VMEM((total, 2 * hidden), bf16),
            pltpu.VMEM((total, hidden), bf16),
            pltpu.VMEM((total, width), bf16),
            pltpu.VMEM((steps, 2, 2 * rows, width), bf16),
            pltpu.VMEM((steps, 2, rows, width), bf16),
            pltpu.VMEM((depth, 2, rows, width), bf16),
            pltpu.VMEM((depth, rows, width), bf16),
        ]
        + semaphores,
        compiler_params=pltpu.CompilerParams(
            collective_id=1, has_side_effects=True, vmem_limit_bytes=58 * 2**20
        ),
        cost_estimate=pl.CostEstimate(
            flops=18 * total * width * hidden, bytes_accessed=20 * total * width, transcendentals=0
        ),
        name="experts",
    )(expert_input, cotangent_all, prob, gate_weight, up_weight, down_weight)


def late_kernel(
    count,
    cuts,
    pay_ref,
    gain_ref,
    tokens_ref,
    attended_ref,
    away_hbm,
    both_away,
    down_away,
    all_out,
    here_hbm,
    both_here,
    down_here,
    attention_all,
    attended_all,
    arrived,
    y_out,
    y_in,
    kept,
    z_in,
    mine,
    swap_send,
    swap_recv,
    m_send,
    m_recv,
    d_send,
    d_recv,
    a_send,
    a_recv,
    y_send,
    y_recv,
    z_send,
    z_recv,
    g_send,
    g_recv,
):
    first, last = cuts
    depth, _, lines, rows = pay_ref.shape
    half = all_out.shape[2]
    me, dp = lax.axis_index("expert"), lax.axis_index("dp")
    place = me - 4 * quotient(me, 4)
    level = quotient(me, 4)
    peer = {"dp": 1 - dp}
    order = [z for z in (2, 3) if z < depth] + list(range(4, depth)) + [1, 0]
    meet(count, True)

    def at_place(ref):
        return lambda index: ref.at[
            pl.ds(pl.multiple_of((index - 4 * quotient(index, 4)) * rows, rows), rows)
        ]

    gathers = [
        Gather(attended_ref, at_place(attended_all), 4, d_send, d_recv),
    ]
    columns = pl.ds(pl.multiple_of(place * rows, rows), rows)

    def share(by):
        there = flip(place, by)
        return send(
            pay_ref.at[:, there],
            arrived.at[:, :, columns],
            a_send.at[by],
            a_recv.at[by],
            expert_at(flip(me, by)),
        )

    swap_down = send(down_away, down_here, swap_send.at[0], swap_recv.at[0], peer)
    swap_both = send(both_away, both_here, swap_send.at[1], swap_recv.at[1], peer)

    def outputs_z(z_rel):
        return send(
            away_hbm.at[z_rel - 1],
            here_hbm.at[z_rel - 1],
            m_send.at[z_rel],
            m_recv.at[z_rel],
            expert_at(flip(me, 4 * z_rel)),
        )

    for gather in gathers:
        gather.begin()
    for by in (2, 3, 1):
        share(by).start()
    swap_down.start()
    for z_rel in range(1, depth):
        outputs_z(z_rel).start()
    attended_all[columns, :] = attended_ref[...]
    arrived[:, :, columns] = pay_ref[:, place]

    def norm_rows(index, carry):
        at = pl.ds(pl.multiple_of(index * rows, rows), rows)
        values = tokens_ref[at, :].astype(jnp.float32)
        mean = jnp.mean(values * values, -1, keepdims=True)
        factor = lax.rsqrt(mean + EPSILON)
        for side, which in ((0, dp), (1, 1 - dp)):
            source = pl.ds(pl.multiple_of(which * half, half), half)
            here = slice(side * half, (side + 1) * half)
            normed = tokens_ref[at, source].astype(jnp.float32) * factor
            attention_all[at, here] = (normed * gain_ref[:, here]).astype(jnp.bfloat16)
        return carry

    lax.fori_loop(0, 4, norm_rows, 0)
    for gather in gathers:
        gather.pass_x(0)
    for by in (2, 3, 1):
        there = flip(place, by)
        send(
            pay_ref.at[:, there],
            arrived.at[:, :, pl.ds(pl.multiple_of(there * rows, rows), rows)],
            a_send.at[by],
            a_recv.at[by],
            expert_at(flip(me, by)),
        ).wait()
    for gather in gathers:
        gather.wait(1)
        gather.wait(3)
        gather.wait_sends()

    blank = jnp.zeros((lines - last - (lines - last) // 2, half), jnp.float32)

    def tile_of(z_rel, side):
        at = flip(level, z_rel)
        where = slice(side * half, (side + 1) * half)
        extra = arrived[at, last:, :].astype(jnp.float32)
        summed = extra[:, :rows]
        for index in range(1, 4):
            summed = summed + extra[:, index * rows : (index + 1) * rows]
        edge = summed.shape[0] // 2
        summed = summed[side * edge : (side + 1) * edge]
        return jnp.concatenate(
            [
                dot_on(arrived[at, :first, :], attention_all[:, where], 1, 0),
                dot_on(arrived[at, first:last, :], attended_all[:, where], 1, 0),
                jnp.concatenate([summed, jnp.zeros((edge, half - rows), jnp.float32)], 1),
                blank,
            ],
            0,
        )

    def over_y(z_rel):
        return send(
            y_out.at[z_rel], y_in.at[z_rel], y_send.at[z_rel], y_recv.at[z_rel], peer
        )

    def over_z(z_rel):
        return send(
            y_out.at[z_rel],
            z_in.at[z_rel],
            z_send.at[z_rel],
            z_recv.at[z_rel],
            expert_at(flip(me, 4 * z_rel)),
        )

    for z_rel in order:
        y_out[z_rel] = tile_of(z_rel, 1).astype(jnp.bfloat16)
        over_y(z_rel).start()
    for z_rel in order:
        kept[z_rel] = tile_of(z_rel, 0)
    total = None
    for z_rel in order:
        over_y(z_rel).wait()
        total = kept[z_rel] + y_in[z_rel].astype(jnp.float32)
        if z_rel:
            y_out[z_rel] = total.astype(jnp.bfloat16)
            over_z(z_rel).start()
    swap_both.start()
    for z_rel in order[:-1]:
        over_z(z_rel).wait()
        total = total + z_in[z_rel].astype(jnp.float32)
    mine[...] = total.astype(jnp.bfloat16)
    gather = Gather(mine, lambda index: all_out.at[index], count, g_send, g_recv)
    gather.begin(range(12, count, 4))
    all_out[me] = mine[...]
    gather.rest()
    swap_down.wait()
    for z_rel in range(1, depth):
        outputs_z(z_rel).wait()
    swap_both.wait()


def late_sums(payload, gain, tokens, attended, away, both, down, cuts):
    count, lines, rows = payload.shape
    width = attended.shape[1]
    half, depth = width // 2, count // 4
    local = pl.BlockSpec(memory_space=pltpu.VMEM)
    anywhere = pl.BlockSpec(memory_space=pl.ANY)
    bf16 = jnp.bfloat16
    sizes = (2, depth, 4, 4, depth, depth, count)
    return pl.pallas_call(
        functools.partial(late_kernel, count, cuts),
        out_shape=[
            jax.ShapeDtypeStruct((count, lines, half), bf16),
            jax.ShapeDtypeStruct(away.shape, bf16),
            jax.ShapeDtypeStruct(both.shape, bf16),
            jax.ShapeDtypeStruct(down.shape, bf16),
        ],
        in_specs=[local] * 4 + [anywhere] * 3,
        out_specs=[local] + [anywhere] * 3,
        scratch_shapes=[
            pltpu.VMEM((4 * rows, width), bf16),
            pltpu.VMEM((4 * rows, width), bf16),
            pltpu.VMEM((depth, lines, 4 * rows), bf16),
            pltpu.VMEM((depth, lines, half), bf16),
            pltpu.VMEM((depth, lines, half), bf16),
            pltpu.VMEM((depth, lines, half), jnp.float32),
            pltpu.VMEM((depth, lines, half), bf16),
            pltpu.VMEM((lines, half), bf16),
        ]
        + [pltpu.SemaphoreType.DMA((size,)) for size in sizes for _ in range(2)],
        compiler_params=pltpu.CompilerParams(
            collective_id=2, has_side_effects=True, vmem_limit_bytes=56 * 2**20
        ),
        name="late",
    )(
        payload.reshape(depth, 4, lines, rows),
        gain.astype(jnp.float32)[None, :],
        tokens,
        attended,
        away,
        both,
        down,
    )


def shards_together(
    tokens,
    segments,
    routes,
    first_gain,
    query_weight,
    key_projection_weight,
    value_projection_weight,
    out_weight,
    second_gain,
    router_weight,
    gate_weight,
    up_weight,
    down_weight,
    cotangent,
):
    token_rows = tokens.shape[0]
    expert_count = router_weight.shape[1]
    owner_count = lax.axis_size("expert")
    dp_count = lax.axis_size("dp")

    small = jnp.concatenate([router_weight, first_gain[:, None], second_gain[:, None]], 1)
    small = jnp.pad(small, ((0, 0), (0, -small.shape[1] % 128)))
    own = [query_weight, key_projection_weight, value_projection_weight, out_weight, small]
    cotangent_all = lax.all_gather(cotangent, "expert", axis=0, tiled=True)
    other, tokens_near = front(own, tokens)
    query_mat, key_matrix, value_matrix, out_mat, small = (list(p) for p in zip(own, other))
    small_mat = jnp.concatenate(small, 0)
    router_mat = turn(small_mat[:, :expert_count], 0)
    gain_first = small_mat[:, expert_count]
    gain_second = turn(small_mat[:, expert_count + 1], 0)

    hidden, saved = halves_forward(
        tokens, segments, gain_first, query_mat, key_matrix, value_matrix, out_mat
    )
    normed_second, factor_second, expert_input = normalize(hidden, gain_second)
    route_prob, chosen_hot = route_weights(expert_input, router_mat, routes)
    dense_prob = jnp.sum(chosen_hot * route_prob[:, :, None], 1)
    prob = jnp.broadcast_to(dense_prob.T[:, None, :], (owner_count, 8, token_rows))
    grad_sum, mixture, mix_away, back_prob, mine, mine_down, peer, peer_down = experts(
        expert_input, cotangent_all, prob, gate_weight, up_weight, down_weight
    )
    grad_prob = jnp.sum(chosen_hot * back_prob[:, 0, :].T[:, None, :], -1)
    router_grad = route_back(route_prob, grad_prob, chosen_hot)
    grad_expert_input = grad_sum + matrix_multiply(router_grad, router_mat.T)
    router_wgrad = matrix_multiply(router_grad.T, expert_input)
    grad_normed, second_gain_grad = normalize_back(
        grad_expert_input, normed_second, factor_second, gain_second
    )
    grad_hidden = cotangent.astype(jnp.float32) + grad_normed
    grad_tokens, first_gain_grad, late = halves_backward(
        grad_hidden, saved, gain_first, query_mat, key_matrix, value_matrix, out_mat
    )

    extras = jnp.concatenate(
        [router_wgrad, first_gain_grad[None, :], second_gain_grad[None, :]], 0
    )
    slices = [
        grad.T.reshape(owner_count, grad.shape[1] // owner_count, token_rows) for grad in late
    ]
    extra_count, extra_width = extras.shape
    part = extra_width // (owner_count * dp_count)
    spread = (
        extras.reshape(extra_count, dp_count, owner_count, part)
        .transpose(2, 1, 0, 3)
        .reshape(owner_count, dp_count, extra_count * part)
        .astype(jnp.bfloat16)
    )
    spread = jnp.pad(spread, ((0, 0), (0, 0), (0, -spread.shape[2] % (8 * token_rows))))
    spread = turn(spread, 1).reshape(owner_count, -1, token_rows)
    payload = jnp.concatenate(slices + [spread], 1)
    last = sum(piece.shape[1] for piece in slices)
    cuts = (last - slices[3].shape[1], last)
    everything, mix_here, peer, peer_down = late_sums(
        payload, gain_first, tokens_near, saved[7], mix_away, peer, peer_down, cuts
    )
    shares, (gate_share, up_share, down_share, output) = finish(
        everything,
        [piece.shape[1] for piece in slices],
        mine,
        mine_down,
        peer,
        peer_down,
        hidden,
        mixture,
        mix_here,
    )
    edge = spread.shape[1] // 2
    extras = everything[:, last : last + edge, :token_rows].reshape(owner_count, -1)
    extras = extras[:, : extra_count * part].reshape(owner_count, extra_count, part)
    extras = extras.transpose(1, 0, 2).reshape(extra_count, -1).astype(jnp.float32)
    query_share, key_share, value_share, out_share = shares
    return (
        output,
        grad_tokens,
        extras[expert_count],
        query_share,
        key_share,
        value_share,
        out_share,
        extras[expert_count + 1],
        extras[:expert_count].T,
        gate_share,
        up_share,
        down_share,
    )


def solution(mesh):
    placed = (
        P(("dp", "expert"), None),
        P(("dp", "expert")),
        P(("dp", "expert"), None),
        P("dp"),
        P("dp", None),
        P("dp", None),
        P("dp", None),
        P("dp", None),
        P("dp"),
        P("dp", None),
        P("expert", None, None),
        P("expert", None, None),
        P("expert", None, None),
        P(("dp", "expert"), None),
    )
    owners = mesh.shape["expert"]
    together = mesh.shape["dp"] == 2 and owners >= 8 and owners & (owners - 1) == 0
    return jax.shard_map(
        shards_together if together else shards,
        mesh=mesh,
        in_specs=placed,
        out_specs=(
            P(("dp", "expert"), None),
            P(("dp", "expert"), None),
            P("dp"),
            P("dp", None),
            P("dp", None),
            P("dp", None),
            P("dp", None),
            P("dp"),
            P("dp", None),
            P("expert", "dp", None),
            P("expert", "dp", None),
            P("expert", None, "dp"),
        ),
        check_vma=False,
    )
```
